32 devices in a mesh: dp: 16 (over z, y, x), seq: 2 (over core).
Axes of the slice: x: 2, y: 2, z: 4, core: 2. Of those that a mesh axis runs over, the one named last changes fastest.
Arguments:
- tokens: bfloat16 [16, 640, 768], P('dp', 'seq'), may hold values from -6 to 6
- cotangent: bfloat16 [16, 640, 768], P('dp', 'seq'), may hold values from -6 to 6
- group: int32 [16], P('dp'), may hold values 0 or 1
- select: int32 [16, 640], P('dp', 'seq'), may hold values from 0 to 1, as said below
- w_qkv: bfloat16 [768, 2304], replicated, may hold values from -0.21875 to 0.21875
- b_query: float32 [768], replicated, may hold values from -3 to 3
- b_value: float32 [768], replicated, may hold values from -0.625 to 0.625
- w_out: bfloat16 [768, 768], replicated, may hold values from -1.75 to 1.75
- b_out: float32 [768], replicated, may hold values from -1.75 to 1.75
- w_up: bfloat16 [768, 3072], replicated, may hold values from -0.21875 to 0.21875
- b_up: float32 [3072], replicated, may hold values from -3 to 3
- w_down: bfloat16 [3072, 768], replicated, may hold values from -0.109375 to 0.109375
- b_down: float32 [768], replicated, may hold values from -1.75 to 1.75
- ln1_gain: float32 [768], replicated, may hold values from 0.5 to 1.5
- ln1_bias: float32 [768], replicated, may hold values from -1.75 to 1.75
- ln2_gain: float32 [768], replicated, may hold values from 0.5 to 1.5
- ln2_bias: float32 [768], replicated, may hold values from -1.75 to 1.75
- w_router: float32 [768], replicated, may hold values from -0.21875 to 0.21875
Outputs:
- output: bfloat16 [16, 640, 768], P('dp', 'seq')
- input_grad: bfloat16 [16, 640, 768], P('dp', 'seq')
- grad_qkv: float32 [768, 2304], P('dp')
- grad_query_bias: float32 [768], P('dp')
- grad_value_bias: float32 [768], P('dp')
- grad_out: float32 [768, 768], P('dp')
- grad_out_bias: float32 [768], P('dp')
- grad_up: float32 [768, 3072], P('dp')
- grad_up_bias: float32 [3072], P('dp')
- grad_down: float32 [3072, 768], P('dp')
- grad_down_bias: float32 [768], P('dp')
- grad_ln1_gain: float32 [768], P('dp')
- grad_ln1_bias: float32 [768], P('dp')
- grad_ln2_gain: float32 [768], P('dp')
- grad_ln2_bias: float32 [768], P('dp')
- grad_router: float32 [768], P('dp')
- fractions: float32 [16, 3], replicated
The draws below stay inside these ranges and needn't reach their ends.
Inputs may be any that keep to these rules, and one draw needn't show every extreme that they name: `select`: slots 0, 197 and 394 of every pack are 1.
All inputs are finite; a program needn't handle non-finite values. No bound on the sum of `group` on one device may be relied on, other than what follows from the above.
Results may differ from the reference program's by a relative error of at most 0.04.
Values may be sent and summed in bfloat16 or wider, within the bound.
A program may use at most 192 MiB of HBM per device.

```python
from functools import partial
import jax
import jax.numpy as jnp
from jax import lax

WIDTH = 768
HEADS = 12
HEAD_DIM = 64
MLP_DIM = 3072
PAD_LEN = 640
LONG_LEN = 577
SHORT_LEN = 197
PACKS = 16


def draw_select(key, part):
    rate_key, digit_key = jax.random.split(jax.random.fold_in(key, 23))
    select_rate = jax.random.randint(rate_key, (PACKS, 1), 3, 8)
    raw_digits = jax.random.randint(digit_key, (PACKS, PAD_LEN), 0, 10)
    chosen = (raw_digits < select_rate).astype(jnp.int32)
    slot_index = jnp.arange(PAD_LEN, dtype=jnp.int32)[None, :]
    forced = (slot_index == 0) | (slot_index == SHORT_LEN) | (slot_index == 2 * SHORT_LEN)
    return jnp.where(forced, 1, chosen).astype(jnp.int32)


def touch_ends(values, own_key, low, high):
    longest = values.shape.index(max(values.shape))
    spots = []
    for shift in (0, 1):
        where = [jax.random.randint(jax.random.fold_in(own_key, axis), (), 0, length) for axis, length in enumerate(values.shape)]
        where[longest] = (where[longest] + shift) % values.shape[longest]
        spots.append(tuple(where))
    return values.at[spots[0]].set(low).at[spots[1]].set(high)


def block_levels(key, extent, cuts, smallest, top_value):
    gain, own = 1.0, jax.random.fold_in(key, 6)
    for position, blocks in cuts:
        heights = jnp.exp(jax.random.uniform(jax.random.fold_in(own, position), (blocks,), jnp.float32, smallest / len(cuts), top_value / len(cuts)))
        gain = gain * jnp.repeat(heights, extent[position] // blocks).reshape([-1 if axis == position else 1 for axis in range(len(extent))])
    return gain


def scatter_about(rng, shape, width, reach, cuts=(), held_as=jnp.bfloat16):
    loudness = block_levels(rng, shape, cuts, -0.22, 0.18) if cuts else 1.0
    values = jax.random.normal(rng, shape, jnp.float32) * width * loudness
    return jnp.minimum(jnp.maximum(values, -reach), reach).astype(held_as)


def setup_inputs(seed: int = 0) -> dict:
    key_of = jax.random.split(jax.random.key(seed), 19)
    tokens = scatter_about(key_of[0], (PACKS, PAD_LEN, WIDTH), 1.0, 6.0, ((0, 16), (1, 2)))
    cotangent = scatter_about(key_of[1], (PACKS, PAD_LEN, WIDTH), 1.0, 6.0, ((0, 16), (1, 2)))
    group = touch_ends((jax.random.randint(key_of[2], (PACKS,), 0, 2) < 1).astype(jnp.int32), jax.random.fold_in(key_of[2], 1), 0, 1)
    select = draw_select(jax.random.fold_in(key_of[18], 71), 0)
    w_qkv = scatter_about(key_of[4], (WIDTH, 3 * WIDTH), WIDTH ** -0.5, 0.21875)
    b_query = scatter_about(key_of[5], (WIDTH,), 0.5, 3.0, (), jnp.float32)
    b_value = scatter_about(key_of[6], (WIDTH,), 0.1, 0.625, (), jnp.float32)
    w_out = scatter_about(key_of[7], (WIDTH, WIDTH), (WIDTH // 64) ** -0.5, 1.75)
    b_out = scatter_about(key_of[8], (WIDTH,), 0.3, 1.75, (), jnp.float32)
    w_up = scatter_about(key_of[9], (WIDTH, MLP_DIM), WIDTH ** -0.5, 0.21875)
    b_up = scatter_about(key_of[10], (MLP_DIM,), 0.5, 3.0, (), jnp.float32)
    w_down = scatter_about(key_of[11], (MLP_DIM, WIDTH), MLP_DIM ** -0.5, 0.109375)
    b_down = scatter_about(key_of[12], (WIDTH,), 0.3, 1.75, (), jnp.float32)
    ln1_gain = jnp.clip(1.0 + 0.1 * jax.random.normal(key_of[13], (WIDTH,), jnp.float32), 0.5, 1.5)
    ln1_bias = scatter_about(key_of[14], (WIDTH,), 0.3, 1.75, (), jnp.float32)
    ln2_gain = jnp.clip(1.0 + 0.1 * jax.random.normal(key_of[15], (WIDTH,), jnp.float32), 0.5, 1.5)
    ln2_bias = scatter_about(key_of[16], (WIDTH,), 0.3, 1.75, (), jnp.float32)
    w_router = scatter_about(key_of[17], (WIDTH,), WIDTH ** -0.5, 0.21875, (), jnp.float32)
    return {"tokens": tokens, "cotangent": cotangent, "group": group, "select": select, "w_qkv": w_qkv, "b_query": b_query, "b_value": b_value, "w_out": w_out, "b_out": b_out, "w_up": w_up, "b_up": b_up, "w_down": w_down, "b_down": b_down, "ln1_gain": ln1_gain, "ln1_bias": ln1_bias, "ln2_gain": ln2_gain, "ln2_bias": ln2_bias, "w_router": w_router}


@jax.custom_vjp
def low(v):
    return lax.optimization_barrier(v.astype(jnp.bfloat16)).astype(jnp.float32)

@jax.custom_vjp
def low_back(v):
    return v

def low_keep(v):
    return (low(v), None)

def low_pass(kept, grad):
    return (grad,)

def back_keep(v):
    return (v, None)

def back_low(kept, grad):
    return (low(grad),)
low.defvjp(low_keep, low_pass)
low_back.defvjp(back_keep, back_low)
epsilon = 1e-06
masked_floor = -1000000000.0
highest = lax.Precision.HIGHEST

def norm_rows(values, norm_gain, norm_shift):
    average = lax.optimization_barrier(jnp.mean(values, axis=-1, keepdims=True))
    centred = values - average
    variance = lax.optimization_barrier(jnp.mean(centred * centred, axis=-1, keepdims=True))
    return centred * lax.rsqrt(variance + epsilon) * norm_gain + norm_shift

def image_block(params, image_rows, active, segment):
    w_qkv, b_query, b_value, w_out, b_out, w_up, b_up, w_down, b_down, ln1_gain, ln1_bias, ln2_gain, ln2_bias, w_router = params
    router = jax.nn.sigmoid(jnp.dot(image_rows, w_router, precision=highest))
    normed = low(norm_rows(image_rows, ln1_gain, ln1_bias))
    qkv_bias = jnp.concatenate([b_query, jnp.zeros_like(b_query), b_value])
    triple = low_back(low(jnp.dot(normed, w_qkv, precision=highest) + qkv_bias))
    queries = triple[:, :WIDTH].reshape(PAD_LEN, HEADS, HEAD_DIM)
    key_heads = triple[:, WIDTH:2 * WIDTH].reshape(PAD_LEN, HEADS, HEAD_DIM)
    value_heads = triple[:, 2 * WIDTH:].reshape(PAD_LEN, HEADS, HEAD_DIM)
    scores = low_back(jnp.einsum('qhe,khe->hqk', queries, key_heads, precision=highest) * HEAD_DIM ** (-0.5))
    key_live = (active[None, :] > 0.5) & (segment[:, None] == segment[None, :])
    live_weight = key_live.astype(jnp.float32)[None, :, :]
    masked = jnp.where(key_live[None, :, :], scores, masked_floor)
    row_max = lax.optimization_barrier(jnp.max(masked, axis=-1, keepdims=True))
    exponent = jnp.exp(masked - row_max) * live_weight
    weights = low(exponent / lax.optimization_barrier(jnp.sum(exponent, axis=-1, keepdims=True)))
    mixed_heads = jnp.einsum('hqk,khe->qhe', weights, value_heads, precision=highest)
    mixed_rows = low_back(low(mixed_heads.reshape(PAD_LEN, WIDTH)))
    attended = low_back(jnp.dot(mixed_rows, w_out, precision=highest) + b_out)
    summed = image_rows + attended
    second = low(norm_rows(summed, ln2_gain, ln2_bias))
    pre_act = low_back(jnp.dot(second, w_up, precision=highest) + b_up)
    hidden = low(jax.nn.gelu(pre_act, approximate=False))
    branch_mlp = low_back(jnp.dot(hidden, w_down, precision=highest) + b_down)
    return image_rows + active[:, None] * router[:, None] * (attended + branch_mlp)

def reference(tokens, cotangent, group, select, w_qkv, b_query, b_value, w_out, b_out, w_up, b_up, w_down, b_down, ln1_gain, ln1_bias, ln2_gain, ln2_bias, w_router):
    positions = jnp.arange(PAD_LEN, dtype=jnp.int32)
    short_place = jnp.minimum(positions // SHORT_LEN, 2).astype(jnp.int32)
    segment = jnp.where(group[:, None] == 1, 0, short_place[None, :]).astype(jnp.int32)
    ends = jnp.where(group == 1, LONG_LEN, 3 * SHORT_LEN).astype(jnp.int32)
    active = ((select > 0) & (positions[None, :] < ends[:, None])).astype(jnp.float32)
    params = tuple((array_in.astype(jnp.float32) for array_in in (w_qkv, b_query, b_value, w_out, b_out, w_up, b_up, w_down, b_down, ln1_gain, ln1_bias, ln2_gain, ln2_bias, w_router)))
    xfloat = tokens.astype(jnp.float32)

    def forward(weights_in, inputs_in):
        checked = jax.checkpoint(partial(image_block, weights_in))

        def run_image(pieces):
            return checked(pieces[0], pieces[1], pieces[2])
        return lax.map(run_image, (inputs_in, active, segment))
    result, pullback = jax.vjp(forward, params, xfloat)
    grads, grad_input = pullback(cotangent.astype(jnp.float32))
    places = jnp.arange(3, dtype=jnp.int32)
    onehot = (segment[:, :, None] == places[None, None, :]).astype(jnp.float32)
    counts = lax.optimization_barrier(jnp.sum(active[:, :, None] * onehot, axis=1))
    image_lengths = jnp.where(group == 1, LONG_LEN, SHORT_LEN).astype(jnp.float32)
    fractions = counts / image_lengths[:, None]
    return (result.astype(jnp.bfloat16), grad_input.astype(jnp.bfloat16), grads[0], grads[1], grads[2], grads[3], grads[4], grads[5], grads[6], grads[7], grads[8], grads[9], grads[10], grads[11], grads[12], grads[13], fractions)
```

```python
from functools import partial

import jax
import jax.numpy as jnp
from jax import lax
from jax.experimental import pallas as pl
from jax.experimental.pallas import tpu as pltpu
from jax.sharding import PartitionSpec as P

HEADS = 12
HEAD_DIM = 64
PAD_LEN = 640
LONG_LEN = 577
SHORT_LEN = 197
WIDTH = 768
HIDDEN = 3072

epsilon = 1e-06
masked_floor = -1000000000.0
MESH_ID = pl.DeviceIdType.MESH
bf16 = jnp.bfloat16
f32 = jnp.float32

HALF = WIDTH // 2
OWN = PAD_LEN // 2
HID = HIDDEN // 2
BLOCKS = HID // HALF
PAIRS = HALF // 128
MT = 320
AT = 128
SMALL = 16
PIECES = 12


def dot_nn(a, b):
    return lax.dot_general(a, b, (((1,), (0,)), ((), ())), preferred_element_type=f32)


def dot_nt(a, b):
    return lax.dot_general(a, b, (((1,), (1,)), ((), ())), preferred_element_type=f32)


def dot_tn(a, b):
    return lax.dot_general(a, b, (((0,), (0,)), ((), ())), preferred_element_type=f32)


def row_stats(values):
    average = jnp.mean(values, axis=-1, keepdims=True)
    centred = values - average
    variance = jnp.mean(centred * centred, axis=-1, keepdims=True)
    rstd = lax.rsqrt(variance + epsilon)
    return centred * rstd, rstd


def norm_back(unit, rstd, grad, gain):
    q = grad * gain
    return rstd * (
        q - jnp.mean(q, axis=-1, keepdims=True) - unit * jnp.mean(q * unit, axis=-1, keepdims=True)
    )


def layer_kernel(
    tokens, cotangent, group, select, w_qkv, b_query, b_value, w_out, b_out, w_up, b_up, w_down,
    b_down, ln1_gain, ln1_bias, ln2_gain, ln2_bias, w_router,
    o_output, o_input, o_qkv, o_out, o_up, o_down, o_small, o_frac,
    X, G, SEL, VEC, BUP, NRM, WQ, WO, WU, WD, TRI, PR, MIX, SUM, SEC, GM, BIAS, GATE, ACT,
    HIDJ, GPJ, ACCD, ACCS, GSB, GSR, DSB, DSR, GATT, GMX, DTR, DK, DV, OUTB, INB, NSB, NSR,
    S4, R14, R24, R34, F4, S1, R11, R21, R31, F1, SB, SBR, FR, FRR,
    lsem, esem_s, esem_r, csem_s, csem_r, ssem_s, ssem_r, fsem_l, fsem_s, fsem_r,
):
    dp = lax.axis_index("dp")
    c = lax.axis_index("seq")
    x = lax.rem(dp, 2)
    y = lax.rem(lax.div(dp, 2), 2)
    z = lax.div(dp, 4)
    peer = (dp, 1 - c)
    xp = ((z * 2 + y) * 2 + (1 - x), c)
    yp = ((z * 2 + (1 - y)) * 2 + x, c)
    zs = [lax.rem(z + k, 4) for k in (1, 2, 3)]
    zp = [((zk * 2 + y) * 2 + x, c) for zk in zs]
    own = pl.multiple_of(c * OWN, OWN)
    oth = pl.multiple_of((1 - c) * OWN, OWN)
    chalf = pl.multiple_of(c * HALF, HALF)
    chid = pl.multiple_of(c * HID, HID)
    lead = (c == 0).astype(f32)

    barrier = pltpu.get_barrier_semaphore()
    for other in [peer, xp, yp] + zp:
        pl.semaphore_signal(barrier, inc=1, device_id=other, device_id_type=MESH_ID)

    loads = {}

    def load(name, src, dst):
        copy = pltpu.make_async_copy(src, dst, lsem.at[len(loads)])
        copy.start()
        loads[name] = copy

    load("tok", tokens.at[0], X.at[pl.ds(own, OWN)])
    load("sel", select, SEL.at[c])
    for i, v in enumerate(
        (b_query, b_value, b_out, b_down, ln1_gain, ln1_bias, ln2_gain, ln2_bias, w_router)
    ):
        load("v%d" % i, v, VEC.at[i])
    for k in range(3):
        load(
            "wq%d" % k,
            w_qkv.at[:, pl.ds(pl.multiple_of(k * WIDTH + c * HALF, 128), HALF)],
            WQ.at[:, pl.ds(k * HALF, HALF)],
        )
    load("cot", cotangent.at[0], G.at[pl.ds(own, OWN)])
    load("bup", b_up, BUP)
    load("wo", w_out, WO)
    load("wu", w_up.at[:, pl.ds(chid, HID)], WU)
    load("wd", w_down.at[pl.ds(chid, HID)], WD)

    pl.semaphore_wait(barrier, 6)

    sends = []
    counts = {"e": 0, "c": 0}

    def to_core(src, dst):
        i = counts["e"]
        counts["e"] += 1
        copy = pltpu.make_async_remote_copy(
            src_ref=src, dst_ref=dst, send_sem=esem_s.at[i], recv_sem=esem_r.at[i],
            device_id=peer, device_id_type=MESH_ID,
        )
        copy.start()
        sends.append(copy)
        return copy

    ex_sel = to_core(select, SEL.at[c])
    ex_tok = to_core(tokens.at[0], X.at[pl.ds(own, OWN)])
    ex_cot = to_core(cotangent.at[0], G.at[pl.ds(own, OWN)])

    SB[...] = jnp.zeros_like(SB)
    FR[...] = jnp.zeros_like(FR)

    loads["sel"].wait()
    ex_sel.wait_recv()
    gv = group[...]
    long_row = jnp.broadcast_to(gv, (1, PAD_LEN)) == 1
    pos_row = lax.broadcasted_iota(jnp.int32, (1, PAD_LEN), 1)
    short_row = (pos_row >= SHORT_LEN).astype(jnp.int32) + (pos_row >= 2 * SHORT_LEN).astype(jnp.int32)
    place_row = jnp.where(long_row, 0, short_row)
    end_row = jnp.where(long_row, LONG_LEN, 3 * SHORT_LEN)
    long_col = jnp.broadcast_to(gv, (PAD_LEN, 1)) == 1
    pos_col = lax.broadcasted_iota(jnp.int32, (PAD_LEN, 1), 0)
    short_col = (pos_col >= SHORT_LEN).astype(jnp.int32) + (pos_col >= 2 * SHORT_LEN).astype(jnp.int32)
    place_col = jnp.where(long_col, 0, short_col)
    end_col = jnp.where(long_col, LONG_LEN, 3 * SHORT_LEN)
    sel_row = jnp.zeros((8, PAD_LEN), f32)
    sel_col = jnp.zeros((PAD_LEN, 8), f32)
    for part in range(2):
        bits = jnp.broadcast_to((SEL[part] > 0).astype(f32), (8, OWN)).astype(bf16)
        spread = (
            lax.broadcasted_iota(jnp.int32, (PAD_LEN, OWN), 0)
            == lax.broadcasted_iota(jnp.int32, (PAD_LEN, OWN), 1) + part * OWN
        ).astype(f32).astype(bf16)
        sel_row = sel_row + dot_nt(bits, spread)
        sel_col = sel_col + dot_nt(spread, bits)
    act_row = jnp.where(pos_row < end_row, sel_row[0:1, :], 0.0)
    act_col = jnp.where(pos_col < end_col, sel_col[:, 0:1], 0.0)
    ACT[...] = act_col
    BIAS[...] = jnp.where(
        (jnp.broadcast_to(act_row, (PAD_LEN, PAD_LEN)) > 0.5)
        & (jnp.broadcast_to(place_col, (PAD_LEN, PAD_LEN)) == jnp.broadcast_to(place_row, (PAD_LEN, PAD_LEN))),
        0.0,
        -1e30,
    )
    lane = lax.broadcasted_iota(jnp.int32, (1, 128), 1)
    length = jnp.where(jnp.broadcast_to(gv, (1, 1)) == 1, float(LONG_LEN), float(SHORT_LEN))
    shares = jnp.zeros((1, 128), f32)
    for j in range(3):
        count = jnp.sum(jnp.where(place_row == j, act_row, 0.0), axis=1, keepdims=True)
        shares = jnp.where(lane == j, count / length, shares)
    FR[0, pl.ds(dp, 1), :] = shares * lead

    loads["tok"].wait()
    for i in range(9):
        loads["v%d" % i].wait()
    ex_tok.wait_recv()

    def vec(i):
        return VEC[i]

    @pl.loop(0, PAD_LEN // AT)
    def _(t):
        rows = pl.ds(pl.multiple_of(t * AT, AT), AT)
        xf = X[rows, :].astype(f32)
        unit, _ = row_stats(xf)
        NRM[rows, :] = (unit * vec(4) + vec(5)).astype(bf16)
        logit = jnp.sum(xf * vec(8), axis=-1, keepdims=True)
        GATE[rows, :] = 1.0 / (1.0 + jnp.exp(-logit))

    for k in range(3):
        loads["wq%d" % k].wait()
    qb = VEC[0, :, pl.ds(chalf, HALF)]
    vb = VEC[1, :, pl.ds(chalf, HALF)]

    @pl.loop(0, PAD_LEN // MT)
    def _(t):
        rows = pl.ds(pl.multiple_of(t * MT, MT), MT)
        nr = NRM[rows, :]
        for k in range(3):
            r = dot_nn(nr, WQ[:, k * HALF : (k + 1) * HALF])
            if k == 0:
                r = (r + qb).astype(bf16).astype(f32) * HEAD_DIM ** (-0.5)
            if k == 2:
                r = r + vb
            TRI[rows, k * HALF : (k + 1) * HALF] = r.astype(bf16)

    low_lanes = lax.broadcasted_iota(jnp.int32, (1, 128), 1) < HEAD_DIM

    def head_part(v, side):
        keep = low_lanes if side == 0 else jnp.logical_not(low_lanes)
        return jnp.where(keep, v, jnp.zeros_like(v))

    def pair_lanes(hp):
        return [slice(k * HALF + hp * 128, k * HALF + hp * 128 + 128) for k in range(3)]

    ex_mix = []
    for hp in range(PAIRS):
        qlanes, klanes, vlanes = pair_lanes(hp)

        @pl.loop(0, PAD_LEN // AT)
        def _(t):
            rows = pl.ds(pl.multiple_of(t * AT, AT), AT)
            qp = TRI[rows, qlanes]
            kp = TRI[:, klanes]
            vp = TRI[:, vlanes]
            bias = BIAS[rows, :]
            total = jnp.zeros((AT, 128), f32)
            for side in range(2):
                s = dot_nt(head_part(qp, side), kp) + bias
                e = jnp.exp(s - jnp.max(s, axis=-1, keepdims=True))
                w = (e * (1.0 / jnp.sum(e, axis=-1, keepdims=True))).astype(bf16)
                PR[2 * hp + side, rows, :] = w
                total = total + dot_nn(w, head_part(vp, side))
            MIX[c, rows, qlanes] = total.astype(bf16)

        ex_mix.append(to_core(MIX.at[c, :, qlanes], MIX.at[c, :, qlanes]))

    loads["cot"].wait()
    ex_cot.wait_recv()
    loads["wo"].wait()

    @pl.loop(0, PAD_LEN // AT)
    def _(t):
        rows = pl.ds(pl.multiple_of(t * AT, AT), AT)
        GM[rows, :] = (ACT[rows, :] * GATE[rows, :] * G[rows, :].astype(f32)).astype(bf16)

    for e in ex_mix:
        e.wait_recv()

    @pl.loop(0, PAD_LEN // MT)
    def _(t):
        rows = pl.ds(pl.multiple_of(t * MT, MT), MT)
        att = dot_nn(MIX[0, rows, :], WO[0:HALF, :]) + dot_nn(MIX[1, rows, :], WO[HALF:, :]) + vec(2)
        s = X[rows, :].astype(f32) + att
        SUM[rows, :] = s
        unit, _ = row_stats(s)
        SEC[rows, :] = (unit * vec(6) + vec(7)).astype(bf16)

    for n in ("bup", "wu", "wd"):
        loads[n].wait()

    def remote(src, dst, dev, i):
        return pltpu.make_async_remote_copy(
            src_ref=src, dst_ref=dst, send_sem=csem_s.at[i], recv_sem=csem_r.at[i],
            device_id=dev, device_id_type=MESH_ID,
        )

    pieces = []

    def launch(order, src, r1, r2, r3, fin, dst_ref, only_z=None):
        number = len(pieces)
        base = number * 5
        zcount = r2.shape[0]
        st = {}

        def e2():
            st["c1"].wait_recv()
            for a in range(zcount):
                for b in range(2):
                    mine = src[a, b, x] if order == "xy" else src[a, y, b]
                    r1[a, b] = mine + r1[a, b]
            if order == "xy":
                st["c2"] = remote(r1.at[:, 1 - y], r2, yp, base + 1)
            else:
                st["c2"] = remote(r1.at[:, 1 - x], r2, xp, base + 1)
            st["c2"].start()
            sends.append(st["c2"])

        def e3():
            st["c2"].wait_recv()
            for a in range(zcount):
                r2[a] = (r1[a, y] if order == "xy" else r1[a, x]) + r2[a]
            st["c3"] = []
            for k in range(3):
                if only_z is None:
                    cp = remote(r2.at[zs[k]], r3.at[k], zp[k], base + 2 + k)
                    cp.start()
                else:
                    cp = remote(r2.at[0], r3.at[k], zp[k], base + 2 + k)
                    pl.when(zs[k] == only_z)(cp.start)
                st["c3"].append(cp)

        def e4():
            keep = pltpu.make_async_copy(fin, dst_ref, fsem_l.at[number])
            give = pltpu.make_async_remote_copy(
                src_ref=fin, dst_ref=dst_ref, send_sem=fsem_s.at[number],
                recv_sem=fsem_r.at[number], device_id=peer, device_id_type=MESH_ID,
            )

            def finish():
                for cp in st["c3"]:
                    cp.wait_recv()
                mine = r2[z] if only_z is None else r2[0]
                fin[...] = mine.astype(f32) + r3[0].astype(f32) + (r3[1].astype(f32) + r3[2].astype(f32))
                keep.start()
                give.start()

            if only_z is None:
                finish()
            else:
                pl.when(z == only_z)(finish)
            st["keep"], st["give"] = keep, give

        def e5():
            keep, give = st["keep"], st["give"]
            if only_z is None:
                keep.wait()
                give.wait()
                for cp in st["c3"]:
                    cp.wait_send()
            else:

                @pl.when(z == only_z)
                def _():
                    keep.wait()
                    give.wait_send()

                @pl.when(lax.div(z, 2) == 1 - c)
                def _():
                    @pl.when(z == only_z + 2 - 4 * c)
                    def _():
                        give.wait_recv()

                for k in range(3):
                    pl.when(zs[k] == only_z)(st["c3"][k].wait_send)

        first = src.at[:, :, 1 - x] if order == "xy" else src.at[:, 1 - y]
        st["c1"] = remote(first, r1, xp if order == "xy" else yp, base)
        st["c1"].start()
        sends.append(st["c1"])
        pieces.append((e2, e3, e4, e5))

    done = [0]

    def pump(n):
        for _ in range(n):
            i = done[0]
            for lag in range(4):
                if 0 <= i - lag < PIECES:
                    pieces[i - lag][lag]()
            done[0] += 1

    for j in range(BLOCKS):
        cols = slice(j * HALF, (j + 1) * HALF)
        bj = BUP[:, pl.ds(pl.multiple_of(chid + j * HALF, 128), HALF)]

        @pl.loop(0, PAD_LEN // MT)
        def _(t):
            rows = pl.ds(pl.multiple_of(t * MT, MT), MT)
            pre = dot_nn(SEC[rows, :], WU[:, cols]) + bj
            cdf = 0.5 * (1.0 + lax.erf(pre * (2.0 ** -0.5)))
            hid = (pre * cdf).astype(bf16)
            slope = cdf + pre * (0.3989422804014327 * jnp.exp(-0.5 * pre * pre))
            gh = dot_nt(GM[rows, :], WD[cols, :])
            gp = (gh * slope).astype(bf16)
            HIDJ[rows, :] = hid
            GPJ[rows, :] = gp
            d = dot_nn(hid, WD[cols, :])
            s = dot_nt(gp, WU[:, cols])
            if j == 0:
                ACCD[rows, :] = d
                ACCS[rows, :] = s
            else:
                ACCD[rows, :] += d
                ACCS[rows, :] += s

        for part in range(2):
            g = dot_tn(SEC[:, part * HALF : (part + 1) * HALF], GPJ[...])
            S4[j, 2 * part : 2 * part + 2] = g.astype(bf16).reshape(2, 2, 2, 48, HALF)
        launch(
            "xy" if j % 2 == 0 else "yx", S4.at[j], R14.at[j], R24.at[j], R34.at[j], F4.at[j],
            o_up.at[:, pl.ds(pl.multiple_of(chid + j * HALF, 128), HALF)],
        )
        SB[0, pl.ds(9 + 2 * c + j // 2, 1), (j % 2) * HALF : (j % 2 + 1) * HALF] = jnp.sum(
            GPJ[...].astype(f32), axis=0, keepdims=True
        )
        for part in range(2):
            g = dot_tn(HIDJ[...], GM[:, part * HALF : (part + 1) * HALF])
            S1[2 * (j // 2) + part, 0, j % 2] = g.astype(bf16).reshape(2, 192, HALF)
        if j % 2 == 1:
            for part in range(2):
                i = 2 * (j // 2) + part
                launch(
                    "xy" if part == 0 else "yx", S1.at[i], R11.at[i], R21.at[i], R31.at[i], F1.at[i],
                    o_down.at[:, part * HALF : (part + 1) * HALF], only_z=2 * c + j // 2,
                )

    @pl.loop(0, PAD_LEN // AT)
    def _(t):
        rows = pl.ds(pl.multiple_of(t * AT, AT), AT)
        GSB[rows, :] = ACCS[rows, :].astype(bf16)

    ex_gs = to_core(GSB, GSR)

    @pl.loop(0, OWN // 80)
    def _(t):
        r = pl.ds(pl.multiple_of(t * 80, 80), 80)
        DSB[r, :] = ACCD[pl.ds(pl.multiple_of(oth + t * 80, 80), 80), :].astype(bf16)

    ex_ds = to_core(DSB, DSR)
    ex_gs.wait_recv()

    zero_row = jnp.zeros((1, WIDTH), f32)

    def col_sum(v):
        return jnp.sum(v, axis=0, keepdims=True)

    def second_back(t, carry):
        rows = pl.ds(pl.multiple_of(t * AT, AT), AT)
        gs = ACCS[rows, :] + GSR[rows, :].astype(f32)
        unit, rstd = row_stats(SUM[rows, :])
        back = norm_back(unit, rstd, gs, vec(6))
        ACCS[rows, :] = back
        ga = (ACT[rows, :] * GATE[rows, :] * G[rows, :].astype(f32) + back).astype(bf16)
        GATT[rows, :] = ga
        return (
            carry[0] + col_sum(gs * unit), carry[1] + col_sum(gs), carry[2] + col_sum(ga.astype(f32)),
            carry[3] + col_sum(GM[rows, :].astype(f32)),
        )

    sums = lax.fori_loop(0, PAD_LEN // AT, second_back, (zero_row,) * 4)
    for row, value in zip((6, 7, 2, 3), sums):
        SB[0, row : row + 1, :] = value * lead

    for part in range(2):
        g = dot_tn(MIX[part], GATT[:, pl.ds(chalf, HALF)])
        S4[4, 2 * part : 2 * part + 2] = g.astype(bf16).reshape(2, 2, 2, 48, HALF)
    launch("xy", S4.at[4], R14.at[4], R24.at[4], R34.at[4], F4.at[4], o_out.at[:, pl.ds(chalf, HALF)])

    @pl.loop(0, PAD_LEN // MT)
    def _(t):
        rows = pl.ds(pl.multiple_of(t * MT, MT), MT)
        GMX[rows, :] = dot_nt(GATT[rows, :], WO[pl.ds(chalf, HALF), :]).astype(bf16)

    for hp in range(PAIRS):
        qlanes, klanes, vlanes = pair_lanes(hp)
        DK[...] = jnp.zeros_like(DK)
        DV[...] = jnp.zeros_like(DV)

        @pl.loop(0, PAD_LEN // AT)
        def _(t):
            rows = pl.ds(pl.multiple_of(t * AT, AT), AT)
            qp = TRI[rows, qlanes]
            kp = TRI[:, klanes]
            vp = TRI[:, vlanes]
            gp = GMX[rows, qlanes]
            dq = jnp.zeros((AT, 128), f32)
            for side in range(2):
                w = PR[2 * hp + side, rows, :]
                wf = w.astype(f32)
                gs = head_part(gp, side)
                dpr = dot_nt(gs, vp)
                delta = jnp.sum(wf * dpr, axis=-1, keepdims=True)
                ds = (wf * (dpr - delta)).astype(bf16)
                dq = dq + dot_nn(ds, head_part(kp, side))
                DK[...] += dot_tn(ds, head_part(qp, side))
                DV[...] += dot_tn(w, gs)
            DTR[rows, qlanes] = (dq * HEAD_DIM ** (-0.5)).astype(bf16)

        DTR[:, klanes] = DK[...].astype(bf16)
        DTR[:, vlanes] = DV[...].astype(bf16)

    for k in range(3):
        blk = DTR[:, k * HALF : (k + 1) * HALF]
        if k != 1:
            SB[0, k // 2 : k // 2 + 1, pl.ds(chalf, HALF)] = col_sum(blk.astype(f32))
        for part in range(2):
            g = dot_tn(NRM[:, part * HALF : (part + 1) * HALF], blk)
            S4[5 + k, 2 * part : 2 * part + 2] = g.astype(bf16).reshape(2, 2, 2, 48, HALF)
        launch(
            "yx" if k != 1 else "xy", S4.at[5 + k], R14.at[5 + k], R24.at[5 + k], R34.at[5 + k], F4.at[5 + k],
            o_qkv.at[:, pl.ds(pl.multiple_of(k * WIDTH + c * HALF, 128), HALF)],
        )

    NSB[...] = dot_nt(DTR[pl.ds(oth, OWN), :], WQ[...]).astype(bf16)
    ex_ns = to_core(NSB, NSR)
    ex_ds.wait_recv()
    ex_ns.wait_recv()

    def first_back(t, carry):
        r = pl.ds(pl.multiple_of(t * 80, 80), 80)
        rows = pl.ds(pl.multiple_of(own + t * 80, 80), 80)
        xf = X[rows, :].astype(f32)
        unit, rstd = row_stats(xf)
        gn = dot_nt(DTR[rows, :], WQ[...]) + NSR[r, :].astype(f32)
        first = norm_back(unit, rstd, gn, vec(4))
        gf = G[rows, :].astype(f32)
        gate = ACT[rows, :] * GATE[rows, :]
        branch = SUM[rows, :] - xf + ACCD[rows, :] + DSR[r, :].astype(f32) + vec(3)
        OUTB[r, :] = (xf + gate * branch).astype(bf16)
        gl = jnp.sum(gf * branch, axis=-1, keepdims=True) * (gate * (1.0 - GATE[rows, :]))
        INB[r, :] = (gf + ACCS[rows, :] + first + gl * vec(8)).astype(bf16)
        return (carry[0] + col_sum(gn * unit), carry[1] + col_sum(gn), carry[2] + col_sum(gl * xf))

    sums = lax.fori_loop(0, OWN // 80, first_back, (zero_row,) * 3)
    for row, value in zip((4, 5, 8), sums):
        SB[0, row : row + 1, :] = value
    keep_out = pltpu.make_async_copy(OUTB, o_output.at[0], lsem.at[len(loads)])
    keep_in = pltpu.make_async_copy(INB, o_input.at[0], lsem.at[len(loads) + 1])
    keep_out.start()
    keep_in.start()

    def small_send(level, slot, dev):
        out = []
        for j, (src, dst) in enumerate(((SB, SBR), (FR, FRR))):
            copy = pltpu.make_async_remote_copy(
                src_ref=src.at[level], dst_ref=dst.at[slot], send_sem=ssem_s.at[2 * slot + j],
                recv_sem=ssem_r.at[2 * slot + j], device_id=dev, device_id_type=MESH_ID,
            )
            copy.start()
            sends.append(copy)
            out.append(copy)
        return out

    def small_add(level, copies, slots):
        for cp in copies:
            cp.wait_recv()
        total, share = SB[level], FR[level]
        for s in slots:
            total = total + SBR[s]
            share = share + FRR[s]
        SB[level + 1] = total
        FR[level + 1] = share

    s0 = small_send(0, 0, peer)
    pump(2)
    small_add(0, s0, (0,))
    s1 = small_send(1, 1, xp)
    pump(2)
    small_add(1, s1, (1,))
    s2 = small_send(2, 2, yp)
    pump(2)
    small_add(2, s2, (2,))
    s3 = []
    for k in range(3):
        s3 += small_send(3, 3 + k, zp[k])
    pump(4)
    small_add(3, s3, (3, 4, 5))
    keep_small = pltpu.make_async_copy(SB.at[4], o_small, lsem.at[len(loads) + 2])
    keep_frac = pltpu.make_async_copy(FR.at[4], o_frac, lsem.at[len(loads) + 3])
    keep_small.start()
    keep_frac.start()
    pump(PIECES + 3 - done[0])
    for cp in sends:
        cp.wait_send()
    for cp in (keep_out, keep_in, keep_small, keep_frac):
        cp.wait()


N_LOADS = 2 + 9 + 3 + 5


def place_kernel(*refs):
    src, dst, (vals, sem) = refs[:8], refs[8:25], refs[25:]
    dp = lax.axis_index("dp")
    (o_output, o_input, o_qkv, o_out, o_up, o_down, o_small, o_frac) = src
    copies = []
    for i, (a, b) in enumerate(
        ((o_output, dst[0]), (o_input, dst[1]), (o_qkv, dst[2]), (o_out, dst[5]), (o_up, dst[7]), (o_down, dst[9]))
    ):
        cp = pltpu.make_async_copy(a, b, sem.at[i])
        cp.start()
        copies.append(cp)
    rows = o_small[...]
    shift = lax.rem(dp * (WIDTH - 48), WIDTH)
    mine = pltpu.roll(rows, shift, 1)[:, :48]
    for row, out in zip(range(9), (3, 4, 6, 10, 11, 12, 13, 14, 15)):
        dst[out][...] = mine[row : row + 1, :]
    vals[...] = pltpu.roll(rows, lax.rem(lax.rem(dp, 4) * (WIDTH - 192), WIDTH), 1)
    dst[8][...] = vals[pl.ds(9 + lax.div(dp, 4), 1), :192]
    dst[16][...] = o_frac[:, :3]
    for cp in copies:
        cp.wait()


def fused(
    tokens, cotangent, group, select, w_qkv, b_query, b_value, w_out, b_out, w_up, b_up, w_down,
    b_down, ln1_gain, ln1_bias, ln2_gain, ln2_bias, w_router,
):
    row = lambda v: v.reshape(1, -1)
    args = (
        tokens, cotangent, group.reshape(1, 1), select, w_qkv, row(b_query), row(b_value), w_out, row(b_out),
        w_up, row(b_up), w_down, row(b_down), row(ln1_gain), row(ln1_bias), row(ln2_gain), row(ln2_bias),
        row(w_router),
    )
    anywhere = pl.BlockSpec(memory_space=pl.ANY)
    vmem = pl.BlockSpec(memory_space=pltpu.VMEM)
    shape = jax.ShapeDtypeStruct
    mids = (
        shape((1, OWN, WIDTH), bf16), shape((1, OWN, WIDTH), bf16), shape((48, 3 * WIDTH), f32),
        shape((48, WIDTH), f32), shape((48, HIDDEN), f32), shape((192, WIDTH), f32),
        shape((SMALL, WIDTH), f32), shape((SMALL, 128), f32),
    )
    v = pltpu.VMEM
    sq = (PAD_LEN, WIDTH)
    scratch = [
        v(sq, bf16), v(sq, bf16), v((2, 1, OWN), jnp.int32), v((9, 1, WIDTH), f32), v((1, HIDDEN), f32),
        v(sq, bf16), v((WIDTH, 3 * HALF), bf16), v((WIDTH, WIDTH), bf16), v((WIDTH, HID), bf16),
        v((HID, WIDTH), bf16), v((PAD_LEN, 3 * HALF), bf16), v((2 * PAIRS, PAD_LEN, PAD_LEN), bf16),
        v((2, PAD_LEN, HALF), bf16), v(sq, f32), v(sq, bf16), v(sq, bf16), v((PAD_LEN, PAD_LEN), f32),
        v((PAD_LEN, 1), f32), v((PAD_LEN, 1), f32),
        v((PAD_LEN, HALF), bf16), v((PAD_LEN, HALF), bf16), v(sq, f32), v(sq, f32), v(sq, bf16), v(sq, bf16),
        v((OWN, WIDTH), bf16), v((OWN, WIDTH), bf16), v(sq, bf16), v((PAD_LEN, HALF), bf16),
        v((PAD_LEN, 3 * HALF), bf16), v((PAD_LEN, 128), f32), v((PAD_LEN, 128), f32),
        v((OWN, WIDTH), bf16), v((OWN, WIDTH), bf16), v((OWN, WIDTH), bf16), v((OWN, WIDTH), bf16),
        v((8, 4, 2, 2, 48, HALF), bf16), v((8, 4, 2, 48, HALF), bf16), v((8, 4, 48, HALF), bf16),
        v((8, 3, 48, HALF), bf16), v((8, 48, HALF), f32),
        v((4, 1, 2, 2, 192, HALF), bf16), v((4, 1, 2, 192, HALF), bf16), v((4, 1, 192, HALF), bf16),
        v((4, 3, 192, HALF), bf16), v((4, 192, HALF), f32),
        v((5, SMALL, WIDTH), f32), v((6, SMALL, WIDTH), f32), v((5, SMALL, 128), f32), v((6, SMALL, 128), f32),
        pltpu.SemaphoreType.DMA((N_LOADS + 4,)),
        pltpu.SemaphoreType.DMA((9,)), pltpu.SemaphoreType.DMA((9,)),
        pltpu.SemaphoreType.DMA((5 * PIECES,)), pltpu.SemaphoreType.DMA((5 * PIECES,)),
        pltpu.SemaphoreType.DMA((12,)), pltpu.SemaphoreType.DMA((12,)),
        pltpu.SemaphoreType.DMA((PIECES,)), pltpu.SemaphoreType.DMA((PIECES,)), pltpu.SemaphoreType.DMA((PIECES,)),
    ]
    mid = pl.pallas_call(
        layer_kernel,
        out_shape=mids,
        in_specs=[anywhere, anywhere, vmem] + [anywhere] * 15,
        out_specs=[anywhere] * 8,
        scratch_shapes=scratch,
        compiler_params=pltpu.CompilerParams(
            collective_id=0, has_side_effects=True, vmem_limit_bytes=60 << 20
        ),
        name="layer",
    )(*args)
    outs = (
        mids[0], mids[1], mids[2], shape((1, 48), f32), shape((1, 48), f32), mids[3], shape((1, 48), f32),
        mids[4], shape((1, 192), f32), mids[5],
    ) + (shape((1, 48), f32),) * 6 + (shape((16, 3), f32),)
    big = (0, 1, 2, 5, 7, 9)
    out = pl.pallas_call(
        place_kernel,
        out_shape=outs,
        in_specs=[anywhere] * 6 + [vmem] * 2,
        out_specs=[anywhere if i in big else vmem for i in range(17)],
        scratch_shapes=[v((SMALL, WIDTH), f32), pltpu.SemaphoreType.DMA((6,))],
        name="place",
    )(*mid)
    return tuple(o.reshape(-1) if o.shape[0] == 1 and o.ndim == 2 else o for o in out)


def norm_rows(values, norm_gain, norm_shift):
    average = jnp.mean(values, axis=-1, keepdims=True)
    centred = values - average
    variance = jnp.mean(centred * centred, axis=-1, keepdims=True)
    return centred * lax.rsqrt(variance + epsilon) * norm_gain + norm_shift


def places_of(group, slot_pos):
    short_place = jnp.minimum(slot_pos // SHORT_LEN, 2)
    return jnp.where(group[:, None] == 1, 0, short_place[None, :])


def split_heads(flat_rows):
    return flat_rows.reshape(flat_rows.shape[0], flat_rows.shape[1], HEADS, HEAD_DIM)


def masked_scores(queries, key_heads, query_place, key_place, key_mask):
    score_scale = HEAD_DIM ** (-0.5)
    scores = (
        jnp.einsum("bqhe,bkhe->bqhk", queries, key_heads, preferred_element_type=jnp.float32)
        * score_scale
    )
    key_live = (key_mask.astype(jnp.float32)[:, None, None, :] > 0.5) & (
        query_place[:, :, None, None] == key_place[:, None, None, :]
    )
    return (jnp.where(key_live, scores, masked_floor), key_live.astype(jnp.float32))


def attend(queries, key_heads, value_heads, query_place, key_place, key_mask):
    masked, key_weight = masked_scores(queries, key_heads, query_place, key_place, key_mask)
    row_max = jnp.max(masked, axis=-1, keepdims=True)
    exponent = jnp.exp(masked - row_max) * key_weight
    row_sum = jnp.sum(exponent, axis=-1, keepdims=True)
    weights = (exponent / row_sum).astype(jnp.bfloat16)
    mixed_heads = jnp.einsum(
        "bqhk,bkhe->bqhe", weights, value_heads, preferred_element_type=jnp.float32
    )
    return (mixed_heads, row_max + jnp.log(row_sum))


def back_parts(
    queries, key_heads, value_heads, query_place, key_place, key_mask, log_total, grad_heads, delta
):
    masked, key_weight = masked_scores(queries, key_heads, query_place, key_place, key_mask)
    key_probs = jnp.exp(masked - log_total) * key_weight
    grad_probs = jnp.einsum(
        "bqhe,bkhe->bqhk", grad_heads, value_heads, preferred_element_type=jnp.float32
    )
    delta = jnp.sum(key_probs * grad_probs, axis=-1, keepdims=True)
    grad_scores = (key_probs * (grad_probs - delta)).astype(jnp.bfloat16)
    return (key_probs, grad_scores, delta)


def key_side_grads(key_probs, grad_scores, queries, grad_heads):
    score_scale = HEAD_DIM ** (-0.5)
    grad_values = jnp.einsum(
        "bqhk,bqhe->bkhe",
        key_probs.astype(jnp.bfloat16),
        grad_heads,
        preferred_element_type=jnp.float32,
    )
    grad_keys = (
        jnp.einsum("bqhk,bqhe->bkhe", grad_scores, queries, preferred_element_type=jnp.float32)
        * score_scale
    )
    return (grad_keys, grad_values)


def on_device(
    tokens,
    cotangent,
    group,
    select,
    w_qkv,
    b_query,
    b_value,
    w_out,
    b_out,
    w_up,
    b_up,
    w_down,
    b_down,
    ln1_gain,
    ln1_bias,
    ln2_gain,
    ln2_bias,
    w_router,
):
    packs, per_piece, features = tokens.shape
    row_count = packs * per_piece
    first_pos = lax.axis_index("seq") * per_piece
    positions = first_pos + jnp.arange(per_piece, dtype=jnp.int32)
    full_positions = jnp.arange(PAD_LEN, dtype=jnp.int32)
    place_own = places_of(group, positions)
    place_full = places_of(group, full_positions)
    ends = jnp.where(group == 1, LONG_LEN, 3 * SHORT_LEN).astype(jnp.int32)
    active = ((select > 0) & (positions[None, :] < ends[:, None])).astype(jnp.float32)
    active_rows = active.reshape(row_count, 1)
    xfloat = tokens.reshape(row_count, features).astype(jnp.float32)
    router = jax.nn.sigmoid(jnp.dot(xfloat, w_router, precision=lax.Precision.HIGHEST))
    normed, first_back = jax.vjp(norm_rows, xfloat, ln1_gain, ln1_bias)
    normed_low = normed.astype(jnp.bfloat16)
    qkv_bias = jnp.concatenate([b_query, jnp.zeros_like(b_query), b_value])
    triple = (jnp.dot(normed_low, w_qkv, preferred_element_type=jnp.float32) + qkv_bias).astype(
        jnp.bfloat16
    )
    queries = triple[:, :features].reshape(packs, per_piece, HEADS, HEAD_DIM)
    keys_own = triple[:, features : 2 * features].reshape(packs, per_piece, features)
    values_own = triple[:, 2 * features :].reshape(packs, per_piece, features)
    mask_own = active.astype(jnp.bfloat16)
    keys_all, values_all, mask_all = (
        lax.all_gather(keys_own, "seq", axis=1, tiled=True),
        lax.all_gather(values_own, "seq", axis=1, tiled=True),
        lax.all_gather(mask_own, "seq", axis=1, tiled=True),
    )
    mixed_heads, log_total = attend(
        queries, split_heads(keys_all), split_heads(values_all), place_own, place_full, mask_all
    )
    mixed_low = mixed_heads.reshape(row_count, features).astype(jnp.bfloat16)
    attended = jnp.dot(mixed_low, w_out, preferred_element_type=jnp.float32) + b_out
    summed = xfloat + attended
    second, second_back = jax.vjp(norm_rows, summed, ln2_gain, ln2_bias)
    second_low = second.astype(jnp.bfloat16)
    pre_act = jnp.dot(second_low, w_up, preferred_element_type=jnp.float32) + b_up
    gelu_out, gelu_back = jax.vjp(partial(jax.nn.gelu, approximate=False), pre_act)
    hidden_low = gelu_out.astype(jnp.bfloat16)
    branch = attended + (jnp.dot(hidden_low, w_down, preferred_element_type=jnp.float32) + b_down)
    gate_rows = active_rows * router[:, None]
    output = (xfloat + gate_rows * branch).astype(jnp.bfloat16).reshape(packs, per_piece, features)
    place_range = jnp.arange(3, dtype=jnp.int32)
    onehot = (place_full[:, :, None] == place_range[None, None, :]).astype(jnp.float32)
    counts = jnp.sum(mask_all.astype(jnp.float32)[:, :, None] * onehot, axis=1)
    image_lengths = jnp.where(group == 1, LONG_LEN, SHORT_LEN).astype(jnp.float32)
    fractions = lax.all_gather(counts / image_lengths[:, None], "dp", axis=0, tiled=True)
    grad_rows = cotangent.reshape(row_count, features).astype(jnp.float32)
    grad_logit = jnp.sum(grad_rows * branch, axis=1) * active_rows[:, 0] * router * (1.0 - router)
    grad_branch = gate_rows * grad_rows
    grad_mlp = grad_branch.astype(jnp.bfloat16)
    grad_down = jnp.einsum("rk,rd->kd", hidden_low, grad_mlp, preferred_element_type=jnp.float32)
    grad_down_bias = jnp.sum(grad_mlp.astype(jnp.float32), axis=0)
    grad_hidden = jnp.einsum("rd,kd->rk", grad_mlp, w_down, preferred_element_type=jnp.float32)
    grad_pre = gelu_back(grad_hidden)[0].astype(jnp.bfloat16)
    grad_up = jnp.einsum("rd,rk->dk", second_low, grad_pre, preferred_element_type=jnp.float32)
    grad_up_bias = jnp.sum(grad_pre.astype(jnp.float32), axis=0)
    grad_second = jnp.einsum("rk,dk->rd", grad_pre, w_up, preferred_element_type=jnp.float32)
    grad_summed, grad_ln2_gain, grad_ln2_bias = second_back(grad_second)
    grad_attended = (grad_branch + grad_summed).astype(jnp.bfloat16)
    grad_out = jnp.einsum("rd,re->de", mixed_low, grad_attended, preferred_element_type=jnp.float32)
    grad_out_bias = jnp.sum(grad_attended.astype(jnp.float32), axis=0)
    grad_mixed = jnp.einsum("re,de->rd", grad_attended, w_out, preferred_element_type=jnp.float32)
    grad_heads = grad_mixed.astype(jnp.bfloat16).reshape(packs, per_piece, HEADS, HEAD_DIM)
    back_k, back_v, back_m = (
        lax.all_gather(keys_own, "seq", axis=1, tiled=True),
        lax.all_gather(values_own, "seq", axis=1, tiled=True),
        lax.all_gather(mask_own, "seq", axis=1, tiled=True),
    )
    back_kh = split_heads(back_k)
    back_vh = split_heads(back_v)
    key_probs, grad_scores, delta = back_parts(
        queries, back_kh, back_vh, place_own, place_full, back_m, log_total, grad_heads, None
    )
    grad_queries = jnp.einsum(
        "bqhk,bkhe->bqhe", grad_scores, back_kh, preferred_element_type=jnp.float32
    ) * HEAD_DIM ** (-0.5)
    grad_keys, grad_values = key_side_grads(key_probs, grad_scores, queries, grad_heads)
    keys_grad_own, values_grad_own = (
        lax.psum_scatter(
            grad_keys.reshape(back_k.shape).astype(jnp.bfloat16),
            "seq",
            scatter_dimension=1,
            tiled=True,
        ).astype(jnp.float32),
        lax.psum_scatter(
            grad_values.reshape(back_v.shape).astype(jnp.bfloat16),
            "seq",
            scatter_dimension=1,
            tiled=True,
        ).astype(jnp.float32),
    )
    grad_triple = jnp.concatenate(
        [
            grad_queries.reshape(row_count, features),
            keys_grad_own.reshape(row_count, features),
            values_grad_own.reshape(row_count, features),
        ],
        axis=1,
    ).astype(jnp.bfloat16)
    grad_qkv = jnp.einsum("rd,rk->dk", normed_low, grad_triple, preferred_element_type=jnp.float32)
    column_sums = jnp.sum(grad_triple.astype(jnp.float32), axis=0)
    grad_query_bias = column_sums[:features]
    grad_value_bias = column_sums[2 * features :]
    grad_normed = jnp.einsum("rk,dk->rd", grad_triple, w_qkv, preferred_element_type=jnp.float32)
    grad_first, grad_ln1_gain, grad_ln1_bias = first_back(grad_normed)
    grad_router = jnp.dot(grad_logit, xfloat, precision=lax.Precision.HIGHEST)
    grad_input = grad_rows + grad_summed + grad_first + grad_logit[:, None] * w_router[None, :]
    input_grad = grad_input.astype(jnp.bfloat16).reshape(packs, per_piece, features)
    (
        share_qkv,
        share_query_bias,
        share_value_bias,
        share_out,
        share_out_bias,
        share_up,
        share_up_bias,
        share_down,
        share_down_bias,
        share_ln1_gain,
        share_ln1_bias,
        share_ln2_gain,
        share_ln2_bias,
        share_router,
    ) = (
        lax.psum_scatter(
            grad_qkv.astype(jnp.bfloat16), "dp", scatter_dimension=0, tiled=True
        ).astype(jnp.float32),
        lax.psum_scatter(
            grad_query_bias.astype(jnp.bfloat16), "dp", scatter_dimension=0, tiled=True
        ).astype(jnp.float32),
        lax.psum_scatter(
            grad_value_bias.astype(jnp.bfloat16), "dp", scatter_dimension=0, tiled=True
        ).astype(jnp.float32),
        lax.psum_scatter(
            grad_out.astype(jnp.bfloat16), "dp", scatter_dimension=0, tiled=True
        ).astype(jnp.float32),
        lax.psum_scatter(
            grad_out_bias.astype(jnp.bfloat16), "dp", scatter_dimension=0, tiled=True
        ).astype(jnp.float32),
        lax.psum_scatter(
            grad_up.astype(jnp.bfloat16), "dp", scatter_dimension=0, tiled=True
        ).astype(jnp.float32),
        lax.psum_scatter(
            grad_up_bias.astype(jnp.bfloat16), "dp", scatter_dimension=0, tiled=True
        ).astype(jnp.float32),
        lax.psum_scatter(
            grad_down.astype(jnp.bfloat16), "dp", scatter_dimension=0, tiled=True
        ).astype(jnp.float32),
        lax.psum_scatter(
            grad_down_bias.astype(jnp.bfloat16), "dp", scatter_dimension=0, tiled=True
        ).astype(jnp.float32),
        lax.psum_scatter(
            grad_ln1_gain.astype(jnp.bfloat16), "dp", scatter_dimension=0, tiled=True
        ).astype(jnp.float32),
        lax.psum_scatter(
            grad_ln1_bias.astype(jnp.bfloat16), "dp", scatter_dimension=0, tiled=True
        ).astype(jnp.float32),
        lax.psum_scatter(
            grad_ln2_gain.astype(jnp.bfloat16), "dp", scatter_dimension=0, tiled=True
        ).astype(jnp.float32),
        lax.psum_scatter(
            grad_ln2_bias.astype(jnp.bfloat16), "dp", scatter_dimension=0, tiled=True
        ).astype(jnp.float32),
        lax.psum_scatter(
            grad_router.astype(jnp.bfloat16), "dp", scatter_dimension=0, tiled=True
        ).astype(jnp.float32),
    )
    totals = (
        lax.psum(share_qkv.astype(jnp.bfloat16), "seq").astype(jnp.float32),
        lax.psum(share_query_bias.astype(jnp.bfloat16), "seq").astype(jnp.float32),
        lax.psum(share_value_bias.astype(jnp.bfloat16), "seq").astype(jnp.float32),
        lax.psum(share_out.astype(jnp.bfloat16), "seq").astype(jnp.float32),
        lax.psum(share_out_bias.astype(jnp.bfloat16), "seq").astype(jnp.float32),
        lax.psum(share_up.astype(jnp.bfloat16), "seq").astype(jnp.float32),
        lax.psum(share_up_bias.astype(jnp.bfloat16), "seq").astype(jnp.float32),
        lax.psum(share_down.astype(jnp.bfloat16), "seq").astype(jnp.float32),
        lax.psum(share_down_bias.astype(jnp.bfloat16), "seq").astype(jnp.float32),
        lax.psum(share_ln1_gain.astype(jnp.bfloat16), "seq").astype(jnp.float32),
        lax.psum(share_ln1_bias.astype(jnp.bfloat16), "seq").astype(jnp.float32),
        lax.psum(share_ln2_gain.astype(jnp.bfloat16), "seq").astype(jnp.float32),
        lax.psum(share_ln2_bias.astype(jnp.bfloat16), "seq").astype(jnp.float32),
        lax.psum(share_router.astype(jnp.bfloat16), "seq").astype(jnp.float32),
    )
    return (
        output,
        input_grad,
        totals[0],
        totals[1],
        totals[2],
        totals[3],
        totals[4],
        totals[5],
        totals[6],
        totals[7],
        totals[8],
        totals[9],
        totals[10],
        totals[11],
        totals[12],
        totals[13],
        fractions,
    )


def solution(mesh):
    in_specs = (
        P("dp", "seq", None),
        P("dp", "seq", None),
        P("dp"),
        P("dp", "seq"),
        P(),
        P(),
        P(),
        P(),
        P(),
        P(),
        P(),
        P(),
        P(),
        P(),
        P(),
        P(),
        P(),
        P(),
    )
    out_specs = (
        P("dp", "seq", None),
        P("dp", "seq", None),
        P("dp", None),
        P("dp"),
        P("dp"),
        P("dp", None),
        P("dp"),
        P("dp", None),
        P("dp"),
        P("dp", None),
        P("dp"),
        P("dp"),
        P("dp"),
        P("dp"),
        P("dp"),
        P("dp"),
        P(),
    )
    fast = mesh.shape["dp"] == 16 and mesh.shape["seq"] == 2
    return jax.shard_map(
        fused if fast else on_device, mesh=mesh, in_specs=in_specs, out_specs=out_specs, check_vma=False
    )
```

```python
from functools import partial

import jax
import jax.numpy as jnp
from jax import lax
from jax.experimental import pallas as pl
from jax.experimental.pallas import tpu as pltpu
from jax.sharding import PartitionSpec as P

HEADS = 12
HEAD_DIM = 64
PAD_LEN = 640
LONG_LEN = 577
SHORT_LEN = 197
WIDTH = 768
HIDDEN = 3072

epsilon = 1e-06
masked_floor = -1000000000.0
MESH_ID = pl.DeviceIdType.MESH
bf16 = jnp.bfloat16
f32 = jnp.float32

HALF = WIDTH // 2
OWN = PAD_LEN // 2
HID = HIDDEN // 2
BLOCKS = HID // HALF
PAIRS = HALF // 128
MT = 320
AT = 128
SMALL = 16
PIECES = 12
ORDER = {
    "up0": "z",
    "dA0": "x",
    "up1": "x",
    "dB0": "y",
    "up2": "y",
    "up3": "x",
    "dA1": "x",
    "dB1": "y",
    "out": "y",
    "q": "x",
    "k": "y",
    "v": "x",
}
HALVED = ("dA0", "dA1")
SCHEDULE = {
    "j0": (
        (0, "dA0"), (1, "up0"),
    ),
    "j1": (
        (1, "dA0"), (1, "up1"), (1, "dB0"),
    ),
    "j2": (
        (0, "dA1"), (1, "up2"),
    ),
    "j3": (
        (1, "up3"), (1, "dB1"), (2, "dA0"), (2, "dB0"),
    ),
    "sb": (
        (2, "up0"), (2, "up1"),
    ),
    "out": (
        (2, "up2"),
    ),
    "h0": (
        (1, "dA1"), (1, "out"), (2, "dB1"), (2, "up3"),
    ),
    "h1": (
        (3, "dA0"), (3, "dB0"), (3, "up0"), (3, "up1"), (3, "up2"),
    ),
    "h2": (
        (2, "dA1"), (4, "dA0"), (2, "out"), (3, "dB1"), (4, "dB0"), (5, "dA0"), (3, "up3"), (4, "up0"), (5, "dB0"),
    ),
    "q": (
        (1, "q"), (4, "up1"), (5, "up0"),
    ),
    "k": (
        (1, "k"), (3, "out"), (5, "up1"), (3, "dA1"),
    ),
    "v": (
        (1, "v"), (4, "up2"),
    ),
    "fb": (
        (5, "up2"),
    ),
    "e1": (
        (4, "dB1"), (2, "q"), (5, "dB1"), (2, "k"),
    ),
    "e2": (
        (4, "up3"), (5, "up3"), (4, "out"), (3, "q"),
    ),
    "e3": (
        (2, "v"), (5, "out"), (4, "dA1"), (3, "k"),
    ),
    "end": (
        (5, "dA1"), (4, "q"), (3, "v"), (5, "q"), (4, "k"), (5, "k"), (4, "v"), (5, "v"),
    ),
}


def dot_nn(a, b):
    return lax.dot_general(a, b, (((1,), (0,)), ((), ())), preferred_element_type=f32)


def dot_nt(a, b):
    return lax.dot_general(a, b, (((1,), (1,)), ((), ())), preferred_element_type=f32)


def dot_tn(a, b):
    return lax.dot_general(a, b, (((0,), (0,)), ((), ())), preferred_element_type=f32)


def row_stats(values):
    average = jnp.mean(values, axis=-1, keepdims=True)
    centred = values - average
    variance = jnp.mean(centred * centred, axis=-1, keepdims=True)
    rstd = lax.rsqrt(variance + epsilon)
    return centred * rstd, rstd


def norm_back(unit, rstd, grad, gain):
    q = grad * gain
    return rstd * (
        q - jnp.mean(q, axis=-1, keepdims=True) - unit * jnp.mean(q * unit, axis=-1, keepdims=True)
    )


def layer_kernel(
    tokens, cotangent, group, select, w_qkv, b_query, b_value, w_out, b_out, w_up, b_up, w_down,
    b_down, ln1_gain, ln1_bias, ln2_gain, ln2_bias, w_router,
    o_output, o_input, o_qkv, o_out, o_up, o_down, o_small, o_frac,
    X, G, SEL, VEC, BUP, NRM, WQ, WO, WU, WD, TRI, PR, MIX, SUM, SEC, GM, BIAS, GATE, ACT,
    HIDJ, GPJ, ACCD, ACCS, GSB, GSR, DSB, DSR, GATT, GMX, DTR, DK, DV, OUTB, INB, NSB, NSR,
    S4, R14, R24, R34, F4, S1, R11, R21, R31, F1, RZ, RZ2, SB, SBR, FR, FRR,
    lsem, esem_s, esem_r, csem_s, csem_r, ssem_s, ssem_r, fsem_l, fsem_s, fsem_r,
):
    dp = lax.axis_index("dp")
    c = lax.axis_index("seq")
    x = lax.rem(dp, 2)
    y = lax.rem(lax.div(dp, 2), 2)
    z = lax.div(dp, 4)
    peer = (dp, 1 - c)
    xp = ((z * 2 + y) * 2 + (1 - x), c)
    yp = ((z * 2 + (1 - y)) * 2 + x, c)
    zs = [lax.rem(z + k, 4) for k in (1, 2, 3)]
    zp = [((zk * 2 + y) * 2 + x, c) for zk in zs]
    own = pl.multiple_of(c * OWN, OWN)
    oth = pl.multiple_of((1 - c) * OWN, OWN)
    chalf = pl.multiple_of(c * HALF, HALF)
    chid = pl.multiple_of(c * HID, HID)
    lead = (c == 0).astype(f32)

    barrier = pltpu.get_barrier_semaphore()
    for other in [peer, xp, yp] + zp:
        pl.semaphore_signal(barrier, inc=1, device_id=other, device_id_type=MESH_ID)

    loads = {}

    def load(name, src, dst):
        copy = pltpu.make_async_copy(src, dst, lsem.at[len(loads)])
        copy.start()
        loads[name] = copy

    load("tok", tokens.at[0], X.at[pl.ds(own, OWN)])
    load("sel", select, SEL.at[c])
    for i, v in enumerate(
        (b_query, b_value, b_out, b_down, ln1_gain, ln1_bias, ln2_gain, ln2_bias, w_router)
    ):
        load("v%d" % i, v, VEC.at[i, 0])
    for k in range(3):
        load(
            "wq%d" % k,
            w_qkv.at[:, pl.ds(pl.multiple_of(k * WIDTH + c * HALF, 128), HALF)],
            WQ.at[:, pl.ds(k * HALF, HALF)],
        )
    load("cot", cotangent.at[0], G.at[pl.ds(own, OWN)])
    load("bup", b_up, BUP.at[0])
    load("wo", w_out, WO)
    load("wu", w_up.at[:, pl.ds(chid, HID)], WU)
    load("wd", w_down.at[pl.ds(chid, HID)], WD)

    pl.semaphore_wait(barrier, 6)

    sends = []
    counts = {"e": 0, "c": 0}

    def to_core(src, dst):
        i = counts["e"]
        counts["e"] += 1
        copy = pltpu.make_async_remote_copy(
            src_ref=src, dst_ref=dst, send_sem=esem_s.at[i], recv_sem=esem_r.at[i],
            device_id=peer, device_id_type=MESH_ID,
        )
        copy.start()
        sends.append(copy)
        return copy

    ex_sel = to_core(select, SEL.at[c])
    ex_tok = to_core(tokens.at[0], X.at[pl.ds(own, OWN)])
    ex_cot = to_core(cotangent.at[0], G.at[pl.ds(own, OWN)])

    SB[...] = jnp.zeros_like(SB)
    FR[...] = jnp.zeros_like(FR)

    loads["sel"].wait()
    ex_sel.wait_recv()
    gv = jnp.full((1, 1), group[0], jnp.int32)
    long_row = jnp.broadcast_to(gv, (1, PAD_LEN)) == 1
    pos_row = lax.broadcasted_iota(jnp.int32, (1, PAD_LEN), 1)
    short_row = (pos_row >= SHORT_LEN).astype(jnp.int32) + (pos_row >= 2 * SHORT_LEN).astype(jnp.int32)
    place_row = jnp.where(long_row, 0, short_row)
    end_row = jnp.where(long_row, LONG_LEN, 3 * SHORT_LEN)
    long_col = jnp.broadcast_to(gv, (PAD_LEN, 1)) == 1
    pos_col = lax.broadcasted_iota(jnp.int32, (PAD_LEN, 1), 0)
    short_col = (pos_col >= SHORT_LEN).astype(jnp.int32) + (pos_col >= 2 * SHORT_LEN).astype(jnp.int32)
    place_col = jnp.where(long_col, 0, short_col)
    end_col = jnp.where(long_col, LONG_LEN, 3 * SHORT_LEN)
    sel_row = jnp.zeros((8, PAD_LEN), f32)
    sel_col = jnp.zeros((PAD_LEN, 8), f32)
    for part in range(2):
        bits = jnp.broadcast_to((SEL[part] > 0).astype(f32), (8, OWN)).astype(bf16)
        spread = (
            lax.broadcasted_iota(jnp.int32, (PAD_LEN, OWN), 0)
            == lax.broadcasted_iota(jnp.int32, (PAD_LEN, OWN), 1) + part * OWN
        ).astype(f32).astype(bf16)
        sel_row = sel_row + dot_nt(bits, spread)
        sel_col = sel_col + dot_nt(spread, bits)
    act_row = jnp.where(pos_row < end_row, sel_row[0:1, :], 0.0)
    act_col = jnp.where(pos_col < end_col, sel_col[:, 0:1], 0.0)
    ACT[...] = act_col
    BIAS[...] = jnp.where(
        (jnp.broadcast_to(act_row, (PAD_LEN, PAD_LEN)) > 0.5)
        & (jnp.broadcast_to(place_col, (PAD_LEN, PAD_LEN)) == jnp.broadcast_to(place_row, (PAD_LEN, PAD_LEN))),
        0.0,
        -1e30,
    )
    lane = lax.broadcasted_iota(jnp.int32, (1, 128), 1)
    length = jnp.where(jnp.broadcast_to(gv, (1, 1)) == 1, float(LONG_LEN), float(SHORT_LEN))
    shares = jnp.zeros((1, 128), f32)
    for j in range(3):
        count = jnp.sum(jnp.where(place_row == j, act_row, 0.0), axis=1, keepdims=True)
        shares = jnp.where(lane == j, count / length, shares)
    FR[0, pl.ds(dp, 1), :] = shares * lead

    loads["tok"].wait()
    for i in range(9):
        loads["v%d" % i].wait()
    ex_tok.wait_recv()

    def vec(i):
        return VEC[i]

    @pl.loop(0, PAD_LEN // AT)
    def _(t):
        rows = pl.ds(pl.multiple_of(t * AT, AT), AT)
        xf = X[rows, :].astype(f32)
        unit, _ = row_stats(xf)
        NRM[rows, :] = (unit * vec(4) + vec(5)).astype(bf16)
        logit = jnp.sum(xf * vec(8), axis=-1, keepdims=True)
        GATE[rows, :] = 1.0 / (1.0 + jnp.exp(-logit))

    for k in range(3):
        loads["wq%d" % k].wait()
    qb = VEC[0, :, pl.ds(chalf, HALF)]
    vb = VEC[1, :, pl.ds(chalf, HALF)]

    @pl.loop(0, PAD_LEN // MT)
    def _(t):
        rows = pl.ds(pl.multiple_of(t * MT, MT), MT)
        nr = NRM[rows, :]
        for k in range(3):
            r = dot_nn(nr, WQ[:, k * HALF : (k + 1) * HALF])
            if k == 0:
                r = (r + qb).astype(bf16).astype(f32) * HEAD_DIM ** (-0.5)
            if k == 2:
                r = r + vb
            TRI[rows, k * HALF : (k + 1) * HALF] = r.astype(bf16)

    low_lanes = lax.broadcasted_iota(jnp.int32, (1, 128), 1) < HEAD_DIM

    def head_part(v, side):
        keep = low_lanes if side == 0 else jnp.logical_not(low_lanes)
        return jnp.where(keep, v, jnp.zeros_like(v))

    def pair_lanes(hp):
        return [slice(k * HALF + hp * 128, k * HALF + hp * 128 + 128) for k in range(3)]

    ex_mix = []
    for hp in range(PAIRS):
        qlanes, klanes, vlanes = pair_lanes(hp)

        @pl.loop(0, PAD_LEN // AT)
        def _(t):
            rows = pl.ds(pl.multiple_of(t * AT, AT), AT)
            qp = TRI[rows, qlanes]
            kp = TRI[:, klanes]
            vp = TRI[:, vlanes]
            bias = BIAS[rows, :]
            total = jnp.zeros((AT, 128), f32)
            for side in range(2):
                s = dot_nt(head_part(qp, side), kp) + bias
                e = jnp.exp(s - jnp.max(s, axis=-1, keepdims=True))
                w = (e * (1.0 / jnp.sum(e, axis=-1, keepdims=True))).astype(bf16)
                PR[2 * hp + side, rows, :] = w
                total = total + dot_nn(w, head_part(vp, side))
            MIX[c, rows, qlanes] = total.astype(bf16)

        ex_mix.append(to_core(MIX.at[c, :, qlanes], MIX.at[c, :, qlanes]))

    loads["cot"].wait()
    ex_cot.wait_recv()
    loads["wo"].wait()

    @pl.loop(0, PAD_LEN // AT)
    def _(t):
        rows = pl.ds(pl.multiple_of(t * AT, AT), AT)
        GM[rows, :] = (ACT[rows, :] * GATE[rows, :] * G[rows, :].astype(f32)).astype(bf16)

    for e in ex_mix:
        e.wait_recv()

    @pl.loop(0, PAD_LEN // MT)
    def _(t):
        rows = pl.ds(pl.multiple_of(t * MT, MT), MT)
        att = dot_nn(MIX[0, rows, :], WO[0:HALF, :]) + dot_nn(MIX[1, rows, :], WO[HALF:, :]) + vec(2)
        s = X[rows, :].astype(f32) + att
        SUM[rows, :] = s
        unit, _ = row_stats(s)
        SEC[rows, :] = (unit * vec(6) + vec(7)).astype(bf16)

    for n in ("bup", "wu", "wd"):
        loads[n].wait()

    def remote(src, dst, dev, i):
        return pltpu.make_async_remote_copy(
            src_ref=src, dst_ref=dst, send_sem=csem_s.at[i], recv_sem=csem_r.at[i],
            device_id=dev, device_id_type=MESH_ID,
        )

    pieces = {}

    def start(st, key, i, src, dst, dev):
        cp = remote(src, dst, dev, i)
        cp.start()
        sends.append(cp)
        st.setdefault(key, []).append(cp)

    def wait(st, key):
        for cp in st[key]:
            cp.wait_recv()

    class Piece:
        def __init__(self, name, src, r1, r2, r3, fin, dst_ref, only_z=None):
            self.order, self.src, self.r1, self.r2, self.r3, self.fin = ORDER[name], src, r1, r2, r3, fin
            if self.order == "z":
                self.r1, self.r2, self.r3 = RZ, RZ2, r3.at[0]
            self.only_z = only_z
            self.number = len(pieces)
            self.base = self.number * 7
            self.st = {}
            self.keep = pltpu.make_async_copy(fin, dst_ref, fsem_l.at[self.number])
            self.give = pltpu.make_async_remote_copy(
                src_ref=fin, dst_ref=dst_ref, send_sem=fsem_s.at[self.number],
                recv_sem=fsem_r.at[self.number], device_id=peer, device_id_type=MESH_ID,
            )
            pieces[name] = self

        def first(self, part=None):
            src, r1, st, b = self.src, self.r1, self.st, self.base
            if self.order == "z":
                for k in range(3):
                    start(st, 1, b + k, src.at[zs[k]], r1.at[k], zp[k])
            elif part is not None:
                start(st, 1, b + part, src.at[:, part, 1 - x], r1.at[:, part], xp)
            elif self.order == "x":
                start(st, 1, b, src.at[:, :, 1 - x], r1, xp)
            else:
                start(st, 1, b, src.at[:, 1 - y], r1, yp)
            return self

        def second(self):
            src, r1, r2, st, b = self.src, self.r1, self.r2, self.st, self.base
            wait(st, 1)
            if self.order == "z":
                for a in range(2):
                    for d in range(2):
                        t = src[z, a, d].astype(f32) + r1[0, a, d].astype(f32)
                        t = t + (r1[1, a, d].astype(f32) + r1[2, a, d].astype(f32))
                        r1[0, a, d] = t.astype(bf16)
                start(st, 2, b + 3, r1.at[0, :, 1 - x], r2, xp)
                return
            for a in range(r1.shape[0]):
                for d in range(2):
                    mine = src[a, d, x] if self.order == "x" else src[a, y, d]
                    r1[a, d] = mine + r1[a, d]
            if self.order == "x":
                start(st, 2, b + 3, r1.at[:, 1 - y], r2, yp)
            else:
                start(st, 2, b + 3, r1.at[:, 1 - x], r2, xp)

        def third(self):
            r1, r2, r3, st, b = self.r1, self.r2, self.r3, self.st, self.base
            wait(st, 2)
            if self.order == "z":
                for a in range(2):
                    r2[a] = r1[0, a, x] + r2[a]
                start(st, 3, b + 4, r2.at[1 - y], r3, yp)
                return
            for a in range(r2.shape[0]):
                r2[a] = (r1[a, y] if self.order == "x" else r1[a, x]) + r2[a]
            for k in range(3):
                if self.only_z is None:
                    start(st, 3, b + 4 + k, r2.at[zs[k]], r3.at[k], zp[k])
                else:
                    cp = remote(r2.at[0], r3.at[k], zp[k], b + 4 + k)
                    pl.when(zs[k] == self.only_z)(cp.start)
                    st.setdefault(3, []).append(cp)

        def fourth(self):
            r2, r3, st, fin = self.r2, self.r3, self.st, self.fin

            def finish():
                wait(st, 3)
                if self.order == "z":
                    fin[...] = r2[y].astype(f32) + r3[...].astype(f32)
                else:
                    mine = r2[z] if self.only_z is None else r2[0]
                    fin[...] = mine.astype(f32) + r3[0].astype(f32) + (r3[1].astype(f32) + r3[2].astype(f32))
                self.keep.start()
                self.give.start()

            if self.only_z is None:
                finish()
            else:
                pl.when(z == self.only_z)(finish)

        def fifth(self):
            keep, give = self.keep, self.give
            if self.only_z is None:
                keep.wait()
                give.wait()
                return

            @pl.when(z == self.only_z)
            def _():
                keep.wait()
                give.wait_send()

            @pl.when(z == self.only_z + 2 - 4 * c)
            def _():
                give.wait_recv()

            for k in range(3):
                pl.when(zs[k] == self.only_z)(self.st[3][k].wait_send)

    def columns(start):
        return pl.ds(pl.multiple_of(start, 128), HALF)

    for i, (name, dst_ref) in enumerate(
        [("up%d" % j, o_up.at[:, columns(chid + j * HALF)]) for j in range(BLOCKS)]
        + [("out", o_out.at[:, columns(chalf)])]
        + [("qkv"[k], o_qkv.at[:, columns(k * WIDTH + chalf)]) for k in range(3)]
    ):
        Piece(name, S4.at[i], R14.at[i], R24.at[i], R34.at[i], F4.at[i], dst_ref)
    for i, name in enumerate(("dA0", "dB0", "dA1", "dB1")):
        Piece(
            name, S1.at[i], R11.at[i], R21.at[i], R31.at[i], F1.at[i],
            o_down.at[:, (i % 2) * HALF : (i % 2 + 1) * HALF], only_z=2 * c + i // 2,
        )

    def at(point):
        for act, name in SCHEDULE.get(point, ()):
            p = pieces[name]
            if act == 0:
                p.first(part=0)
            elif act == 1:
                p.first(part=1 if name in HALVED else None)
            else:
                (p.second, p.third, p.fourth, p.fifth)[act - 2]()

    for j in range(BLOCKS):
        cols = slice(j * HALF, (j + 1) * HALF)
        bj = BUP[:, pl.ds(pl.multiple_of(chid + j * HALF, 128), HALF)]

        @pl.loop(0, PAD_LEN // MT)
        def _(t):
            rows = pl.ds(pl.multiple_of(t * MT, MT), MT)
            pre = dot_nn(SEC[rows, :], WU[:, cols]) + bj
            cdf = 0.5 * (1.0 + lax.erf(pre * (2.0 ** -0.5)))
            hid = (pre * cdf).astype(bf16)
            slope = cdf + pre * (0.3989422804014327 * jnp.exp(-0.5 * pre * pre))
            gh = dot_nt(GM[rows, :], WD[cols, :])
            gp = (gh * slope).astype(bf16)
            HIDJ[rows, :] = hid
            GPJ[rows, :] = gp
            d = dot_nn(hid, WD[cols, :])
            s = dot_nt(gp, WU[:, cols])
            if j == 0:
                ACCD[rows, :] = d
                ACCS[rows, :] = s
            else:
                ACCD[rows, :] += d
                ACCS[rows, :] += s

        for part in range(2):
            g = dot_tn(SEC[:, part * HALF : (part + 1) * HALF], GPJ[...])
            S4[j, 2 * part : 2 * part + 2] = g.astype(bf16).reshape(2, 2, 2, 48, HALF)
        SB[0, pl.ds(9 + 2 * c + j // 2, 1), (j % 2) * HALF : (j % 2 + 1) * HALF] = jnp.sum(
            GPJ[...].astype(f32), axis=0, keepdims=True
        )
        for part in range(2):
            g = dot_tn(HIDJ[...], GM[:, part * HALF : (part + 1) * HALF])
            S1[2 * (j // 2) + part, 0, j % 2] = g.astype(bf16).reshape(2, 192, HALF)
        at("j%d" % j)

    @pl.loop(0, PAD_LEN // AT)
    def _(t):
        rows = pl.ds(pl.multiple_of(t * AT, AT), AT)
        GSB[rows, :] = ACCS[rows, :].astype(bf16)

    ex_gs = to_core(GSB, GSR)

    @pl.loop(0, OWN // 80)
    def _(t):
        r = pl.ds(pl.multiple_of(t * 80, 80), 80)
        DSB[r, :] = ACCD[pl.ds(pl.multiple_of(oth + t * 80, 80), 80), :].astype(bf16)

    ex_ds = to_core(DSB, DSR)
    at("ln2")
    ex_gs.wait_recv()

    zero_row = jnp.zeros((1, WIDTH), f32)

    def col_sum(v):
        return jnp.sum(v, axis=0, keepdims=True)

    def second_back(t, carry):
        rows = pl.ds(pl.multiple_of(t * AT, AT), AT)
        gs = ACCS[rows, :] + GSR[rows, :].astype(f32)
        unit, rstd = row_stats(SUM[rows, :])
        back = norm_back(unit, rstd, gs, vec(6))
        ACCS[rows, :] = back
        ga = (ACT[rows, :] * GATE[rows, :] * G[rows, :].astype(f32) + back).astype(bf16)
        GATT[rows, :] = ga
        return (
            carry[0] + col_sum(gs * unit), carry[1] + col_sum(gs), carry[2] + col_sum(ga.astype(f32)),
            carry[3] + col_sum(GM[rows, :].astype(f32)),
        )

    sums = lax.fori_loop(0, PAD_LEN // AT, second_back, (zero_row,) * 4)
    for row, value in zip((6, 7, 2, 3), sums):
        SB[0, row : row + 1, :] = value * lead
    at("sb")

    for part in range(2):
        g = dot_tn(MIX[part], GATT[:, pl.ds(chalf, HALF)])
        S4[4, 2 * part : 2 * part + 2] = g.astype(bf16).reshape(2, 2, 2, 48, HALF)
    at("out")

    @pl.loop(0, PAD_LEN // MT)
    def _(t):
        rows = pl.ds(pl.multiple_of(t * MT, MT), MT)
        GMX[rows, :] = dot_nt(GATT[rows, :], WO[pl.ds(chalf, HALF), :]).astype(bf16)

    at("gmx")

    for hp in range(PAIRS):
        qlanes, klanes, vlanes = pair_lanes(hp)
        DK[...] = jnp.zeros_like(DK)
        DV[...] = jnp.zeros_like(DV)

        @pl.loop(0, PAD_LEN // AT)
        def _(t):
            rows = pl.ds(pl.multiple_of(t * AT, AT), AT)
            qp = TRI[rows, qlanes]
            kp = TRI[:, klanes]
            vp = TRI[:, vlanes]
            gp = GMX[rows, qlanes]
            dq = jnp.zeros((AT, 128), f32)
            for side in range(2):
                w = PR[2 * hp + side, rows, :]
                wf = w.astype(f32)
                gs = head_part(gp, side)
                dpr = dot_nt(gs, vp)
                delta = jnp.sum(wf * dpr, axis=-1, keepdims=True)
                ds = (wf * (dpr - delta)).astype(bf16)
                dq = dq + dot_nn(ds, head_part(kp, side))
                DK[...] += dot_tn(ds, head_part(qp, side))
                DV[...] += dot_tn(w, gs)
            DTR[rows, qlanes] = (dq * HEAD_DIM ** (-0.5)).astype(bf16)

        DTR[:, klanes] = DK[...].astype(bf16)
        DTR[:, vlanes] = DV[...].astype(bf16)
        at("h%d" % hp)

    for k in range(3):
        blk = DTR[:, k * HALF : (k + 1) * HALF]
        if k != 1:
            SB[0, k // 2 : k // 2 + 1, pl.ds(chalf, HALF)] = col_sum(blk.astype(f32))
        for part in range(2):
            g = dot_tn(NRM[:, part * HALF : (part + 1) * HALF], blk)
            S4[5 + k, 2 * part : 2 * part + 2] = g.astype(bf16).reshape(2, 2, 2, 48, HALF)
        at("qkv"[k])

    NSB[...] = dot_nt(DTR[pl.ds(oth, OWN), :], WQ[...]).astype(bf16)
    ex_ns = to_core(NSB, NSR)
    at("ns")
    ex_ds.wait_recv()
    ex_ns.wait_recv()

    def first_back(t, carry):
        r = pl.ds(pl.multiple_of(t * 80, 80), 80)
        rows = pl.ds(pl.multiple_of(own + t * 80, 80), 80)
        xf = X[rows, :].astype(f32)
        unit, rstd = row_stats(xf)
        gn = dot_nt(DTR[rows, :], WQ[...]) + NSR[r, :].astype(f32)
        first = norm_back(unit, rstd, gn, vec(4))
        gf = G[rows, :].astype(f32)
        gate = ACT[rows, :] * GATE[rows, :]
        branch = SUM[rows, :] - xf + ACCD[rows, :] + DSR[r, :].astype(f32) + vec(3)
        OUTB[r, :] = (xf + gate * branch).astype(bf16)
        gl = jnp.sum(gf * branch, axis=-1, keepdims=True) * (gate * (1.0 - GATE[rows, :]))
        INB[r, :] = (gf + ACCS[rows, :] + first + gl * vec(8)).astype(bf16)
        return (carry[0] + col_sum(gn * unit), carry[1] + col_sum(gn), carry[2] + col_sum(gl * xf))

    sums = lax.fori_loop(0, OWN // 80, first_back, (zero_row,) * 3)
    for row, value in zip((4, 5, 8), sums):
        SB[0, row : row + 1, :] = value
    keep_out = pltpu.make_async_copy(OUTB, o_output.at[0], lsem.at[len(loads)])
    keep_in = pltpu.make_async_copy(INB, o_input.at[0], lsem.at[len(loads) + 1])
    keep_out.start()
    keep_in.start()

    def small_send(level, slot, dev):
        out = []
        for j, (src, dst) in enumerate(((SB, SBR), (FR, FRR))):
            copy = pltpu.make_async_remote_copy(
                src_ref=src.at[level], dst_ref=dst.at[slot], send_sem=ssem_s.at[2 * slot + j],
                recv_sem=ssem_r.at[2 * slot + j], device_id=dev, device_id_type=MESH_ID,
            )
            copy.start()
            sends.append(copy)
            out.append(copy)
        return out

    def small_add(level, copies, slots):
        for cp in copies:
            cp.wait_recv()
        total, share = SB[level], FR[level]
        for s in slots:
            total = total + SBR[s]
            share = share + FRR[s]
        SB[level + 1] = total
        FR[level + 1] = share

    s0 = small_send(0, 0, peer)
    at("fb")
    small_add(0, s0, (0,))
    s1 = small_send(1, 1, xp)
    at("e1")
    small_add(1, s1, (1,))
    s2 = small_send(2, 2, yp)
    at("e2")
    small_add(2, s2, (2,))
    s3 = []
    for k in range(3):
        s3 += small_send(3, 3 + k, zp[k])
    at("e3")
    small_add(3, s3, (3, 4, 5))
    keep_small = pltpu.make_async_copy(SB.at[4], o_small, lsem.at[len(loads) + 2])
    keep_frac = pltpu.make_async_copy(FR.at[4], o_frac, lsem.at[len(loads) + 3])
    keep_small.start()
    keep_frac.start()
    at("end")
    for cp in sends:
        cp.wait_send()
    for cp in (keep_out, keep_in, keep_small, keep_frac):
        cp.wait()


N_LOADS = 2 + 9 + 3 + 5
BIG = (0, 1, 2, 5, 7, 9)


def place_kernel(*refs):
    src, dst, bufs, (vals, sem) = refs[:8], refs[8:25], refs[25:31], refs[31:]
    dp = lax.axis_index("dp")
    o_small, o_frac = src[6:]
    ins = [pltpu.make_async_copy(src[i], bufs[i], sem.at[i]) for i in range(6)]
    outs = [pltpu.make_async_copy(bufs[i], dst[k], sem.at[6 + i]) for i, k in enumerate(BIG)]
    for cp in ins:
        cp.start()
    rows = o_small[...]
    shift = lax.rem(dp * (WIDTH - 48), WIDTH)
    mine = pltpu.roll(rows, shift, 1)[:, :48]
    for row, out in zip(range(9), (3, 4, 6, 10, 11, 12, 13, 14, 15)):
        dst[out][...] = mine[row : row + 1, :]
    vals[...] = pltpu.roll(rows, lax.rem(lax.rem(dp, 4) * (WIDTH - 192), WIDTH), 1)
    dst[8][...] = vals[pl.ds(9 + lax.div(dp, 4), 1), :192]
    dst[16][...] = o_frac[:, :3]
    for a, b in zip(ins, outs):
        a.wait()
        b.start()
    for cp in outs:
        cp.wait()


def fused(
    tokens, cotangent, group, select, w_qkv, b_query, b_value, w_out, b_out, w_up, b_up, w_down,
    b_down, ln1_gain, ln1_bias, ln2_gain, ln2_bias, w_router,
):
    args = (
        tokens, cotangent, group, select, w_qkv, b_query, b_value, w_out, b_out, w_up, b_up, w_down,
        b_down, ln1_gain, ln1_bias, ln2_gain, ln2_bias, w_router,
    )
    anywhere = pl.BlockSpec(memory_space=pl.ANY)
    vmem = pl.BlockSpec(memory_space=pltpu.VMEM)
    shape = jax.ShapeDtypeStruct
    mids = (
        shape((1, OWN, WIDTH), bf16), shape((1, OWN, WIDTH), bf16), shape((48, 3 * WIDTH), f32),
        shape((48, WIDTH), f32), shape((48, HIDDEN), f32), shape((192, WIDTH), f32),
        shape((SMALL, WIDTH), f32), shape((SMALL, 128), f32),
    )
    v = pltpu.VMEM
    sq = (PAD_LEN, WIDTH)
    scratch = [
        v(sq, bf16), v(sq, bf16), v((2, 1, OWN), jnp.int32), v((9, 1, WIDTH), f32), v((1, HIDDEN), f32),
        v(sq, bf16), v((WIDTH, 3 * HALF), bf16), v((WIDTH, WIDTH), bf16), v((WIDTH, HID), bf16),
        v((HID, WIDTH), bf16), v((PAD_LEN, 3 * HALF), bf16), v((2 * PAIRS, PAD_LEN, PAD_LEN), bf16),
        v((2, PAD_LEN, HALF), bf16), v(sq, f32), v(sq, bf16), v(sq, bf16), v((PAD_LEN, PAD_LEN), f32),
        v((PAD_LEN, 1), f32), v((PAD_LEN, 1), f32),
        v((PAD_LEN, HALF), bf16), v((PAD_LEN, HALF), bf16), v(sq, f32), v(sq, f32), v(sq, bf16), v(sq, bf16),
        v((OWN, WIDTH), bf16), v((OWN, WIDTH), bf16), v(sq, bf16), v((PAD_LEN, HALF), bf16),
        v((PAD_LEN, 3 * HALF), bf16), v((PAD_LEN, 128), f32), v((PAD_LEN, 128), f32),
        v((OWN, WIDTH), bf16), v((OWN, WIDTH), bf16), v((OWN, WIDTH), bf16), v((OWN, WIDTH), bf16),
        v((8, 4, 2, 2, 48, HALF), bf16), v((8, 4, 2, 48, HALF), bf16), v((8, 4, 48, HALF), bf16),
        v((8, 3, 48, HALF), bf16), v((8, 48, HALF), f32),
        v((4, 1, 2, 2, 192, HALF), bf16), v((4, 1, 2, 192, HALF), bf16), v((4, 1, 192, HALF), bf16),
        v((4, 3, 192, HALF), bf16), v((4, 192, HALF), f32),
        v((3, 2, 2, 48, HALF), bf16), v((2, 48, HALF), bf16),
        v((5, SMALL, WIDTH), f32), v((6, SMALL, WIDTH), f32), v((5, SMALL, 128), f32), v((6, SMALL, 128), f32),
        pltpu.SemaphoreType.DMA((N_LOADS + 4,)),
        pltpu.SemaphoreType.DMA((9,)), pltpu.SemaphoreType.DMA((9,)),
        pltpu.SemaphoreType.DMA((7 * PIECES,)), pltpu.SemaphoreType.DMA((7 * PIECES,)),
        pltpu.SemaphoreType.DMA((12,)), pltpu.SemaphoreType.DMA((12,)),
        pltpu.SemaphoreType.DMA((PIECES,)), pltpu.SemaphoreType.DMA((PIECES,)), pltpu.SemaphoreType.DMA((PIECES,)),
    ]
    mid = pl.pallas_call(
        layer_kernel,
        out_shape=mids,
        in_specs=[anywhere, anywhere, pl.BlockSpec(memory_space=pltpu.SMEM)] + [anywhere] * 15,
        out_specs=[anywhere] * 8,
        scratch_shapes=scratch,
        compiler_params=pltpu.CompilerParams(
            collective_id=0, has_side_effects=True, vmem_limit_bytes=60 << 20
        ),
        name="layer",
    )(*args)
    outs = (
        mids[0], mids[1], mids[2], shape((1, 48), f32), shape((1, 48), f32), mids[3], shape((1, 48), f32),
        mids[4], shape((1, 192), f32), mids[5],
    ) + (shape((1, 48), f32),) * 6 + (shape((16, 3), f32),)
    out = pl.pallas_call(
        place_kernel,
        out_shape=outs,
        in_specs=[anywhere] * 6 + [vmem] * 2,
        out_specs=[anywhere if i in BIG else vmem for i in range(17)],
        scratch_shapes=[v(mids[i].shape, mids[i].dtype) for i in range(6)]
        + [v((SMALL, WIDTH), f32), pltpu.SemaphoreType.DMA((12,))],
        name="place",
    )(*mid)
    return tuple(o.reshape(-1) if o.shape[0] == 1 and o.ndim == 2 else o for o in out)


def norm_rows(values, norm_gain, norm_shift):
    average = jnp.mean(values, axis=-1, keepdims=True)
    centred = values - average
    variance = jnp.mean(centred * centred, axis=-1, keepdims=True)
    return centred * lax.rsqrt(variance + epsilon) * norm_gain + norm_shift


def places_of(group, slot_pos):
    short_place = jnp.minimum(slot_pos // SHORT_LEN, 2)
    return jnp.where(group[:, None] == 1, 0, short_place[None, :])


def split_heads(flat_rows):
    return flat_rows.reshape(flat_rows.shape[0], flat_rows.shape[1], HEADS, HEAD_DIM)


def masked_scores(queries, key_heads, query_place, key_place, key_mask):
    score_scale = HEAD_DIM ** (-0.5)
    scores = (
        jnp.einsum("bqhe,bkhe->bqhk", queries, key_heads, preferred_element_type=jnp.float32)
        * score_scale
    )
    key_live = (key_mask.astype(jnp.float32)[:, None, None, :] > 0.5) & (
        query_place[:, :, None, None] == key_place[:, None, None, :]
    )
    return (jnp.where(key_live, scores, masked_floor), key_live.astype(jnp.float32))


def attend(queries, key_heads, value_heads, query_place, key_place, key_mask):
    masked, key_weight = masked_scores(queries, key_heads, query_place, key_place, key_mask)
    row_max = jnp.max(masked, axis=-1, keepdims=True)
    exponent = jnp.exp(masked - row_max) * key_weight
    row_sum = jnp.sum(exponent, axis=-1, keepdims=True)
    weights = (exponent / row_sum).astype(jnp.bfloat16)
    mixed_heads = jnp.einsum(
        "bqhk,bkhe->bqhe", weights, value_heads, preferred_element_type=jnp.float32
    )
    return (mixed_heads, row_max + jnp.log(row_sum))


def back_parts(
    queries, key_heads, value_heads, query_place, key_place, key_mask, log_total, grad_heads, delta
):
    masked, key_weight = masked_scores(queries, key_heads, query_place, key_place, key_mask)
    key_probs = jnp.exp(masked - log_total) * key_weight
    grad_probs = jnp.einsum(
        "bqhe,bkhe->bqhk", grad_heads, value_heads, preferred_element_type=jnp.float32
    )
    delta = jnp.sum(key_probs * grad_probs, axis=-1, keepdims=True)
    grad_scores = (key_probs * (grad_probs - delta)).astype(jnp.bfloat16)
    return (key_probs, grad_scores, delta)


def key_side_grads(key_probs, grad_scores, queries, grad_heads):
    score_scale = HEAD_DIM ** (-0.5)
    grad_values = jnp.einsum(
        "bqhk,bqhe->bkhe",
        key_probs.astype(jnp.bfloat16),
        grad_heads,
        preferred_element_type=jnp.float32,
    )
    grad_keys = (
        jnp.einsum("bqhk,bqhe->bkhe", grad_scores, queries, preferred_element_type=jnp.float32)
        * score_scale
    )
    return (grad_keys, grad_values)


def on_device(
    tokens,
    cotangent,
    group,
    select,
    w_qkv,
    b_query,
    b_value,
    w_out,
    b_out,
    w_up,
    b_up,
    w_down,
    b_down,
    ln1_gain,
    ln1_bias,
    ln2_gain,
    ln2_bias,
    w_router,
):
    packs, per_piece, features = tokens.shape
    row_count = packs * per_piece
    first_pos = lax.axis_index("seq") * per_piece
    positions = first_pos + jnp.arange(per_piece, dtype=jnp.int32)
    full_positions = jnp.arange(PAD_LEN, dtype=jnp.int32)
    place_own = places_of(group, positions)
    place_full = places_of(group, full_positions)
    ends = jnp.where(group == 1, LONG_LEN, 3 * SHORT_LEN).astype(jnp.int32)
    active = ((select > 0) & (positions[None, :] < ends[:, None])).astype(jnp.float32)
    active_rows = active.reshape(row_count, 1)
    xfloat = tokens.reshape(row_count, features).astype(jnp.float32)
    router = jax.nn.sigmoid(jnp.dot(xfloat, w_router, precision=lax.Precision.HIGHEST))
    normed, first_back = jax.vjp(norm_rows, xfloat, ln1_gain, ln1_bias)
    normed_low = normed.astype(jnp.bfloat16)
    qkv_bias = jnp.concatenate([b_query, jnp.zeros_like(b_query), b_value])
    triple = (jnp.dot(normed_low, w_qkv, preferred_element_type=jnp.float32) + qkv_bias).astype(
        jnp.bfloat16
    )
    queries = triple[:, :features].reshape(packs, per_piece, HEADS, HEAD_DIM)
    keys_own = triple[:, features : 2 * features].reshape(packs, per_piece, features)
    values_own = triple[:, 2 * features :].reshape(packs, per_piece, features)
    mask_own = active.astype(jnp.bfloat16)
    keys_all, values_all, mask_all = (
        lax.all_gather(keys_own, "seq", axis=1, tiled=True),
        lax.all_gather(values_own, "seq", axis=1, tiled=True),
        lax.all_gather(mask_own, "seq", axis=1, tiled=True),
    )
    mixed_heads, log_total = attend(
        queries, split_heads(keys_all), split_heads(values_all), place_own, place_full, mask_all
    )
    mixed_low = mixed_heads.reshape(row_count, features).astype(jnp.bfloat16)
    attended = jnp.dot(mixed_low, w_out, preferred_element_type=jnp.float32) + b_out
    summed = xfloat + attended
    second, second_back = jax.vjp(norm_rows, summed, ln2_gain, ln2_bias)
    second_low = second.astype(jnp.bfloat16)
    pre_act = jnp.dot(second_low, w_up, preferred_element_type=jnp.float32) + b_up
    gelu_out, gelu_back = jax.vjp(partial(jax.nn.gelu, approximate=False), pre_act)
    hidden_low = gelu_out.astype(jnp.bfloat16)
    branch = attended + (jnp.dot(hidden_low, w_down, preferred_element_type=jnp.float32) + b_down)
    gate_rows = active_rows * router[:, None]
    output = (xfloat + gate_rows * branch).astype(jnp.bfloat16).reshape(packs, per_piece, features)
    place_range = jnp.arange(3, dtype=jnp.int32)
    onehot = (place_full[:, :, None] == place_range[None, None, :]).astype(jnp.float32)
    counts = jnp.sum(mask_all.astype(jnp.float32)[:, :, None] * onehot, axis=1)
    image_lengths = jnp.where(group == 1, LONG_LEN, SHORT_LEN).astype(jnp.float32)
    fractions = lax.all_gather(counts / image_lengths[:, None], "dp", axis=0, tiled=True)
    grad_rows = cotangent.reshape(row_count, features).astype(jnp.float32)
    grad_logit = jnp.sum(grad_rows * branch, axis=1) * active_rows[:, 0] * router * (1.0 - router)
    grad_branch = gate_rows * grad_rows
    grad_mlp = grad_branch.astype(jnp.bfloat16)
    grad_down = jnp.einsum("rk,rd->kd", hidden_low, grad_mlp, preferred_element_type=jnp.float32)
    grad_down_bias = jnp.sum(grad_mlp.astype(jnp.float32), axis=0)
    grad_hidden = jnp.einsum("rd,kd->rk", grad_mlp, w_down, preferred_element_type=jnp.float32)
    grad_pre = gelu_back(grad_hidden)[0].astype(jnp.bfloat16)
    grad_up = jnp.einsum("rd,rk->dk", second_low, grad_pre, preferred_element_type=jnp.float32)
    grad_up_bias = jnp.sum(grad_pre.astype(jnp.float32), axis=0)
    grad_second = jnp.einsum("rk,dk->rd", grad_pre, w_up, preferred_element_type=jnp.float32)
    grad_summed, grad_ln2_gain, grad_ln2_bias = second_back(grad_second)
    grad_attended = (grad_branch + grad_summed).astype(jnp.bfloat16)
    grad_out = jnp.einsum("rd,re->de", mixed_low, grad_attended, preferred_element_type=jnp.float32)
    grad_out_bias = jnp.sum(grad_attended.astype(jnp.float32), axis=0)
    grad_mixed = jnp.einsum("re,de->rd", grad_attended, w_out, preferred_element_type=jnp.float32)
    grad_heads = grad_mixed.astype(jnp.bfloat16).reshape(packs, per_piece, HEADS, HEAD_DIM)
    back_k, back_v, back_m = (
        lax.all_gather(keys_own, "seq", axis=1, tiled=True),
        lax.all_gather(values_own, "seq", axis=1, tiled=True),
        lax.all_gather(mask_own, "seq", axis=1, tiled=True),
    )
    back_kh = split_heads(back_k)
    back_vh = split_heads(back_v)
    key_probs, grad_scores, delta = back_parts(
        queries, back_kh, back_vh, place_own, place_full, back_m, log_total, grad_heads, None
    )
    grad_queries = jnp.einsum(
        "bqhk,bkhe->bqhe", grad_scores, back_kh, preferred_element_type=jnp.float32
    ) * HEAD_DIM ** (-0.5)
    grad_keys, grad_values = key_side_grads(key_probs, grad_scores, queries, grad_heads)
    keys_grad_own, values_grad_own = (
        lax.psum_scatter(
            grad_keys.reshape(back_k.shape).astype(jnp.bfloat16),
            "seq",
            scatter_dimension=1,
            tiled=True,
        ).astype(jnp.float32),
        lax.psum_scatter(
            grad_values.reshape(back_v.shape).astype(jnp.bfloat16),
            "seq",
            scatter_dimension=1,
            tiled=True,
        ).astype(jnp.float32),
    )
    grad_triple = jnp.concatenate(
        [
            grad_queries.reshape(row_count, features),
            keys_grad_own.reshape(row_count, features),
            values_grad_own.reshape(row_count, features),
        ],
        axis=1,
    ).astype(jnp.bfloat16)
    grad_qkv = jnp.einsum("rd,rk->dk", normed_low, grad_triple, preferred_element_type=jnp.float32)
    column_sums = jnp.sum(grad_triple.astype(jnp.float32), axis=0)
    grad_query_bias = column_sums[:features]
    grad_value_bias = column_sums[2 * features :]
    grad_normed = jnp.einsum("rk,dk->rd", grad_triple, w_qkv, preferred_element_type=jnp.float32)
    grad_first, grad_ln1_gain, grad_ln1_bias = first_back(grad_normed)
    grad_router = jnp.dot(grad_logit, xfloat, precision=lax.Precision.HIGHEST)
    grad_input = grad_rows + grad_summed + grad_first + grad_logit[:, None] * w_router[None, :]
    input_grad = grad_input.astype(jnp.bfloat16).reshape(packs, per_piece, features)
    (
        share_qkv,
        share_query_bias,
        share_value_bias,
        share_out,
        share_out_bias,
        share_up,
        share_up_bias,
        share_down,
        share_down_bias,
        share_ln1_gain,
        share_ln1_bias,
        share_ln2_gain,
        share_ln2_bias,
        share_router,
    ) = (
        lax.psum_scatter(
            grad_qkv.astype(jnp.bfloat16), "dp", scatter_dimension=0, tiled=True
        ).astype(jnp.float32),
        lax.psum_scatter(
            grad_query_bias.astype(jnp.bfloat16), "dp", scatter_dimension=0, tiled=True
        ).astype(jnp.float32),
        lax.psum_scatter(
            grad_value_bias.astype(jnp.bfloat16), "dp", scatter_dimension=0, tiled=True
        ).astype(jnp.float32),
        lax.psum_scatter(
            grad_out.astype(jnp.bfloat16), "dp", scatter_dimension=0, tiled=True
        ).astype(jnp.float32),
        lax.psum_scatter(
            grad_out_bias.astype(jnp.bfloat16), "dp", scatter_dimension=0, tiled=True
        ).astype(jnp.float32),
        lax.psum_scatter(
            grad_up.astype(jnp.bfloat16), "dp", scatter_dimension=0, tiled=True
        ).astype(jnp.float32),
        lax.psum_scatter(
            grad_up_bias.astype(jnp.bfloat16), "dp", scatter_dimension=0, tiled=True
        ).astype(jnp.float32),
        lax.psum_scatter(
            grad_down.astype(jnp.bfloat16), "dp", scatter_dimension=0, tiled=True
        ).astype(jnp.float32),
        lax.psum_scatter(
            grad_down_bias.astype(jnp.bfloat16), "dp", scatter_dimension=0, tiled=True
        ).astype(jnp.float32),
        lax.psum_scatter(
            grad_ln1_gain.astype(jnp.bfloat16), "dp", scatter_dimension=0, tiled=True
        ).astype(jnp.float32),
        lax.psum_scatter(
            grad_ln1_bias.astype(jnp.bfloat16), "dp", scatter_dimension=0, tiled=True
        ).astype(jnp.float32),
        lax.psum_scatter(
            grad_ln2_gain.astype(jnp.bfloat16), "dp", scatter_dimension=0, tiled=True
        ).astype(jnp.float32),
        lax.psum_scatter(
            grad_ln2_bias.astype(jnp.bfloat16), "dp", scatter_dimension=0, tiled=True
        ).astype(jnp.float32),
        lax.psum_scatter(
            grad_router.astype(jnp.bfloat16), "dp", scatter_dimension=0, tiled=True
        ).astype(jnp.float32),
    )
    totals = (
        lax.psum(share_qkv.astype(jnp.bfloat16), "seq").astype(jnp.float32),
        lax.psum(share_query_bias.astype(jnp.bfloat16), "seq").astype(jnp.float32),
        lax.psum(share_value_bias.astype(jnp.bfloat16), "seq").astype(jnp.float32),
        lax.psum(share_out.astype(jnp.bfloat16), "seq").astype(jnp.float32),
        lax.psum(share_out_bias.astype(jnp.bfloat16), "seq").astype(jnp.float32),
        lax.psum(share_up.astype(jnp.bfloat16), "seq").astype(jnp.float32),
        lax.psum(share_up_bias.astype(jnp.bfloat16), "seq").astype(jnp.float32),
        lax.psum(share_down.astype(jnp.bfloat16), "seq").astype(jnp.float32),
        lax.psum(share_down_bias.astype(jnp.bfloat16), "seq").astype(jnp.float32),
        lax.psum(share_ln1_gain.astype(jnp.bfloat16), "seq").astype(jnp.float32),
        lax.psum(share_ln1_bias.astype(jnp.bfloat16), "seq").astype(jnp.float32),
        lax.psum(share_ln2_gain.astype(jnp.bfloat16), "seq").astype(jnp.float32),
        lax.psum(share_ln2_bias.astype(jnp.bfloat16), "seq").astype(jnp.float32),
        lax.psum(share_router.astype(jnp.bfloat16), "seq").astype(jnp.float32),
    )
    return (
        output,
        input_grad,
        totals[0],
        totals[1],
        totals[2],
        totals[3],
        totals[4],
        totals[5],
        totals[6],
        totals[7],
        totals[8],
        totals[9],
        totals[10],
        totals[11],
        totals[12],
        totals[13],
        fractions,
    )


def solution(mesh):
    in_specs = (
        P("dp", "seq", None),
        P("dp", "seq", None),
        P("dp"),
        P("dp", "seq"),
        P(),
        P(),
        P(),
        P(),
        P(),
        P(),
        P(),
        P(),
        P(),
        P(),
        P(),
        P(),
        P(),
        P(),
    )
    out_specs = (
        P("dp", "seq", None),
        P("dp", "seq", None),
        P("dp", None),
        P("dp"),
        P("dp"),
        P("dp", None),
        P("dp"),
        P("dp", None),
        P("dp"),
        P("dp", None),
        P("dp"),
        P("dp"),
        P("dp"),
        P("dp"),
        P("dp"),
        P("dp"),
        P(),
    )
    fast = mesh.shape["dp"] == 16 and mesh.shape["seq"] == 2
    return jax.shard_map(
        fused if fast else on_device, mesh=mesh, in_specs=in_specs, out_specs=out_specs, check_vma=False
    )
```

```python
from functools import partial

import jax
import jax.numpy as jnp
from jax import lax
from jax.experimental import pallas as pl
from jax.experimental.pallas import tpu as pltpu
from jax.sharding import PartitionSpec as P

HEADS = 12
HEAD_DIM = 64
PAD_LEN = 640
LONG_LEN = 577
SHORT_LEN = 197
WIDTH = 768
HIDDEN = 3072

epsilon = 1e-06
masked_floor = -1000000000.0
MESH_ID = pl.DeviceIdType.MESH
bf16 = jnp.bfloat16
f32 = jnp.float32

HALF = WIDTH // 2
OWN = PAD_LEN // 2
HID = HIDDEN // 2
BLOCKS = HID // HALF
PAIRS = HALF // 128
MT = 320
AT = 640
LT = 160
SMALL = 16
PIECES = 12
ORDER = {
    "up0": "z",
    "dA0": "x",
    "up1": "x",
    "dB0": "y",
    "up2": "y",
    "up3": "x",
    "dA1": "x",
    "dB1": "x",
    "out": "y",
    "q": "y",
    "k": "y",
    "v": "x",
}
HALVED = ("dA0", "dA1")
SCHEDULE = {
    "u0": (
        (1, "up0"),
    ),
    "j0": (
        (0, "dA0"),
    ),
    "u1": (
        (1, "up1"),
    ),
    "j1": (
        (1, "dB0"),
    ),
    "u2": (
        (1, "dA0"),
    ),
    "j2": (
        (0, "dA1"), (1, "up2"),
    ),
    "u3": (
        (2, "up1"), (2, "dB0"),
    ),
    "j3": (
        (2, "up0"), (2, "dA0"),
    ),
    "gmx": (
        (1, "up3"),
    ),
    "h0": (
        (2, "up2"),
    ),
    "h1": (
        (1, "out"), (3, "dB0"), (3, "up1"), (3, "up0"),
    ),
    "q": (
        (3, "dA0"),
    ),
    "ns": (
        (4, "dB0"),
    ),
    "fb": (
        (1, "dA1"), (1, "q"), (1, "small"), (2, "up3"), (5, "dB0"),
    ),
    "end": (
        (4, "up1"), (2, "small"), (2, "out"), (5, "up1"), (3, "up2"), (4, "up0"), (4, "dA0"), (5, "up0"),
        (5, "dA0"), (1, "dB1"), (2, "dA1"), (3, "small"), (4, "up2"), (5, "up2"), (2, "q"), (3, "out"), (3, "up3"),
        (1, "k"), (4, "out"), (3, "dA1"), (1, "v"), (2, "dB1"), (4, "small"), (5, "out"), (4, "up3"), (3, "q"),
        (5, "up3"), (4, "dA1"), (2, "k"), (5, "dA1"), (5, "small"), (6, "small"), (2, "v"), (3, "dB1"), (4, "q"),
        (5, "q"), (3, "k"), (3, "v"), (4, "dB1"), (5, "dB1"), (4, "k"), (5, "k"), (4, "v"), (5, "v"),
    ),
}


def dot_nn(a, b):
    return lax.dot_general(a, b, (((1,), (0,)), ((), ())), preferred_element_type=f32)


def dot_nt(a, b):
    return lax.dot_general(a, b, (((1,), (1,)), ((), ())), preferred_element_type=f32)


def dot_tn(a, b):
    return lax.dot_general(a, b, (((0,), (0,)), ((), ())), preferred_element_type=f32)


def row_stats(values):
    average = jnp.mean(values, axis=-1, keepdims=True)
    centred = values - average
    variance = jnp.mean(centred * centred, axis=-1, keepdims=True)
    rstd = lax.rsqrt(variance + epsilon)
    return centred * rstd, rstd


def norm_back(unit, rstd, grad, gain):
    q = grad * gain
    return rstd * (
        q - jnp.mean(q, axis=-1, keepdims=True) - unit * jnp.mean(q * unit, axis=-1, keepdims=True)
    )


def layer_kernel(
    tokens, cotangent, group, select, w_qkv, b_query, b_value, w_out, b_out, w_up, b_up, w_down,
    b_down, ln1_gain, ln1_bias, ln2_gain, ln2_bias, w_router,
    o_output, o_input, o_qkv, o_out, o_up, o_down, o_small,
    X, G, SEL, VEC, BUP, NRM, WQ, WO, WU, WD, TRI, PR, MIX, SUM, SEC, GM, BIAS, GATE, ACT,
    HIDJ, GPJ, ACCD, ACCS, GSB, GSR, DSB, DSR, GATT, GMX, DTR, DKT, DVT, INV, SECT, NSR,
    S4, R14, R24, R34, F4, S1, R11, R21, R31, F1, RZ, RZ2, SB, SBL, SBR,
    lsem, esem_s, esem_r, csem_s, csem_r, ssem_s, ssem_r, fsem_l, fsem_s, fsem_r,
):
    dp = lax.axis_index("dp")
    c = lax.axis_index("seq")
    x = lax.rem(dp, 2)
    y = lax.rem(lax.div(dp, 2), 2)
    z = lax.div(dp, 4)
    peer = (dp, 1 - c)
    xp = ((z * 2 + y) * 2 + (1 - x), c)
    yp = ((z * 2 + (1 - y)) * 2 + x, c)
    zs = [lax.rem(z + k, 4) for k in (1, 2, 3)]
    zp = [((zk * 2 + y) * 2 + x, c) for zk in zs]
    own = pl.multiple_of(c * OWN, OWN)
    oth = pl.multiple_of((1 - c) * OWN, OWN)
    chalf = pl.multiple_of(c * HALF, HALF)
    chid = pl.multiple_of(c * HID, HID)
    lead = (c == 0).astype(f32)

    barrier = pltpu.get_barrier_semaphore()
    for other in [peer, xp, yp] + zp:
        pl.semaphore_signal(barrier, inc=1, device_id=other, device_id_type=MESH_ID)

    loads = {}

    def load(name, src, dst):
        copy = pltpu.make_async_copy(src, dst, lsem.at[len(loads)])
        copy.start()
        loads[name] = copy

    load("tok", tokens.at[0], X.at[pl.ds(own, OWN)])
    load("sel", select, SEL.at[c])
    for i, v in enumerate(
        (b_query, b_value, b_out, b_down, ln1_gain, ln1_bias, ln2_gain, ln2_bias, w_router)
    ):
        load("v%d" % i, v, VEC.at[i, 0])
    for k in range(3):
        load(
            "wq%d" % k,
            w_qkv.at[:, pl.ds(pl.multiple_of(k * WIDTH + c * HALF, 128), HALF)],
            WQ.at[:, pl.ds(k * HALF, HALF)],
        )
    load("cot", cotangent.at[0], G.at[pl.ds(own, OWN)])
    load("bup", b_up, BUP.at[0])
    load("wo", w_out, WO)
    load("wu", w_up.at[:, pl.ds(chid, HID)], WU)
    load("wd", w_down.at[pl.ds(chid, HID)], WD)

    pl.semaphore_wait(barrier, 6)

    sends = []
    counts = {"e": 0, "c": 0}

    def to_core(src, dst):
        i = counts["e"]
        counts["e"] += 1
        copy = pltpu.make_async_remote_copy(
            src_ref=src, dst_ref=dst, send_sem=esem_s.at[i], recv_sem=esem_r.at[i],
            device_id=peer, device_id_type=MESH_ID,
        )
        copy.start()
        sends.append(copy)
        return copy

    ex_sel = to_core(select, SEL.at[c])
    ex_tok = to_core(tokens.at[0], X.at[pl.ds(own, OWN)])
    ex_cot = to_core(cotangent.at[0], G.at[pl.ds(own, OWN)])

    SB[...] = jnp.zeros_like(SB)

    def vec(i):
        return VEC[i]

    def project(start):
        @pl.loop(0, OWN // LT)
        def _(t):
            rows = pl.ds(pl.multiple_of(start + t * LT, 32), LT)
            xf = X[rows, :].astype(f32)
            unit, _ = row_stats(xf)
            NRM[rows, :] = (unit * vec(4) + vec(5)).astype(bf16)
            logit = jnp.sum(xf * vec(8), axis=-1, keepdims=True)
            GATE[rows, :] = 1.0 / (1.0 + jnp.exp(-logit))

        if start is own:
            for k in range(3):
                loads["wq%d" % k].wait()
        rows = pl.ds(start, OWN)
        nr = NRM[rows, :]
        for k in range(3):
            r = dot_nn(nr, WQ[:, k * HALF : (k + 1) * HALF])
            if k == 0:
                r = (r + VEC[0, :, pl.ds(chalf, HALF)]).astype(bf16).astype(f32) * HEAD_DIM ** (-0.5)
            if k == 2:
                r = r + VEC[1, :, pl.ds(chalf, HALF)]
            TRI[rows, k * HALF : (k + 1) * HALF] = r.astype(bf16)

    loads["tok"].wait()
    for i in range(9):
        loads["v%d" % i].wait()
    project(own)

    loads["sel"].wait()
    ex_sel.wait_recv()
    gv = jnp.full((1, 1), group[0], jnp.int32)
    long_row = jnp.broadcast_to(gv, (1, PAD_LEN)) == 1
    pos_row = lax.broadcasted_iota(jnp.int32, (1, PAD_LEN), 1)
    short_row = (pos_row >= SHORT_LEN).astype(jnp.int32) + (pos_row >= 2 * SHORT_LEN).astype(jnp.int32)
    place_row = jnp.where(long_row, 0, short_row)
    end_row = jnp.where(long_row, LONG_LEN, 3 * SHORT_LEN)
    long_col = jnp.broadcast_to(gv, (PAD_LEN, 1)) == 1
    pos_col = lax.broadcasted_iota(jnp.int32, (PAD_LEN, 1), 0)
    short_col = (pos_col >= SHORT_LEN).astype(jnp.int32) + (pos_col >= 2 * SHORT_LEN).astype(jnp.int32)
    place_col = jnp.where(long_col, 0, short_col)
    end_col = jnp.where(long_col, LONG_LEN, 3 * SHORT_LEN)
    sel_row = jnp.zeros((8, PAD_LEN), f32)
    sel_col = jnp.zeros((PAD_LEN, 8), f32)
    for part in range(2):
        bits = jnp.broadcast_to((SEL[part] > 0).astype(f32), (8, OWN)).astype(bf16)
        spread = (
            lax.broadcasted_iota(jnp.int32, (PAD_LEN, OWN), 0)
            == lax.broadcasted_iota(jnp.int32, (PAD_LEN, OWN), 1) + part * OWN
        ).astype(f32).astype(bf16)
        sel_row = sel_row + dot_nt(bits, spread)
        sel_col = sel_col + dot_nt(spread, bits)
    act_row = jnp.where(pos_row < end_row, sel_row[0:1, :], 0.0)
    act_col = jnp.where(pos_col < end_col, sel_col[:, 0:1], 0.0)
    ACT[...] = act_col
    BIAS[...] = jnp.where(
        (jnp.broadcast_to(act_row, (PAD_LEN, PAD_LEN)) > 0.5)
        & (jnp.broadcast_to(place_col, (PAD_LEN, PAD_LEN)) == jnp.broadcast_to(place_row, (PAD_LEN, PAD_LEN))),
        0.0,
        -1e30,
    )
    lane = lax.broadcasted_iota(jnp.int32, (1, 128), 1)
    length = jnp.where(jnp.broadcast_to(gv, (1, 1)) == 1, float(LONG_LEN), float(SHORT_LEN))
    for j in range(3):
        count = jnp.sum(jnp.where(place_row == j, act_row, 0.0), axis=1, keepdims=True)
        SB[13 + j : 14 + j, 0:128] = jnp.where(lane == dp, count / length * lead, 0.0)

    ex_tok.wait_recv()
    project(oth)

    low_lanes = lax.broadcasted_iota(jnp.int32, (1, 128), 1) < HEAD_DIM

    def head_part(v, side):
        keep = low_lanes if side == 0 else jnp.logical_not(low_lanes)
        return jnp.where(keep, v, jnp.zeros_like(v))

    def pair_lanes(hp):
        return [slice(k * HALF + hp * 128, k * HALF + hp * 128 + 128) for k in range(3)]

    def with_ones(v, side):
        return jnp.where(lane == (1 - side) * HEAD_DIM, jnp.ones_like(v), head_part(v, side))

    ex_mix = []
    for hp in range(PAIRS):
        qlanes, klanes, vlanes = pair_lanes(hp)

        @pl.loop(0, PAD_LEN // AT)
        def _(t):
            rows = pl.ds(pl.multiple_of(t * AT, AT), AT)
            qp = TRI[rows, qlanes]
            kp = TRI[:, klanes]
            vp = TRI[:, vlanes]
            both = []
            for side in range(2):
                s = dot_nt(head_part(qp, side), kp) + BIAS[rows, :]
                e = jnp.exp(s - jnp.max(s, axis=-1, keepdims=True)).astype(bf16)
                PR[2 * hp + side, rows, :] = e
                both.append(dot_nn(e, with_ones(vp, side)))
            scale = 1.0 / jnp.where(low_lanes, both[0][:, HEAD_DIM : HEAD_DIM + 1], both[1][:, 0:1])
            INV[rows, qlanes] = scale
            MIX[c, rows, qlanes] = (jnp.where(low_lanes, both[0], both[1]) * scale).astype(bf16)

        ex_mix.append(to_core(MIX.at[c, :, qlanes], MIX.at[c, :, qlanes]))

    loads["wo"].wait()

    @pl.loop(0, PAD_LEN // MT)
    def _(t):
        rows = pl.ds(pl.multiple_of(t * MT, MT), MT)
        SUM[rows, :] = X[rows, :].astype(f32) + (dot_nn(MIX[c, rows, :], WO[pl.ds(chalf, HALF), :]) + vec(2))

    loads["cot"].wait()
    ex_cot.wait_recv()

    @pl.loop(0, PAD_LEN // LT)
    def _(t):
        rows = pl.ds(pl.multiple_of(t * LT, LT), LT)
        GM[rows, :] = (ACT[rows, :] * GATE[rows, :] * G[rows, :].astype(f32)).astype(bf16)

    for e in ex_mix:
        e.wait_recv()

    @pl.loop(0, PAD_LEN // MT)
    def _(t):
        rows = pl.ds(pl.multiple_of(t * MT, MT), MT)
        s = SUM[rows, :] + dot_nn(MIX[1 - c, rows, :], WO[pl.ds(pl.multiple_of(HALF - chalf, HALF), HALF), :])
        SUM[rows, :] = s
        unit, _ = row_stats(s)
        SEC[rows, :] = (unit * vec(6) + vec(7)).astype(bf16)

    SECT[...] = jnp.swapaxes(SEC[...], 0, 1)

    for n in ("bup", "wu", "wd"):
        loads[n].wait()

    def remote(src, dst, dev, i):
        return pltpu.make_async_remote_copy(
            src_ref=src, dst_ref=dst, send_sem=csem_s.at[i], recv_sem=csem_r.at[i],
            device_id=dev, device_id_type=MESH_ID,
        )

    pieces = {}

    def start(st, key, i, src, dst, dev):
        cp = remote(src, dst, dev, i)
        cp.start()
        sends.append(cp)
        st.setdefault(key, []).append(cp)

    def wait(st, key):
        for cp in st[key]:
            cp.wait_recv()

    class Piece:
        def __init__(self, name, src, r1, r2, r3, fin, dst_ref, only_z=None):
            self.order, self.src, self.r1, self.r2, self.r3, self.fin = ORDER[name], src, r1, r2, r3, fin
            if self.order == "z":
                self.r1, self.r2, self.r3 = RZ, RZ2, r3.at[0]
            self.only_z = only_z
            self.number = len(pieces)
            self.base = self.number * 7
            self.st = {}
            self.keep = pltpu.make_async_copy(fin, dst_ref, fsem_l.at[self.number])
            self.give = pltpu.make_async_remote_copy(
                src_ref=fin, dst_ref=dst_ref, send_sem=fsem_s.at[self.number],
                recv_sem=fsem_r.at[self.number], device_id=peer, device_id_type=MESH_ID,
            )
            pieces[name] = self

        def first(self, part=None):
            src, r1, st, b = self.src, self.r1, self.st, self.base
            if self.order == "z":
                for k in range(3):
                    start(st, 1, b + k, src.at[zs[k]], r1.at[k], zp[k])
            elif part is not None:
                start(st, 1, b + part, src.at[:, part, 1 - x], r1.at[:, part], xp)
            elif self.order == "x":
                start(st, 1, b, src.at[:, :, 1 - x], r1, xp)
            else:
                start(st, 1, b, src.at[:, 1 - y], r1, yp)
            return self

        def second(self):
            src, r1, r2, st, b = self.src, self.r1, self.r2, self.st, self.base
            wait(st, 1)
            if self.order == "z":
                for a in range(2):
                    for d in range(2):
                        t = src[z, a, d].astype(f32) + r1[0, a, d].astype(f32)
                        t = t + (r1[1, a, d].astype(f32) + r1[2, a, d].astype(f32))
                        r1[0, a, d] = t.astype(bf16)
                start(st, 2, b + 3, r1.at[0, :, 1 - x], r2, xp)
                return
            for a in range(r1.shape[0]):
                for d in range(2):
                    mine = src[a, d, x] if self.order == "x" else src[a, y, d]
                    r1[a, d] = mine + r1[a, d]
            if self.order == "x":
                start(st, 2, b + 3, r1.at[:, 1 - y], r2, yp)
            else:
                start(st, 2, b + 3, r1.at[:, 1 - x], r2, xp)

        def third(self):
            r1, r2, r3, st, b = self.r1, self.r2, self.r3, self.st, self.base
            wait(st, 2)
            if self.order == "z":
                for a in range(2):
                    r2[a] = r1[0, a, x] + r2[a]
                start(st, 3, b + 4, r2.at[1 - y], r3, yp)
                return
            for a in range(r2.shape[0]):
                r2[a] = (r1[a, y] if self.order == "x" else r1[a, x]) + r2[a]
            for k in range(3):
                if self.only_z is None:
                    start(st, 3, b + 4 + k, r2.at[zs[k]], r3.at[k], zp[k])
                else:
                    cp = remote(r2.at[0], r3.at[k], zp[k], b + 4 + k)
                    pl.when(zs[k] == self.only_z)(cp.start)
                    st.setdefault(3, []).append(cp)

        def fourth(self):
            r2, r3, st, fin = self.r2, self.r3, self.st, self.fin

            def finish():
                wait(st, 3)
                if self.order == "z":
                    fin[...] = r2[y].astype(f32) + r3[...].astype(f32)
                else:
                    mine = r2[z] if self.only_z is None else r2[0]
                    fin[...] = mine.astype(f32) + r3[0].astype(f32) + (r3[1].astype(f32) + r3[2].astype(f32))
                self.keep.start()
                self.give.start()

            if self.only_z is None:
                finish()
            else:
                pl.when(z == self.only_z)(finish)

        def fifth(self):
            keep, give = self.keep, self.give
            if self.only_z is None:
                keep.wait()
                give.wait()
                return

            @pl.when(z == self.only_z)
            def _():
                keep.wait()
                give.wait_send()

            @pl.when(z == self.only_z + 2 - 4 * c)
            def _():
                give.wait_recv()

            for k in range(3):
                pl.when(zs[k] == self.only_z)(self.st[3][k].wait_send)

    def columns(start):
        return pl.ds(pl.multiple_of(start, 128), HALF)

    for i, (name, dst_ref) in enumerate(
        [("up%d" % j, o_up.at[:, columns(chid + j * HALF)]) for j in range(BLOCKS)]
        + [("out", o_out.at[:, columns(chalf)])]
        + [("qkv"[k], o_qkv.at[:, columns(k * WIDTH + chalf)]) for k in range(3)]
    ):
        Piece(name, S4.at[i], R14.at[i], R24.at[i], R34.at[i], F4.at[i], dst_ref)
    for i, name in enumerate(("dA0", "dB0", "dA1", "dB1")):
        Piece(
            name, S1.at[i], R11.at[i], R21.at[i], R31.at[i], F1.at[i],
            o_down.at[:, (i % 2) * HALF : (i % 2 + 1) * HALF], only_z=2 * c + i // 2,
        )

    class Small:
        def first(self, part=None):
            self.got = self.send(0, SB.at[pl.ds(pl.multiple_of(8 - 8 * c, 8), 8)], peer)

        def send(self, slot, src, dev):
            copy = pltpu.make_async_remote_copy(
                src_ref=src, dst_ref=SBR.at[slot], send_sem=ssem_s.at[slot], recv_sem=ssem_r.at[slot],
                device_id=dev, device_id_type=MESH_ID,
            )
            copy.start()
            sends.append(copy)
            return [copy]

        def gather(self, mine, slots):
            for cp in self.got:
                cp.wait_recv()
            for slot in slots:
                mine = mine + SBR[slot]
            return mine

        def second(self):
            SBL[0] = self.gather(SB[pl.ds(pl.multiple_of(8 * c, 8), 8), :], (0,))
            self.got = self.send(1, SBL.at[0], xp)

        def third(self):
            SBL[1] = self.gather(SBL[0], (1,))
            self.got = self.send(2, SBL.at[1], yp)

        def fourth(self):
            SBL[2] = self.gather(SBL[1], (2,))
            self.got = []
            for k in range(3):
                self.got += self.send(3 + k, SBL.at[2], zp[k])

        def fifth(self):
            SBL[3] = self.gather(SBL[2], (3, 4, 5))
            rows = o_small.at[pl.ds(pl.multiple_of(8 * c, 8), 8)]
            self.keep = pltpu.make_async_copy(SBL.at[3], rows, lsem.at[N_LOADS + 2])
            self.give = pltpu.make_async_remote_copy(
                src_ref=SBL.at[3], dst_ref=rows, send_sem=ssem_s.at[6], recv_sem=ssem_r.at[6],
                device_id=peer, device_id_type=MESH_ID,
            )
            self.keep.start()
            self.give.start()

        def sixth(self):
            self.keep.wait()
            self.give.wait()

    pieces["small"] = Small()

    def at(point):
        for act, name in SCHEDULE.get(point, ()):
            p = pieces[name]
            if act == 0:
                p.first(part=0)
            elif act == 1:
                p.first(part=1 if name in HALVED else None)
            else:
                getattr(p, ("second", "third", "fourth", "fifth", "sixth")[act - 2])()

    for j in range(BLOCKS):
        cols = slice(j * HALF, (j + 1) * HALF)
        bj = BUP[:, pl.ds(pl.multiple_of(chid + j * HALF, 128), HALF)]

        @pl.loop(0, PAD_LEN // MT)
        def _(t):
            rows = pl.ds(pl.multiple_of(t * MT, MT), MT)
            pre = dot_nn(SEC[rows, :], WU[:, cols]) + bj
            gh = dot_nt(GM[rows, :], WD[cols, :])
            cdf = 0.5 * (1.0 + lax.erf(pre * (2.0 ** -0.5)))
            hid = (pre * cdf).astype(bf16)
            slope = cdf + pre * (0.3989422804014327 * jnp.exp(-0.5 * pre * pre))
            gp = (gh * slope).astype(bf16)
            HIDJ[rows, :] = hid
            GPJ[rows, :] = gp
            d = dot_nn(hid, WD[cols, :])
            s = dot_nt(gp, WU[:, cols])
            if j > 0:
                d = ACCD[rows, :] + d
                s = ACCS[rows, :] + s
            ACCD[rows, :] = d
            ACCS[rows, :] = s
            if j == BLOCKS - 1:
                GSB[rows, :] = s.astype(bf16)

        if j == BLOCKS - 1:
            ex_gs = to_core(GSB, GSR)

            @pl.loop(0, OWN // LT)
            def _(t):
                r = pl.ds(pl.multiple_of(t * LT, LT), LT)
                DSB[r, :] = ACCD[pl.ds(pl.multiple_of(oth + t * LT, 32), LT), :].astype(bf16)

            ex_ds = to_core(DSB, DSR)

        for part in range(2):
            g = dot_nn(SECT[part * HALF : (part + 1) * HALF, :], GPJ[...])
            S4[j, 2 * part : 2 * part + 2] = g.astype(bf16).reshape(2, 2, 2, 48, HALF)
        at("u%d" % j)
        SB[pl.ds(9 + 2 * c + j // 2, 1), (j % 2) * HALF : (j % 2 + 1) * HALF] = jnp.sum(
            GPJ[...].astype(f32), axis=0, keepdims=True
        )
        for part in range(2):
            g = dot_tn(HIDJ[...], GM[:, part * HALF : (part + 1) * HALF])
            S1[2 * (j // 2) + part, 0, j % 2] = g.astype(bf16).reshape(2, 192, HALF)
        at("j%d" % j)

    ex_gs.wait_recv()

    zero_row = jnp.zeros((1, WIDTH), f32)

    def col_sum(v):
        return jnp.sum(v, axis=0, keepdims=True)

    def second_back(t, carry):
        rows = pl.ds(pl.multiple_of(t * LT, LT), LT)
        gs = ACCS[rows, :] + GSR[rows, :].astype(f32)
        unit, rstd = row_stats(SUM[rows, :])
        back = norm_back(unit, rstd, gs, vec(6))
        ACCS[rows, :] = back
        ga = (ACT[rows, :] * GATE[rows, :] * G[rows, :].astype(f32) + back).astype(bf16)
        GATT[rows, :] = ga
        return (
            carry[0] + col_sum(gs * unit), carry[1] + col_sum(gs), carry[2] + col_sum(ga.astype(f32)),
            carry[3] + col_sum(GM[rows, :].astype(f32)),
        )

    sums = lax.fori_loop(0, PAD_LEN // LT, second_back, (zero_row,) * 4)
    for row, value in zip((6, 7, 2, 3), sums):
        SB[row : row + 1, :] = value * lead
    at("sb")

    for part in range(2):
        g = dot_tn(MIX[part], GATT[:, pl.ds(chalf, HALF)])
        S4[4, 2 * part : 2 * part + 2] = g.astype(bf16).reshape(2, 2, 2, 48, HALF)
    at("out")

    @pl.loop(0, PAD_LEN // MT)
    def _(t):
        rows = pl.ds(pl.multiple_of(t * MT, MT), MT)
        GMX[rows, :] = (dot_nt(GATT[rows, :], WO[pl.ds(chalf, HALF), :]) * INV[rows, :]).astype(bf16)

    at("gmx")

    for hp in range(PAIRS):
        qlanes, klanes, vlanes = pair_lanes(hp)
        kp = TRI[:, klanes]
        vp = TRI[:, vlanes]
        gp = GMX[:, qlanes]
        dots = gp.astype(f32) * MIX[c, :, qlanes].astype(f32)
        qt = jnp.swapaxes(TRI[:, qlanes], 0, 1)
        gt = jnp.swapaxes(gp, 0, 1)
        dq = jnp.zeros((PAD_LEN, 128), f32)
        for side in range(2):
            half = slice(side * HEAD_DIM, (side + 1) * HEAD_DIM)
            e = PR[2 * hp + side]
            dpr = dot_nt(head_part(gp, side), vp)
            delta = jnp.sum(head_part(dots, side), axis=-1, keepdims=True)
            ds = (e.astype(f32) * (dpr - delta)).astype(bf16)
            dq = dq + dot_nn(ds, head_part(kp, side))
            DKT[half, :] = dot_nn(qt[half, :], ds)
            DVT[half, :] = dot_nn(gt[half, :], e)
        DTR[:, qlanes] = (dq * HEAD_DIM ** (-0.5)).astype(bf16)
        DTR[:, klanes] = jnp.swapaxes(DKT[...], 0, 1).astype(bf16)
        DTR[:, vlanes] = jnp.swapaxes(DVT[...], 0, 1).astype(bf16)
        at("h%d" % hp)

    for k in range(3):
        blk = DTR[:, k * HALF : (k + 1) * HALF]
        if k != 1:
            SB[k // 2 : k // 2 + 1, pl.ds(chalf, HALF)] = col_sum(blk.astype(f32))
        for part in range(2):
            g = dot_tn(NRM[:, part * HALF : (part + 1) * HALF], blk)
            S4[5 + k, 2 * part : 2 * part + 2] = g.astype(bf16).reshape(2, 2, 2, 48, HALF)
        at("qkv"[k])

    ex_ds.wait_send()
    DSB[...] = dot_nt(DTR[pl.ds(oth, OWN), :], WQ[...]).astype(bf16)
    ex_ns = to_core(DSB, NSR)
    at("ns")
    ex_ds.wait_recv()
    ex_gs.wait_send()
    ex_ns.wait_recv()
    OUTB, INB = GSB.at[0:OWN], GSB.at[OWN:PAD_LEN]

    def first_back(t, carry):
        r = pl.ds(pl.multiple_of(t * 80, 80), 80)
        rows = pl.ds(pl.multiple_of(own + t * 80, 80), 80)
        xf = X[rows, :].astype(f32)
        unit, rstd = row_stats(xf)
        gn = dot_nt(DTR[rows, :], WQ[...]) + NSR[r, :].astype(f32)
        first = norm_back(unit, rstd, gn, vec(4))
        gf = G[rows, :].astype(f32)
        gate = ACT[rows, :] * GATE[rows, :]
        branch = SUM[rows, :] - xf + ACCD[rows, :] + DSR[r, :].astype(f32) + vec(3)
        OUTB[r, :] = (xf + gate * branch).astype(bf16)
        gl = jnp.sum(gf * branch, axis=-1, keepdims=True) * (gate * (1.0 - GATE[rows, :]))
        INB[r, :] = (gf + ACCS[rows, :] + first + gl * vec(8)).astype(bf16)
        return (carry[0] + col_sum(gn * unit), carry[1] + col_sum(gn), carry[2] + col_sum(gl * xf))

    sums = lax.fori_loop(0, OWN // 80, first_back, (zero_row,) * 3)
    for row, value in zip((4, 5, 8), sums):
        SB[row : row + 1, :] = value
    keep_out = pltpu.make_async_copy(OUTB, o_output.at[0], lsem.at[len(loads)])
    keep_in = pltpu.make_async_copy(INB, o_input.at[0], lsem.at[len(loads) + 1])
    keep_out.start()
    keep_in.start()

    at("fb")
    at("end")
    for cp in sends:
        if cp is not ex_ds and cp is not ex_gs:
            cp.wait_send()
    for cp in (keep_out, keep_in):
        cp.wait()


N_LOADS = 2 + 9 + 3 + 5
BIG = (0, 1, 2, 5, 7, 9)


def place_kernel(*refs):
    src, dst, bufs, (vals, sem) = refs[:7], refs[7:24], refs[24:30], refs[30:]
    dp = lax.axis_index("dp")
    ins = [pltpu.make_async_copy(src[i], bufs[i], sem.at[i]) for i in range(6)]
    outs = [pltpu.make_async_copy(bufs[i], dst[k], sem.at[6 + i]) for i, k in enumerate(BIG)]
    for cp in ins:
        cp.start()
    rows = src[6][...]
    shift = lax.rem(dp * (WIDTH - 48), WIDTH)
    mine = pltpu.roll(rows, shift, 1)[:, :48]
    for row, out in zip(range(9), (3, 4, 6, 10, 11, 12, 13, 14, 15)):
        dst[out][...] = mine[row : row + 1, :]
    vals[...] = pltpu.roll(rows, lax.rem(lax.rem(dp, 4) * (WIDTH - 192), WIDTH), 1)
    dst[8][...] = vals[pl.ds(9 + lax.div(dp, 4), 1), :192]
    dst[16][...] = jnp.swapaxes(rows[8:16, :128], 0, 1)[:16, 5:8]
    for a, b in zip(ins, outs):
        a.wait()
        b.start()
    for cp in outs:
        cp.wait()


def fused(
    tokens, cotangent, group, select, w_qkv, b_query, b_value, w_out, b_out, w_up, b_up, w_down,
    b_down, ln1_gain, ln1_bias, ln2_gain, ln2_bias, w_router,
):
    args = (
        tokens, cotangent, group, select, w_qkv, b_query, b_value, w_out, b_out, w_up, b_up, w_down,
        b_down, ln1_gain, ln1_bias, ln2_gain, ln2_bias, w_router,
    )
    anywhere = pl.BlockSpec(memory_space=pl.ANY)
    vmem = pl.BlockSpec(memory_space=pltpu.VMEM)
    shape = jax.ShapeDtypeStruct
    mids = (
        shape((1, OWN, WIDTH), bf16), shape((1, OWN, WIDTH), bf16), shape((48, 3 * WIDTH), f32),
        shape((48, WIDTH), f32), shape((48, HIDDEN), f32), shape((192, WIDTH), f32),
        shape((SMALL, WIDTH), f32),
    )
    v = pltpu.VMEM
    sq = (PAD_LEN, WIDTH)
    scratch = [
        v(sq, bf16), v(sq, bf16), v((2, 1, OWN), jnp.int32), v((9, 1, WIDTH), f32), v((1, HIDDEN), f32),
        v(sq, bf16), v((WIDTH, 3 * HALF), bf16), v((WIDTH, WIDTH), bf16), v((WIDTH, HID), bf16),
        v((HID, WIDTH), bf16), v((PAD_LEN, 3 * HALF), bf16), v((2 * PAIRS, PAD_LEN, PAD_LEN), bf16),
        v((2, PAD_LEN, HALF), bf16), v(sq, f32), v(sq, bf16), v(sq, bf16), v((PAD_LEN, PAD_LEN), f32),
        v((PAD_LEN, 1), f32), v((PAD_LEN, 1), f32),
        v((PAD_LEN, HALF), bf16), v((PAD_LEN, HALF), bf16), v(sq, f32), v(sq, f32), v(sq, bf16), v(sq, bf16),
        v((OWN, WIDTH), bf16), v((OWN, WIDTH), bf16), v(sq, bf16), v((PAD_LEN, HALF), bf16),
        v((PAD_LEN, 3 * HALF), bf16), v((128, PAD_LEN), f32), v((128, PAD_LEN), f32),
        v((PAD_LEN, HALF), f32), v((WIDTH, PAD_LEN), bf16), v((OWN, WIDTH), bf16),
        v((8, 4, 2, 2, 48, HALF), bf16), v((8, 4, 2, 48, HALF), bf16), v((8, 4, 48, HALF), bf16),
        v((8, 3, 48, HALF), bf16), v((8, 48, HALF), f32),
        v((4, 1, 2, 2, 192, HALF), bf16), v((4, 1, 2, 192, HALF), bf16), v((4, 1, 192, HALF), bf16),
        v((4, 3, 192, HALF), bf16), v((4, 192, HALF), f32),
        v((3, 2, 2, 48, HALF), bf16), v((2, 48, HALF), bf16),
        v((SMALL, WIDTH), f32), v((4, 8, WIDTH), f32), v((6, 8, WIDTH), f32),
        pltpu.SemaphoreType.DMA((N_LOADS + 4,)),
        pltpu.SemaphoreType.DMA((9,)), pltpu.SemaphoreType.DMA((9,)),
        pltpu.SemaphoreType.DMA((7 * PIECES,)), pltpu.SemaphoreType.DMA((7 * PIECES,)),
        pltpu.SemaphoreType.DMA((7,)), pltpu.SemaphoreType.DMA((7,)),
        pltpu.SemaphoreType.DMA((PIECES,)), pltpu.SemaphoreType.DMA((PIECES,)), pltpu.SemaphoreType.DMA((PIECES,)),
    ]
    mid = pl.pallas_call(
        layer_kernel,
        out_shape=mids,
        in_specs=[anywhere, anywhere, pl.BlockSpec(memory_space=pltpu.SMEM)] + [anywhere] * 15,
        out_specs=[anywhere] * 7,
        scratch_shapes=scratch,
        compiler_params=pltpu.CompilerParams(
            collective_id=0, has_side_effects=True, vmem_limit_bytes=60 << 20
        ),
        name="layer",
    )(*args)
    outs = (
        mids[0], mids[1], mids[2], shape((1, 48), f32), shape((1, 48), f32), mids[3], shape((1, 48), f32),
        mids[4], shape((1, 192), f32), mids[5],
    ) + (shape((1, 48), f32),) * 6 + (shape((16, 3), f32),)
    out = pl.pallas_call(
        place_kernel,
        out_shape=outs,
        in_specs=[anywhere] * 6 + [vmem],
        out_specs=[anywhere if i in BIG else vmem for i in range(17)],
        scratch_shapes=[v(mids[i].shape, mids[i].dtype) for i in range(6)]
        + [v((SMALL, WIDTH), f32), pltpu.SemaphoreType.DMA((12,))],
        name="place",
    )(*mid)
    return tuple(o.reshape(-1) if o.shape[0] == 1 and o.ndim == 2 else o for o in out)


def norm_rows(values, norm_gain, norm_shift):
    average = jnp.mean(values, axis=-1, keepdims=True)
    centred = values - average
    variance = jnp.mean(centred * centred, axis=-1, keepdims=True)
    return centred * lax.rsqrt(variance + epsilon) * norm_gain + norm_shift


def places_of(group, slot_pos):
    short_place = jnp.minimum(slot_pos // SHORT_LEN, 2)
    return jnp.where(group[:, None] == 1, 0, short_place[None, :])


def split_heads(flat_rows):
    return flat_rows.reshape(flat_rows.shape[0], flat_rows.shape[1], HEADS, HEAD_DIM)


def masked_scores(queries, key_heads, query_place, key_place, key_mask):
    score_scale = HEAD_DIM ** (-0.5)
    scores = (
        jnp.einsum("bqhe,bkhe->bqhk", queries, key_heads, preferred_element_type=jnp.float32)
        * score_scale
    )
    key_live = (key_mask.astype(jnp.float32)[:, None, None, :] > 0.5) & (
        query_place[:, :, None, None] == key_place[:, None, None, :]
    )
    return (jnp.where(key_live, scores, masked_floor), key_live.astype(jnp.float32))


def attend(queries, key_heads, value_heads, query_place, key_place, key_mask):
    masked, key_weight = masked_scores(queries, key_heads, query_place, key_place, key_mask)
    row_max = jnp.max(masked, axis=-1, keepdims=True)
    exponent = jnp.exp(masked - row_max) * key_weight
    row_sum = jnp.sum(exponent, axis=-1, keepdims=True)
    weights = (exponent / row_sum).astype(jnp.bfloat16)
    mixed_heads = jnp.einsum(
        "bqhk,bkhe->bqhe", weights, value_heads, preferred_element_type=jnp.float32
    )
    return (mixed_heads, row_max + jnp.log(row_sum))


def back_parts(
    queries, key_heads, value_heads, query_place, key_place, key_mask, log_total, grad_heads, delta
):
    masked, key_weight = masked_scores(queries, key_heads, query_place, key_place, key_mask)
    key_probs = jnp.exp(masked - log_total) * key_weight
    grad_probs = jnp.einsum(
        "bqhe,bkhe->bqhk", grad_heads, value_heads, preferred_element_type=jnp.float32
    )
    delta = jnp.sum(key_probs * grad_probs, axis=-1, keepdims=True)
    grad_scores = (key_probs * (grad_probs - delta)).astype(jnp.bfloat16)
    return (key_probs, grad_scores, delta)


def key_side_grads(key_probs, grad_scores, queries, grad_heads):
    score_scale = HEAD_DIM ** (-0.5)
    grad_values = jnp.einsum(
        "bqhk,bqhe->bkhe",
        key_probs.astype(jnp.bfloat16),
        grad_heads,
        preferred_element_type=jnp.float32,
    )
    grad_keys = (
        jnp.einsum("bqhk,bqhe->bkhe", grad_scores, queries, preferred_element_type=jnp.float32)
        * score_scale
    )
    return (grad_keys, grad_values)


def on_device(
    tokens,
    cotangent,
    group,
    select,
    w_qkv,
    b_query,
    b_value,
    w_out,
    b_out,
    w_up,
    b_up,
    w_down,
    b_down,
    ln1_gain,
    ln1_bias,
    ln2_gain,
    ln2_bias,
    w_router,
):
    packs, per_piece, features = tokens.shape
    row_count = packs * per_piece
    first_pos = lax.axis_index("seq") * per_piece
    positions = first_pos + jnp.arange(per_piece, dtype=jnp.int32)
    full_positions = jnp.arange(PAD_LEN, dtype=jnp.int32)
    place_own = places_of(group, positions)
    place_full = places_of(group, full_positions)
    ends = jnp.where(group == 1, LONG_LEN, 3 * SHORT_LEN).astype(jnp.int32)
    active = ((select > 0) & (positions[None, :] < ends[:, None])).astype(jnp.float32)
    active_rows = active.reshape(row_count, 1)
    xfloat = tokens.reshape(row_count, features).astype(jnp.float32)
    router = jax.nn.sigmoid(jnp.dot(xfloat, w_router, precision=lax.Precision.HIGHEST))
    normed, first_back = jax.vjp(norm_rows, xfloat, ln1_gain, ln1_bias)
    normed_low = normed.astype(jnp.bfloat16)
    qkv_bias = jnp.concatenate([b_query, jnp.zeros_like(b_query), b_value])
    triple = (jnp.dot(normed_low, w_qkv, preferred_element_type=jnp.float32) + qkv_bias).astype(
        jnp.bfloat16
    )
    queries = triple[:, :features].reshape(packs, per_piece, HEADS, HEAD_DIM)
    keys_own = triple[:, features : 2 * features].reshape(packs, per_piece, features)
    values_own = triple[:, 2 * features :].reshape(packs, per_piece, features)
    mask_own = active.astype(jnp.bfloat16)
    keys_all, values_all, mask_all = (
        lax.all_gather(keys_own, "seq", axis=1, tiled=True),
        lax.all_gather(values_own, "seq", axis=1, tiled=True),
        lax.all_gather(mask_own, "seq", axis=1, tiled=True),
    )
    mixed_heads, log_total = attend(
        queries, split_heads(keys_all), split_heads(values_all), place_own, place_full, mask_all
    )
    mixed_low = mixed_heads.reshape(row_count, features).astype(jnp.bfloat16)
    attended = jnp.dot(mixed_low, w_out, preferred_element_type=jnp.float32) + b_out
    summed = xfloat + attended
    second, second_back = jax.vjp(norm_rows, summed, ln2_gain, ln2_bias)
    second_low = second.astype(jnp.bfloat16)
    pre_act = jnp.dot(second_low, w_up, preferred_element_type=jnp.float32) + b_up
    gelu_out, gelu_back = jax.vjp(partial(jax.nn.gelu, approximate=False), pre_act)
    hidden_low = gelu_out.astype(jnp.bfloat16)
    branch = attended + (jnp.dot(hidden_low, w_down, preferred_element_type=jnp.float32) + b_down)
    gate_rows = active_rows * router[:, None]
    output = (xfloat + gate_rows * branch).astype(jnp.bfloat16).reshape(packs, per_piece, features)
    place_range = jnp.arange(3, dtype=jnp.int32)
    onehot = (place_full[:, :, None] == place_range[None, None, :]).astype(jnp.float32)
    counts = jnp.sum(mask_all.astype(jnp.float32)[:, :, None] * onehot, axis=1)
    image_lengths = jnp.where(group == 1, LONG_LEN, SHORT_LEN).astype(jnp.float32)
    fractions = lax.all_gather(counts / image_lengths[:, None], "dp", axis=0, tiled=True)
    grad_rows = cotangent.reshape(row_count, features).astype(jnp.float32)
    grad_logit = jnp.sum(grad_rows * branch, axis=1) * active_rows[:, 0] * router * (1.0 - router)
    grad_branch = gate_rows * grad_rows
    grad_mlp = grad_branch.astype(jnp.bfloat16)
    grad_down = jnp.einsum("rk,rd->kd", hidden_low, grad_mlp, preferred_element_type=jnp.float32)
    grad_down_bias = jnp.sum(grad_mlp.astype(jnp.float32), axis=0)
    grad_hidden = jnp.einsum("rd,kd->rk", grad_mlp, w_down, preferred_element_type=jnp.float32)
    grad_pre = gelu_back(grad_hidden)[0].astype(jnp.bfloat16)
    grad_up = jnp.einsum("rd,rk->dk", second_low, grad_pre, preferred_element_type=jnp.float32)
    grad_up_bias = jnp.sum(grad_pre.astype(jnp.float32), axis=0)
    grad_second = jnp.einsum("rk,dk->rd", grad_pre, w_up, preferred_element_type=jnp.float32)
    grad_summed, grad_ln2_gain, grad_ln2_bias = second_back(grad_second)
    grad_attended = (grad_branch + grad_summed).astype(jnp.bfloat16)
    grad_out = jnp.einsum("rd,re->de", mixed_low, grad_attended, preferred_element_type=jnp.float32)
    grad_out_bias = jnp.sum(grad_attended.astype(jnp.float32), axis=0)
    grad_mixed = jnp.einsum("re,de->rd", grad_attended, w_out, preferred_element_type=jnp.float32)
    grad_heads = grad_mixed.astype(jnp.bfloat16).reshape(packs, per_piece, HEADS, HEAD_DIM)
    back_k, back_v, back_m = (
        lax.all_gather(keys_own, "seq", axis=1, tiled=True),
        lax.all_gather(values_own, "seq", axis=1, tiled=True),
        lax.all_gather(mask_own, "seq", axis=1, tiled=True),
    )
    back_kh = split_heads(back_k)
    back_vh = split_heads(back_v)
    key_probs, grad_scores, delta = back_parts(
        queries, back_kh, back_vh, place_own, place_full, back_m, log_total, grad_heads, None
    )
    grad_queries = jnp.einsum(
        "bqhk,bkhe->bqhe", grad_scores, back_kh, preferred_element_type=jnp.float32
    ) * HEAD_DIM ** (-0.5)
    grad_keys, grad_values = key_side_grads(key_probs, grad_scores, queries, grad_heads)
    keys_grad_own, values_grad_own = (
        lax.psum_scatter(
            grad_keys.reshape(back_k.shape).astype(jnp.bfloat16),
            "seq",
            scatter_dimension=1,
            tiled=True,
        ).astype(jnp.float32),
        lax.psum_scatter(
            grad_values.reshape(back_v.shape).astype(jnp.bfloat16),
            "seq",
            scatter_dimension=1,
            tiled=True,
        ).astype(jnp.float32),
    )
    grad_triple = jnp.concatenate(
        [
            grad_queries.reshape(row_count, features),
            keys_grad_own.reshape(row_count, features),
            values_grad_own.reshape(row_count, features),
        ],
        axis=1,
    ).astype(jnp.bfloat16)
    grad_qkv = jnp.einsum("rd,rk->dk", normed_low, grad_triple, preferred_element_type=jnp.float32)
    column_sums = jnp.sum(grad_triple.astype(jnp.float32), axis=0)
    grad_query_bias = column_sums[:features]
    grad_value_bias = column_sums[2 * features :]
    grad_normed = jnp.einsum("rk,dk->rd", grad_triple, w_qkv, preferred_element_type=jnp.float32)
    grad_first, grad_ln1_gain, grad_ln1_bias = first_back(grad_normed)
    grad_router = jnp.dot(grad_logit, xfloat, precision=lax.Precision.HIGHEST)
    grad_input = grad_rows + grad_summed + grad_first + grad_logit[:, None] * w_router[None, :]
    input_grad = grad_input.astype(jnp.bfloat16).reshape(packs, per_piece, features)
    (
        share_qkv,
        share_query_bias,
        share_value_bias,
        share_out,
        share_out_bias,
        share_up,
        share_up_bias,
        share_down,
        share_down_bias,
        share_ln1_gain,
        share_ln1_bias,
        share_ln2_gain,
        share_ln2_bias,
        share_router,
    ) = (
        lax.psum_scatter(
            grad_qkv.astype(jnp.bfloat16), "dp", scatter_dimension=0, tiled=True
        ).astype(jnp.float32),
        lax.psum_scatter(
            grad_query_bias.astype(jnp.bfloat16), "dp", scatter_dimension=0, tiled=True
        ).astype(jnp.float32),
        lax.psum_scatter(
            grad_value_bias.astype(jnp.bfloat16), "dp", scatter_dimension=0, tiled=True
        ).astype(jnp.float32),
        lax.psum_scatter(
            grad_out.astype(jnp.bfloat16), "dp", scatter_dimension=0, tiled=True
        ).astype(jnp.float32),
        lax.psum_scatter(
            grad_out_bias.astype(jnp.bfloat16), "dp", scatter_dimension=0, tiled=True
        ).astype(jnp.float32),
        lax.psum_scatter(
            grad_up.astype(jnp.bfloat16), "dp", scatter_dimension=0, tiled=True
        ).astype(jnp.float32),
        lax.psum_scatter(
            grad_up_bias.astype(jnp.bfloat16), "dp", scatter_dimension=0, tiled=True
        ).astype(jnp.float32),
        lax.psum_scatter(
            grad_down.astype(jnp.bfloat16), "dp", scatter_dimension=0, tiled=True
        ).astype(jnp.float32),
        lax.psum_scatter(
            grad_down_bias.astype(jnp.bfloat16), "dp", scatter_dimension=0, tiled=True
        ).astype(jnp.float32),
        lax.psum_scatter(
            grad_ln1_gain.astype(jnp.bfloat16), "dp", scatter_dimension=0, tiled=True
        ).astype(jnp.float32),
        lax.psum_scatter(
            grad_ln1_bias.astype(jnp.bfloat16), "dp", scatter_dimension=0, tiled=True
        ).astype(jnp.float32),
        lax.psum_scatter(
            grad_ln2_gain.astype(jnp.bfloat16), "dp", scatter_dimension=0, tiled=True
        ).astype(jnp.float32),
        lax.psum_scatter(
            grad_ln2_bias.astype(jnp.bfloat16), "dp", scatter_dimension=0, tiled=True
        ).astype(jnp.float32),
        lax.psum_scatter(
            grad_router.astype(jnp.bfloat16), "dp", scatter_dimension=0, tiled=True
        ).astype(jnp.float32),
    )
    totals = (
        lax.psum(share_qkv.astype(jnp.bfloat16), "seq").astype(jnp.float32),
        lax.psum(share_query_bias.astype(jnp.bfloat16), "seq").astype(jnp.float32),
        lax.psum(share_value_bias.astype(jnp.bfloat16), "seq").astype(jnp.float32),
        lax.psum(share_out.astype(jnp.bfloat16), "seq").astype(jnp.float32),
        lax.psum(share_out_bias.astype(jnp.bfloat16), "seq").astype(jnp.float32),
        lax.psum(share_up.astype(jnp.bfloat16), "seq").astype(jnp.float32),
        lax.psum(share_up_bias.astype(jnp.bfloat16), "seq").astype(jnp.float32),
        lax.psum(share_down.astype(jnp.bfloat16), "seq").astype(jnp.float32),
        lax.psum(share_down_bias.astype(jnp.bfloat16), "seq").astype(jnp.float32),
        lax.psum(share_ln1_gain.astype(jnp.bfloat16), "seq").astype(jnp.float32),
        lax.psum(share_ln1_bias.astype(jnp.bfloat16), "seq").astype(jnp.float32),
        lax.psum(share_ln2_gain.astype(jnp.bfloat16), "seq").astype(jnp.float32),
        lax.psum(share_ln2_bias.astype(jnp.bfloat16), "seq").astype(jnp.float32),
        lax.psum(share_router.astype(jnp.bfloat16), "seq").astype(jnp.float32),
    )
    return (
        output,
        input_grad,
        totals[0],
        totals[1],
        totals[2],
        totals[3],
        totals[4],
        totals[5],
        totals[6],
        totals[7],
        totals[8],
        totals[9],
        totals[10],
        totals[11],
        totals[12],
        totals[13],
        fractions,
    )


def solution(mesh):
    in_specs = (
        P("dp", "seq", None),
        P("dp", "seq", None),
        P("dp"),
        P("dp", "seq"),
        P(),
        P(),
        P(),
        P(),
        P(),
        P(),
        P(),
        P(),
        P(),
        P(),
        P(),
        P(),
        P(),
        P(),
    )
    out_specs = (
        P("dp", "seq", None),
        P("dp", "seq", None),
        P("dp", None),
        P("dp"),
        P("dp"),
        P("dp", None),
        P("dp"),
        P("dp", None),
        P("dp"),
        P("dp", None),
        P("dp"),
        P("dp"),
        P("dp"),
        P("dp"),
        P("dp"),
        P("dp"),
        P(),
    )
    fast = mesh.shape["dp"] == 16 and mesh.shape["seq"] == 2
    return jax.shard_map(
        fused if fast else on_device, mesh=mesh, in_specs=in_specs, out_specs=out_specs, check_vma=False
    )
```

```python
from functools import partial
from itertools import product

import jax
import jax.numpy as jnp
from jax import lax
from jax.experimental import pallas as pl
from jax.experimental.pallas import tpu as pltpu
from jax.sharding import PartitionSpec as P

HEADS = 12
HEAD_DIM = 64
PAD_LEN = 640
LONG_LEN = 577
SHORT_LEN = 197
WIDTH = 768
HIDDEN = 3072

epsilon = 1e-06
masked_floor = -1000000000.0
MESH_ID = pl.DeviceIdType.MESH
bf16 = jnp.bfloat16
f32 = jnp.float32

HALF = WIDTH // 2
OWN = PAD_LEN // 2
HID = HIDDEN // 2
BLOCKS = HID // HALF
PAIRS = HALF // 128
MT = 320
AT = 640
LT = 160
SMALL = 16
PIECES = {
    "up0_0": ("up0", "zxy", 0, 128),
    "up0_1": ("up0", "yxz", 128, 256),
    "up1": ("up1", "zxy", 0, 384),
    "up2": ("up2", "xzy", 0, 384),
    "up3": ("up3", "yzx", 0, 384),
    "dA0": ("dA0", "yxz", 0, 384),
    "dB0": ("dB0", "xyz", 0, 384),
    "dA1": ("dA1", "xyz", 0, 384),
    "dB1": ("dB1", "yxz", 0, 384),
    "out": ("out", "xyz", 0, 384),
    "q": ("q", "yxz", 0, 384),
    "k": ("k", "yxz", 0, 384),
    "v_0": ("v", "yxz", 0, 128),
    "v_1": ("v", "xyz", 128, 256),
}
HALVED = ("dB0", "dA1")
SCHEDULE = {
    "u0": (
        (1, "up0_0"), (1, "up0_1"),
    ),
    "j0": (
        (0, "dB0"),
    ),
    "u1": (
        (1, "up1"),
    ),
    "j1": (
        (1, "dA0"), (1, "dB0"), (2, "up0_0"), (2, "up0_1"),
    ),
    "j2": (
        (0, "dA1"), (2, "dB0"), (3, "up0_0"),
    ),
    "u3": (
        (2, "dA0"), (3, "up0_1"), (1, "up3"),
    ),
    "j3": (
        (3, "dB0"), (4, "up0_0"), (1, "dA1"),
    ),
    "out": (
        (2, "up1"), (3, "dA0"), (1, "dB1"), (5, "up0_0"),
    ),
    "gmx": (
        (4, "up0_1"),
    ),
    "h0": (
        (1, "up2"), (5, "up0_1"), (2, "dA1"), (2, "up3"),
    ),
    "h1": (
        (3, "up1"), (4, "dB0"),
    ),
    "h2": (
        (4, "dA0"), (5, "dB0"),
    ),
    "q": (
        (1, "out"),
    ),
    "k": (
        (5, "dA0"),
    ),
    "v": (
        (2, "dB1"),
    ),
    "ns": (
        (2, "up2"), (1, "q"),
    ),
    "fb": (
        (3, "dA1"), (3, "up3"), (1, "small"), (4, "up1"),
    ),
    "end": (
        (2, "small"), (5, "up1"), (2, "out"), (2, "q"), (3, "up2"), (3, "dB1"), (1, "k"), (4, "up3"), (3, "small"),
        (3, "out"), (1, "v_1"), (5, "up3"), (4, "dA1"), (4, "up2"), (3, "q"), (5, "dA1"), (4, "dB1"), (5, "up2"),
        (2, "v_1"), (5, "dB1"), (4, "out"), (2, "k"), (1, "v_0"), (4, "small"), (5, "out"), (4, "q"), (3, "v_1"),
        (5, "small"), (5, "q"), (2, "v_0"), (3, "k"), (4, "v_1"), (6, "small"), (3, "v_0"), (4, "k"), (5, "v_1"),
        (4, "v_0"), (5, "k"), (5, "v_0"),
    ),
}


def dot_nn(a, b):
    return lax.dot_general(a, b, (((1,), (0,)), ((), ())), preferred_element_type=f32)


def dot_nt(a, b):
    return lax.dot_general(a, b, (((1,), (1,)), ((), ())), preferred_element_type=f32)


def dot_tn(a, b):
    return lax.dot_general(a, b, (((0,), (0,)), ((), ())), preferred_element_type=f32)


def row_stats(values):
    average = jnp.mean(values, axis=-1, keepdims=True)
    centred = values - average
    variance = jnp.mean(centred * centred, axis=-1, keepdims=True)
    rstd = lax.rsqrt(variance + epsilon)
    return centred * rstd, rstd


def norm_back(unit, rstd, grad, gain):
    q = grad * gain
    return rstd * (
        q - jnp.mean(q, axis=-1, keepdims=True) - unit * jnp.mean(q * unit, axis=-1, keepdims=True)
    )


def piece_shapes(name):
    grad, order, _, width = PIECES[name]
    left = [{"z": 1 if grad[0] == "d" else 4, "y": 2, "x": 2}[axis] for axis in order]
    tile = [192 if grad[0] == "d" else 48, width]
    shapes = [(left + tile, bf16)]
    for k, axis in enumerate(order):
        shapes.append(([3] * (axis == "z") + left[k + 1 :] + tile, bf16))
    return shapes + [(tile, f32)]


def layer_kernel(*refs):
    (tokens, cotangent, group, select, w_qkv, b_query, b_value, w_out, b_out, w_up, b_up, w_down,
     b_down, ln1_gain, ln1_bias, ln2_gain, ln2_bias, w_router) = refs[:18]
    o_output, o_input, o_qkv, o_out, o_up, o_down, o_small = refs[18:25]
    (X, G, SEL, VEC, BUP, NRM, WQ, WO, WU, WD, TRI, PR, MIX, SUM, SEC, GM, BIAS, GATE, ACT,
     HIDJ, GPJ, ACCD, ACCS, GSB, GSR, DSB, DSR, GATT, GMX, DTR, DKT, DVT, INV, SECT, NSR, SB, SBL, SBR) = refs[25:63]
    piece_bufs = refs[63 : 63 + 5 * len(PIECES)]
    (lsem, esem_s, esem_r, csem_s, csem_r, ssem_s, ssem_r, fsem_l, fsem_s, fsem_r) = refs[63 + 5 * len(PIECES) :]
    dp = lax.axis_index("dp")
    c = lax.axis_index("seq")
    x = lax.rem(dp, 2)
    y = lax.rem(lax.div(dp, 2), 2)
    z = lax.div(dp, 4)
    peer = (dp, 1 - c)
    xp = ((z * 2 + y) * 2 + (1 - x), c)
    yp = ((z * 2 + (1 - y)) * 2 + x, c)
    zs = [lax.rem(z + k, 4) for k in (1, 2, 3)]
    zp = [((zk * 2 + y) * 2 + x, c) for zk in zs]
    own = pl.multiple_of(c * OWN, OWN)
    oth = pl.multiple_of((1 - c) * OWN, OWN)
    chalf = pl.multiple_of(c * HALF, HALF)
    chid = pl.multiple_of(c * HID, HID)
    lead = (c == 0).astype(f32)

    barrier = pltpu.get_barrier_semaphore()
    for other in [peer, xp, yp] + zp:
        pl.semaphore_signal(barrier, inc=1, device_id=other, device_id_type=MESH_ID)

    loads = {}

    def load(name, src, dst):
        copy = pltpu.make_async_copy(src, dst, lsem.at[len(loads)])
        copy.start()
        loads[name] = copy

    load("tok", tokens.at[0], X.at[pl.ds(own, OWN)])
    load("sel", select, SEL.at[c])
    for i, v in enumerate(
        (b_query, b_value, b_out, b_down, ln1_gain, ln1_bias, ln2_gain, ln2_bias, w_router)
    ):
        load("v%d" % i, v, VEC.at[i, 0])
    for k in range(3):
        load(
            "wq%d" % k,
            w_qkv.at[:, pl.ds(pl.multiple_of(k * WIDTH + c * HALF, 128), HALF)],
            WQ.at[:, pl.ds(k * HALF, HALF)],
        )
    load("cot", cotangent.at[0], G.at[pl.ds(own, OWN)])
    load("bup", b_up, BUP.at[0])
    load("wo", w_out, WO)
    load("wu", w_up.at[:, pl.ds(chid, HID)], WU)
    load("wd", w_down.at[pl.ds(chid, HID)], WD)

    pl.semaphore_wait(barrier, 6)

    sends = []
    counts = {"e": 0, "c": 0}

    def to_core(src, dst):
        i = counts["e"]
        counts["e"] += 1
        copy = pltpu.make_async_remote_copy(
            src_ref=src, dst_ref=dst, send_sem=esem_s.at[i], recv_sem=esem_r.at[i],
            device_id=peer, device_id_type=MESH_ID,
        )
        copy.start()
        sends.append(copy)
        return copy

    ex_sel = to_core(select, SEL.at[c])
    ex_tok = to_core(tokens.at[0], X.at[pl.ds(own, OWN)])
    ex_cot = to_core(cotangent.at[0], G.at[pl.ds(own, OWN)])

    SB[...] = jnp.zeros_like(SB)

    def vec(i):
        return VEC[i]

    def project(start):
        @pl.loop(0, OWN // LT)
        def _(t):
            rows = pl.ds(pl.multiple_of(start + t * LT, 32), LT)
            xf = X[rows, :].astype(f32)
            unit, _ = row_stats(xf)
            NRM[rows, :] = (unit * vec(4) + vec(5)).astype(bf16)
            logit = jnp.sum(xf * vec(8), axis=-1, keepdims=True)
            GATE[rows, :] = 1.0 / (1.0 + jnp.exp(-logit))

        if start is own:
            for k in range(3):
                loads["wq%d" % k].wait()
        rows = pl.ds(start, OWN)
        nr = NRM[rows, :]
        for k in range(3):
            r = dot_nn(nr, WQ[:, k * HALF : (k + 1) * HALF])
            if k == 0:
                r = (r + VEC[0, :, pl.ds(chalf, HALF)]).astype(bf16).astype(f32) * HEAD_DIM ** (-0.5)
            if k == 2:
                r = r + VEC[1, :, pl.ds(chalf, HALF)]
            TRI[rows, k * HALF : (k + 1) * HALF] = r.astype(bf16)

    loads["tok"].wait()
    for i in range(9):
        loads["v%d" % i].wait()
    project(own)

    loads["sel"].wait()
    ex_sel.wait_recv()
    gv = jnp.full((1, 1), group[0], jnp.int32)
    long_row = jnp.broadcast_to(gv, (1, PAD_LEN)) == 1
    pos_row = lax.broadcasted_iota(jnp.int32, (1, PAD_LEN), 1)
    short_row = (pos_row >= SHORT_LEN).astype(jnp.int32) + (pos_row >= 2 * SHORT_LEN).astype(jnp.int32)
    place_row = jnp.where(long_row, 0, short_row)
    end_row = jnp.where(long_row, LONG_LEN, 3 * SHORT_LEN)
    long_col = jnp.broadcast_to(gv, (PAD_LEN, 1)) == 1
    pos_col = lax.broadcasted_iota(jnp.int32, (PAD_LEN, 1), 0)
    short_col = (pos_col >= SHORT_LEN).astype(jnp.int32) + (pos_col >= 2 * SHORT_LEN).astype(jnp.int32)
    place_col = jnp.where(long_col, 0, short_col)
    end_col = jnp.where(long_col, LONG_LEN, 3 * SHORT_LEN)
    sel_row = jnp.zeros((8, PAD_LEN), f32)
    sel_col = jnp.zeros((PAD_LEN, 8), f32)
    for part in range(2):
        bits = jnp.broadcast_to((SEL[part] > 0).astype(f32), (8, OWN)).astype(bf16)
        spread = (
            lax.broadcasted_iota(jnp.int32, (PAD_LEN, OWN), 0)
            == lax.broadcasted_iota(jnp.int32, (PAD_LEN, OWN), 1) + part * OWN
        ).astype(f32).astype(bf16)
        sel_row = sel_row + dot_nt(bits, spread)
        sel_col = sel_col + dot_nt(spread, bits)
    act_row = jnp.where(pos_row < end_row, sel_row[0:1, :], 0.0)
    act_col = jnp.where(pos_col < end_col, sel_col[:, 0:1], 0.0)
    ACT[...] = act_col
    BIAS[...] = jnp.where(
        (jnp.broadcast_to(act_row, (PAD_LEN, PAD_LEN)) > 0.5)
        & (jnp.broadcast_to(place_col, (PAD_LEN, PAD_LEN)) == jnp.broadcast_to(place_row, (PAD_LEN, PAD_LEN))),
        0.0,
        -1e30,
    )
    lane = lax.broadcasted_iota(jnp.int32, (1, 128), 1)
    length = jnp.where(jnp.broadcast_to(gv, (1, 1)) == 1, float(LONG_LEN), float(SHORT_LEN))
    for j in range(3):
        count = jnp.sum(jnp.where(place_row == j, act_row, 0.0), axis=1, keepdims=True)
        SB[13 + j : 14 + j, 0:128] = jnp.where(lane == dp, count / length * lead, 0.0)

    ex_tok.wait_recv()
    project(oth)

    low_lanes = lax.broadcasted_iota(jnp.int32, (1, 128), 1) < HEAD_DIM

    def head_part(v, side):
        keep = low_lanes if side == 0 else jnp.logical_not(low_lanes)
        return jnp.where(keep, v, jnp.zeros_like(v))

    def pair_lanes(hp):
        return [slice(k * HALF + hp * 128, k * HALF + hp * 128 + 128) for k in range(3)]

    def with_ones(v, side):
        return jnp.where(lane == (1 - side) * HEAD_DIM, jnp.ones_like(v), head_part(v, side))

    ex_mix = []
    for hp in range(PAIRS):
        qlanes, klanes, vlanes = pair_lanes(hp)

        @pl.loop(0, PAD_LEN // AT)
        def _(t):
            rows = pl.ds(pl.multiple_of(t * AT, AT), AT)
            qp = TRI[rows, qlanes]
            kp = TRI[:, klanes]
            vp = TRI[:, vlanes]
            both = []
            for side in range(2):
                s = dot_nt(head_part(qp, side), kp) + BIAS[rows, :]
                e = jnp.exp(s - jnp.max(s, axis=-1, keepdims=True)).astype(bf16)
                PR[2 * hp + side, rows, :] = e
                both.append(dot_nn(e, with_ones(vp, side)))
            scale = 1.0 / jnp.where(low_lanes, both[0][:, HEAD_DIM : HEAD_DIM + 1], both[1][:, 0:1])
            INV[rows, qlanes] = scale
            MIX[c, rows, qlanes] = (jnp.where(low_lanes, both[0], both[1]) * scale).astype(bf16)

        ex_mix.append(to_core(MIX.at[c, :, qlanes], MIX.at[c, :, qlanes]))

    loads["wo"].wait()

    @pl.loop(0, PAD_LEN // MT)
    def _(t):
        rows = pl.ds(pl.multiple_of(t * MT, MT), MT)
        SUM[rows, :] = X[rows, :].astype(f32) + (dot_nn(MIX[c, rows, :], WO[pl.ds(chalf, HALF), :]) + vec(2))

    loads["cot"].wait()
    ex_cot.wait_recv()

    @pl.loop(0, PAD_LEN // LT)
    def _(t):
        rows = pl.ds(pl.multiple_of(t * LT, LT), LT)
        GM[rows, :] = (ACT[rows, :] * GATE[rows, :] * G[rows, :].astype(f32)).astype(bf16)

    for e in ex_mix:
        e.wait_recv()

    @pl.loop(0, PAD_LEN // MT)
    def _(t):
        rows = pl.ds(pl.multiple_of(t * MT, MT), MT)
        s = SUM[rows, :] + dot_nn(MIX[1 - c, rows, :], WO[pl.ds(pl.multiple_of(HALF - chalf, HALF), HALF), :])
        SUM[rows, :] = s
        unit, _ = row_stats(s)
        SEC[rows, :] = (unit * vec(6) + vec(7)).astype(bf16)

    SECT[...] = jnp.swapaxes(SEC[...], 0, 1)

    for n in ("bup", "wu", "wd"):
        loads[n].wait()

    def remote(src, dst, dev, i):
        return pltpu.make_async_remote_copy(
            src_ref=src, dst_ref=dst, send_sem=csem_s.at[i], recv_sem=csem_r.at[i],
            device_id=dev, device_id_type=MESH_ID,
        )

    pieces = {}

    where = {"x": x, "y": y}

    class Piece:
        def __init__(self, name, buffers, dst_ref, only_z=None):
            self.order = PIECES[name][1]
            self.src, self.recv, self.fin = buffers[0], buffers[1:4], buffers[4]
            self.only_z = only_z
            self.cur = self.src
            self.number = len(pieces)
            self.copies = []
            self.keep = pltpu.make_async_copy(self.fin, dst_ref, fsem_l.at[self.number])
            self.give = pltpu.make_async_remote_copy(
                src_ref=self.fin, dst_ref=dst_ref, send_sem=fsem_s.at[self.number],
                recv_sem=fsem_r.at[self.number], device_id=peer, device_id_type=MESH_ID,
            )
            pieces[name] = self

        def send(self, k, part=None):
            axis, recv = self.order[k], self.recv[k]
            slot = self.base(k)
            if axis != "z":
                src, dst = self.cur.at[1 - where[axis]], recv
                if part is not None:
                    src, dst, slot = src.at[part], dst.at[part], slot + part
                cp = remote(src, dst, xp if axis == "x" else yp, slot)
                cp.start()
                sends.append(cp)
                self.copies.append(cp)
                return
            for kk in range(3):
                if self.only_z is None:
                    cp = remote(self.cur.at[zs[kk]], recv.at[kk], zp[kk], slot + kk)
                    cp.start()
                    sends.append(cp)
                else:
                    cp = remote(self.cur.at[0], recv.at[kk], zp[kk], slot + kk)
                    pl.when(zs[kk] == self.only_z)(cp.start)
                self.copies.append(cp)

        def base(self, k):
            return 7 * self.number + sum(3 if a == "z" else 2 for a in self.order[:k])

        def add(self, k):
            for cp in self.copies:
                cp.wait_recv()
            self.copies = self.copies if k == 2 else []
            axis, recv = self.order[k], self.recv[k]
            mine_at = z if axis == "z" else where[axis]
            if axis == "z" and self.only_z is not None:
                mine_at = 0
            for idx in product(*(range(n) for n in self.src.shape[k + 1 : 3])):
                mine = self.cur[(mine_at,) + idx]
                if axis == "z":
                    total = mine.astype(f32) + recv[(0,) + idx].astype(f32)
                    total = total + (recv[(1,) + idx].astype(f32) + recv[(2,) + idx].astype(f32))
                elif k == 2:
                    total = mine.astype(f32) + recv[idx].astype(f32)
                else:
                    total = mine + recv[idx]
                if k == 2:
                    self.fin[...] = total
                elif axis == "z":
                    recv[(0,) + idx] = total.astype(bf16)
                else:
                    recv[idx] = total
            self.cur = recv.at[0] if axis == "z" else recv

        def first(self, part=None):
            self.send(0, part)

        def second(self):
            self.add(0)
            self.send(1)

        def third(self):
            self.add(1)
            self.send(2)

        def fourth(self):
            def finish():
                self.add(2)
                self.keep.start()
                self.give.start()

            if self.only_z is None:
                finish()
            else:
                pl.when(z == self.only_z)(finish)

        def fifth(self):
            keep, give = self.keep, self.give
            if self.only_z is None:
                keep.wait()
                give.wait()
                return

            @pl.when(z == self.only_z)
            def _():
                keep.wait()
                give.wait_send()

            @pl.when(z == self.only_z + 2 - 4 * c)
            def _():
                give.wait_recv()

            for kk in range(3):
                pl.when(zs[kk] == self.only_z)(self.copies[kk].wait_send)

    for i, (name, (grad, _, first_col, width)) in enumerate(PIECES.items()):
        lanes_from = {"up": (o_up, chid), "ou": (o_out, chalf), "q": (o_qkv, chalf), "k": (o_qkv, chalf + WIDTH),
                      "v": (o_qkv, chalf + 2 * WIDTH), "dA": (o_down, 0), "dB": (o_down, HALF)}[grad[:2]]
        start_at = lanes_from[1] + first_col + (int(grad[2:]) * HALF if grad[:2] == "up" else 0)
        dst_ref = lanes_from[0].at[:, pl.ds(pl.multiple_of(start_at, 128), width)]
        Piece(name, piece_bufs[5 * i : 5 * i + 5], dst_ref, 2 * c + int(grad[2:]) if grad[0] == "d" else None)

    def keep_grad(grad, rows, value):
        for name, (g, _, first_col, width) in PIECES.items():
            if g == grad:
                src, order = pieces[name].src, pieces[name].order
                tile = src.shape[3]
                for i in range(HALF // tile):
                    if grad[0] == "d":
                        place = {"z": 0, "y": rows, "x": i}
                    else:
                        place = {"z": 2 * rows + i // 4, "y": i // 2 % 2, "x": i % 2}
                    src[tuple(place[axis] for axis in order)] = value[
                        tile * i : tile * (i + 1), first_col : first_col + width
                    ].astype(bf16)

    class Small:
        def first(self, part=None):
            self.got = self.send(0, SB.at[pl.ds(pl.multiple_of(8 - 8 * c, 8), 8)], peer)

        def send(self, slot, src, dev):
            copy = pltpu.make_async_remote_copy(
                src_ref=src, dst_ref=SBR.at[slot], send_sem=ssem_s.at[slot], recv_sem=ssem_r.at[slot],
                device_id=dev, device_id_type=MESH_ID,
            )
            copy.start()
            sends.append(copy)
            return [copy]

        def gather(self, mine, slots):
            for cp in self.got:
                cp.wait_recv()
            for slot in slots:
                mine = mine + SBR[slot]
            return mine

        def second(self):
            SBL[0] = self.gather(SB[pl.ds(pl.multiple_of(8 * c, 8), 8), :], (0,))
            self.got = self.send(1, SBL.at[0], xp)

        def third(self):
            SBL[1] = self.gather(SBL[0], (1,))
            self.got = self.send(2, SBL.at[1], yp)

        def fourth(self):
            SBL[2] = self.gather(SBL[1], (2,))
            self.got = []
            for k in range(3):
                self.got += self.send(3 + k, SBL.at[2], zp[k])

        def fifth(self):
            SBL[3] = self.gather(SBL[2], (3, 4, 5))
            rows = o_small.at[pl.ds(pl.multiple_of(8 * c, 8), 8)]
            self.keep = pltpu.make_async_copy(SBL.at[3], rows, lsem.at[N_LOADS + 2])
            self.give = pltpu.make_async_remote_copy(
                src_ref=SBL.at[3], dst_ref=rows, send_sem=ssem_s.at[6], recv_sem=ssem_r.at[6],
                device_id=peer, device_id_type=MESH_ID,
            )
            self.keep.start()
            self.give.start()

        def sixth(self):
            self.keep.wait()
            self.give.wait()

    pieces["small"] = Small()

    def at(point):
        for act, name in SCHEDULE.get(point, ()):
            p = pieces[name]
            if act == 0:
                p.first(part=0)
            elif act == 1:
                p.first(part=1 if name in HALVED else None)
            else:
                getattr(p, ("second", "third", "fourth", "fifth", "sixth")[act - 2])()

    for j in range(BLOCKS):
        cols = slice(j * HALF, (j + 1) * HALF)
        bj = BUP[:, pl.ds(pl.multiple_of(chid + j * HALF, 128), HALF)]

        @pl.loop(0, PAD_LEN // MT)
        def _(t):
            rows = pl.ds(pl.multiple_of(t * MT, MT), MT)
            pre = dot_nn(SEC[rows, :], WU[:, cols]) + bj
            gh = dot_nt(GM[rows, :], WD[cols, :])
            cdf = 0.5 * (1.0 + lax.erf(pre * (2.0 ** -0.5)))
            hid = (pre * cdf).astype(bf16)
            slope = cdf + pre * (0.3989422804014327 * jnp.exp(-0.5 * pre * pre))
            gp = (gh * slope).astype(bf16)
            HIDJ[rows, :] = hid
            GPJ[rows, :] = gp
            d = dot_nn(hid, WD[cols, :])
            s = dot_nt(gp, WU[:, cols])
            if j > 0:
                d = ACCD[rows, :] + d
                s = ACCS[rows, :] + s
            ACCD[rows, :] = d
            ACCS[rows, :] = s
            if j == BLOCKS - 1:
                GSB[rows, :] = s.astype(bf16)

        if j == BLOCKS - 1:
            ex_gs = to_core(GSB, GSR)

            @pl.loop(0, OWN // LT)
            def _(t):
                r = pl.ds(pl.multiple_of(t * LT, LT), LT)
                DSB[r, :] = ACCD[pl.ds(pl.multiple_of(oth + t * LT, 32), LT), :].astype(bf16)

            ex_ds = to_core(DSB, DSR)

        for part in range(2):
            g = dot_nn(SECT[part * HALF : (part + 1) * HALF, :], GPJ[...])
            keep_grad("up%d" % j, part, g)
        at("u%d" % j)
        SB[pl.ds(9 + 2 * c + j // 2, 1), (j % 2) * HALF : (j % 2 + 1) * HALF] = jnp.sum(
            GPJ[...].astype(f32), axis=0, keepdims=True
        )
        for part in range(2):
            g = dot_tn(HIDJ[...], GM[:, part * HALF : (part + 1) * HALF])
            keep_grad("d%s%d" % ("AB"[part], j // 2), j % 2, g)
        at("j%d" % j)

    ex_gs.wait_recv()

    zero_row = jnp.zeros((1, WIDTH), f32)

    def col_sum(v):
        return jnp.sum(v, axis=0, keepdims=True)

    def second_back(t, carry):
        rows = pl.ds(pl.multiple_of(t * LT, LT), LT)
        gs = ACCS[rows, :] + GSR[rows, :].astype(f32)
        unit, rstd = row_stats(SUM[rows, :])
        back = norm_back(unit, rstd, gs, vec(6))
        ACCS[rows, :] = back
        ga = (ACT[rows, :] * GATE[rows, :] * G[rows, :].astype(f32) + back).astype(bf16)
        GATT[rows, :] = ga
        return (
            carry[0] + col_sum(gs * unit), carry[1] + col_sum(gs), carry[2] + col_sum(ga.astype(f32)),
            carry[3] + col_sum(GM[rows, :].astype(f32)),
        )

    sums = lax.fori_loop(0, PAD_LEN // LT, second_back, (zero_row,) * 4)
    for row, value in zip((6, 7, 2, 3), sums):
        SB[row : row + 1, :] = value * lead
    at("sb")

    for part in range(2):
        g = dot_tn(MIX[part], GATT[:, pl.ds(chalf, HALF)])
        keep_grad("out", part, g)
    at("out")

    @pl.loop(0, PAD_LEN // MT)
    def _(t):
        rows = pl.ds(pl.multiple_of(t * MT, MT), MT)
        GMX[rows, :] = (dot_nt(GATT[rows, :], WO[pl.ds(chalf, HALF), :]) * INV[rows, :]).astype(bf16)

    at("gmx")

    for hp in range(PAIRS):
        qlanes, klanes, vlanes = pair_lanes(hp)
        kp = TRI[:, klanes]
        vp = TRI[:, vlanes]
        gp = GMX[:, qlanes]
        dots = gp.astype(f32) * MIX[c, :, qlanes].astype(f32)
        qt = jnp.swapaxes(TRI[:, qlanes], 0, 1)
        gt = jnp.swapaxes(gp, 0, 1)
        dq = jnp.zeros((PAD_LEN, 128), f32)
        for side in range(2):
            half = slice(side * HEAD_DIM, (side + 1) * HEAD_DIM)
            e = PR[2 * hp + side]
            dpr = dot_nt(head_part(gp, side), vp)
            delta = jnp.sum(head_part(dots, side), axis=-1, keepdims=True)
            ds = (e.astype(f32) * (dpr - delta)).astype(bf16)
            dq = dq + dot_nn(ds, head_part(kp, side))
            DKT[half, :] = dot_nn(qt[half, :], ds)
            DVT[half, :] = dot_nn(gt[half, :], e)
        DTR[:, qlanes] = (dq * HEAD_DIM ** (-0.5)).astype(bf16)
        DTR[:, klanes] = jnp.swapaxes(DKT[...], 0, 1).astype(bf16)
        DTR[:, vlanes] = jnp.swapaxes(DVT[...], 0, 1).astype(bf16)
        at("h%d" % hp)

    for k in range(3):
        blk = DTR[:, k * HALF : (k + 1) * HALF]
        if k != 1:
            SB[k // 2 : k // 2 + 1, pl.ds(chalf, HALF)] = col_sum(blk.astype(f32))
        for part in range(2):
            g = dot_tn(NRM[:, part * HALF : (part + 1) * HALF], blk)
            keep_grad("qkv"[k], part, g)
        at("qkv"[k])

    ex_ds.wait_send()
    DSB[...] = dot_nt(DTR[pl.ds(oth, OWN), :], WQ[...]).astype(bf16)
    ex_ns = to_core(DSB, NSR)
    at("ns")
    ex_ds.wait_recv()
    ex_gs.wait_send()
    ex_ns.wait_recv()
    OUTB, INB = GSB.at[0:OWN], GSB.at[OWN:PAD_LEN]

    def first_back(t, carry):
        r = pl.ds(pl.multiple_of(t * 80, 80), 80)
        rows = pl.ds(pl.multiple_of(own + t * 80, 80), 80)
        xf = X[rows, :].astype(f32)
        unit, rstd = row_stats(xf)
        gn = dot_nt(DTR[rows, :], WQ[...]) + NSR[r, :].astype(f32)
        first = norm_back(unit, rstd, gn, vec(4))
        gf = G[rows, :].astype(f32)
        gate = ACT[rows, :] * GATE[rows, :]
        branch = SUM[rows, :] - xf + ACCD[rows, :] + DSR[r, :].astype(f32) + vec(3)
        OUTB[r, :] = (xf + gate * branch).astype(bf16)
        gl = jnp.sum(gf * branch, axis=-1, keepdims=True) * (gate * (1.0 - GATE[rows, :]))
        INB[r, :] = (gf + ACCS[rows, :] + first + gl * vec(8)).astype(bf16)
        return (carry[0] + col_sum(gn * unit), carry[1] + col_sum(gn), carry[2] + col_sum(gl * xf))

    sums = lax.fori_loop(0, OWN // 80, first_back, (zero_row,) * 3)
    for row, value in zip((4, 5, 8), sums):
        SB[row : row + 1, :] = value
    keep_out = pltpu.make_async_copy(OUTB, o_output.at[0], lsem.at[len(loads)])
    keep_in = pltpu.make_async_copy(INB, o_input.at[0], lsem.at[len(loads) + 1])
    keep_out.start()
    keep_in.start()

    at("fb")
    at("end")
    for cp in sends:
        if cp is not ex_ds and cp is not ex_gs:
            cp.wait_send()
    for cp in (keep_out, keep_in):
        cp.wait()


N_LOADS = 2 + 9 + 3 + 5
BIG = (0, 1, 2, 5, 7, 9)
SMALLS = (3, 4, 6, 10, 11, 12, 13, 14, 15)


def place_kernel(*refs):
    src, dst, bufs, (vec, up, share, sem) = refs[:7], refs[7:24], refs[24:31], refs[31:]
    dp = lax.axis_index("dp")
    ins = [pltpu.make_async_copy(src[i], bufs[i], sem.at[i]) for i in range(7)]
    outs = [pltpu.make_async_copy(bufs[i], dst[k], sem.at[7 + i]) for i, k in enumerate(BIG)]
    for i in (6, 0, 1, 2, 3, 4, 5):
        ins[i].start()
    ins[6].wait()
    rows = bufs[6][...]
    mine = pltpu.roll(rows, lax.rem(dp * (WIDTH - 48), WIDTH), 1)
    for i in range(9):
        vec[i] = mine[i : i + 1, :48]
    bufs[6][...] = pltpu.roll(rows, lax.rem(lax.rem(dp, 4) * (WIDTH - 192), WIDTH), 1)
    up[...] = bufs[6][pl.ds(9 + lax.div(dp, 4), 1), :192]
    share[...] = rows[13:16, :16]
    smalls = [pltpu.make_async_copy(vec.at[i], dst[k], sem.at[13 + i]) for i, k in enumerate(SMALLS)]
    smalls += [pltpu.make_async_copy(up, dst[8], sem.at[22]), pltpu.make_async_copy(share, dst[16], sem.at[23])]
    for cp in smalls:
        cp.start()
    for a, b in zip(ins, outs):
        a.wait()
        b.start()
    for cp in outs + smalls:
        cp.wait()


def fused(
    tokens, cotangent, group, select, w_qkv, b_query, b_value, w_out, b_out, w_up, b_up, w_down,
    b_down, ln1_gain, ln1_bias, ln2_gain, ln2_bias, w_router,
):
    args = (
        tokens, cotangent, group, select, w_qkv, b_query, b_value, w_out, b_out, w_up, b_up, w_down,
        b_down, ln1_gain, ln1_bias, ln2_gain, ln2_bias, w_router,
    )
    anywhere = pl.BlockSpec(memory_space=pl.ANY)
    shape = jax.ShapeDtypeStruct
    mids = (
        shape((1, OWN, WIDTH), bf16), shape((1, OWN, WIDTH), bf16), shape((48, 3 * WIDTH), f32),
        shape((48, WIDTH), f32), shape((48, HIDDEN), f32), shape((192, WIDTH), f32),
        shape((SMALL, WIDTH), f32),
    )
    v = pltpu.VMEM
    sq = (PAD_LEN, WIDTH)
    scratch = [
        v(sq, bf16), v(sq, bf16), v((2, 1, OWN), jnp.int32), v((9, 1, WIDTH), f32), v((1, HIDDEN), f32),
        v(sq, bf16), v((WIDTH, 3 * HALF), bf16), v((WIDTH, WIDTH), bf16), v((WIDTH, HID), bf16),
        v((HID, WIDTH), bf16), v((PAD_LEN, 3 * HALF), bf16), v((2 * PAIRS, PAD_LEN, PAD_LEN), bf16),
        v((2, PAD_LEN, HALF), bf16), v(sq, f32), v(sq, bf16), v(sq, bf16), v((PAD_LEN, PAD_LEN), f32),
        v((PAD_LEN, 1), f32), v((PAD_LEN, 1), f32),
        v((PAD_LEN, HALF), bf16), v((PAD_LEN, HALF), bf16), v(sq, f32), v(sq, f32), v(sq, bf16), v(sq, bf16),
        v((OWN, WIDTH), bf16), v((OWN, WIDTH), bf16), v(sq, bf16), v((PAD_LEN, HALF), bf16),
        v((PAD_LEN, 3 * HALF), bf16), v((128, PAD_LEN), f32), v((128, PAD_LEN), f32),
        v((PAD_LEN, HALF), f32), v((WIDTH, PAD_LEN), bf16), v((OWN, WIDTH), bf16),
        v((SMALL, WIDTH), f32), v((4, 8, WIDTH), f32), v((6, 8, WIDTH), f32),
    ] + [v(*b) for name in PIECES for b in piece_shapes(name)] + [
        pltpu.SemaphoreType.DMA((N_LOADS + 4,)),
        pltpu.SemaphoreType.DMA((9,)), pltpu.SemaphoreType.DMA((9,)),
        pltpu.SemaphoreType.DMA((7 * len(PIECES),)), pltpu.SemaphoreType.DMA((7 * len(PIECES),)),
        pltpu.SemaphoreType.DMA((7,)), pltpu.SemaphoreType.DMA((7,)),
        pltpu.SemaphoreType.DMA((len(PIECES),)), pltpu.SemaphoreType.DMA((len(PIECES),)), pltpu.SemaphoreType.DMA((len(PIECES),)),
    ]
    mid = pl.pallas_call(
        layer_kernel,
        out_shape=mids,
        in_specs=[anywhere, anywhere, pl.BlockSpec(memory_space=pltpu.SMEM)] + [anywhere] * 15,
        out_specs=[anywhere] * 7,
        scratch_shapes=scratch,
        compiler_params=pltpu.CompilerParams(
            collective_id=0, has_side_effects=True, vmem_limit_bytes=60 << 20
        ),
        name="layer",
    )(*args)
    outs = (
        mids[0], mids[1], mids[2], shape((1, 48), f32), shape((1, 48), f32), mids[3], shape((1, 48), f32),
        mids[4], shape((1, 192), f32), mids[5],
    ) + (shape((1, 48), f32),) * 6 + (shape((3, 16), f32),)
    out = pl.pallas_call(
        place_kernel,
        out_shape=outs,
        in_specs=[anywhere] * 7,
        out_specs=[anywhere] * 17,
        scratch_shapes=[v(m.shape, m.dtype) for m in mids]
        + [v((9, 1, 48), f32), v((1, 192), f32), v((3, 16), f32), pltpu.SemaphoreType.DMA((24,))],
        name="place",
    )(*mid)
    return tuple(o.reshape(-1) if o.shape[0] == 1 and o.ndim == 2 else o for o in out[:16]) + (out[16].T,)


def norm_rows(values, norm_gain, norm_shift):
    average = jnp.mean(values, axis=-1, keepdims=True)
    centred = values - average
    variance = jnp.mean(centred * centred, axis=-1, keepdims=True)
    return centred * lax.rsqrt(variance + epsilon) * norm_gain + norm_shift


def places_of(group, slot_pos):
    short_place = jnp.minimum(slot_pos // SHORT_LEN, 2)
    return jnp.where(group[:, None] == 1, 0, short_place[None, :])


def split_heads(flat_rows):
    return flat_rows.reshape(flat_rows.shape[0], flat_rows.shape[1], HEADS, HEAD_DIM)


def masked_scores(queries, key_heads, query_place, key_place, key_mask):
    score_scale = HEAD_DIM ** (-0.5)
    scores = (
        jnp.einsum("bqhe,bkhe->bqhk", queries, key_heads, preferred_element_type=jnp.float32)
        * score_scale
    )
    key_live = (key_mask.astype(jnp.float32)[:, None, None, :] > 0.5) & (
        query_place[:, :, None, None] == key_place[:, None, None, :]
    )
    return (jnp.where(key_live, scores, masked_floor), key_live.astype(jnp.float32))


def attend(queries, key_heads, value_heads, query_place, key_place, key_mask):
    masked, key_weight = masked_scores(queries, key_heads, query_place, key_place, key_mask)
    row_max = jnp.max(masked, axis=-1, keepdims=True)
    exponent = jnp.exp(masked - row_max) * key_weight
    row_sum = jnp.sum(exponent, axis=-1, keepdims=True)
    weights = (exponent / row_sum).astype(jnp.bfloat16)
    mixed_heads = jnp.einsum(
        "bqhk,bkhe->bqhe", weights, value_heads, preferred_element_type=jnp.float32
    )
    return (mixed_heads, row_max + jnp.log(row_sum))


def back_parts(
    queries, key_heads, value_heads, query_place, key_place, key_mask, log_total, grad_heads, delta
):
    masked, key_weight = masked_scores(queries, key_heads, query_place, key_place, key_mask)
    key_probs = jnp.exp(masked - log_total) * key_weight
    grad_probs = jnp.einsum(
        "bqhe,bkhe->bqhk", grad_heads, value_heads, preferred_element_type=jnp.float32
    )
    delta = jnp.sum(key_probs * grad_probs, axis=-1, keepdims=True)
    grad_scores = (key_probs * (grad_probs - delta)).astype(jnp.bfloat16)
    return (key_probs, grad_scores, delta)


def key_side_grads(key_probs, grad_scores, queries, grad_heads):
    score_scale = HEAD_DIM ** (-0.5)
    grad_values = jnp.einsum(
        "bqhk,bqhe->bkhe",
        key_probs.astype(jnp.bfloat16),
        grad_heads,
        preferred_element_type=jnp.float32,
    )
    grad_keys = (
        jnp.einsum("bqhk,bqhe->bkhe", grad_scores, queries, preferred_element_type=jnp.float32)
        * score_scale
    )
    return (grad_keys, grad_values)


def on_device(
    tokens,
    cotangent,
    group,
    select,
    w_qkv,
    b_query,
    b_value,
    w_out,
    b_out,
    w_up,
    b_up,
    w_down,
    b_down,
    ln1_gain,
    ln1_bias,
    ln2_gain,
    ln2_bias,
    w_router,
):
    packs, per_piece, features = tokens.shape
    row_count = packs * per_piece
    first_pos = lax.axis_index("seq") * per_piece
    positions = first_pos + jnp.arange(per_piece, dtype=jnp.int32)
    full_positions = jnp.arange(PAD_LEN, dtype=jnp.int32)
    place_own = places_of(group, positions)
    place_full = places_of(group, full_positions)
    ends = jnp.where(group == 1, LONG_LEN, 3 * SHORT_LEN).astype(jnp.int32)
    active = ((select > 0) & (positions[None, :] < ends[:, None])).astype(jnp.float32)
    active_rows = active.reshape(row_count, 1)
    xfloat = tokens.reshape(row_count, features).astype(jnp.float32)
    router = jax.nn.sigmoid(jnp.dot(xfloat, w_router, precision=lax.Precision.HIGHEST))
    normed, first_back = jax.vjp(norm_rows, xfloat, ln1_gain, ln1_bias)
    normed_low = normed.astype(jnp.bfloat16)
    qkv_bias = jnp.concatenate([b_query, jnp.zeros_like(b_query), b_value])
    triple = (jnp.dot(normed_low, w_qkv, preferred_element_type=jnp.float32) + qkv_bias).astype(
        jnp.bfloat16
    )
    queries = triple[:, :features].reshape(packs, per_piece, HEADS, HEAD_DIM)
    keys_own = triple[:, features : 2 * features].reshape(packs, per_piece, features)
    values_own = triple[:, 2 * features :].reshape(packs, per_piece, features)
    mask_own = active.astype(jnp.bfloat16)
    keys_all, values_all, mask_all = (
        lax.all_gather(keys_own, "seq", axis=1, tiled=True),
        lax.all_gather(values_own, "seq", axis=1, tiled=True),
        lax.all_gather(mask_own, "seq", axis=1, tiled=True),
    )
    mixed_heads, log_total = attend(
        queries, split_heads(keys_all), split_heads(values_all), place_own, place_full, mask_all
    )
    mixed_low = mixed_heads.reshape(row_count, features).astype(jnp.bfloat16)
    attended = jnp.dot(mixed_low, w_out, preferred_element_type=jnp.float32) + b_out
    summed = xfloat + attended
    second, second_back = jax.vjp(norm_rows, summed, ln2_gain, ln2_bias)
    second_low = second.astype(jnp.bfloat16)
    pre_act = jnp.dot(second_low, w_up, preferred_element_type=jnp.float32) + b_up
    gelu_out, gelu_back = jax.vjp(partial(jax.nn.gelu, approximate=False), pre_act)
    hidden_low = gelu_out.astype(jnp.bfloat16)
    branch = attended + (jnp.dot(hidden_low, w_down, preferred_element_type=jnp.float32) + b_down)
    gate_rows = active_rows * router[:, None]
    output = (xfloat + gate_rows * branch).astype(jnp.bfloat16).reshape(packs, per_piece, features)
    place_range = jnp.arange(3, dtype=jnp.int32)
    onehot = (place_full[:, :, None] == place_range[None, None, :]).astype(jnp.float32)
    counts = jnp.sum(mask_all.astype(jnp.float32)[:, :, None] * onehot, axis=1)
    image_lengths = jnp.where(group == 1, LONG_LEN, SHORT_LEN).astype(jnp.float32)
    fractions = lax.all_gather(counts / image_lengths[:, None], "dp", axis=0, tiled=True)
    grad_rows = cotangent.reshape(row_count, features).astype(jnp.float32)
    grad_logit = jnp.sum(grad_rows * branch, axis=1) * active_rows[:, 0] * router * (1.0 - router)
    grad_branch = gate_rows * grad_rows
    grad_mlp = grad_branch.astype(jnp.bfloat16)
    grad_down = jnp.einsum("rk,rd->kd", hidden_low, grad_mlp, preferred_element_type=jnp.float32)
    grad_down_bias = jnp.sum(grad_mlp.astype(jnp.float32), axis=0)
    grad_hidden = jnp.einsum("rd,kd->rk", grad_mlp, w_down, preferred_element_type=jnp.float32)
    grad_pre = gelu_back(grad_hidden)[0].astype(jnp.bfloat16)
    grad_up = jnp.einsum("rd,rk->dk", second_low, grad_pre, preferred_element_type=jnp.float32)
    grad_up_bias = jnp.sum(grad_pre.astype(jnp.float32), axis=0)
    grad_second = jnp.einsum("rk,dk->rd", grad_pre, w_up, preferred_element_type=jnp.float32)
    grad_summed, grad_ln2_gain, grad_ln2_bias = second_back(grad_second)
    grad_attended = (grad_branch + grad_summed).astype(jnp.bfloat16)
    grad_out = jnp.einsum("rd,re->de", mixed_low, grad_attended, preferred_element_type=jnp.float32)
    grad_out_bias = jnp.sum(grad_attended.astype(jnp.float32), axis=0)
    grad_mixed = jnp.einsum("re,de->rd", grad_attended, w_out, preferred_element_type=jnp.float32)
    grad_heads = grad_mixed.astype(jnp.bfloat16).reshape(packs, per_piece, HEADS, HEAD_DIM)
    back_k, back_v, back_m = (
        lax.all_gather(keys_own, "seq", axis=1, tiled=True),
        lax.all_gather(values_own, "seq", axis=1, tiled=True),
        lax.all_gather(mask_own, "seq", axis=1, tiled=True),
    )
    back_kh = split_heads(back_k)
    back_vh = split_heads(back_v)
    key_probs, grad_scores, delta = back_parts(
        queries, back_kh, back_vh, place_own, place_full, back_m, log_total, grad_heads, None
    )
    grad_queries = jnp.einsum(
        "bqhk,bkhe->bqhe", grad_scores, back_kh, preferred_element_type=jnp.float32
    ) * HEAD_DIM ** (-0.5)
    grad_keys, grad_values = key_side_grads(key_probs, grad_scores, queries, grad_heads)
    keys_grad_own, values_grad_own = (
        lax.psum_scatter(
            grad_keys.reshape(back_k.shape).astype(jnp.bfloat16),
            "seq",
            scatter_dimension=1,
            tiled=True,
        ).astype(jnp.float32),
        lax.psum_scatter(
            grad_values.reshape(back_v.shape).astype(jnp.bfloat16),
            "seq",
            scatter_dimension=1,
            tiled=True,
        ).astype(jnp.float32),
    )
    grad_triple = jnp.concatenate(
        [
            grad_queries.reshape(row_count, features),
            keys_grad_own.reshape(row_count, features),
            values_grad_own.reshape(row_count, features),
        ],
        axis=1,
    ).astype(jnp.bfloat16)
    grad_qkv = jnp.einsum("rd,rk->dk", normed_low, grad_triple, preferred_element_type=jnp.float32)
    column_sums = jnp.sum(grad_triple.astype(jnp.float32), axis=0)
    grad_query_bias = column_sums[:features]
    grad_value_bias = column_sums[2 * features :]
    grad_normed = jnp.einsum("rk,dk->rd", grad_triple, w_qkv, preferred_element_type=jnp.float32)
    grad_first, grad_ln1_gain, grad_ln1_bias = first_back(grad_normed)
    grad_router = jnp.dot(grad_logit, xfloat, precision=lax.Precision.HIGHEST)
    grad_input = grad_rows + grad_summed + grad_first + grad_logit[:, None] * w_router[None, :]
    input_grad = grad_input.astype(jnp.bfloat16).reshape(packs, per_piece, features)
    (
        share_qkv,
        share_query_bias,
        share_value_bias,
        share_out,
        share_out_bias,
        share_up,
        share_up_bias,
        share_down,
        share_down_bias,
        share_ln1_gain,
        share_ln1_bias,
        share_ln2_gain,
        share_ln2_bias,
        share_router,
    ) = (
        lax.psum_scatter(
            grad_qkv.astype(jnp.bfloat16), "dp", scatter_dimension=0, tiled=True
        ).astype(jnp.float32),
        lax.psum_scatter(
            grad_query_bias.astype(jnp.bfloat16), "dp", scatter_dimension=0, tiled=True
        ).astype(jnp.float32),
        lax.psum_scatter(
            grad_value_bias.astype(jnp.bfloat16), "dp", scatter_dimension=0, tiled=True
        ).astype(jnp.float32),
        lax.psum_scatter(
            grad_out.astype(jnp.bfloat16), "dp", scatter_dimension=0, tiled=True
        ).astype(jnp.float32),
        lax.psum_scatter(
            grad_out_bias.astype(jnp.bfloat16), "dp", scatter_dimension=0, tiled=True
        ).astype(jnp.float32),
        lax.psum_scatter(
            grad_up.astype(jnp.bfloat16), "dp", scatter_dimension=0, tiled=True
        ).astype(jnp.float32),
        lax.psum_scatter(
            grad_up_bias.astype(jnp.bfloat16), "dp", scatter_dimension=0, tiled=True
        ).astype(jnp.float32),
        lax.psum_scatter(
            grad_down.astype(jnp.bfloat16), "dp", scatter_dimension=0, tiled=True
        ).astype(jnp.float32),
        lax.psum_scatter(
            grad_down_bias.astype(jnp.bfloat16), "dp", scatter_dimension=0, tiled=True
        ).astype(jnp.float32),
        lax.psum_scatter(
            grad_ln1_gain.astype(jnp.bfloat16), "dp", scatter_dimension=0, tiled=True
        ).astype(jnp.float32),
        lax.psum_scatter(
            grad_ln1_bias.astype(jnp.bfloat16), "dp", scatter_dimension=0, tiled=True
        ).astype(jnp.float32),
        lax.psum_scatter(
            grad_ln2_gain.astype(jnp.bfloat16), "dp", scatter_dimension=0, tiled=True
        ).astype(jnp.float32),
        lax.psum_scatter(
            grad_ln2_bias.astype(jnp.bfloat16), "dp", scatter_dimension=0, tiled=True
        ).astype(jnp.float32),
        lax.psum_scatter(
            grad_router.astype(jnp.bfloat16), "dp", scatter_dimension=0, tiled=True
        ).astype(jnp.float32),
    )
    totals = (
        lax.psum(share_qkv.astype(jnp.bfloat16), "seq").astype(jnp.float32),
        lax.psum(share_query_bias.astype(jnp.bfloat16), "seq").astype(jnp.float32),
        lax.psum(share_value_bias.astype(jnp.bfloat16), "seq").astype(jnp.float32),
        lax.psum(share_out.astype(jnp.bfloat16), "seq").astype(jnp.float32),
        lax.psum(share_out_bias.astype(jnp.bfloat16), "seq").astype(jnp.float32),
        lax.psum(share_up.astype(jnp.bfloat16), "seq").astype(jnp.float32),
        lax.psum(share_up_bias.astype(jnp.bfloat16), "seq").astype(jnp.float32),
        lax.psum(share_down.astype(jnp.bfloat16), "seq").astype(jnp.float32),
        lax.psum(share_down_bias.astype(jnp.bfloat16), "seq").astype(jnp.float32),
        lax.psum(share_ln1_gain.astype(jnp.bfloat16), "seq").astype(jnp.float32),
        lax.psum(share_ln1_bias.astype(jnp.bfloat16), "seq").astype(jnp.float32),
        lax.psum(share_ln2_gain.astype(jnp.bfloat16), "seq").astype(jnp.float32),
        lax.psum(share_ln2_bias.astype(jnp.bfloat16), "seq").astype(jnp.float32),
        lax.psum(share_router.astype(jnp.bfloat16), "seq").astype(jnp.float32),
    )
    return (
        output,
        input_grad,
        totals[0],
        totals[1],
        totals[2],
        totals[3],
        totals[4],
        totals[5],
        totals[6],
        totals[7],
        totals[8],
        totals[9],
        totals[10],
        totals[11],
        totals[12],
        totals[13],
        fractions,
    )


def solution(mesh):
    in_specs = (
        P("dp", "seq", None),
        P("dp", "seq", None),
        P("dp"),
        P("dp", "seq"),
        P(),
        P(),
        P(),
        P(),
        P(),
        P(),
        P(),
        P(),
        P(),
        P(),
        P(),
        P(),
        P(),
        P(),
    )
    out_specs = (
        P("dp", "seq", None),
        P("dp", "seq", None),
        P("dp", None),
        P("dp"),
        P("dp"),
        P("dp", None),
        P("dp"),
        P("dp", None),
        P("dp"),
        P("dp", None),
        P("dp"),
        P("dp"),
        P("dp"),
        P("dp"),
        P("dp"),
        P("dp"),
        P(),
    )
    fast = mesh.shape["dp"] == 16 and mesh.shape["seq"] == 2
    return jax.shard_map(
        fused if fast else on_device, mesh=mesh, in_specs=in_specs, out_specs=out_specs, check_vma=False
    )
```

```python
from functools import partial
from itertools import product

import jax
import jax.numpy as jnp
from jax import lax
from jax.experimental import pallas as pl
from jax.experimental.pallas import tpu as pltpu
from jax.sharding import PartitionSpec as P

HEADS = 12
HEAD_DIM = 64
PAD_LEN = 640
LONG_LEN = 577
SHORT_LEN = 197
WIDTH = 768
HIDDEN = 3072

epsilon = 1e-06
masked_floor = -1000000000.0
MESH_ID = pl.DeviceIdType.MESH
bf16 = jnp.bfloat16
f32 = jnp.float32

HALF = WIDTH // 2
OWN = PAD_LEN // 2
HID = HIDDEN // 2
BLOCKS = HID // HALF
PAIRS = HALF // 128
MT = 320
AT = 640
LT = 160
SMALL = 16
PIECES = {
    "up0_0": ("up0", "zxy", 0, 128),
    "up0_1": ("up0", "yxz", 128, 256),
    "up1": ("up1", "zyx", 0, 384),
    "up2": ("up2", "yzx", 0, 384),
    "up3": ("up3", "xzy", 0, 384),
    "dA0": ("dA0", "xyz", 0, 384),
    "dB0": ("dB0", "yxz", 0, 384),
    "dA1": ("dA1", "xyz", 0, 384),
    "dB1": ("dB1", "yxz", 0, 384),
    "out": ("out", "xyz", 0, 384),
    "q": ("q", "yxz", 0, 384),
    "k_0": ("k", "xyz", 0, 128),
    "k_1": ("k", "yxz", 128, 256),
    "v_0": ("v", "yxz", 0, 128),
    "v_1": ("v", "xyz", 128, 128),
    "v_2": ("v", "xyz", 256, 128),
}
HALVED = ("dA0", "dA1")
SCHEDULE = {
    "u0": (
        (1, "up0_1"), (1, "up0_0"),
    ),
    "j0": (
        (0, "dA0"),
    ),
    "j1": (
        (1, "dB0"), (1, "up1"), (1, "dA0"), (2, "up0_1"),
    ),
    "j2": (
        (1, "up2"), (0, "dA1"),
    ),
    "u3": (
        (1, "up3"),
    ),
    "sb": (
        (3, "up0_1"),
    ),
    "out": (
        (1, "dB1"), (1, "dA1"), (2, "dA0"),
    ),
    "gmx": (
        (2, "up2"), (2, "dB0"),
    ),
    "h0": (
        (2, "up3"), (1, "out"),
    ),
    "h1": (
        (2, "dA1"), (2, "up0_0"),
    ),
    "h2": (
        (3, "dB0"),
    ),
    "q": (
        (2, "dB1"), (1, "q"),
    ),
    "k": (
        (3, "dA0"),
    ),
    "v": (
        (3, "dA1"), (1, "v_2"), (2, "out"), (3, "dB1"), (1, "v_1"), (1, "k_1"), (1, "v_0"), (2, "q"),
    ),
    "ns": (
        (1, "k_0"),
    ),
    "fb": (
        (2, "v_2"), (1, "small"), (3, "out"), (4, "up0_1"), (2, "small"), (3, "q"), (2, "k_1"), (3, "up3"),
        (2, "up1"), (3, "v_2"), (2, "v_0"), (3, "small"), (3, "up0_0"), (2, "v_1"), (3, "k_1"), (4, "out"),
        (2, "k_0"), (4, "small"), (4, "dB1"),
    ),
    "end": (
        (3, "up1"), (4, "dA1"), (4, "up0_0"), (4, "dA0"), (3, "v_1"), (3, "k_0"), (3, "up2"), (4, "up3"),
        (4, "up1"), (3, "v_0"), (4, "v_2"), (4, "q"), (4, "dB0"), (5, "small"), (4, "up2"), (4, "k_1"), (4, "v_1"),
        (4, "k_0"), (4, "v_0"),
    ),
}


def dot_nn(a, b):
    return lax.dot_general(a, b, (((1,), (0,)), ((), ())), preferred_element_type=f32)


def dot_nt(a, b):
    return lax.dot_general(a, b, (((1,), (1,)), ((), ())), preferred_element_type=f32)


def dot_tn(a, b):
    return lax.dot_general(a, b, (((0,), (0,)), ((), ())), preferred_element_type=f32)


def row_stats(values):
    average = jnp.mean(values, axis=-1, keepdims=True)
    centred = values - average
    variance = jnp.mean(centred * centred, axis=-1, keepdims=True)
    rstd = lax.rsqrt(variance + epsilon)
    return centred * rstd, rstd


def norm_back(unit, rstd, grad, gain):
    q = grad * gain
    return rstd * (
        q - jnp.mean(q, axis=-1, keepdims=True) - unit * jnp.mean(q * unit, axis=-1, keepdims=True)
    )


def piece_shapes(name):
    grad, order, _, width = PIECES[name]
    left = [{"z": 1 if grad[0] == "d" else 4, "y": 2, "x": 2}[axis] for axis in order]
    tile = [192 if grad[0] == "d" else 48, width]
    shapes = [(left + tile, bf16)]
    for k, axis in enumerate(order):
        shapes.append(([3] * (axis == "z") + left[k + 1 :] + tile, bf16))
    return shapes + [(tile, f32)]


def layer_kernel(*refs):
    (tokens, cotangent, group, select, w_qkv, b_query, b_value, w_out, b_out, w_up, b_up, w_down,
     b_down, ln1_gain, ln1_bias, ln2_gain, ln2_bias, w_router) = refs[:18]
    o_output, o_input, o_qkv, o_out, o_up, o_down, o_small = refs[18:25]
    (X, G, SEL, VEC, BUP, NRM, WQ, WO, WU, WD, TRI, PR, MIX, SUM, SEC, GM, QAUX, KAUX, GATE, ACT,
     HIDJ, GPJ, ACCD, ACCS, GSB, GSR, DSB, DSR, GATT, GMX, DTR, DKT, DVT, INV, SECT, NSR, SB, SBL, SBR) = refs[25:64]
    piece_bufs = refs[64 : 64 + 5 * len(PIECES)]
    (lsem, esem_s, esem_r, csem_s, csem_r, ssem_s, ssem_r, fsem_l, fsem_s, fsem_r) = refs[64 + 5 * len(PIECES) :]
    dp = lax.axis_index("dp")
    c = lax.axis_index("seq")
    x = lax.rem(dp, 2)
    y = lax.rem(lax.div(dp, 2), 2)
    z = lax.div(dp, 4)
    peer = (dp, 1 - c)
    xp = ((z * 2 + y) * 2 + (1 - x), c)
    yp = ((z * 2 + (1 - y)) * 2 + x, c)
    zs = [lax.rem(z + k, 4) for k in (1, 2, 3)]
    zp = [((zk * 2 + y) * 2 + x, c) for zk in zs]
    own = pl.multiple_of(c * OWN, OWN)
    oth = pl.multiple_of((1 - c) * OWN, OWN)
    chalf = pl.multiple_of(c * HALF, HALF)
    chid = pl.multiple_of(c * HID, HID)
    lead = (c == 0).astype(f32)

    barrier = pltpu.get_barrier_semaphore()
    for other in [peer, xp, yp] + zp:
        pl.semaphore_signal(barrier, inc=1, device_id=other, device_id_type=MESH_ID)

    loads = {}

    def load(name, src, dst):
        copy = pltpu.make_async_copy(src, dst, lsem.at[len(loads)])
        copy.start()
        loads[name] = copy

    load("tok", tokens.at[0], X.at[pl.ds(own, OWN)])
    load("sel", select, SEL.at[c])
    for i, v in enumerate(
        (b_query, b_value, b_out, b_down, ln1_gain, ln1_bias, ln2_gain, ln2_bias, w_router)
    ):
        load("v%d" % i, v, VEC.at[i, 0])
    for k in range(3):
        load(
            "wq%d" % k,
            w_qkv.at[:, pl.ds(pl.multiple_of(k * WIDTH + c * HALF, 128), HALF)],
            WQ.at[:, pl.ds(k * HALF, HALF)],
        )
    load("cot", cotangent.at[0], G.at[pl.ds(own, OWN)])
    load("bup", b_up, BUP.at[0])
    load("wo", w_out, WO)
    load("wu", w_up.at[:, pl.ds(chid, HID)], WU)
    load("wd", w_down.at[pl.ds(chid, HID)], WD)

    pl.semaphore_wait(barrier, 6)

    sends = []
    counts = {"e": 0, "c": 0}

    def to_core(src, dst):
        i = counts["e"]
        counts["e"] += 1
        copy = pltpu.make_async_remote_copy(
            src_ref=src, dst_ref=dst, send_sem=esem_s.at[i], recv_sem=esem_r.at[i],
            device_id=peer, device_id_type=MESH_ID,
        )
        copy.start()
        sends.append(copy)
        return copy

    ex_sel = to_core(select, SEL.at[c])
    ex_tok = to_core(tokens.at[0], X.at[pl.ds(own, OWN)])
    ex_cot = to_core(cotangent.at[0], G.at[pl.ds(own, OWN)])

    SB[...] = jnp.zeros_like(SB)

    def vec(i):
        return VEC[i]

    def project(start):
        @pl.loop(0, OWN // LT)
        def _(t):
            rows = pl.ds(pl.multiple_of(start + t * LT, 32), LT)
            xf = X[rows, :].astype(f32)
            unit, _ = row_stats(xf)
            NRM[rows, :] = (unit * vec(4) + vec(5)).astype(bf16)
            logit = jnp.sum(xf * vec(8), axis=-1, keepdims=True)
            GATE[rows, :] = 1.0 / (1.0 + jnp.exp(-logit))

        if start is own:
            for k in range(3):
                loads["wq%d" % k].wait()
        rows = pl.ds(start, OWN)
        nr = NRM[rows, :]
        for k in range(3):
            r = dot_nn(nr, WQ[:, k * HALF : (k + 1) * HALF])
            if k == 0:
                r = (r + VEC[0, :, pl.ds(chalf, HALF)]).astype(bf16).astype(f32) * HEAD_DIM ** (-0.5)
            if k == 2:
                r = r + VEC[1, :, pl.ds(chalf, HALF)]
            TRI[rows, k * HALF : (k + 1) * HALF] = r.astype(bf16)

    loads["tok"].wait()
    for i in range(9):
        loads["v%d" % i].wait()
    project(own)

    loads["sel"].wait()
    ex_sel.wait_recv()
    gv = jnp.full((1, 1), group[0], jnp.int32)
    long_col = jnp.broadcast_to(gv, (PAD_LEN, 1)) == 1
    pos_col = lax.broadcasted_iota(jnp.int32, (PAD_LEN, 1), 0)
    short_col = (pos_col >= SHORT_LEN).astype(jnp.int32) + (pos_col >= 2 * SHORT_LEN).astype(jnp.int32)
    place_col = jnp.where(long_col, 0, short_col)
    end_col = jnp.where(long_col, LONG_LEN, 3 * SHORT_LEN)
    sel_col = jnp.zeros((PAD_LEN, 8), f32)
    for part in range(2):
        bits = jnp.broadcast_to((SEL[part] > 0).astype(f32), (8, OWN)).astype(bf16)
        spread = (
            lax.broadcasted_iota(jnp.int32, (PAD_LEN, OWN), 0)
            == lax.broadcasted_iota(jnp.int32, (PAD_LEN, OWN), 1) + part * OWN
        ).astype(f32).astype(bf16)
        sel_col = sel_col + dot_nt(spread, bits)
    act_col = jnp.where(pos_col < end_col, sel_col[:, 0:1], 0.0)
    ACT[...] = act_col
    lane = lax.broadcasted_iota(jnp.int32, (1, 128), 1)
    same = jnp.bitwise_and(lane, HEAD_DIM - 1) == place_col
    QAUX[...] = jnp.where(same, 1.0, 0.0).astype(bf16)
    KAUX[...] = jnp.where(same & (act_col > 0.5), 0.0, -1e30).astype(bf16)
    length = jnp.where(jnp.broadcast_to(gv, (1, 1)) == 1, float(LONG_LEN), float(SHORT_LEN))
    for j in range(3):
        count = jnp.sum(jnp.where(place_col == j, act_col, 0.0), axis=0, keepdims=True)
        SB[13 + j : 14 + j, 0:128] = jnp.where(lane == dp, count / length * lead, 0.0)

    ex_tok.wait_recv()
    project(oth)

    low_lanes = lax.broadcasted_iota(jnp.int32, (1, 128), 1) < HEAD_DIM

    def head_part(v, side):
        keep = low_lanes if side == 0 else jnp.logical_not(low_lanes)
        return jnp.where(keep, v, jnp.zeros_like(v))

    def pair_lanes(hp):
        return [slice(k * HALF + hp * 128, k * HALF + hp * 128 + 128) for k in range(3)]

    def with_ones(v, side):
        return jnp.where(lane == (1 - side) * HEAD_DIM, jnp.ones_like(v), head_part(v, side))

    def scores(head):
        qlanes, klanes, _ = pair_lanes(head // 2)
        keep = low_lanes if head % 2 == 0 else jnp.logical_not(low_lanes)
        return dot_nt(
            jnp.where(keep, TRI[:, qlanes], QAUX[...]), jnp.where(keep, TRI[:, klanes], KAUX[...])
        )

    ex_mix, both = [], []
    ahead = scores(0)
    for head in range(2 * PAIRS):
        s = ahead
        if head + 1 < 2 * PAIRS:
            ahead = scores(head + 1)
        qlanes, _, vlanes = pair_lanes(head // 2)
        e = jnp.exp(s - jnp.max(s, axis=-1, keepdims=True)).astype(bf16)
        PR[head] = e
        both.append(dot_nn(e, with_ones(TRI[:, vlanes], head % 2)))
        if head % 2 == 1:
            scale = 1.0 / jnp.where(low_lanes, both[-2][:, HEAD_DIM : HEAD_DIM + 1], both[-1][:, 0:1])
            INV[:, qlanes] = scale
            MIX[c, :, qlanes] = (jnp.where(low_lanes, both[-2], both[-1]) * scale).astype(bf16)
            ex_mix.append(to_core(MIX.at[c, :, qlanes], MIX.at[c, :, qlanes]))

    loads["wo"].wait()

    @pl.loop(0, PAD_LEN // MT)
    def _(t):
        rows = pl.ds(pl.multiple_of(t * MT, MT), MT)
        SUM[rows, :] = X[rows, :].astype(f32) + (dot_nn(MIX[c, rows, :], WO[pl.ds(chalf, HALF), :]) + vec(2))

    loads["cot"].wait()
    ex_cot.wait_recv()

    @pl.loop(0, PAD_LEN // LT)
    def _(t):
        rows = pl.ds(pl.multiple_of(t * LT, LT), LT)
        GM[rows, :] = (ACT[rows, :] * GATE[rows, :] * G[rows, :].astype(f32)).astype(bf16)

    for e in ex_mix:
        e.wait_recv()

    @pl.loop(0, PAD_LEN // MT)
    def _(t):
        rows = pl.ds(pl.multiple_of(t * MT, MT), MT)
        s = SUM[rows, :] + dot_nn(MIX[1 - c, rows, :], WO[pl.ds(pl.multiple_of(HALF - chalf, HALF), HALF), :])
        SUM[rows, :] = s
        unit, _ = row_stats(s)
        SEC[rows, :] = (unit * vec(6) + vec(7)).astype(bf16)

    SECT[...] = jnp.swapaxes(SEC[...], 0, 1)

    for n in ("bup", "wu", "wd"):
        loads[n].wait()

    def remote(src, dst, dev, i):
        return pltpu.make_async_remote_copy(
            src_ref=src, dst_ref=dst, send_sem=csem_s.at[i], recv_sem=csem_r.at[i],
            device_id=dev, device_id_type=MESH_ID,
        )

    pieces = {}

    where = {"x": x, "y": y}

    class Piece:
        def __init__(self, name, buffers, dst_ref, only_z=None):
            self.order = PIECES[name][1]
            self.src, self.recv, self.fin = buffers[0], buffers[1:4], buffers[4]
            self.only_z = only_z
            self.cur = self.src
            self.number = len(pieces)
            self.copies = []
            self.keep = pltpu.make_async_copy(self.fin, dst_ref, fsem_l.at[self.number])
            self.give = pltpu.make_async_remote_copy(
                src_ref=self.fin, dst_ref=dst_ref, send_sem=fsem_s.at[self.number],
                recv_sem=fsem_r.at[self.number], device_id=peer, device_id_type=MESH_ID,
            )
            pieces[name] = self

        def send(self, k, part=None):
            axis, recv = self.order[k], self.recv[k]
            slot = self.base(k)
            if axis != "z":
                src, dst = self.cur.at[1 - where[axis]], recv
                if part is not None:
                    src, dst, slot = src.at[part], dst.at[part], slot + part
                cp = remote(src, dst, xp if axis == "x" else yp, slot)
                cp.start()
                sends.append(cp)
                self.copies.append(cp)
                return
            for kk in range(3):
                if self.only_z is None:
                    cp = remote(self.cur.at[zs[kk]], recv.at[kk], zp[kk], slot + kk)
                    cp.start()
                    sends.append(cp)
                else:
                    cp = remote(self.cur.at[0], recv.at[kk], zp[kk], slot + kk)
                    pl.when(zs[kk] == self.only_z)(cp.start)
                self.copies.append(cp)

        def base(self, k):
            return 7 * self.number + sum(3 if a == "z" else 2 for a in self.order[:k])

        def add(self, k):
            for cp in self.copies:
                cp.wait_recv()
            self.copies = self.copies if k == 2 else []
            axis, recv = self.order[k], self.recv[k]
            mine_at = z if axis == "z" else where[axis]
            if axis == "z" and self.only_z is not None:
                mine_at = 0
            for idx in product(*(range(n) for n in self.src.shape[k + 1 : 3])):
                mine = self.cur[(mine_at,) + idx]
                if axis == "z":
                    total = mine.astype(f32) + recv[(0,) + idx].astype(f32)
                    total = total + (recv[(1,) + idx].astype(f32) + recv[(2,) + idx].astype(f32))
                elif k == 2:
                    total = mine.astype(f32) + recv[idx].astype(f32)
                else:
                    total = mine + recv[idx]
                if k == 2:
                    self.fin[...] = total
                elif axis == "z":
                    recv[(0,) + idx] = total.astype(bf16)
                else:
                    recv[idx] = total
            self.cur = recv.at[0] if axis == "z" else recv

        def first(self, part=None):
            self.send(0, part)

        def second(self):
            self.add(0)
            self.send(1)

        def third(self):
            self.add(1)
            self.send(2)

        def fourth(self):
            def finish():
                self.add(2)
                self.keep.start()
                self.give.start()

            if self.only_z is None:
                finish()
            else:
                pl.when(z == self.only_z)(finish)

        def fifth(self):
            keep, give = self.keep, self.give
            if self.only_z is None:
                keep.wait()
                give.wait()
                return

            @pl.when(z == self.only_z)
            def _():
                keep.wait()
                give.wait_send()

            @pl.when(z == self.only_z + 2 - 4 * c)
            def _():
                give.wait_recv()

            for kk in range(3):
                pl.when(zs[kk] == self.only_z)(self.copies[kk].wait_send)

    for i, (name, (grad, _, first_col, width)) in enumerate(PIECES.items()):
        lanes_from = {"up": (o_up, chid), "ou": (o_out, chalf), "q": (o_qkv, chalf), "k": (o_qkv, chalf + WIDTH),
                      "v": (o_qkv, chalf + 2 * WIDTH), "dA": (o_down, 0), "dB": (o_down, HALF)}[grad[:2]]
        start_at = lanes_from[1] + first_col + (int(grad[2:]) * HALF if grad[:2] == "up" else 0)
        dst_ref = lanes_from[0].at[:, pl.ds(pl.multiple_of(start_at, 128), width)]
        Piece(name, piece_bufs[5 * i : 5 * i + 5], dst_ref, 2 * c + int(grad[2:]) if grad[0] == "d" else None)

    def keep_grad(grad, rows, value):
        for name, (g, _, first_col, width) in PIECES.items():
            if g == grad:
                src, order = pieces[name].src, pieces[name].order
                tile = src.shape[3]
                for i in range(HALF // tile):
                    if grad[0] == "d":
                        place = {"z": 0, "y": rows, "x": i}
                    else:
                        place = {"z": 2 * rows + i // 4, "y": i // 2 % 2, "x": i % 2}
                    src[tuple(place[axis] for axis in order)] = value[
                        tile * i : tile * (i + 1), first_col : first_col + width
                    ].astype(bf16)

    class Small:
        def first(self, part=None):
            self.got = self.send(0, SB.at[pl.ds(pl.multiple_of(8 - 8 * c, 8), 8)], peer)

        def send(self, slot, src, dev):
            copy = pltpu.make_async_remote_copy(
                src_ref=src, dst_ref=SBR.at[slot], send_sem=ssem_s.at[slot], recv_sem=ssem_r.at[slot],
                device_id=dev, device_id_type=MESH_ID,
            )
            copy.start()
            sends.append(copy)
            return [copy]

        def gather(self, mine, slots):
            for cp in self.got:
                cp.wait_recv()
            for slot in slots:
                mine = mine + SBR[slot]
            return mine

        def second(self):
            SBL[0] = self.gather(SB[pl.ds(pl.multiple_of(8 * c, 8), 8), :], (0,))
            self.got = self.send(1, SBL.at[0], xp)

        def third(self):
            SBL[1] = self.gather(SBL[0], (1,))
            self.got = self.send(2, SBL.at[1], yp)

        def fourth(self):
            SBL[2] = self.gather(SBL[1], (2,))
            self.got = []
            for k in range(3):
                self.got += self.send(3 + k, SBL.at[2], zp[k])

        def fifth(self):
            SBL[3] = self.gather(SBL[2], (3, 4, 5))
            rows = o_small.at[pl.ds(pl.multiple_of(8 * c, 8), 8)]
            self.keep = pltpu.make_async_copy(SBL.at[3], rows, lsem.at[N_LOADS + 2])
            self.give = pltpu.make_async_remote_copy(
                src_ref=SBL.at[3], dst_ref=rows, send_sem=ssem_s.at[6], recv_sem=ssem_r.at[6],
                device_id=peer, device_id_type=MESH_ID,
            )
            self.keep.start()
            self.give.start()

        def sixth(self):
            self.keep.wait()
            self.give.wait()

    pieces["small"] = Small()

    def at(point):
        for act, name in SCHEDULE.get(point, ()):
            p = pieces[name]
            if act == 0:
                p.first(part=0)
            elif act == 1:
                p.first(part=1 if name in HALVED else None)
            else:
                getattr(p, ("second", "third", "fourth", "fifth", "sixth")[act - 2])()

    for j in range(BLOCKS):
        cols = slice(j * HALF, (j + 1) * HALF)
        bj = BUP[:, pl.ds(pl.multiple_of(chid + j * HALF, 128), HALF)]

        @pl.loop(0, PAD_LEN // MT)
        def _(t):
            rows = pl.ds(pl.multiple_of(t * MT, MT), MT)
            pre = dot_nn(SEC[rows, :], WU[:, cols]) + bj
            gh = dot_nt(GM[rows, :], WD[cols, :])
            cdf = 0.5 * (1.0 + lax.erf(pre * (2.0 ** -0.5)))
            hid = (pre * cdf).astype(bf16)
            slope = cdf + pre * (0.3989422804014327 * jnp.exp(-0.5 * pre * pre))
            gp = (gh * slope).astype(bf16)
            HIDJ[rows, :] = hid
            GPJ[rows, :] = gp
            d = dot_nn(hid, WD[cols, :])
            s = dot_nt(gp, WU[:, cols])
            if j > 0:
                d = ACCD[rows, :] + d
                s = ACCS[rows, :] + s
            ACCD[rows, :] = d
            ACCS[rows, :] = s
            if j == BLOCKS - 1:
                GSB[rows, :] = s.astype(bf16)

        if j == BLOCKS - 1:
            ex_gs = to_core(GSB, GSR)

            @pl.loop(0, OWN // LT)
            def _(t):
                r = pl.ds(pl.multiple_of(t * LT, LT), LT)
                DSB[r, :] = ACCD[pl.ds(pl.multiple_of(oth + t * LT, 32), LT), :].astype(bf16)

            ex_ds = to_core(DSB, DSR)

        for part in range(2):
            g = dot_nn(SECT[part * HALF : (part + 1) * HALF, :], GPJ[...])
            keep_grad("up%d" % j, part, g)
        at("u%d" % j)
        SB[pl.ds(9 + 2 * c + j // 2, 1), (j % 2) * HALF : (j % 2 + 1) * HALF] = jnp.sum(
            GPJ[...].astype(f32), axis=0, keepdims=True
        )
        for part in range(2):
            g = dot_tn(HIDJ[...], GM[:, part * HALF : (part + 1) * HALF])
            keep_grad("d%s%d" % ("AB"[part], j // 2), j % 2, g)
        at("j%d" % j)

    ex_gs.wait_recv()

    zero_row = jnp.zeros((1, WIDTH), f32)

    def col_sum(v):
        return jnp.sum(v, axis=0, keepdims=True)

    def second_back(t, carry):
        rows = pl.ds(pl.multiple_of(t * LT, LT), LT)
        gs = ACCS[rows, :] + GSR[rows, :].astype(f32)
        unit, rstd = row_stats(SUM[rows, :])
        back = norm_back(unit, rstd, gs, vec(6))
        ACCS[rows, :] = back
        ga = (ACT[rows, :] * GATE[rows, :] * G[rows, :].astype(f32) + back).astype(bf16)
        GATT[rows, :] = ga
        return (
            carry[0] + col_sum(gs * unit), carry[1] + col_sum(gs), carry[2] + col_sum(ga.astype(f32)),
            carry[3] + col_sum(GM[rows, :].astype(f32)),
        )

    sums = lax.fori_loop(0, PAD_LEN // LT, second_back, (zero_row,) * 4)
    for row, value in zip((6, 7, 2, 3), sums):
        SB[row : row + 1, :] = value * lead
    at("sb")

    for part in range(2):
        g = dot_tn(MIX[part], GATT[:, pl.ds(chalf, HALF)])
        keep_grad("out", part, g)
    at("out")

    @pl.loop(0, PAD_LEN // MT)
    def _(t):
        rows = pl.ds(pl.multiple_of(t * MT, MT), MT)
        GMX[rows, :] = (dot_nt(GATT[rows, :], WO[pl.ds(chalf, HALF), :]) * INV[rows, :]).astype(bf16)

    at("gmx")

    for hp in range(PAIRS):
        qlanes, klanes, vlanes = pair_lanes(hp)
        kp = TRI[:, klanes]
        vp = TRI[:, vlanes]
        gp = GMX[:, qlanes]
        dots = gp.astype(f32) * MIX[c, :, qlanes].astype(f32)
        qt = jnp.swapaxes(TRI[:, qlanes], 0, 1)
        gt = jnp.swapaxes(gp, 0, 1)
        dq = jnp.zeros((PAD_LEN, 128), f32)
        for side in range(2):
            half = slice(side * HEAD_DIM, (side + 1) * HEAD_DIM)
            e = PR[2 * hp + side]
            dpr = dot_nt(head_part(gp, side), vp)
            delta = jnp.sum(head_part(dots, side), axis=-1, keepdims=True)
            ds = (e.astype(f32) * (dpr - delta)).astype(bf16)
            dq = dq + dot_nn(ds, head_part(kp, side))
            DKT[half, :] = dot_nn(qt[half, :], ds)
            DVT[half, :] = dot_nn(gt[half, :], e)
        DTR[:, qlanes] = (dq * HEAD_DIM ** (-0.5)).astype(bf16)
        DTR[:, klanes] = jnp.swapaxes(DKT[...], 0, 1).astype(bf16)
        DTR[:, vlanes] = jnp.swapaxes(DVT[...], 0, 1).astype(bf16)
        at("h%d" % hp)

    for k in range(3):
        blk = DTR[:, k * HALF : (k + 1) * HALF]
        if k != 1:
            SB[k // 2 : k // 2 + 1, pl.ds(chalf, HALF)] = col_sum(blk.astype(f32))
        for part in range(2):
            g = dot_tn(NRM[:, part * HALF : (part + 1) * HALF], blk)
            keep_grad("qkv"[k], part, g)
        at("qkv"[k])

    ex_ds.wait_send()
    DSB[...] = dot_nt(DTR[pl.ds(oth, OWN), :], WQ[...]).astype(bf16)
    ex_ns = to_core(DSB, NSR)
    at("ns")
    ex_ds.wait_recv()
    ex_gs.wait_send()
    ex_ns.wait_recv()
    OUTB, INB = GSB.at[0:OWN], GSB.at[OWN:PAD_LEN]

    def first_back(t, carry):
        r = pl.ds(pl.multiple_of(t * 80, 80), 80)
        rows = pl.ds(pl.multiple_of(own + t * 80, 80), 80)
        xf = X[rows, :].astype(f32)
        unit, rstd = row_stats(xf)
        gn = dot_nt(DTR[rows, :], WQ[...]) + NSR[r, :].astype(f32)
        first = norm_back(unit, rstd, gn, vec(4))
        gf = G[rows, :].astype(f32)
        gate = ACT[rows, :] * GATE[rows, :]
        branch = SUM[rows, :] - xf + ACCD[rows, :] + DSR[r, :].astype(f32) + vec(3)
        OUTB[r, :] = (xf + gate * branch).astype(bf16)
        gl = jnp.sum(gf * branch, axis=-1, keepdims=True) * (gate * (1.0 - GATE[rows, :]))
        INB[r, :] = (gf + ACCS[rows, :] + first + gl * vec(8)).astype(bf16)
        return (carry[0] + col_sum(gn * unit), carry[1] + col_sum(gn), carry[2] + col_sum(gl * xf))

    sums = lax.fori_loop(0, OWN // 80, first_back, (zero_row,) * 3)
    for row, value in zip((4, 5, 8), sums):
        SB[row : row + 1, :] = value
    keep_out = pltpu.make_async_copy(OUTB, o_output.at[0], lsem.at[len(loads)])
    keep_in = pltpu.make_async_copy(INB, o_input.at[0], lsem.at[len(loads) + 1])
    keep_out.start()
    keep_in.start()

    at("fb")
    at("end")
    for name, p in pieces.items():
        if name == "small":
            p.sixth()
        else:
            p.fifth()
    for cp in sends:
        if cp is not ex_ds and cp is not ex_gs:
            cp.wait_send()
    for cp in (keep_out, keep_in):
        cp.wait()


N_LOADS = 2 + 9 + 3 + 5
BIG = (0, 1, 2, 5, 7, 9)
SMALLS = (3, 4, 6, 10, 11, 12, 13, 14, 15)


def place_kernel(*refs):
    src, dst, bufs, (vec, up, share, sem) = refs[:7], refs[7:24], refs[24:31], refs[31:]
    dp = lax.axis_index("dp")
    ins = [pltpu.make_async_copy(src[i], bufs[i], sem.at[i]) for i in range(7)]
    outs = [pltpu.make_async_copy(bufs[i], dst[k], sem.at[7 + i]) for i, k in enumerate(BIG)]
    for i in (6, 0, 1, 2, 3, 4, 5):
        ins[i].start()
    ins[6].wait()
    rows = bufs[6][...]
    mine = pltpu.roll(rows, lax.rem(dp * (WIDTH - 48), WIDTH), 1)
    for i in range(9):
        vec[i] = mine[i : i + 1, :48]
    bufs[6][...] = pltpu.roll(rows, lax.rem(lax.rem(dp, 4) * (WIDTH - 192), WIDTH), 1)
    up[...] = bufs[6][pl.ds(9 + lax.div(dp, 4), 1), :192]
    share[...] = rows[13:16, :16]
    smalls = [pltpu.make_async_copy(vec.at[i], dst[k], sem.at[13 + i]) for i, k in enumerate(SMALLS)]
    smalls += [pltpu.make_async_copy(up, dst[8], sem.at[22]), pltpu.make_async_copy(share, dst[16], sem.at[23])]
    for cp in smalls:
        cp.start()
    for a, b in zip(ins, outs):
        a.wait()
        b.start()
    for cp in outs + smalls:
        cp.wait()


def fused(
    tokens, cotangent, group, select, w_qkv, b_query, b_value, w_out, b_out, w_up, b_up, w_down,
    b_down, ln1_gain, ln1_bias, ln2_gain, ln2_bias, w_router,
):
    args = (
        tokens, cotangent, group, select, w_qkv, b_query, b_value, w_out, b_out, w_up, b_up, w_down,
        b_down, ln1_gain, ln1_bias, ln2_gain, ln2_bias, w_router,
    )
    anywhere = pl.BlockSpec(memory_space=pl.ANY)
    shape = jax.ShapeDtypeStruct
    mids = (
        shape((1, OWN, WIDTH), bf16), shape((1, OWN, WIDTH), bf16), shape((48, 3 * WIDTH), f32),
        shape((48, WIDTH), f32), shape((48, HIDDEN), f32), shape((192, WIDTH), f32),
        shape((SMALL, WIDTH), f32),
    )
    v = pltpu.VMEM
    sq = (PAD_LEN, WIDTH)
    scratch = [
        v(sq, bf16), v(sq, bf16), v((2, 1, OWN), jnp.int32), v((9, 1, WIDTH), f32), v((1, HIDDEN), f32),
        v(sq, bf16), v((WIDTH, 3 * HALF), bf16), v((WIDTH, WIDTH), bf16), v((WIDTH, HID), bf16),
        v((HID, WIDTH), bf16), v((PAD_LEN, 3 * HALF), bf16), v((2 * PAIRS, PAD_LEN, PAD_LEN), bf16),
        v((2, PAD_LEN, HALF), bf16), v(sq, f32), v(sq, bf16), v(sq, bf16), v((PAD_LEN, 128), bf16), v((PAD_LEN, 128), bf16),
        v((PAD_LEN, 1), f32), v((PAD_LEN, 1), f32),
        v((PAD_LEN, HALF), bf16), v((PAD_LEN, HALF), bf16), v(sq, f32), v(sq, f32), v(sq, bf16), v(sq, bf16),
        v((OWN, WIDTH), bf16), v((OWN, WIDTH), bf16), v(sq, bf16), v((PAD_LEN, HALF), bf16),
        v((PAD_LEN, 3 * HALF), bf16), v((128, PAD_LEN), f32), v((128, PAD_LEN), f32),
        v((PAD_LEN, HALF), f32), v((WIDTH, PAD_LEN), bf16), v((OWN, WIDTH), bf16),
        v((SMALL, WIDTH), f32), v((4, 8, WIDTH), f32), v((6, 8, WIDTH), f32),
    ] + [v(*b) for name in PIECES for b in piece_shapes(name)] + [
        pltpu.SemaphoreType.DMA((N_LOADS + 4,)),
        pltpu.SemaphoreType.DMA((9,)), pltpu.SemaphoreType.DMA((9,)),
        pltpu.SemaphoreType.DMA((7 * len(PIECES),)), pltpu.SemaphoreType.DMA((7 * len(PIECES),)),
        pltpu.SemaphoreType.DMA((7,)), pltpu.SemaphoreType.DMA((7,)),
        pltpu.SemaphoreType.DMA((len(PIECES),)), pltpu.SemaphoreType.DMA((len(PIECES),)), pltpu.SemaphoreType.DMA((len(PIECES),)),
    ]
    mid = pl.pallas_call(
        layer_kernel,
        out_shape=mids,
        in_specs=[anywhere, anywhere, pl.BlockSpec(memory_space=pltpu.SMEM)] + [anywhere] * 15,
        out_specs=[anywhere] * 7,
        scratch_shapes=scratch,
        compiler_params=pltpu.CompilerParams(
            collective_id=0, has_side_effects=True, vmem_limit_bytes=60 << 20
        ),
        name="layer",
    )(*args)
    outs = (
        mids[0], mids[1], mids[2], shape((1, 48), f32), shape((1, 48), f32), mids[3], shape((1, 48), f32),
        mids[4], shape((1, 192), f32), mids[5],
    ) + (shape((1, 48), f32),) * 6 + (shape((3, 16), f32),)
    out = pl.pallas_call(
        place_kernel,
        out_shape=outs,
        in_specs=[anywhere] * 7,
        out_specs=[anywhere] * 17,
        scratch_shapes=[v(m.shape, m.dtype) for m in mids]
        + [v((9, 1, 48), f32), v((1, 192), f32), v((3, 16), f32), pltpu.SemaphoreType.DMA((24,))],
        name="place",
    )(*mid)
    return tuple(o.reshape(-1) if o.shape[0] == 1 and o.ndim == 2 else o for o in out[:16]) + (out[16].T,)


def norm_rows(values, norm_gain, norm_shift):
    average = jnp.mean(values, axis=-1, keepdims=True)
    centred = values - average
    variance = jnp.mean(centred * centred, axis=-1, keepdims=True)
    return centred * lax.rsqrt(variance + epsilon) * norm_gain + norm_shift


def places_of(group, slot_pos):
    short_place = jnp.minimum(slot_pos // SHORT_LEN, 2)
    return jnp.where(group[:, None] == 1, 0, short_place[None, :])


def split_heads(flat_rows):
    return flat_rows.reshape(flat_rows.shape[0], flat_rows.shape[1], HEADS, HEAD_DIM)


def masked_scores(queries, key_heads, query_place, key_place, key_mask):
    score_scale = HEAD_DIM ** (-0.5)
    scores = (
        jnp.einsum("bqhe,bkhe->bqhk", queries, key_heads, preferred_element_type=jnp.float32)
        * score_scale
    )
    key_live = (key_mask.astype(jnp.float32)[:, None, None, :] > 0.5) & (
        query_place[:, :, None, None] == key_place[:, None, None, :]
    )
    return (jnp.where(key_live, scores, masked_floor), key_live.astype(jnp.float32))


def attend(queries, key_heads, value_heads, query_place, key_place, key_mask):
    masked, key_weight = masked_scores(queries, key_heads, query_place, key_place, key_mask)
    row_max = jnp.max(masked, axis=-1, keepdims=True)
    exponent = jnp.exp(masked - row_max) * key_weight
    row_sum = jnp.sum(exponent, axis=-1, keepdims=True)
    weights = (exponent / row_sum).astype(jnp.bfloat16)
    mixed_heads = jnp.einsum(
        "bqhk,bkhe->bqhe", weights, value_heads, preferred_element_type=jnp.float32
    )
    return (mixed_heads, row_max + jnp.log(row_sum))


def back_parts(
    queries, key_heads, value_heads, query_place, key_place, key_mask, log_total, grad_heads, delta
):
    masked, key_weight = masked_scores(queries, key_heads, query_place, key_place, key_mask)
    key_probs = jnp.exp(masked - log_total) * key_weight
    grad_probs = jnp.einsum(
        "bqhe,bkhe->bqhk", grad_heads, value_heads, preferred_element_type=jnp.float32
    )
    delta = jnp.sum(key_probs * grad_probs, axis=-1, keepdims=True)
    grad_scores = (key_probs * (grad_probs - delta)).astype(jnp.bfloat16)
    return (key_probs, grad_scores, delta)


def key_side_grads(key_probs, grad_scores, queries, grad_heads):
    score_scale = HEAD_DIM ** (-0.5)
    grad_values = jnp.einsum(
        "bqhk,bqhe->bkhe",
        key_probs.astype(jnp.bfloat16),
        grad_heads,
        preferred_element_type=jnp.float32,
    )
    grad_keys = (
        jnp.einsum("bqhk,bqhe->bkhe", grad_scores, queries, preferred_element_type=jnp.float32)
        * score_scale
    )
    return (grad_keys, grad_values)


def on_device(
    tokens,
    cotangent,
    group,
    select,
    w_qkv,
    b_query,
    b_value,
    w_out,
    b_out,
    w_up,
    b_up,
    w_down,
    b_down,
    ln1_gain,
    ln1_bias,
    ln2_gain,
    ln2_bias,
    w_router,
):
    packs, per_piece, features = tokens.shape
    row_count = packs * per_piece
    first_pos = lax.axis_index("seq") * per_piece
    positions = first_pos + jnp.arange(per_piece, dtype=jnp.int32)
    full_positions = jnp.arange(PAD_LEN, dtype=jnp.int32)
    place_own = places_of(group, positions)
    place_full = places_of(group, full_positions)
    ends = jnp.where(group == 1, LONG_LEN, 3 * SHORT_LEN).astype(jnp.int32)
    active = ((select > 0) & (positions[None, :] < ends[:, None])).astype(jnp.float32)
    active_rows = active.reshape(row_count, 1)
    xfloat = tokens.reshape(row_count, features).astype(jnp.float32)
    router = jax.nn.sigmoid(jnp.dot(xfloat, w_router, precision=lax.Precision.HIGHEST))
    normed, first_back = jax.vjp(norm_rows, xfloat, ln1_gain, ln1_bias)
    normed_low = normed.astype(jnp.bfloat16)
    qkv_bias = jnp.concatenate([b_query, jnp.zeros_like(b_query), b_value])
    triple = (jnp.dot(normed_low, w_qkv, preferred_element_type=jnp.float32) + qkv_bias).astype(
        jnp.bfloat16
    )
    queries = triple[:, :features].reshape(packs, per_piece, HEADS, HEAD_DIM)
    keys_own = triple[:, features : 2 * features].reshape(packs, per_piece, features)
    values_own = triple[:, 2 * features :].reshape(packs, per_piece, features)
    mask_own = active.astype(jnp.bfloat16)
    keys_all, values_all, mask_all = (
        lax.all_gather(keys_own, "seq", axis=1, tiled=True),
        lax.all_gather(values_own, "seq", axis=1, tiled=True),
        lax.all_gather(mask_own, "seq", axis=1, tiled=True),
    )
    mixed_heads, log_total = attend(
        queries, split_heads(keys_all), split_heads(values_all), place_own, place_full, mask_all
    )
    mixed_low = mixed_heads.reshape(row_count, features).astype(jnp.bfloat16)
    attended = jnp.dot(mixed_low, w_out, preferred_element_type=jnp.float32) + b_out
    summed = xfloat + attended
    second, second_back = jax.vjp(norm_rows, summed, ln2_gain, ln2_bias)
    second_low = second.astype(jnp.bfloat16)
    pre_act = jnp.dot(second_low, w_up, preferred_element_type=jnp.float32) + b_up
    gelu_out, gelu_back = jax.vjp(partial(jax.nn.gelu, approximate=False), pre_act)
    hidden_low = gelu_out.astype(jnp.bfloat16)
    branch = attended + (jnp.dot(hidden_low, w_down, preferred_element_type=jnp.float32) + b_down)
    gate_rows = active_rows * router[:, None]
    output = (xfloat + gate_rows * branch).astype(jnp.bfloat16).reshape(packs, per_piece, features)
    place_range = jnp.arange(3, dtype=jnp.int32)
    onehot = (place_full[:, :, None] == place_range[None, None, :]).astype(jnp.float32)
    counts = jnp.sum(mask_all.astype(jnp.float32)[:, :, None] * onehot, axis=1)
    image_lengths = jnp.where(group == 1, LONG_LEN, SHORT_LEN).astype(jnp.float32)
    fractions = lax.all_gather(counts / image_lengths[:, None], "dp", axis=0, tiled=True)
    grad_rows = cotangent.reshape(row_count, features).astype(jnp.float32)
    grad_logit = jnp.sum(grad_rows * branch, axis=1) * active_rows[:, 0] * router * (1.0 - router)
    grad_branch = gate_rows * grad_rows
    grad_mlp = grad_branch.astype(jnp.bfloat16)
    grad_down = jnp.einsum("rk,rd->kd", hidden_low, grad_mlp, preferred_element_type=jnp.float32)
    grad_down_bias = jnp.sum(grad_mlp.astype(jnp.float32), axis=0)
    grad_hidden = jnp.einsum("rd,kd->rk", grad_mlp, w_down, preferred_element_type=jnp.float32)
    grad_pre = gelu_back(grad_hidden)[0].astype(jnp.bfloat16)
    grad_up = jnp.einsum("rd,rk->dk", second_low, grad_pre, preferred_element_type=jnp.float32)
    grad_up_bias = jnp.sum(grad_pre.astype(jnp.float32), axis=0)
    grad_second = jnp.einsum("rk,dk->rd", grad_pre, w_up, preferred_element_type=jnp.float32)
    grad_summed, grad_ln2_gain, grad_ln2_bias = second_back(grad_second)
    grad_attended = (grad_branch + grad_summed).astype(jnp.bfloat16)
    grad_out = jnp.einsum("rd,re->de", mixed_low, grad_attended, preferred_element_type=jnp.float32)
    grad_out_bias = jnp.sum(grad_attended.astype(jnp.float32), axis=0)
    grad_mixed = jnp.einsum("re,de->rd", grad_attended, w_out, preferred_element_type=jnp.float32)
    grad_heads = grad_mixed.astype(jnp.bfloat16).reshape(packs, per_piece, HEADS, HEAD_DIM)
    back_k, back_v, back_m = (
        lax.all_gather(keys_own, "seq", axis=1, tiled=True),
        lax.all_gather(values_own, "seq", axis=1, tiled=True),
        lax.all_gather(mask_own, "seq", axis=1, tiled=True),
    )
    back_kh = split_heads(back_k)
    back_vh = split_heads(back_v)
    key_probs, grad_scores, delta = back_parts(
        queries, back_kh, back_vh, place_own, place_full, back_m, log_total, grad_heads, None
    )
    grad_queries = jnp.einsum(
        "bqhk,bkhe->bqhe", grad_scores, back_kh, preferred_element_type=jnp.float32
    ) * HEAD_DIM ** (-0.5)
    grad_keys, grad_values = key_side_grads(key_probs, grad_scores, queries, grad_heads)
    keys_grad_own, values_grad_own = (
        lax.psum_scatter(
            grad_keys.reshape(back_k.shape).astype(jnp.bfloat16),
            "seq",
            scatter_dimension=1,
            tiled=True,
        ).astype(jnp.float32),
        lax.psum_scatter(
            grad_values.reshape(back_v.shape).astype(jnp.bfloat16),
            "seq",
            scatter_dimension=1,
            tiled=True,
        ).astype(jnp.float32),
    )
    grad_triple = jnp.concatenate(
        [
            grad_queries.reshape(row_count, features),
            keys_grad_own.reshape(row_count, features),
            values_grad_own.reshape(row_count, features),
        ],
        axis=1,
    ).astype(jnp.bfloat16)
    grad_qkv = jnp.einsum("rd,rk->dk", normed_low, grad_triple, preferred_element_type=jnp.float32)
    column_sums = jnp.sum(grad_triple.astype(jnp.float32), axis=0)
    grad_query_bias = column_sums[:features]
    grad_value_bias = column_sums[2 * features :]
    grad_normed = jnp.einsum("rk,dk->rd", grad_triple, w_qkv, preferred_element_type=jnp.float32)
    grad_first, grad_ln1_gain, grad_ln1_bias = first_back(grad_normed)
    grad_router = jnp.dot(grad_logit, xfloat, precision=lax.Precision.HIGHEST)
    grad_input = grad_rows + grad_summed + grad_first + grad_logit[:, None] * w_router[None, :]
    input_grad = grad_input.astype(jnp.bfloat16).reshape(packs, per_piece, features)
    (
        share_qkv,
        share_query_bias,
        share_value_bias,
        share_out,
        share_out_bias,
        share_up,
        share_up_bias,
        share_down,
        share_down_bias,
        share_ln1_gain,
        share_ln1_bias,
        share_ln2_gain,
        share_ln2_bias,
        share_router,
    ) = (
        lax.psum_scatter(
            grad_qkv.astype(jnp.bfloat16), "dp", scatter_dimension=0, tiled=True
        ).astype(jnp.float32),
        lax.psum_scatter(
            grad_query_bias.astype(jnp.bfloat16), "dp", scatter_dimension=0, tiled=True
        ).astype(jnp.float32),
        lax.psum_scatter(
            grad_value_bias.astype(jnp.bfloat16), "dp", scatter_dimension=0, tiled=True
        ).astype(jnp.float32),
        lax.psum_scatter(
            grad_out.astype(jnp.bfloat16), "dp", scatter_dimension=0, tiled=True
        ).astype(jnp.float32),
        lax.psum_scatter(
            grad_out_bias.astype(jnp.bfloat16), "dp", scatter_dimension=0, tiled=True
        ).astype(jnp.float32),
        lax.psum_scatter(
            grad_up.astype(jnp.bfloat16), "dp", scatter_dimension=0, tiled=True
        ).astype(jnp.float32),
        lax.psum_scatter(
            grad_up_bias.astype(jnp.bfloat16), "dp", scatter_dimension=0, tiled=True
        ).astype(jnp.float32),
        lax.psum_scatter(
            grad_down.astype(jnp.bfloat16), "dp", scatter_dimension=0, tiled=True
        ).astype(jnp.float32),
        lax.psum_scatter(
            grad_down_bias.astype(jnp.bfloat16), "dp", scatter_dimension=0, tiled=True
        ).astype(jnp.float32),
        lax.psum_scatter(
            grad_ln1_gain.astype(jnp.bfloat16), "dp", scatter_dimension=0, tiled=True
        ).astype(jnp.float32),
        lax.psum_scatter(
            grad_ln1_bias.astype(jnp.bfloat16), "dp", scatter_dimension=0, tiled=True
        ).astype(jnp.float32),
        lax.psum_scatter(
            grad_ln2_gain.astype(jnp.bfloat16), "dp", scatter_dimension=0, tiled=True
        ).astype(jnp.float32),
        lax.psum_scatter(
            grad_ln2_bias.astype(jnp.bfloat16), "dp", scatter_dimension=0, tiled=True
        ).astype(jnp.float32),
        lax.psum_scatter(
            grad_router.astype(jnp.bfloat16), "dp", scatter_dimension=0, tiled=True
        ).astype(jnp.float32),
    )
    totals = (
        lax.psum(share_qkv.astype(jnp.bfloat16), "seq").astype(jnp.float32),
        lax.psum(share_query_bias.astype(jnp.bfloat16), "seq").astype(jnp.float32),
        lax.psum(share_value_bias.astype(jnp.bfloat16), "seq").astype(jnp.float32),
        lax.psum(share_out.astype(jnp.bfloat16), "seq").astype(jnp.float32),
        lax.psum(share_out_bias.astype(jnp.bfloat16), "seq").astype(jnp.float32),
        lax.psum(share_up.astype(jnp.bfloat16), "seq").astype(jnp.float32),
        lax.psum(share_up_bias.astype(jnp.bfloat16), "seq").astype(jnp.float32),
        lax.psum(share_down.astype(jnp.bfloat16), "seq").astype(jnp.float32),
        lax.psum(share_down_bias.astype(jnp.bfloat16), "seq").astype(jnp.float32),
        lax.psum(share_ln1_gain.astype(jnp.bfloat16), "seq").astype(jnp.float32),
        lax.psum(share_ln1_bias.astype(jnp.bfloat16), "seq").astype(jnp.float32),
        lax.psum(share_ln2_gain.astype(jnp.bfloat16), "seq").astype(jnp.float32),
        lax.psum(share_ln2_bias.astype(jnp.bfloat16), "seq").astype(jnp.float32),
        lax.psum(share_router.astype(jnp.bfloat16), "seq").astype(jnp.float32),
    )
    return (
        output,
        input_grad,
        totals[0],
        totals[1],
        totals[2],
        totals[3],
        totals[4],
        totals[5],
        totals[6],
        totals[7],
        totals[8],
        totals[9],
        totals[10],
        totals[11],
        totals[12],
        totals[13],
        fractions,
    )


def solution(mesh):
    in_specs = (
        P("dp", "seq", None),
        P("dp", "seq", None),
        P("dp"),
        P("dp", "seq"),
        P(),
        P(),
        P(),
        P(),
        P(),
        P(),
        P(),
        P(),
        P(),
        P(),
        P(),
        P(),
        P(),
        P(),
    )
    out_specs = (
        P("dp", "seq", None),
        P("dp", "seq", None),
        P("dp", None),
        P("dp"),
        P("dp"),
        P("dp", None),
        P("dp"),
        P("dp", None),
        P("dp"),
        P("dp", None),
        P("dp"),
        P("dp"),
        P("dp"),
        P("dp"),
        P("dp"),
        P("dp"),
        P(),
    )
    fast = mesh.shape["dp"] == 16 and mesh.shape["seq"] == 2
    return jax.shard_map(
        fused if fast else on_device, mesh=mesh, in_specs=in_specs, out_specs=out_specs, check_vma=False
    )
```

```python
from functools import partial
from itertools import product

import jax
import jax.numpy as jnp
from jax import lax
from jax.experimental import pallas as pl
from jax.experimental.pallas import tpu as pltpu
from jax.sharding import PartitionSpec as P

HEADS = 12
HEAD_DIM = 64
PAD_LEN = 640
LONG_LEN = 577
SHORT_LEN = 197
WIDTH = 768
HIDDEN = 3072

epsilon = 1e-06
masked_floor = -1000000000.0
MESH_ID = pl.DeviceIdType.MESH
bf16 = jnp.bfloat16
f32 = jnp.float32

HALF = WIDTH // 2
OWN = PAD_LEN // 2
HID = HIDDEN // 2
BLOCKS = HID // HALF
PAIRS = HALF // 128
MT = 640
AT = 640
LT = 320
SMALL = 16
PIECES = {
    "up0_0": ("up0", "lxyh", 0, 128),
    "up0_1": ("up0", "xzy", 128, 128),
    "up0_2": ("up0", "zyx", 256, 128),
    "up1_0": ("up1", "lxyh", 0, 128),
    "up1_1": ("up1", "zxy", 128, 256),
    "up2": ("up2", "yzx", 0, 384),
    "up3": ("up3", "zyx", 0, 384),
    "dA0": ("dA0", "yxlh", 0, 384),
    "dB0": ("dB0", "xylh", 0, 384),
    "dA1": ("dA1", "xylh", 0, 384),
    "dB1": ("dB1", "xylh", 0, 384),
    "out_0": ("out", "xylh", 0, 128),
    "out_1": ("out", "yzx", 128, 256),
    "q_0": ("q", "xylh", 0, 128),
    "q_1": ("q", "xyz", 128, 256),
    "k_0": ("k", "xyz", 0, 128),
    "k_1": ("k", "yxlh", 128, 256),
    "v_0": ("v", "xyz", 0, 128),
    "v_1": ("v", "xylh", 128, 128),
    "v_2": ("v", "yxlh", 256, 128),
}
HALVED = ("dB0", "dA1", "dB1")
SCHEDULE = {
    "u0": (
        (1, "up0_2"), (1, "up0_0"),
    ),
    "j0": (
        (0, "dB0"),
    ),
    "u1": (
        (1, "up1_1"), (1, "up0_1"),
    ),
    "j1": (
        (1, "dA0"), (1, "dB0"),
    ),
    "j2": (
        (0, "dA1"), (0, "dB1"), (2, "up0_1"), (1, "up1_0"), (1, "up2"),
    ),
    "u3": (
        (1, "up3"), (2, "dB0"),
    ),
    "j3": (
        (1, "dA1"),
    ),
    "out": (
        (1, "out_1"), (1, "dB1"),
    ),
    "gmx": (
        (1, "out_0"), (2, "up1_0"), (2, "up0_0"), (2, "up2"),
    ),
    "h0": (
        (2, "dA1"),
    ),
    "h1": (
        (3, "dB0"), (2, "dA0"), (2, "dB1"), (2, "out_1"),
    ),
    "q": (
        (1, "q_0"), (3, "up0_0"), (3, "dA1"), (1, "q_1"), (2, "out_0"),
    ),
    "k": (
        (1, "k_1"), (3, "dA0"),
    ),
    "v": (
        (3, "dB1"), (3, "up0_1"), (1, "v_1"), (1, "k_0"), (4, "dB0"), (4, "up0_0"), (2, "q_0"), (1, "v_2"),
    ),
    "fb": (
        (1, "small"), (3, "out_0"), (4, "dA1"), (2, "q_1"), (2, "k_1"), (4, "dB1"), (3, "q_0"), (2, "v_1"),
        (4, "up0_1"), (4, "dA0"), (2, "small"), (5, "up0_0"), (3, "up1_0"), (2, "v_2"), (2, "k_0"), (1, "v_0"),
        (4, "out_0"), (3, "out_1"), (3, "q_1"), (3, "small"), (2, "up3"),
    ),
    "end": (
        (3, "v_1"), (3, "k_1"), (4, "up1_0"), (3, "up2"), (4, "q_0"), (3, "k_0"), (2, "up0_2"), (3, "v_2"),
        (2, "up1_1"), (4, "small"), (2, "v_0"), (5, "dA0"), (5, "dB1"), (3, "up3"), (4, "v_1"), (4, "out_1"),
        (4, "k_1"), (3, "up0_2"), (3, "up1_1"), (5, "dA1"), (5, "up1_0"), (3, "v_0"), (4, "up2"), (5, "dB0"),
        (4, "v_2"), (5, "q_0"), (4, "q_1"), (4, "k_0"), (5, "out_0"), (4, "up3"), (5, "small"), (4, "up0_2"),
        (5, "v_1"), (4, "up1_1"), (5, "k_1"), (4, "v_0"), (5, "v_2"),
    ),
}


def dot_nn(a, b):
    return lax.dot_general(a, b, (((1,), (0,)), ((), ())), preferred_element_type=f32)


def dot_nt(a, b):
    return lax.dot_general(a, b, (((1,), (1,)), ((), ())), preferred_element_type=f32)


def dot_tn(a, b):
    return lax.dot_general(a, b, (((0,), (0,)), ((), ())), preferred_element_type=f32)


def row_stats(values):
    average = jnp.mean(values, axis=-1, keepdims=True)
    centred = values - average
    variance = jnp.mean(centred * centred, axis=-1, keepdims=True)
    rstd = lax.rsqrt(variance + epsilon)
    return centred * rstd, rstd


def norm_back(unit, rstd, grad, gain):
    q = grad * gain
    return rstd * (
        q - jnp.mean(q, axis=-1, keepdims=True) - unit * jnp.mean(q * unit, axis=-1, keepdims=True)
    )


def piece_shapes(name):
    grad, order, _, width = PIECES[name]
    left = [1 if grad[0] == "d" and axis in "lh" else 4 if axis == "z" else 2 for axis in order]
    tile = [192 if grad[0] == "d" else 48, width]
    shapes = [(left + tile, bf16)]
    for k, axis in enumerate(order):
        shapes.append(([3] * (axis == "z") + left[k + 1 :] + tile, bf16))
    return shapes + [(tile, f32)]


def layer_kernel(*refs):
    (tokens, cotangent, group, select, w_qkv, b_query, b_value, w_out, b_out, w_up, b_up, w_down,
     b_down, ln1_gain, ln1_bias, ln2_gain, ln2_bias, w_router) = refs[:18]
    o_output, o_input, o_qkv, o_out, o_up, o_down, o_small = refs[18:25]
    (X, G, SEL, VEC, BUP, NRM, WQ, WO, WU, WD, TRI, PR, MIX, SUM, SEC, GM, QAUX, KAUX, GATE, ACT,
     HIDJ, GPJ, ACCD, ACCS, GSB, GSR, DSB, DSR, GATT, GMX, DTR, DKT, DVT, INV, SECT, NSR, SB, SBL, SBR) = refs[25:64]
    n_bufs = sum(len(p[1]) + 2 for p in PIECES.values())
    piece_bufs = refs[64 : 64 + n_bufs]
    (lsem, esem_s, esem_r, csem_s, csem_r, ssem_s, ssem_r, fsem_l, fsem_s, fsem_r) = refs[64 + n_bufs :]
    dp = lax.axis_index("dp")
    c = lax.axis_index("seq")
    x = lax.rem(dp, 2)
    y = lax.rem(lax.div(dp, 2), 2)
    z = lax.div(dp, 4)
    peer = (dp, 1 - c)
    xp = ((z * 2 + y) * 2 + (1 - x), c)
    yp = ((z * 2 + (1 - y)) * 2 + x, c)
    zs = [lax.rem(z + k, 4) for k in (1, 2, 3)]
    zp = [((zk * 2 + y) * 2 + x, c) for zk in zs]
    own = pl.multiple_of(c * OWN, OWN)
    oth = pl.multiple_of((1 - c) * OWN, OWN)
    chalf = pl.multiple_of(c * HALF, HALF)
    chid = pl.multiple_of(c * HID, HID)
    lead = (c == 0).astype(f32)

    barrier = pltpu.get_barrier_semaphore()
    for other in [peer, xp, yp] + zp:
        pl.semaphore_signal(barrier, inc=1, device_id=other, device_id_type=MESH_ID)

    loads = {}

    def load(name, src, dst):
        copy = pltpu.make_async_copy(src, dst, lsem.at[len(loads)])
        copy.start()
        loads[name] = copy

    load("tok", tokens.at[0], X.at[pl.ds(own, OWN)])
    load("sel", select, SEL.at[c])
    for i, v in enumerate(
        (b_query, b_value, b_out, b_down, ln1_gain, ln1_bias, ln2_gain, ln2_bias, w_router)
    ):
        load("v%d" % i, v, VEC.at[i, 0])
    for k in range(3):
        load(
            "wq%d" % k,
            w_qkv.at[:, pl.ds(pl.multiple_of(k * WIDTH + c * HALF, 128), HALF)],
            WQ.at[:, pl.ds(k * HALF, HALF)],
        )
    load("cot", cotangent.at[0], G.at[pl.ds(own, OWN)])

    pl.semaphore_wait(barrier, 6)

    sends = []
    counts = {"e": 0, "c": 0}

    def to_core(src, dst):
        i = counts["e"]
        counts["e"] += 1
        copy = pltpu.make_async_remote_copy(
            src_ref=src, dst_ref=dst, send_sem=esem_s.at[i], recv_sem=esem_r.at[i],
            device_id=peer, device_id_type=MESH_ID,
        )
        copy.start()
        sends.append(copy)
        return copy

    ex_sel = to_core(select, SEL.at[c])
    ex_tok = to_core(tokens.at[0], X.at[pl.ds(own, OWN)])
    ex_cot = to_core(cotangent.at[0], G.at[pl.ds(own, OWN)])
    load("bup", b_up, BUP.at[0])
    load("wo", w_out, WO)
    load("wu", w_up.at[:, pl.ds(chid, HID)], WU)
    load("wd", w_down.at[pl.ds(chid, HID)], WD)

    SB[...] = jnp.zeros_like(SB)

    def vec(i):
        return VEC[i]

    def project(start):
        @pl.loop(0, OWN // LT)
        def _(t):
            rows = pl.ds(pl.multiple_of(start + t * LT, 32), LT)
            xf = X[rows, :].astype(f32)
            unit, _ = row_stats(xf)
            NRM[rows, :] = (unit * vec(4) + vec(5)).astype(bf16)
            logit = jnp.sum(xf * vec(8), axis=-1, keepdims=True)
            GATE[rows, :] = 1.0 / (1.0 + jnp.exp(-logit))

        if start is own:
            for k in range(3):
                loads["wq%d" % k].wait()
        rows = pl.ds(start, OWN)
        nr = NRM[rows, :]
        for k in range(3):
            r = dot_nn(nr, WQ[:, k * HALF : (k + 1) * HALF])
            if k == 0:
                r = (r + VEC[0, :, pl.ds(chalf, HALF)]).astype(bf16).astype(f32) * HEAD_DIM ** (-0.5)
            if k == 2:
                r = r + VEC[1, :, pl.ds(chalf, HALF)]
            TRI[rows, k * HALF : (k + 1) * HALF] = r.astype(bf16)

    loads["tok"].wait()
    for i in range(9):
        loads["v%d" % i].wait()
    project(own)

    loads["sel"].wait()
    ex_sel.wait_recv()
    gv = jnp.full((1, 1), group[0], jnp.int32)
    long_col = jnp.broadcast_to(gv, (PAD_LEN, 1)) == 1
    pos_col = lax.broadcasted_iota(jnp.int32, (PAD_LEN, 1), 0)
    short_col = (pos_col >= SHORT_LEN).astype(jnp.int32) + (pos_col >= 2 * SHORT_LEN).astype(jnp.int32)
    place_col = jnp.where(long_col, 0, short_col)
    end_col = jnp.where(long_col, LONG_LEN, 3 * SHORT_LEN)
    sel_col = jnp.zeros((PAD_LEN, 8), f32)
    for part in range(2):
        bits = jnp.broadcast_to((SEL[part] > 0).astype(f32), (8, OWN)).astype(bf16)
        spread = (
            lax.broadcasted_iota(jnp.int32, (PAD_LEN, OWN), 0)
            == lax.broadcasted_iota(jnp.int32, (PAD_LEN, OWN), 1) + part * OWN
        ).astype(f32).astype(bf16)
        sel_col = sel_col + dot_nt(spread, bits)
    act_col = jnp.where(pos_col < end_col, sel_col[:, 0:1], 0.0)
    ACT[...] = act_col
    lane = lax.broadcasted_iota(jnp.int32, (1, 128), 1)
    same = jnp.bitwise_and(lane, HEAD_DIM - 1) == place_col
    QAUX[...] = jnp.where(same, 1.0, 0.0).astype(bf16)
    KAUX[...] = jnp.where(same & (act_col > 0.5), 0.0, -1e30).astype(bf16)
    length = jnp.where(jnp.broadcast_to(gv, (1, 1)) == 1, float(LONG_LEN), float(SHORT_LEN))
    for j in range(3):
        count = jnp.sum(jnp.where(place_col == j, act_col, 0.0), axis=0, keepdims=True)
        SB[13 + j : 14 + j, 0:128] = jnp.where(lane == dp, count / length * lead, 0.0)

    ex_tok.wait_recv()
    project(oth)

    low_lanes = lax.broadcasted_iota(jnp.int32, (1, 128), 1) < HEAD_DIM

    def head_part(v, side):
        keep = low_lanes if side == 0 else jnp.logical_not(low_lanes)
        return jnp.where(keep, v, jnp.zeros_like(v))

    def pair_lanes(hp):
        return [slice(k * HALF + hp * 128, k * HALF + hp * 128 + 128) for k in range(3)]

    def with_ones(v, side):
        return jnp.where(lane == (1 - side) * HEAD_DIM, jnp.ones_like(v), head_part(v, side))

    def scores(head):
        qlanes, klanes, _ = pair_lanes(head // 2)
        keep = low_lanes if head % 2 == 0 else jnp.logical_not(low_lanes)
        return dot_nt(
            jnp.where(keep, TRI[:, qlanes], QAUX[...]), jnp.where(keep, TRI[:, klanes], KAUX[...])
        )

    ex_mix, both = [], []
    ahead = scores(0)
    for head in range(2 * PAIRS):
        s = ahead
        if head + 1 < 2 * PAIRS:
            ahead = scores(head + 1)
        qlanes, _, vlanes = pair_lanes(head // 2)
        e = jnp.exp(s - jnp.max(s, axis=-1, keepdims=True)).astype(bf16)
        PR[head] = e
        both.append(dot_nn(e, with_ones(TRI[:, vlanes], head % 2)))
        if head % 2 == 1:
            scale = 1.0 / jnp.where(low_lanes, both[-2][:, HEAD_DIM : HEAD_DIM + 1], both[-1][:, 0:1])
            INV[:, qlanes] = scale
            MIX[c, :, qlanes] = (jnp.where(low_lanes, both[-2], both[-1]) * scale).astype(bf16)
            ex_mix.append(to_core(MIX.at[c, :, qlanes], MIX.at[c, :, qlanes]))

    loads["wo"].wait()

    @pl.loop(0, PAD_LEN // MT)
    def _(t):
        rows = pl.ds(pl.multiple_of(t * MT, MT), MT)
        SUM[rows, :] = X[rows, :].astype(f32) + (dot_nn(MIX[c, rows, :], WO[pl.ds(chalf, HALF), :]) + vec(2))

    loads["cot"].wait()
    ex_cot.wait_recv()

    @pl.loop(0, PAD_LEN // LT)
    def _(t):
        rows = pl.ds(pl.multiple_of(t * LT, LT), LT)
        GM[rows, :] = (ACT[rows, :] * GATE[rows, :] * G[rows, :].astype(f32)).astype(bf16)

    for e in ex_mix:
        e.wait_recv()

    @pl.loop(0, PAD_LEN // MT)
    def _(t):
        rows = pl.ds(pl.multiple_of(t * MT, MT), MT)
        s = SUM[rows, :] + dot_nn(MIX[1 - c, rows, :], WO[pl.ds(pl.multiple_of(HALF - chalf, HALF), HALF), :])
        SUM[rows, :] = s
        unit, _ = row_stats(s)
        SEC[rows, :] = (unit * vec(6) + vec(7)).astype(bf16)

    SECT[...] = jnp.swapaxes(SEC[...], 0, 1)

    for n in ("bup", "wu", "wd"):
        loads[n].wait()

    def remote(src, dst, dev, i):
        return pltpu.make_async_remote_copy(
            src_ref=src, dst_ref=dst, send_sem=csem_s.at[i], recv_sem=csem_r.at[i],
            device_id=dev, device_id_type=MESH_ID,
        )

    pieces = {}

    zl, zh = lax.rem(z, 2), lax.div(z, 2)
    lp = (((z + 1 - 2 * zl) * 2 + y) * 2 + x, c)
    where = {"x": x, "y": y, "l": zl, "h": zh}
    partner = {"x": xp, "y": yp, "l": lp, "h": zp[1]}

    class Piece:
        def __init__(self, name, buffers, dst_ref, only_z=None):
            self.order = PIECES[name][1]
            self.src, self.recv, self.fin = buffers[0], buffers[1:-1], buffers[-1]
            self.only_z = only_z
            self.cur = self.src
            self.number = len(pieces)
            self.copies = []
            self.keep = pltpu.make_async_copy(self.fin, dst_ref, fsem_l.at[self.number])
            self.give = pltpu.make_async_remote_copy(
                src_ref=self.fin, dst_ref=dst_ref, send_sem=fsem_s.at[self.number],
                recv_sem=fsem_r.at[self.number], device_id=peer, device_id_type=MESH_ID,
            )
            pieces[name] = self

        def send(self, k, part=None):
            axis, recv = self.order[k], self.recv[k]
            slot = 12 * self.number + 3 * k
            self.copies = self.copies if k == 0 else []
            if axis == "z":
                for kk in range(3):
                    self.begin(self.cur.at[zs[kk]], recv.at[kk], zp[kk], slot + kk)
            elif part is not None:
                self.begin(self.cur.at[1 - where[axis], part], recv.at[part], partner[axis], slot + part)
            else:
                self.begin(self.cur.at[1 - where[axis]], recv, partner[axis], slot)

        def begin(self, src, dst, dev, slot):
            cp = remote(src, dst, dev, slot)
            cp.start()
            sends.append(cp)
            self.copies.append(cp)

        def add(self, k):
            for cp in self.copies:
                cp.wait_recv()
            axis, recv = self.order[k], self.recv[k]
            last = k == len(self.order) - 1
            mine_at = z if axis == "z" else where[axis]
            if axis in "lh" and self.only_z is not None:
                mine_at = 0
            for idx in product(*(range(n) for n in self.src.shape[k + 1 : -2])):
                mine = self.cur[(mine_at,) + idx]
                if axis == "z":
                    total = mine.astype(f32) + recv[(0,) + idx].astype(f32)
                    total = total + (recv[(1,) + idx].astype(f32) + recv[(2,) + idx].astype(f32))
                elif last:
                    total = mine.astype(f32) + recv[idx].astype(f32)
                else:
                    total = mine + recv[idx]
                if last:
                    self.fin[...] = total
                elif axis == "z":
                    recv[(0,) + idx] = total.astype(bf16)
                else:
                    recv[idx] = total
            self.cur = recv.at[0] if axis == "z" else recv

        def step(self, act, part=None):
            k = act - 1
            if act <= 1:
                self.send(0, part)
            elif k < len(self.order):
                if self.only_z is None or k < 2:
                    self.add(k - 1)
                    self.send(k)
                elif k == 2:
                    self.add(1)
                    self.copies = [remote(self.cur.at[0], self.recv[2], lp, 12 * self.number + 6)]
                    self.copy_l = self.copies[0]
                    pl.when(zl != self.down_l)(self.copy_l.start)
                else:
                    self.copy_h = remote(self.recv[2].at[0], self.recv[3], zp[1], 12 * self.number + 9)

                    @pl.when(zl == self.down_l)
                    def _():
                        self.add(2)
                        pl.when(zh != c)(self.copy_h.start)

                    self.cur = self.recv[2]
                    self.copies = [self.copy_h]
            else:

                def finish():
                    self.add(len(self.order) - 1)
                    self.keep.start()
                    self.give.start()

                if self.only_z is None:
                    finish()
                else:
                    pl.when(z == self.only_z)(finish)

        def end(self):
            keep, give = self.keep, self.give
            if self.only_z is None:
                keep.wait()
                give.wait()
                return

            @pl.when(z == self.only_z)
            def _():
                keep.wait()
                give.wait_send()

            pl.when(z == self.only_z + 2 - 4 * c)(give.wait_recv)
            pl.when(zl != self.down_l)(self.copy_l.wait_send)

            @pl.when(zl == self.down_l)
            def _():
                pl.when(zh != c)(self.copy_h.wait_send)

    for i, (name, (grad, _, first_col, width)) in enumerate(PIECES.items()):
        lanes_from = {"up": (o_up, chid), "ou": (o_out, chalf), "q": (o_qkv, chalf), "k": (o_qkv, chalf + WIDTH),
                      "v": (o_qkv, chalf + 2 * WIDTH), "dA": (o_down, 0), "dB": (o_down, HALF)}[grad[:2]]
        start_at = lanes_from[1] + first_col + (int(grad[2:]) * HALF if grad[:2] == "up" else 0)
        dst_ref = lanes_from[0].at[:, pl.ds(pl.multiple_of(start_at, 128), width)]
        n_bufs = len(PIECES[name][1]) + 2
        p = Piece(name, piece_bufs[:n_bufs], dst_ref, 2 * c + int(grad[2:]) if grad[0] == "d" else None)
        p.down_l = int(grad[2:]) if grad[0] == "d" else None
        piece_bufs = piece_bufs[n_bufs:]

    def keep_grad(grad, rows, value):
        for name, (g, _, first_col, width) in PIECES.items():
            if g == grad:
                src, order = pieces[name].src, pieces[name].order
                tile = src.shape[-2]
                for i in range(HALF // tile):
                    if grad[0] == "d":
                        place = {"l": 0, "h": 0, "y": rows, "x": i}
                    else:
                        place = {"z": 2 * rows + i // 4, "h": rows, "l": i // 4, "y": i // 2 % 2, "x": i % 2}
                    src[tuple(place[axis] for axis in order)] = value[
                        tile * i : tile * (i + 1), first_col : first_col + width
                    ].astype(bf16)

    class Small:
        def step(self, act, part=None):
            (self.first, self.second, self.third, self.fourth, self.fifth)[act - 1]()

        def first(self):
            self.got = self.send(0, SB.at[pl.ds(pl.multiple_of(8 - 8 * c, 8), 8)], peer)

        def send(self, slot, src, dev):
            copy = pltpu.make_async_remote_copy(
                src_ref=src, dst_ref=SBR.at[slot], send_sem=ssem_s.at[slot], recv_sem=ssem_r.at[slot],
                device_id=dev, device_id_type=MESH_ID,
            )
            copy.start()
            sends.append(copy)
            return [copy]

        def gather(self, mine, slots):
            for cp in self.got:
                cp.wait_recv()
            for slot in slots:
                mine = mine + SBR[slot]
            return mine

        def second(self):
            SBL[0] = self.gather(SB[pl.ds(pl.multiple_of(8 * c, 8), 8), :], (0,))
            self.got = self.send(1, SBL.at[0], xp)

        def third(self):
            SBL[1] = self.gather(SBL[0], (1,))
            self.got = self.send(2, SBL.at[1], yp)

        def fourth(self):
            SBL[2] = self.gather(SBL[1], (2,))
            self.got = []
            for k in range(3):
                self.got += self.send(3 + k, SBL.at[2], zp[k])

        def fifth(self):
            SBL[3] = self.gather(SBL[2], (3, 4, 5))
            rows = o_small.at[pl.ds(pl.multiple_of(8 * c, 8), 8)]
            self.keep = pltpu.make_async_copy(SBL.at[3], rows, lsem.at[N_LOADS + 2])
            self.give = pltpu.make_async_remote_copy(
                src_ref=SBL.at[3], dst_ref=rows, send_sem=ssem_s.at[6], recv_sem=ssem_r.at[6],
                device_id=peer, device_id_type=MESH_ID,
            )
            self.keep.start()
            self.give.start()

        def end(self):
            self.keep.wait()
            self.give.wait()

    pieces["small"] = Small()

    def at(point):
        for act, name in SCHEDULE.get(point, ()):
            p = pieces[name]
            p.step(act, None if act > 1 or name not in HALVED else act)

    for j in range(BLOCKS):
        cols = slice(j * HALF, (j + 1) * HALF)
        bj = BUP[:, pl.ds(pl.multiple_of(chid + j * HALF, 128), HALF)]

        @pl.loop(0, PAD_LEN // MT)
        def _(t):
            rows = pl.ds(pl.multiple_of(t * MT, MT), MT)
            pre = dot_nn(SEC[rows, :], WU[:, cols]) + bj
            gh = dot_nt(GM[rows, :], WD[cols, :])
            cdf = 0.5 * (1.0 + lax.erf(pre * (2.0 ** -0.5)))
            hid = (pre * cdf).astype(bf16)
            slope = cdf + pre * (0.3989422804014327 * jnp.exp(-0.5 * pre * pre))
            gp = (gh * slope).astype(bf16)
            HIDJ[rows, :] = hid
            GPJ[rows, :] = gp
            d = dot_nn(hid, WD[cols, :])
            s = dot_nt(gp, WU[:, cols])
            if j > 0:
                d = ACCD[rows, :] + d
                s = ACCS[rows, :] + s
            ACCD[rows, :] = d
            ACCS[rows, :] = s
            if j == BLOCKS - 1:
                GSB[rows, :] = s.astype(bf16)

        if j == BLOCKS - 1:
            ex_gs = to_core(GSB, GSR)

            @pl.loop(0, OWN // LT)
            def _(t):
                r = pl.ds(pl.multiple_of(t * LT, LT), LT)
                DSB[r, :] = ACCD[pl.ds(pl.multiple_of(oth + t * LT, 32), LT), :].astype(bf16)

            ex_ds = to_core(DSB, DSR)

        for part in range(2):
            g = dot_nn(SECT[part * HALF : (part + 1) * HALF, :], GPJ[...])
            keep_grad("up%d" % j, part, g)
        at("u%d" % j)
        SB[pl.ds(9 + 2 * c + j // 2, 1), (j % 2) * HALF : (j % 2 + 1) * HALF] = jnp.sum(
            GPJ[...].astype(f32), axis=0, keepdims=True
        )
        for part in range(2):
            g = dot_tn(HIDJ[...], GM[:, part * HALF : (part + 1) * HALF])
            keep_grad("d%s%d" % ("AB"[part], j // 2), j % 2, g)
        at("j%d" % j)

    ex_gs.wait_recv()

    zero_row = jnp.zeros((1, WIDTH), f32)

    def col_sum(v):
        return jnp.sum(v, axis=0, keepdims=True)

    def second_back(t, carry):
        rows = pl.ds(pl.multiple_of(t * LT, LT), LT)
        gs = ACCS[rows, :] + GSR[rows, :].astype(f32)
        unit, rstd = row_stats(SUM[rows, :])
        back = norm_back(unit, rstd, gs, vec(6))
        ACCS[rows, :] = back
        ga = (ACT[rows, :] * GATE[rows, :] * G[rows, :].astype(f32) + back).astype(bf16)
        GATT[rows, :] = ga
        return (
            carry[0] + col_sum(gs * unit), carry[1] + col_sum(gs), carry[2] + col_sum(ga.astype(f32)),
            carry[3] + col_sum(GM[rows, :].astype(f32)),
        )

    sums = lax.fori_loop(0, PAD_LEN // LT, second_back, (zero_row,) * 4)
    for row, value in zip((6, 7, 2, 3), sums):
        SB[row : row + 1, :] = value * lead
    at("sb")

    for part in range(2):
        g = dot_tn(MIX[part], GATT[:, pl.ds(chalf, HALF)])
        keep_grad("out", part, g)
    at("out")

    @pl.loop(0, PAD_LEN // MT)
    def _(t):
        rows = pl.ds(pl.multiple_of(t * MT, MT), MT)
        GMX[rows, :] = (dot_nt(GATT[rows, :], WO[pl.ds(chalf, HALF), :]) * INV[rows, :]).astype(bf16)

    at("gmx")

    for hp in range(PAIRS):
        qlanes, klanes, vlanes = pair_lanes(hp)
        kp = TRI[:, klanes]
        vp = TRI[:, vlanes]
        gp = GMX[:, qlanes]
        dots = gp.astype(f32) * MIX[c, :, qlanes].astype(f32)
        qt = jnp.swapaxes(TRI[:, qlanes], 0, 1)
        gt = jnp.swapaxes(gp, 0, 1)
        dq = jnp.zeros((PAD_LEN, 128), f32)
        for side in range(2):
            half = slice(side * HEAD_DIM, (side + 1) * HEAD_DIM)
            e = PR[2 * hp + side]
            dpr = dot_nt(head_part(gp, side), vp)
            delta = jnp.sum(head_part(dots, side), axis=-1, keepdims=True)
            ds = (e.astype(f32) * (dpr - delta)).astype(bf16)
            dq = dq + dot_nn(ds, head_part(kp, side))
            DKT[half, :] = dot_nn(qt[half, :], ds)
            DVT[half, :] = dot_nn(gt[half, :], e)
        DTR[:, qlanes] = (dq * HEAD_DIM ** (-0.5)).astype(bf16)
        DTR[:, klanes] = jnp.swapaxes(DKT[...], 0, 1).astype(bf16)
        DTR[:, vlanes] = jnp.swapaxes(DVT[...], 0, 1).astype(bf16)
        at("h%d" % hp)

    for k in range(3):
        blk = DTR[:, k * HALF : (k + 1) * HALF]
        if k != 1:
            SB[k // 2 : k // 2 + 1, pl.ds(chalf, HALF)] = col_sum(blk.astype(f32))
        for part in range(2):
            g = dot_tn(NRM[:, part * HALF : (part + 1) * HALF], blk)
            keep_grad("qkv"[k], part, g)
        at("qkv"[k])

    ex_ds.wait_send()
    DSB[...] = dot_nt(DTR[pl.ds(oth, OWN), :], WQ[...]).astype(bf16)
    ex_ns = to_core(DSB, NSR)
    at("ns")
    ex_ds.wait_recv()
    ex_gs.wait_send()
    ex_ns.wait_recv()
    OUTB, INB = GSB.at[0:OWN], GSB.at[OWN:PAD_LEN]

    def first_back(t, carry):
        r = pl.ds(pl.multiple_of(t * 80, 80), 80)
        rows = pl.ds(pl.multiple_of(own + t * 80, 80), 80)
        xf = X[rows, :].astype(f32)
        unit, rstd = row_stats(xf)
        gn = dot_nt(DTR[rows, :], WQ[...]) + NSR[r, :].astype(f32)
        first = norm_back(unit, rstd, gn, vec(4))
        gf = G[rows, :].astype(f32)
        gate = ACT[rows, :] * GATE[rows, :]
        branch = SUM[rows, :] - xf + ACCD[rows, :] + DSR[r, :].astype(f32) + vec(3)
        OUTB[r, :] = (xf + gate * branch).astype(bf16)
        gl = jnp.sum(gf * branch, axis=-1, keepdims=True) * (gate * (1.0 - GATE[rows, :]))
        INB[r, :] = (gf + ACCS[rows, :] + first + gl * vec(8)).astype(bf16)
        return (carry[0] + col_sum(gn * unit), carry[1] + col_sum(gn), carry[2] + col_sum(gl * xf))

    sums = lax.fori_loop(0, OWN // 80, first_back, (zero_row,) * 3)
    for row, value in zip((4, 5, 8), sums):
        SB[row : row + 1, :] = value
    keep_out = pltpu.make_async_copy(OUTB, o_output.at[0], lsem.at[len(loads)])
    keep_in = pltpu.make_async_copy(INB, o_input.at[0], lsem.at[len(loads) + 1])
    keep_out.start()
    keep_in.start()

    at("fb")
    at("end")
    for p in pieces.values():
        p.end()
    for cp in sends:
        if cp is not ex_ds and cp is not ex_gs:
            cp.wait_send()
    for cp in (keep_out, keep_in):
        cp.wait()


N_LOADS = 2 + 9 + 3 + 5
BIG = (0, 1, 2, 5, 7, 9)
SMALLS = (3, 4, 6, 10, 11, 12, 13, 14, 15)


def place_kernel(*refs):
    src, dst, bufs, (vec, up, share, sem) = refs[:7], refs[7:24], refs[24:31], refs[31:]
    dp = lax.axis_index("dp")
    ins = [pltpu.make_async_copy(src[i], bufs[i], sem.at[i]) for i in range(7)]
    outs = [pltpu.make_async_copy(bufs[i], dst[k], sem.at[7 + i]) for i, k in enumerate(BIG)]
    for i in (6, 0, 1, 2, 3, 4, 5):
        ins[i].start()
    ins[6].wait()
    rows = bufs[6][...]
    mine = pltpu.roll(rows, lax.rem(dp * (WIDTH - 48), WIDTH), 1)
    for i in range(9):
        vec[i] = mine[i : i + 1, :48]
    bufs[6][...] = pltpu.roll(rows, lax.rem(lax.rem(dp, 4) * (WIDTH - 192), WIDTH), 1)
    up[...] = bufs[6][pl.ds(9 + lax.div(dp, 4), 1), :192]
    share[...] = rows[13:16, :16]
    smalls = [pltpu.make_async_copy(vec.at[i], dst[k], sem.at[13 + i]) for i, k in enumerate(SMALLS)]
    smalls += [pltpu.make_async_copy(up, dst[8], sem.at[22]), pltpu.make_async_copy(share, dst[16], sem.at[23])]
    for cp in smalls:
        cp.start()
    for a, b in zip(ins, outs):
        a.wait()
        b.start()
    for cp in outs + smalls:
        cp.wait()


def fused(
    tokens, cotangent, group, select, w_qkv, b_query, b_value, w_out, b_out, w_up, b_up, w_down,
    b_down, ln1_gain, ln1_bias, ln2_gain, ln2_bias, w_router,
):
    args = (
        tokens, cotangent, group, select, w_qkv, b_query, b_value, w_out, b_out, w_up, b_up, w_down,
        b_down, ln1_gain, ln1_bias, ln2_gain, ln2_bias, w_router,
    )
    anywhere = pl.BlockSpec(memory_space=pl.ANY)
    shape = jax.ShapeDtypeStruct
    mids = (
        shape((1, OWN, WIDTH), bf16), shape((1, OWN, WIDTH), bf16), shape((48, 3 * WIDTH), f32),
        shape((48, WIDTH), f32), shape((48, HIDDEN), f32), shape((192, WIDTH), f32),
        shape((SMALL, WIDTH), f32),
    )
    v = pltpu.VMEM
    sq = (PAD_LEN, WIDTH)
    scratch = [
        v(sq, bf16), v(sq, bf16), v((2, 1, OWN), jnp.int32), v((9, 1, WIDTH), f32), v((1, HIDDEN), f32),
        v(sq, bf16), v((WIDTH, 3 * HALF), bf16), v((WIDTH, WIDTH), bf16), v((WIDTH, HID), bf16),
        v((HID, WIDTH), bf16), v((PAD_LEN, 3 * HALF), bf16), v((2 * PAIRS, PAD_LEN, PAD_LEN), bf16),
        v((2, PAD_LEN, HALF), bf16), v(sq, f32), v(sq, bf16), v(sq, bf16), v((PAD_LEN, 128), bf16), v((PAD_LEN, 128), bf16),
        v((PAD_LEN, 1), f32), v((PAD_LEN, 1), f32),
        v((PAD_LEN, HALF), bf16), v((PAD_LEN, HALF), bf16), v(sq, f32), v(sq, f32), v(sq, bf16), v(sq, bf16),
        v((OWN, WIDTH), bf16), v((OWN, WIDTH), bf16), v(sq, bf16), v((PAD_LEN, HALF), bf16),
        v((PAD_LEN, 3 * HALF), bf16), v((128, PAD_LEN), f32), v((128, PAD_LEN), f32),
        v((PAD_LEN, HALF), f32), v((WIDTH, PAD_LEN), bf16), v((OWN, WIDTH), bf16),
        v((SMALL, WIDTH), f32), v((4, 8, WIDTH), f32), v((6, 8, WIDTH), f32),
    ] + [v(*b) for name in PIECES for b in piece_shapes(name)] + [
        pltpu.SemaphoreType.DMA((N_LOADS + 4,)),
        pltpu.SemaphoreType.DMA((9,)), pltpu.SemaphoreType.DMA((9,)),
        pltpu.SemaphoreType.DMA((12 * len(PIECES),)), pltpu.SemaphoreType.DMA((12 * len(PIECES),)),
        pltpu.SemaphoreType.DMA((7,)), pltpu.SemaphoreType.DMA((7,)),
        pltpu.SemaphoreType.DMA((len(PIECES),)), pltpu.SemaphoreType.DMA((len(PIECES),)), pltpu.SemaphoreType.DMA((len(PIECES),)),
    ]
    mid = pl.pallas_call(
        layer_kernel,
        out_shape=mids,
        in_specs=[anywhere, anywhere, pl.BlockSpec(memory_space=pltpu.SMEM)] + [anywhere] * 15,
        out_specs=[anywhere] * 7,
        scratch_shapes=scratch,
        compiler_params=pltpu.CompilerParams(
            collective_id=0, has_side_effects=True, vmem_limit_bytes=60 << 20
        ),
        name="layer",
    )(*args)
    outs = (
        mids[0], mids[1], mids[2], shape((1, 48), f32), shape((1, 48), f32), mids[3], shape((1, 48), f32),
        mids[4], shape((1, 192), f32), mids[5],
    ) + (shape((1, 48), f32),) * 6 + (shape((3, 16), f32),)
    out = pl.pallas_call(
        place_kernel,
        out_shape=outs,
        in_specs=[anywhere] * 7,
        out_specs=[anywhere] * 17,
        scratch_shapes=[v(m.shape, m.dtype) for m in mids]
        + [v((9, 1, 48), f32), v((1, 192), f32), v((3, 16), f32), pltpu.SemaphoreType.DMA((24,))],
        name="place",
    )(*mid)
    return tuple(o.reshape(-1) if o.shape[0] == 1 and o.ndim == 2 else o for o in out[:16]) + (out[16].T,)


def norm_rows(values, norm_gain, norm_shift):
    average = jnp.mean(values, axis=-1, keepdims=True)
    centred = values - average
    variance = jnp.mean(centred * centred, axis=-1, keepdims=True)
    return centred * lax.rsqrt(variance + epsilon) * norm_gain + norm_shift


def places_of(group, slot_pos):
    short_place = jnp.minimum(slot_pos // SHORT_LEN, 2)
    return jnp.where(group[:, None] == 1, 0, short_place[None, :])


def split_heads(flat_rows):
    return flat_rows.reshape(flat_rows.shape[0], flat_rows.shape[1], HEADS, HEAD_DIM)


def masked_scores(queries, key_heads, query_place, key_place, key_mask):
    score_scale = HEAD_DIM ** (-0.5)
    scores = (
        jnp.einsum("bqhe,bkhe->bqhk", queries, key_heads, preferred_element_type=jnp.float32)
        * score_scale
    )
    key_live = (key_mask.astype(jnp.float32)[:, None, None, :] > 0.5) & (
        query_place[:, :, None, None] == key_place[:, None, None, :]
    )
    return (jnp.where(key_live, scores, masked_floor), key_live.astype(jnp.float32))


def attend(queries, key_heads, value_heads, query_place, key_place, key_mask):
    masked, key_weight = masked_scores(queries, key_heads, query_place, key_place, key_mask)
    row_max = jnp.max(masked, axis=-1, keepdims=True)
    exponent = jnp.exp(masked - row_max) * key_weight
    row_sum = jnp.sum(exponent, axis=-1, keepdims=True)
    weights = (exponent / row_sum).astype(jnp.bfloat16)
    mixed_heads = jnp.einsum(
        "bqhk,bkhe->bqhe", weights, value_heads, preferred_element_type=jnp.float32
    )
    return (mixed_heads, row_max + jnp.log(row_sum))


def back_parts(
    queries, key_heads, value_heads, query_place, key_place, key_mask, log_total, grad_heads, delta
):
    masked, key_weight = masked_scores(queries, key_heads, query_place, key_place, key_mask)
    key_probs = jnp.exp(masked - log_total) * key_weight
    grad_probs = jnp.einsum(
        "bqhe,bkhe->bqhk", grad_heads, value_heads, preferred_element_type=jnp.float32
    )
    delta = jnp.sum(key_probs * grad_probs, axis=-1, keepdims=True)
    grad_scores = (key_probs * (grad_probs - delta)).astype(jnp.bfloat16)
    return (key_probs, grad_scores, delta)


def key_side_grads(key_probs, grad_scores, queries, grad_heads):
    score_scale = HEAD_DIM ** (-0.5)
    grad_values = jnp.einsum(
        "bqhk,bqhe->bkhe",
        key_probs.astype(jnp.bfloat16),
        grad_heads,
        preferred_element_type=jnp.float32,
    )
    grad_keys = (
        jnp.einsum("bqhk,bqhe->bkhe", grad_scores, queries, preferred_element_type=jnp.float32)
        * score_scale
    )
    return (grad_keys, grad_values)


def on_device(
    tokens,
    cotangent,
    group,
    select,
    w_qkv,
    b_query,
    b_value,
    w_out,
    b_out,
    w_up,
    b_up,
    w_down,
    b_down,
    ln1_gain,
    ln1_bias,
    ln2_gain,
    ln2_bias,
    w_router,
):
    packs, per_piece, features = tokens.shape
    row_count = packs * per_piece
    first_pos = lax.axis_index("seq") * per_piece
    positions = first_pos + jnp.arange(per_piece, dtype=jnp.int32)
    full_positions = jnp.arange(PAD_LEN, dtype=jnp.int32)
    place_own = places_of(group, positions)
    place_full = places_of(group, full_positions)
    ends = jnp.where(group == 1, LONG_LEN, 3 * SHORT_LEN).astype(jnp.int32)
    active = ((select > 0) & (positions[None, :] < ends[:, None])).astype(jnp.float32)
    active_rows = active.reshape(row_count, 1)
    xfloat = tokens.reshape(row_count, features).astype(jnp.float32)
    router = jax.nn.sigmoid(jnp.dot(xfloat, w_router, precision=lax.Precision.HIGHEST))
    normed, first_back = jax.vjp(norm_rows, xfloat, ln1_gain, ln1_bias)
    normed_low = normed.astype(jnp.bfloat16)
    qkv_bias = jnp.concatenate([b_query, jnp.zeros_like(b_query), b_value])
    triple = (jnp.dot(normed_low, w_qkv, preferred_element_type=jnp.float32) + qkv_bias).astype(
        jnp.bfloat16
    )
    queries = triple[:, :features].reshape(packs, per_piece, HEADS, HEAD_DIM)
    keys_own = triple[:, features : 2 * features].reshape(packs, per_piece, features)
    values_own = triple[:, 2 * features :].reshape(packs, per_piece, features)
    mask_own = active.astype(jnp.bfloat16)
    keys_all, values_all, mask_all = (
        lax.all_gather(keys_own, "seq", axis=1, tiled=True),
        lax.all_gather(values_own, "seq", axis=1, tiled=True),
        lax.all_gather(mask_own, "seq", axis=1, tiled=True),
    )
    mixed_heads, log_total = attend(
        queries, split_heads(keys_all), split_heads(values_all), place_own, place_full, mask_all
    )
    mixed_low = mixed_heads.reshape(row_count, features).astype(jnp.bfloat16)
    attended = jnp.dot(mixed_low, w_out, preferred_element_type=jnp.float32) + b_out
    summed = xfloat + attended
    second, second_back = jax.vjp(norm_rows, summed, ln2_gain, ln2_bias)
    second_low = second.astype(jnp.bfloat16)
    pre_act = jnp.dot(second_low, w_up, preferred_element_type=jnp.float32) + b_up
    gelu_out, gelu_back = jax.vjp(partial(jax.nn.gelu, approximate=False), pre_act)
    hidden_low = gelu_out.astype(jnp.bfloat16)
    branch = attended + (jnp.dot(hidden_low, w_down, preferred_element_type=jnp.float32) + b_down)
    gate_rows = active_rows * router[:, None]
    output = (xfloat + gate_rows * branch).astype(jnp.bfloat16).reshape(packs, per_piece, features)
    place_range = jnp.arange(3, dtype=jnp.int32)
    onehot = (place_full[:, :, None] == place_range[None, None, :]).astype(jnp.float32)
    counts = jnp.sum(mask_all.astype(jnp.float32)[:, :, None] * onehot, axis=1)
    image_lengths = jnp.where(group == 1, LONG_LEN, SHORT_LEN).astype(jnp.float32)
    fractions = lax.all_gather(counts / image_lengths[:, None], "dp", axis=0, tiled=True)
    grad_rows = cotangent.reshape(row_count, features).astype(jnp.float32)
    grad_logit = jnp.sum(grad_rows * branch, axis=1) * active_rows[:, 0] * router * (1.0 - router)
    grad_branch = gate_rows * grad_rows
    grad_mlp = grad_branch.astype(jnp.bfloat16)
    grad_down = jnp.einsum("rk,rd->kd", hidden_low, grad_mlp, preferred_element_type=jnp.float32)
    grad_down_bias = jnp.sum(grad_mlp.astype(jnp.float32), axis=0)
    grad_hidden = jnp.einsum("rd,kd->rk", grad_mlp, w_down, preferred_element_type=jnp.float32)
    grad_pre = gelu_back(grad_hidden)[0].astype(jnp.bfloat16)
    grad_up = jnp.einsum("rd,rk->dk", second_low, grad_pre, preferred_element_type=jnp.float32)
    grad_up_bias = jnp.sum(grad_pre.astype(jnp.float32), axis=0)
    grad_second = jnp.einsum("rk,dk->rd", grad_pre, w_up, preferred_element_type=jnp.float32)
    grad_summed, grad_ln2_gain, grad_ln2_bias = second_back(grad_second)
    grad_attended = (grad_branch + grad_summed).astype(jnp.bfloat16)
    grad_out = jnp.einsum("rd,re->de", mixed_low, grad_attended, preferred_element_type=jnp.float32)
    grad_out_bias = jnp.sum(grad_attended.astype(jnp.float32), axis=0)
    grad_mixed = jnp.einsum("re,de->rd", grad_attended, w_out, preferred_element_type=jnp.float32)
    grad_heads = grad_mixed.astype(jnp.bfloat16).reshape(packs, per_piece, HEADS, HEAD_DIM)
    back_k, back_v, back_m = (
        lax.all_gather(keys_own, "seq", axis=1, tiled=True),
        lax.all_gather(values_own, "seq", axis=1, tiled=True),
        lax.all_gather(mask_own, "seq", axis=1, tiled=True),
    )
    back_kh = split_heads(back_k)
    back_vh = split_heads(back_v)
    key_probs, grad_scores, delta = back_parts(
        queries, back_kh, back_vh, place_own, place_full, back_m, log_total, grad_heads, None
    )
    grad_queries = jnp.einsum(
        "bqhk,bkhe->bqhe", grad_scores, back_kh, preferred_element_type=jnp.float32
    ) * HEAD_DIM ** (-0.5)
    grad_keys, grad_values = key_side_grads(key_probs, grad_scores, queries, grad_heads)
    keys_grad_own, values_grad_own = (
        lax.psum_scatter(
            grad_keys.reshape(back_k.shape).astype(jnp.bfloat16),
            "seq",
            scatter_dimension=1,
            tiled=True,
        ).astype(jnp.float32),
        lax.psum_scatter(
            grad_values.reshape(back_v.shape).astype(jnp.bfloat16),
            "seq",
            scatter_dimension=1,
            tiled=True,
        ).astype(jnp.float32),
    )
    grad_triple = jnp.concatenate(
        [
            grad_queries.reshape(row_count, features),
            keys_grad_own.reshape(row_count, features),
            values_grad_own.reshape(row_count, features),
        ],
        axis=1,
    ).astype(jnp.bfloat16)
    grad_qkv = jnp.einsum("rd,rk->dk", normed_low, grad_triple, preferred_element_type=jnp.float32)
    column_sums = jnp.sum(grad_triple.astype(jnp.float32), axis=0)
    grad_query_bias = column_sums[:features]
    grad_value_bias = column_sums[2 * features :]
    grad_normed = jnp.einsum("rk,dk->rd", grad_triple, w_qkv, preferred_element_type=jnp.float32)
    grad_first, grad_ln1_gain, grad_ln1_bias = first_back(grad_normed)
    grad_router = jnp.dot(grad_logit, xfloat, precision=lax.Precision.HIGHEST)
    grad_input = grad_rows + grad_summed + grad_first + grad_logit[:, None] * w_router[None, :]
    input_grad = grad_input.astype(jnp.bfloat16).reshape(packs, per_piece, features)
    (
        share_qkv,
        share_query_bias,
        share_value_bias,
        share_out,
        share_out_bias,
        share_up,
        share_up_bias,
        share_down,
        share_down_bias,
        share_ln1_gain,
        share_ln1_bias,
        share_ln2_gain,
        share_ln2_bias,
        share_router,
    ) = (
        lax.psum_scatter(
            grad_qkv.astype(jnp.bfloat16), "dp", scatter_dimension=0, tiled=True
        ).astype(jnp.float32),
        lax.psum_scatter(
            grad_query_bias.astype(jnp.bfloat16), "dp", scatter_dimension=0, tiled=True
        ).astype(jnp.float32),
        lax.psum_scatter(
            grad_value_bias.astype(jnp.bfloat16), "dp", scatter_dimension=0, tiled=True
        ).astype(jnp.float32),
        lax.psum_scatter(
            grad_out.astype(jnp.bfloat16), "dp", scatter_dimension=0, tiled=True
        ).astype(jnp.float32),
        lax.psum_scatter(
            grad_out_bias.astype(jnp.bfloat16), "dp", scatter_dimension=0, tiled=True
        ).astype(jnp.float32),
        lax.psum_scatter(
            grad_up.astype(jnp.bfloat16), "dp", scatter_dimension=0, tiled=True
        ).astype(jnp.float32),
        lax.psum_scatter(
            grad_up_bias.astype(jnp.bfloat16), "dp", scatter_dimension=0, tiled=True
        ).astype(jnp.float32),
        lax.psum_scatter(
            grad_down.astype(jnp.bfloat16), "dp", scatter_dimension=0, tiled=True
        ).astype(jnp.float32),
        lax.psum_scatter(
            grad_down_bias.astype(jnp.bfloat16), "dp", scatter_dimension=0, tiled=True
        ).astype(jnp.float32),
        lax.psum_scatter(
            grad_ln1_gain.astype(jnp.bfloat16), "dp", scatter_dimension=0, tiled=True
        ).astype(jnp.float32),
        lax.psum_scatter(
            grad_ln1_bias.astype(jnp.bfloat16), "dp", scatter_dimension=0, tiled=True
        ).astype(jnp.float32),
        lax.psum_scatter(
            grad_ln2_gain.astype(jnp.bfloat16), "dp", scatter_dimension=0, tiled=True
        ).astype(jnp.float32),
        lax.psum_scatter(
            grad_ln2_bias.astype(jnp.bfloat16), "dp", scatter_dimension=0, tiled=True
        ).astype(jnp.float32),
        lax.psum_scatter(
            grad_router.astype(jnp.bfloat16), "dp", scatter_dimension=0, tiled=True
        ).astype(jnp.float32),
    )
    totals = (
        lax.psum(share_qkv.astype(jnp.bfloat16), "seq").astype(jnp.float32),
        lax.psum(share_query_bias.astype(jnp.bfloat16), "seq").astype(jnp.float32),
        lax.psum(share_value_bias.astype(jnp.bfloat16), "seq").astype(jnp.float32),
        lax.psum(share_out.astype(jnp.bfloat16), "seq").astype(jnp.float32),
        lax.psum(share_out_bias.astype(jnp.bfloat16), "seq").astype(jnp.float32),
        lax.psum(share_up.astype(jnp.bfloat16), "seq").astype(jnp.float32),
        lax.psum(share_up_bias.astype(jnp.bfloat16), "seq").astype(jnp.float32),
        lax.psum(share_down.astype(jnp.bfloat16), "seq").astype(jnp.float32),
        lax.psum(share_down_bias.astype(jnp.bfloat16), "seq").astype(jnp.float32),
        lax.psum(share_ln1_gain.astype(jnp.bfloat16), "seq").astype(jnp.float32),
        lax.psum(share_ln1_bias.astype(jnp.bfloat16), "seq").astype(jnp.float32),
        lax.psum(share_ln2_gain.astype(jnp.bfloat16), "seq").astype(jnp.float32),
        lax.psum(share_ln2_bias.astype(jnp.bfloat16), "seq").astype(jnp.float32),
        lax.psum(share_router.astype(jnp.bfloat16), "seq").astype(jnp.float32),
    )
    return (
        output,
        input_grad,
        totals[0],
        totals[1],
        totals[2],
        totals[3],
        totals[4],
        totals[5],
        totals[6],
        totals[7],
        totals[8],
        totals[9],
        totals[10],
        totals[11],
        totals[12],
        totals[13],
        fractions,
    )


def solution(mesh):
    in_specs = (
        P("dp", "seq", None),
        P("dp", "seq", None),
        P("dp"),
        P("dp", "seq"),
        P(),
        P(),
        P(),
        P(),
        P(),
        P(),
        P(),
        P(),
        P(),
        P(),
        P(),
        P(),
        P(),
        P(),
    )
    out_specs = (
        P("dp", "seq", None),
        P("dp", "seq", None),
        P("dp", None),
        P("dp"),
        P("dp"),
        P("dp", None),
        P("dp"),
        P("dp", None),
        P("dp"),
        P("dp", None),
        P("dp"),
        P("dp"),
        P("dp"),
        P("dp"),
        P("dp"),
        P("dp"),
        P(),
    )
    fast = mesh.shape["dp"] == 16 and mesh.shape["seq"] == 2
    return jax.shard_map(
        fused if fast else on_device, mesh=mesh, in_specs=in_specs, out_specs=out_specs, check_vma=False
    )
```

```python
from functools import partial
from itertools import product

import jax
import jax.numpy as jnp
from jax import lax
from jax.experimental import pallas as pl
from jax.experimental.pallas import tpu as pltpu
from jax.sharding import PartitionSpec as P

HEADS = 12
HEAD_DIM = 64
PAD_LEN = 640
LONG_LEN = 577
SHORT_LEN = 197
WIDTH = 768
HIDDEN = 3072

epsilon = 1e-06
masked_floor = -1000000000.0
MESH_ID = pl.DeviceIdType.MESH
bf16 = jnp.bfloat16
f32 = jnp.float32

HALF = WIDTH // 2
OWN = PAD_LEN // 2
HID = HIDDEN // 2
BLOCKS = HID // HALF
PAIRS = HALF // 128
MT = 640
AT = 640
LT = 320
SMALL = 16
PIECES = {
    "up0_0": ("up0", "lxyh", 0, 128),
    "up0_1": ("up0", "xzy", 128, 128),
    "up0_2": ("up0", "zyx", 256, 128),
    "up1_0": ("up1", "lxyh", 0, 128),
    "up1_1": ("up1", "zxy", 128, 256),
    "up2": ("up2", "yzx", 0, 384),
    "up3": ("up3", "zyx", 0, 384),
    "dA0": ("dA0", "yxlh", 0, 384),
    "dB0": ("dB0", "xylh", 0, 384),
    "dA1": ("dA1", "xylh", 0, 384),
    "dB1": ("dB1", "xylh", 0, 384),
    "out_0": ("out", "xylh", 0, 128),
    "out_1": ("out", "yzx", 128, 256),
    "q_0": ("q", "xylh", 0, 128),
    "q_1": ("q", "xyz", 128, 256),
    "k_0": ("k", "xyz", 0, 128),
    "k_1": ("k", "yxlh", 128, 256),
    "v_0": ("v", "xyz", 0, 128),
    "v_1": ("v", "xylh", 128, 128),
    "v_2": ("v", "yxlh", 256, 128),
}
HALVED = ("dB0", "dA1", "dB1")
SCHEDULE = {
    "u0": (
        (1, "up0_2"), (1, "up0_0"),
    ),
    "j0": (
        (0, "dB0"),
    ),
    "u1": (
        (1, "up1_1"), (1, "up0_1"),
    ),
    "j1": (
        (1, "dA0"), (1, "dB0"),
    ),
    "j2": (
        (0, "dA1"), (0, "dB1"), (2, "up0_1"), (1, "up1_0"), (1, "up2"),
    ),
    "u3": (
        (1, "up3"), (2, "dB0"),
    ),
    "j3": (
        (1, "dA1"),
    ),
    "out": (
        (1, "out_1"), (1, "dB1"),
    ),
    "gmx": (
        (1, "out_0"), (2, "up1_0"), (2, "up0_0"), (2, "up2"),
    ),
    "h0": (
        (2, "dA1"),
    ),
    "h1": (
        (3, "dB0"), (2, "dA0"), (2, "dB1"), (2, "out_1"),
    ),
    "q": (
        (1, "q_0"), (3, "up0_0"), (3, "dA1"), (1, "q_1"), (2, "out_0"),
    ),
    "k": (
        (1, "k_1"), (3, "dA0"),
    ),
    "v": (
        (3, "dB1"), (3, "up0_1"), (1, "v_1"), (1, "k_0"), (4, "dB0"), (4, "up0_0"), (2, "q_0"), (1, "v_2"),
    ),
    "fb": (
        (1, "small"), (3, "out_0"), (4, "dA1"), (2, "q_1"), (2, "k_1"), (4, "dB1"), (3, "q_0"), (2, "v_1"),
        (4, "up0_1"), (4, "dA0"), (2, "small"), (5, "up0_0"), (3, "up1_0"), (2, "v_2"), (2, "k_0"), (1, "v_0"),
        (4, "out_0"), (3, "out_1"), (3, "q_1"), (3, "small"), (2, "up3"),
    ),
    "end": (
        (3, "v_1"), (3, "k_1"), (4, "up1_0"), (3, "up2"), (4, "q_0"), (3, "k_0"), (2, "up0_2"), (3, "v_2"),
        (2, "up1_1"), (4, "small"), (2, "v_0"), (5, "dA0"), (5, "dB1"), (3, "up3"), (4, "v_1"), (4, "out_1"),
        (4, "k_1"), (3, "up0_2"), (3, "up1_1"), (5, "dA1"), (5, "up1_0"), (3, "v_0"), (4, "up2"), (5, "dB0"),
        (4, "v_2"), (5, "q_0"), (4, "q_1"), (4, "k_0"), (5, "out_0"), (4, "up3"), (5, "small"), (4, "up0_2"),
        (5, "v_1"), (4, "up1_1"), (5, "k_1"), (4, "v_0"), (5, "v_2"),
    ),
}


def dot_nn(a, b):
    return lax.dot_general(a, b, (((1,), (0,)), ((), ())), preferred_element_type=f32)


def dot_nt(a, b):
    return lax.dot_general(a, b, (((1,), (1,)), ((), ())), preferred_element_type=f32)


def dot_tn(a, b):
    return lax.dot_general(a, b, (((0,), (0,)), ((), ())), preferred_element_type=f32)


def row_stats(values):
    average = jnp.mean(values, axis=-1, keepdims=True)
    centred = values - average
    variance = jnp.mean(centred * centred, axis=-1, keepdims=True)
    rstd = lax.rsqrt(variance + epsilon)
    return centred * rstd, rstd


def norm_back(unit, rstd, grad, gain):
    q = grad * gain
    return rstd * (
        q - jnp.mean(q, axis=-1, keepdims=True) - unit * jnp.mean(q * unit, axis=-1, keepdims=True)
    )


def piece_shapes(name):
    grad, order, _, width = PIECES[name]
    left = [1 if grad[0] == "d" and axis in "lh" else 4 if axis == "z" else 2 for axis in order]
    tile = [192 if grad[0] == "d" else 48, width]
    shapes = [(left + tile, bf16)]
    for k, axis in enumerate(order):
        shapes.append(([3] * (axis == "z") + left[k + 1 :] + tile, bf16))
    return shapes + [(tile, f32)]


def first_slot(name, k):
    slot = 0
    for other, (_, order, _, _) in PIECES.items():
        for i, axis in enumerate(order):
            if other == name and i == k:
                return slot
            slot += 3 if axis == "z" else 2 if i == 0 and other in HALVED else 1
    return slot


def layer_kernel(*refs):
    (tokens, cotangent, group, select, w_qkv, b_query, b_value, w_out, b_out, w_up, b_up, w_down,
     b_down, ln1_gain, ln1_bias, ln2_gain, ln2_bias, w_router) = refs[:18]
    o_output, o_input, o_qkv, o_out, o_up, o_down, o_small = refs[18:25]
    (X, G, SEL, VEC, BUP, NRM, WQ, WO, WU, WD, TRI, PR, MIX, SUM, SEC, GM, QAUX, KAUX, GATE, ACT,
     HIDJ, GPJ, ACCD, ACCS, GSB, GSR, DSB, DSR, GATT, GMX, DTR, DKT, DVT, INV, SECT, NSR, SB, SBL, SBR) = refs[25:64]
    n_bufs = sum(len(p[1]) + 2 for p in PIECES.values())
    piece_bufs = refs[64 : 64 + n_bufs]
    (lsem, esem_s, esem_r, csem_s, csem_r, ssem_s, ssem_r, fsem_l, fsem_s, fsem_r) = refs[64 + n_bufs :]
    dp = lax.axis_index("dp")
    c = lax.axis_index("seq")
    x = lax.rem(dp, 2)
    y = lax.rem(lax.div(dp, 2), 2)
    z = lax.div(dp, 4)
    peer = (dp, 1 - c)
    xp = ((z * 2 + y) * 2 + (1 - x), c)
    yp = ((z * 2 + (1 - y)) * 2 + x, c)
    zs = [lax.rem(z + k, 4) for k in (1, 2, 3)]
    zp = [((zk * 2 + y) * 2 + x, c) for zk in zs]
    own = pl.multiple_of(c * OWN, OWN)
    oth = pl.multiple_of((1 - c) * OWN, OWN)
    chalf = pl.multiple_of(c * HALF, HALF)
    chid = pl.multiple_of(c * HID, HID)
    lead = (c == 0).astype(f32)

    barrier = pltpu.get_barrier_semaphore()
    for other in [peer, xp, yp] + zp:
        pl.semaphore_signal(barrier, inc=1, device_id=other, device_id_type=MESH_ID)

    loads = {}

    def load(name, src, dst):
        copy = pltpu.make_async_copy(src, dst, lsem.at[len(loads)])
        copy.start()
        loads[name] = copy

    load("tok", tokens.at[0], X.at[pl.ds(own, OWN)])
    load("sel", select, SEL.at[c])
    for i, v in enumerate(
        (b_query, b_value, b_out, b_down, ln1_gain, ln1_bias, ln2_gain, ln2_bias, w_router)
    ):
        load("v%d" % i, v, VEC.at[i, 0])
    for k in range(3):
        load(
            "wq%d" % k,
            w_qkv.at[:, pl.ds(pl.multiple_of(k * WIDTH + c * HALF, 128), HALF)],
            WQ.at[:, pl.ds(k * HALF, HALF)],
        )
    load("cot", cotangent.at[0], G.at[pl.ds(own, OWN)])

    pl.semaphore_wait(barrier, 6)

    sends = []
    counts = {"e": 0, "c": 0}

    def to_core(src, dst):
        i = counts["e"]
        counts["e"] += 1
        copy = pltpu.make_async_remote_copy(
            src_ref=src, dst_ref=dst, send_sem=esem_s.at[i], recv_sem=esem_r.at[i],
            device_id=peer, device_id_type=MESH_ID,
        )
        copy.start()
        sends.append(copy)
        return copy

    ex_sel = to_core(select, SEL.at[c])
    ex_tok = to_core(tokens.at[0], X.at[pl.ds(own, OWN)])
    ex_cot = to_core(cotangent.at[0], G.at[pl.ds(own, OWN)])
    load("bup", b_up, BUP.at[0])
    load("wo", w_out, WO)
    load("wu", w_up.at[:, pl.ds(chid, HID)], WU)
    load("wd", w_down.at[pl.ds(chid, HID)], WD)

    SB[...] = jnp.zeros_like(SB)

    def vec(i):
        return VEC[i]

    def project(start):
        @pl.loop(0, OWN // LT)
        def _(t):
            rows = pl.ds(pl.multiple_of(start + t * LT, 32), LT)
            xf = X[rows, :].astype(f32)
            unit, _ = row_stats(xf)
            NRM[rows, :] = (unit * vec(4) + vec(5)).astype(bf16)
            logit = jnp.sum(xf * vec(8), axis=-1, keepdims=True)
            GATE[rows, :] = 1.0 / (1.0 + jnp.exp(-logit))

        if start is own:
            for k in range(3):
                loads["wq%d" % k].wait()
        rows = pl.ds(start, OWN)
        nr = NRM[rows, :]
        for k in range(3):
            r = dot_nn(nr, WQ[:, k * HALF : (k + 1) * HALF])
            if k == 0:
                r = (r + VEC[0, :, pl.ds(chalf, HALF)]).astype(bf16).astype(f32) * HEAD_DIM ** (-0.5)
            if k == 2:
                r = r + VEC[1, :, pl.ds(chalf, HALF)]
            TRI[rows, k * HALF : (k + 1) * HALF] = r.astype(bf16)

    loads["tok"].wait()
    for i in range(9):
        loads["v%d" % i].wait()
    project(own)

    loads["sel"].wait()
    ex_sel.wait_recv()
    gv = jnp.full((1, 1), group[0], jnp.int32)
    long_col = jnp.broadcast_to(gv, (PAD_LEN, 1)) == 1
    pos_col = lax.broadcasted_iota(jnp.int32, (PAD_LEN, 1), 0)
    short_col = (pos_col >= SHORT_LEN).astype(jnp.int32) + (pos_col >= 2 * SHORT_LEN).astype(jnp.int32)
    place_col = jnp.where(long_col, 0, short_col)
    end_col = jnp.where(long_col, LONG_LEN, 3 * SHORT_LEN)
    sel_col = jnp.zeros((PAD_LEN, 8), f32)
    for part in range(2):
        bits = jnp.broadcast_to((SEL[part] > 0).astype(f32), (8, OWN)).astype(bf16)
        spread = (
            lax.broadcasted_iota(jnp.int32, (PAD_LEN, OWN), 0)
            == lax.broadcasted_iota(jnp.int32, (PAD_LEN, OWN), 1) + part * OWN
        ).astype(f32).astype(bf16)
        sel_col = sel_col + dot_nt(spread, bits)
    act_col = jnp.where(pos_col < end_col, sel_col[:, 0:1], 0.0)
    ACT[...] = act_col
    lane = lax.broadcasted_iota(jnp.int32, (1, 128), 1)
    same = jnp.bitwise_and(lane, HEAD_DIM - 1) == place_col
    QAUX[...] = jnp.where(same, 1.0, 0.0).astype(bf16)
    KAUX[...] = jnp.where(same & (act_col > 0.5), 0.0, -1e30).astype(bf16)
    length = jnp.where(jnp.broadcast_to(gv, (1, 1)) == 1, float(LONG_LEN), float(SHORT_LEN))
    for j in range(3):
        count = jnp.sum(jnp.where(place_col == j, act_col, 0.0), axis=0, keepdims=True)
        SB[13 + j : 14 + j, 0:128] = jnp.where(lane == dp, count / length * lead, 0.0)

    ex_tok.wait_recv()
    project(oth)

    low_lanes = lax.broadcasted_iota(jnp.int32, (1, 128), 1) < HEAD_DIM

    def head_part(v, side):
        keep = low_lanes if side == 0 else jnp.logical_not(low_lanes)
        return jnp.where(keep, v, jnp.zeros_like(v))

    def pair_lanes(hp):
        return [slice(k * HALF + hp * 128, k * HALF + hp * 128 + 128) for k in range(3)]

    def with_ones(v, side):
        return jnp.where(lane == (1 - side) * HEAD_DIM, jnp.ones_like(v), head_part(v, side))

    def scores(head):
        qlanes, klanes, _ = pair_lanes(head // 2)
        keep = low_lanes if head % 2 == 0 else jnp.logical_not(low_lanes)
        return dot_nt(
            jnp.where(keep, TRI[:, qlanes], QAUX[...]), jnp.where(keep, TRI[:, klanes], KAUX[...])
        )

    ex_mix, both = [], []
    ahead = scores(0)
    for head in range(2 * PAIRS):
        s = ahead
        if head + 1 < 2 * PAIRS:
            ahead = scores(head + 1)
        qlanes, _, vlanes = pair_lanes(head // 2)
        e = jnp.exp(s - jnp.max(s, axis=-1, keepdims=True)).astype(bf16)
        PR[head] = e
        both.append(dot_nn(e, with_ones(TRI[:, vlanes], head % 2)))
        if head % 2 == 1:
            scale = 1.0 / jnp.where(low_lanes, both[-2][:, HEAD_DIM : HEAD_DIM + 1], both[-1][:, 0:1])
            INV[:, qlanes] = scale
            MIX[c, :, qlanes] = (jnp.where(low_lanes, both[-2], both[-1]) * scale).astype(bf16)
            ex_mix.append(to_core(MIX.at[c, :, qlanes], MIX.at[c, :, qlanes]))

    loads["wo"].wait()

    @pl.loop(0, PAD_LEN // MT)
    def _(t):
        rows = pl.ds(pl.multiple_of(t * MT, MT), MT)
        SUM[rows, :] = X[rows, :].astype(f32) + (dot_nn(MIX[c, rows, :], WO[pl.ds(chalf, HALF), :]) + vec(2))

    loads["cot"].wait()
    ex_cot.wait_recv()

    @pl.loop(0, PAD_LEN // LT)
    def _(t):
        rows = pl.ds(pl.multiple_of(t * LT, LT), LT)
        GM[rows, :] = (ACT[rows, :] * GATE[rows, :] * G[rows, :].astype(f32)).astype(bf16)

    for e in ex_mix:
        e.wait_recv()

    @pl.loop(0, PAD_LEN // MT)
    def _(t):
        rows = pl.ds(pl.multiple_of(t * MT, MT), MT)
        s = SUM[rows, :] + dot_nn(MIX[1 - c, rows, :], WO[pl.ds(pl.multiple_of(HALF - chalf, HALF), HALF), :])
        SUM[rows, :] = s
        unit, _ = row_stats(s)
        SEC[rows, :] = (unit * vec(6) + vec(7)).astype(bf16)

    SECT[...] = jnp.swapaxes(SEC[...], 0, 1)

    for n in ("bup", "wu", "wd"):
        loads[n].wait()

    def remote(src, dst, dev, i):
        return pltpu.make_async_remote_copy(
            src_ref=src, dst_ref=dst, send_sem=csem_s.at[i], recv_sem=csem_r.at[i],
            device_id=dev, device_id_type=MESH_ID,
        )

    pieces = {}

    zl, zh = lax.rem(z, 2), lax.div(z, 2)
    lp = (((z + 1 - 2 * zl) * 2 + y) * 2 + x, c)
    where = {"x": x, "y": y, "l": zl, "h": zh}
    partner = {"x": xp, "y": yp, "l": lp, "h": zp[1]}

    class Piece:
        def __init__(self, name, buffers, dst_ref, only_z=None):
            self.name, self.order = name, PIECES[name][1]
            self.src, self.recv, self.fin = buffers[0], buffers[1:-1], buffers[-1]
            self.only_z = only_z
            self.cur = self.src
            self.number = len(pieces)
            self.copies = []
            self.keep = pltpu.make_async_copy(self.fin, dst_ref, fsem_l.at[self.number])
            self.give = pltpu.make_async_remote_copy(
                src_ref=self.fin, dst_ref=dst_ref, send_sem=fsem_s.at[self.number],
                recv_sem=fsem_r.at[self.number], device_id=peer, device_id_type=MESH_ID,
            )
            pieces[name] = self

        def send(self, k, part=None):
            axis, recv = self.order[k], self.recv[k]
            slot = first_slot(self.name, k)
            self.copies = self.copies if k == 0 else []
            if axis == "z":
                for kk in range(3):
                    self.begin(self.cur.at[zs[kk]], recv.at[kk], zp[kk], slot + kk)
            elif part is not None:
                self.begin(self.cur.at[1 - where[axis], part], recv.at[part], partner[axis], slot + part)
            else:
                self.begin(self.cur.at[1 - where[axis]], recv, partner[axis], slot)

        def begin(self, src, dst, dev, slot):
            cp = remote(src, dst, dev, slot)
            cp.start()
            sends.append(cp)
            self.copies.append(cp)

        def add(self, k):
            for cp in self.copies:
                cp.wait_recv()
            axis, recv = self.order[k], self.recv[k]
            last = k == len(self.order) - 1
            mine_at = z if axis == "z" else where[axis]
            if axis in "lh" and self.only_z is not None:
                mine_at = 0
            for idx in product(*(range(n) for n in self.src.shape[k + 1 : -2])):
                mine = self.cur[(mine_at,) + idx]
                if axis == "z":
                    total = mine.astype(f32) + recv[(0,) + idx].astype(f32)
                    total = total + (recv[(1,) + idx].astype(f32) + recv[(2,) + idx].astype(f32))
                elif last:
                    total = mine.astype(f32) + recv[idx].astype(f32)
                else:
                    total = mine + recv[idx]
                if last:
                    self.fin[...] = total
                elif axis == "z":
                    recv[(0,) + idx] = total.astype(bf16)
                else:
                    recv[idx] = total
            self.cur = recv.at[0] if axis == "z" else recv

        def step(self, act, part=None):
            k = act - 1
            if act <= 1:
                self.send(0, part)
            elif k < len(self.order):
                if self.only_z is None or k < 2:
                    self.add(k - 1)
                    self.send(k)
                elif k == 2:
                    self.add(1)
                    self.copies = [remote(self.cur.at[0], self.recv[2], lp, first_slot(self.name, 2))]
                    self.copy_l = self.copies[0]
                    pl.when(zl != self.down_l)(self.copy_l.start)
                else:
                    self.copy_h = remote(self.recv[2].at[0], self.recv[3], zp[1], first_slot(self.name, 3))

                    @pl.when(zl == self.down_l)
                    def _():
                        self.add(2)
                        pl.when(zh != c)(self.copy_h.start)

                    self.cur = self.recv[2]
                    self.copies = [self.copy_h]
            else:

                def finish():
                    self.add(len(self.order) - 1)
                    self.keep.start()
                    self.give.start()

                if self.only_z is None:
                    finish()
                else:
                    pl.when(z == self.only_z)(finish)

        def end(self):
            keep, give = self.keep, self.give
            if self.only_z is None:
                keep.wait()
                give.wait()
                return

            @pl.when(z == self.only_z)
            def _():
                keep.wait()
                give.wait_send()

            pl.when(z == self.only_z + 2 - 4 * c)(give.wait_recv)
            pl.when(zl != self.down_l)(self.copy_l.wait_send)

            @pl.when(zl == self.down_l)
            def _():
                pl.when(zh != c)(self.copy_h.wait_send)

    for i, (name, (grad, _, first_col, width)) in enumerate(PIECES.items()):
        lanes_from = {"up": (o_up, chid), "ou": (o_out, chalf), "q": (o_qkv, chalf), "k": (o_qkv, chalf + WIDTH),
                      "v": (o_qkv, chalf + 2 * WIDTH), "dA": (o_down, 0), "dB": (o_down, HALF)}[grad[:2]]
        start_at = lanes_from[1] + first_col + (int(grad[2:]) * HALF if grad[:2] == "up" else 0)
        dst_ref = lanes_from[0].at[:, pl.ds(pl.multiple_of(start_at, 128), width)]
        n_bufs = len(PIECES[name][1]) + 2
        p = Piece(name, piece_bufs[:n_bufs], dst_ref, 2 * c + int(grad[2:]) if grad[0] == "d" else None)
        p.down_l = int(grad[2:]) if grad[0] == "d" else None
        piece_bufs = piece_bufs[n_bufs:]

    def keep_grad(grad, rows, value):
        for name, (g, _, first_col, width) in PIECES.items():
            if g == grad:
                src, order = pieces[name].src, pieces[name].order
                tile = src.shape[-2]
                for i in range(HALF // tile):
                    if grad[0] == "d":
                        place = {"l": 0, "h": 0, "y": rows, "x": i}
                    else:
                        place = {"z": 2 * rows + i // 4, "h": rows, "l": i // 4, "y": i // 2 % 2, "x": i % 2}
                    src[tuple(place[axis] for axis in order)] = value[
                        tile * i : tile * (i + 1), first_col : first_col + width
                    ].astype(bf16)

    class Small:
        def step(self, act, part=None):
            (self.first, self.second, self.third, self.fourth, self.fifth)[act - 1]()

        def first(self):
            self.got = self.send(0, SB.at[pl.ds(pl.multiple_of(8 - 8 * c, 8), 8)], peer)

        def send(self, slot, src, dev):
            copy = pltpu.make_async_remote_copy(
                src_ref=src, dst_ref=SBR.at[slot], send_sem=ssem_s.at[slot], recv_sem=ssem_r.at[slot],
                device_id=dev, device_id_type=MESH_ID,
            )
            copy.start()
            sends.append(copy)
            return [copy]

        def gather(self, mine, slots):
            for cp in self.got:
                cp.wait_recv()
            for slot in slots:
                mine = mine + SBR[slot]
            return mine

        def second(self):
            SBL[0] = self.gather(SB[pl.ds(pl.multiple_of(8 * c, 8), 8), :], (0,))
            self.got = self.send(1, SBL.at[0], xp)

        def third(self):
            SBL[1] = self.gather(SBL[0], (1,))
            self.got = self.send(2, SBL.at[1], yp)

        def fourth(self):
            SBL[2] = self.gather(SBL[1], (2,))
            self.got = []
            for k in range(3):
                self.got += self.send(3 + k, SBL.at[2], zp[k])

        def fifth(self):
            SBL[3] = self.gather(SBL[2], (3, 4, 5))
            rows = o_small.at[pl.ds(pl.multiple_of(8 * c, 8), 8)]
            self.keep = pltpu.make_async_copy(SBL.at[3], rows, lsem.at[N_LOADS + 2])
            self.give = pltpu.make_async_remote_copy(
                src_ref=SBL.at[3], dst_ref=rows, send_sem=ssem_s.at[6], recv_sem=ssem_r.at[6],
                device_id=peer, device_id_type=MESH_ID,
            )
            self.keep.start()
            self.give.start()

        def end(self):
            self.keep.wait()
            self.give.wait()

    pieces["small"] = Small()

    def at(point):
        for act, name in SCHEDULE.get(point, ()):
            p = pieces[name]
            p.step(act, None if act > 1 or name not in HALVED else act)

    for j in range(BLOCKS):
        cols = slice(j * HALF, (j + 1) * HALF)
        bj = BUP[:, pl.ds(pl.multiple_of(chid + j * HALF, 128), HALF)]

        pre = dot_nn(SEC[...], WU[:, cols]) + bj
        gh = dot_nt(GM[...], WD[cols, :])
        cdf = 0.5 * (1.0 + lax.erf(pre * (2.0 ** -0.5)))
        HIDJ[...] = (pre * cdf).astype(bf16)
        slope = cdf + pre * (0.3989422804014327 * jnp.exp(-0.5 * pre * pre))
        GPJ[...] = (gh * slope).astype(bf16)

        def accumulate():
            d = dot_nn(HIDJ[...], WD[cols, :])
            s = dot_nt(GPJ[...], WU[:, cols])
            if j > 0:
                d = ACCD[...] + d
                s = ACCS[...] + s
            ACCD[...] = d
            ACCS[...] = s
            if j == BLOCKS - 1:
                GSB[...] = s.astype(bf16)

        if j == BLOCKS - 1:
            accumulate()

        if j == BLOCKS - 1:
            ex_gs = to_core(GSB, GSR)

            @pl.loop(0, OWN // LT)
            def _(t):
                r = pl.ds(pl.multiple_of(t * LT, LT), LT)
                DSB[r, :] = ACCD[pl.ds(pl.multiple_of(oth + t * LT, 32), LT), :].astype(bf16)

            ex_ds = to_core(DSB, DSR)

        for part in range(2):
            g = dot_nn(SECT[part * HALF : (part + 1) * HALF, :], GPJ[...])
            keep_grad("up%d" % j, part, g)
        at("u%d" % j)
        SB[pl.ds(9 + 2 * c + j // 2, 1), (j % 2) * HALF : (j % 2 + 1) * HALF] = jnp.sum(
            GPJ[...].astype(f32), axis=0, keepdims=True
        )
        for part in range(2):
            g = dot_tn(HIDJ[...], GM[:, part * HALF : (part + 1) * HALF])
            keep_grad("d%s%d" % ("AB"[part], j // 2), j % 2, g)
        at("j%d" % j)
        if j < BLOCKS - 1:
            accumulate()

    ex_gs.wait_recv()

    zero_row = jnp.zeros((1, WIDTH), f32)

    def col_sum(v):
        return jnp.sum(v, axis=0, keepdims=True)

    def second_back(t, carry):
        rows = pl.ds(pl.multiple_of(t * LT, LT), LT)
        gs = ACCS[rows, :] + GSR[rows, :].astype(f32)
        unit, rstd = row_stats(SUM[rows, :])
        back = norm_back(unit, rstd, gs, vec(6))
        ACCS[rows, :] = back
        ga = (ACT[rows, :] * GATE[rows, :] * G[rows, :].astype(f32) + back).astype(bf16)
        GATT[rows, :] = ga
        return (
            carry[0] + col_sum(gs * unit), carry[1] + col_sum(gs), carry[2] + col_sum(ga.astype(f32)),
            carry[3] + col_sum(GM[rows, :].astype(f32)),
        )

    sums = lax.fori_loop(0, PAD_LEN // LT, second_back, (zero_row,) * 4)
    for row, value in zip((6, 7, 2, 3), sums):
        SB[row : row + 1, :] = value * lead
    at("sb")

    for part in range(2):
        g = dot_tn(MIX[part], GATT[:, pl.ds(chalf, HALF)])
        keep_grad("out", part, g)
    at("out")

    @pl.loop(0, PAD_LEN // MT)
    def _(t):
        rows = pl.ds(pl.multiple_of(t * MT, MT), MT)
        GMX[rows, :] = (dot_nt(GATT[rows, :], WO[pl.ds(chalf, HALF), :]) * INV[rows, :]).astype(bf16)

    at("gmx")

    for hp in range(PAIRS):
        qlanes, klanes, vlanes = pair_lanes(hp)
        kp = TRI[:, klanes]
        vp = TRI[:, vlanes]
        gp = GMX[:, qlanes]
        dots = gp.astype(f32) * MIX[c, :, qlanes].astype(f32)
        qt = jnp.swapaxes(TRI[:, qlanes], 0, 1)
        gt = jnp.swapaxes(gp, 0, 1)
        dq = jnp.zeros((PAD_LEN, 128), f32)
        for side in range(2):
            half = slice(side * HEAD_DIM, (side + 1) * HEAD_DIM)
            e = PR[2 * hp + side]
            dpr = dot_nt(head_part(gp, side), vp)
            delta = jnp.sum(head_part(dots, side), axis=-1, keepdims=True)
            ds = (e.astype(f32) * (dpr - delta)).astype(bf16)
            dq = dq + dot_nn(ds, head_part(kp, side))
            DKT[half, :] = dot_nn(qt[half, :], ds)
            DVT[half, :] = dot_nn(gt[half, :], e)
        DTR[:, qlanes] = (dq * HEAD_DIM ** (-0.5)).astype(bf16)
        DTR[:, klanes] = jnp.swapaxes(DKT[...], 0, 1).astype(bf16)
        DTR[:, vlanes] = jnp.swapaxes(DVT[...], 0, 1).astype(bf16)
        at("h%d" % hp)

    for k in range(3):
        blk = DTR[:, k * HALF : (k + 1) * HALF]
        if k != 1:
            SB[k // 2 : k // 2 + 1, pl.ds(chalf, HALF)] = col_sum(blk.astype(f32))
        for part in range(2):
            g = dot_tn(NRM[:, part * HALF : (part + 1) * HALF], blk)
            keep_grad("qkv"[k], part, g)
        at("qkv"[k])

    ex_ds.wait_send()
    DSB[...] = dot_nt(DTR[pl.ds(oth, OWN), :], WQ[...]).astype(bf16)
    ex_ns = to_core(DSB, NSR)
    at("ns")
    ex_ds.wait_recv()
    ex_gs.wait_send()
    ex_ns.wait_recv()
    OUTB, INB = GSB.at[0:OWN], GSB.at[OWN:PAD_LEN]

    def first_back(t, carry):
        r = pl.ds(pl.multiple_of(t * 80, 80), 80)
        rows = pl.ds(pl.multiple_of(own + t * 80, 80), 80)
        xf = X[rows, :].astype(f32)
        unit, rstd = row_stats(xf)
        gn = dot_nt(DTR[rows, :], WQ[...]) + NSR[r, :].astype(f32)
        first = norm_back(unit, rstd, gn, vec(4))
        gf = G[rows, :].astype(f32)
        gate = ACT[rows, :] * GATE[rows, :]
        branch = SUM[rows, :] - xf + ACCD[rows, :] + DSR[r, :].astype(f32) + vec(3)
        OUTB[r, :] = (xf + gate * branch).astype(bf16)
        gl = jnp.sum(gf * branch, axis=-1, keepdims=True) * (gate * (1.0 - GATE[rows, :]))
        INB[r, :] = (gf + ACCS[rows, :] + first + gl * vec(8)).astype(bf16)
        return (carry[0] + col_sum(gn * unit), carry[1] + col_sum(gn), carry[2] + col_sum(gl * xf))

    sums = lax.fori_loop(0, OWN // 80, first_back, (zero_row,) * 3)
    for row, value in zip((4, 5, 8), sums):
        SB[row : row + 1, :] = value
    keep_out = pltpu.make_async_copy(OUTB, o_output.at[0], lsem.at[len(loads)])
    keep_in = pltpu.make_async_copy(INB, o_input.at[0], lsem.at[len(loads) + 1])
    keep_out.start()
    keep_in.start()

    at("fb")
    at("end")
    for p in pieces.values():
        p.end()
    for cp in sends:
        if cp is not ex_ds and cp is not ex_gs:
            cp.wait_send()
    for cp in (keep_out, keep_in):
        cp.wait()


N_LOADS = 2 + 9 + 3 + 5
BIG = (0, 1, 2, 5, 7, 9)
SMALLS = (3, 4, 6, 10, 11, 12, 13, 14, 15)


def place_kernel(*refs):
    src, dst, bufs, (vec, up, share, sem) = refs[:7], refs[7:24], refs[24:31], refs[31:]
    dp = lax.axis_index("dp")
    ins = [pltpu.make_async_copy(src[i], bufs[i], sem.at[i]) for i in range(7)]
    outs = [pltpu.make_async_copy(bufs[i], dst[k], sem.at[7 + i]) for i, k in enumerate(BIG)]
    for i in (6, 0, 1, 2, 3, 4, 5):
        ins[i].start()
    ins[6].wait()
    rows = bufs[6][...]
    mine = pltpu.roll(rows, lax.rem(dp * (WIDTH - 48), WIDTH), 1)
    for i in range(9):
        vec[i] = mine[i : i + 1, :48]
    bufs[6][...] = pltpu.roll(rows, lax.rem(lax.rem(dp, 4) * (WIDTH - 192), WIDTH), 1)
    up[...] = bufs[6][pl.ds(9 + lax.div(dp, 4), 1), :192]
    share[...] = rows[13:16, :16]
    smalls = [pltpu.make_async_copy(vec.at[i], dst[k], sem.at[13 + i]) for i, k in enumerate(SMALLS)]
    smalls += [pltpu.make_async_copy(up, dst[8], sem.at[22]), pltpu.make_async_copy(share, dst[16], sem.at[23])]
    for cp in smalls:
        cp.start()
    for a, b in zip(ins, outs):
        a.wait()
        b.start()
    for cp in outs + smalls:
        cp.wait()


def fused(
    tokens, cotangent, group, select, w_qkv, b_query, b_value, w_out, b_out, w_up, b_up, w_down,
    b_down, ln1_gain, ln1_bias, ln2_gain, ln2_bias, w_router,
):
    args = (
        tokens, cotangent, group, select, w_qkv, b_query, b_value, w_out, b_out, w_up, b_up, w_down,
        b_down, ln1_gain, ln1_bias, ln2_gain, ln2_bias, w_router,
    )
    anywhere = pl.BlockSpec(memory_space=pl.ANY)
    shape = jax.ShapeDtypeStruct
    mids = (
        shape((1, OWN, WIDTH), bf16), shape((1, OWN, WIDTH), bf16), shape((48, 3 * WIDTH), f32),
        shape((48, WIDTH), f32), shape((48, HIDDEN), f32), shape((192, WIDTH), f32),
        shape((SMALL, WIDTH), f32),
    )
    v = pltpu.VMEM
    sq = (PAD_LEN, WIDTH)
    scratch = [
        v(sq, bf16), v(sq, bf16), v((2, 1, OWN), jnp.int32), v((9, 1, WIDTH), f32), v((1, HIDDEN), f32),
        v(sq, bf16), v((WIDTH, 3 * HALF), bf16), v((WIDTH, WIDTH), bf16), v((WIDTH, HID), bf16),
        v((HID, WIDTH), bf16), v((PAD_LEN, 3 * HALF), bf16), v((2 * PAIRS, PAD_LEN, PAD_LEN), bf16),
        v((2, PAD_LEN, HALF), bf16), v(sq, f32), v(sq, bf16), v(sq, bf16), v((PAD_LEN, 128), bf16), v((PAD_LEN, 128), bf16),
        v((PAD_LEN, 1), f32), v((PAD_LEN, 1), f32),
        v((PAD_LEN, HALF), bf16), v((PAD_LEN, HALF), bf16), v(sq, f32), v(sq, f32), v(sq, bf16), v(sq, bf16),
        v((OWN, WIDTH), bf16), v((OWN, WIDTH), bf16), v(sq, bf16), v((PAD_LEN, HALF), bf16),
        v((PAD_LEN, 3 * HALF), bf16), v((128, PAD_LEN), f32), v((128, PAD_LEN), f32),
        v((PAD_LEN, HALF), f32), v((WIDTH, PAD_LEN), bf16), v((OWN, WIDTH), bf16),
        v((SMALL, WIDTH), f32), v((4, 8, WIDTH), f32), v((6, 8, WIDTH), f32),
    ] + [v(*b) for name in PIECES for b in piece_shapes(name)] + [
        pltpu.SemaphoreType.DMA((N_LOADS + 4,)),
        pltpu.SemaphoreType.DMA((9,)), pltpu.SemaphoreType.DMA((9,)),
        pltpu.SemaphoreType.DMA((first_slot(None, 0),)), pltpu.SemaphoreType.DMA((first_slot(None, 0),)),
        pltpu.SemaphoreType.DMA((7,)), pltpu.SemaphoreType.DMA((7,)),
        pltpu.SemaphoreType.DMA((len(PIECES),)), pltpu.SemaphoreType.DMA((len(PIECES),)), pltpu.SemaphoreType.DMA((len(PIECES),)),
    ]
    mid = pl.pallas_call(
        layer_kernel,
        out_shape=mids,
        in_specs=[anywhere, anywhere, pl.BlockSpec(memory_space=pltpu.SMEM)] + [anywhere] * 15,
        out_specs=[anywhere] * 7,
        scratch_shapes=scratch,
        compiler_params=pltpu.CompilerParams(
            collective_id=0, has_side_effects=True, vmem_limit_bytes=60 << 20
        ),
        name="layer",
    )(*args)
    outs = (
        mids[0], mids[1], mids[2], shape((1, 48), f32), shape((1, 48), f32), mids[3], shape((1, 48), f32),
        mids[4], shape((1, 192), f32), mids[5],
    ) + (shape((1, 48), f32),) * 6 + (shape((3, 16), f32),)
    out = pl.pallas_call(
        place_kernel,
        out_shape=outs,
        in_specs=[anywhere] * 7,
        out_specs=[anywhere] * 17,
        scratch_shapes=[v(m.shape, m.dtype) for m in mids]
        + [v((9, 1, 48), f32), v((1, 192), f32), v((3, 16), f32), pltpu.SemaphoreType.DMA((24,))],
        name="place",
    )(*mid)
    return tuple(o.reshape(-1) if o.shape[0] == 1 and o.ndim == 2 else o for o in out[:16]) + (out[16].T,)


def norm_rows(values, norm_gain, norm_shift):
    average = jnp.mean(values, axis=-1, keepdims=True)
    centred = values - average
    variance = jnp.mean(centred * centred, axis=-1, keepdims=True)
    return centred * lax.rsqrt(variance + epsilon) * norm_gain + norm_shift


def places_of(group, slot_pos):
    short_place = jnp.minimum(slot_pos // SHORT_LEN, 2)
    return jnp.where(group[:, None] == 1, 0, short_place[None, :])


def split_heads(flat_rows):
    return flat_rows.reshape(flat_rows.shape[0], flat_rows.shape[1], HEADS, HEAD_DIM)


def masked_scores(queries, key_heads, query_place, key_place, key_mask):
    score_scale = HEAD_DIM ** (-0.5)
    scores = (
        jnp.einsum("bqhe,bkhe->bqhk", queries, key_heads, preferred_element_type=jnp.float32)
        * score_scale
    )
    key_live = (key_mask.astype(jnp.float32)[:, None, None, :] > 0.5) & (
        query_place[:, :, None, None] == key_place[:, None, None, :]
    )
    return (jnp.where(key_live, scores, masked_floor), key_live.astype(jnp.float32))


def attend(queries, key_heads, value_heads, query_place, key_place, key_mask):
    masked, key_weight = masked_scores(queries, key_heads, query_place, key_place, key_mask)
    row_max = jnp.max(masked, axis=-1, keepdims=True)
    exponent = jnp.exp(masked - row_max) * key_weight
    row_sum = jnp.sum(exponent, axis=-1, keepdims=True)
    weights = (exponent / row_sum).astype(jnp.bfloat16)
    mixed_heads = jnp.einsum(
        "bqhk,bkhe->bqhe", weights, value_heads, preferred_element_type=jnp.float32
    )
    return (mixed_heads, row_max + jnp.log(row_sum))


def back_parts(
    queries, key_heads, value_heads, query_place, key_place, key_mask, log_total, grad_heads, delta
):
    masked, key_weight = masked_scores(queries, key_heads, query_place, key_place, key_mask)
    key_probs = jnp.exp(masked - log_total) * key_weight
    grad_probs = jnp.einsum(
        "bqhe,bkhe->bqhk", grad_heads, value_heads, preferred_element_type=jnp.float32
    )
    delta = jnp.sum(key_probs * grad_probs, axis=-1, keepdims=True)
    grad_scores = (key_probs * (grad_probs - delta)).astype(jnp.bfloat16)
    return (key_probs, grad_scores, delta)


def key_side_grads(key_probs, grad_scores, queries, grad_heads):
    score_scale = HEAD_DIM ** (-0.5)
    grad_values = jnp.einsum(
        "bqhk,bqhe->bkhe",
        key_probs.astype(jnp.bfloat16),
        grad_heads,
        preferred_element_type=jnp.float32,
    )
    grad_keys = (
        jnp.einsum("bqhk,bqhe->bkhe", grad_scores, queries, preferred_element_type=jnp.float32)
        * score_scale
    )
    return (grad_keys, grad_values)


def on_device(
    tokens,
    cotangent,
    group,
    select,
    w_qkv,
    b_query,
    b_value,
    w_out,
    b_out,
    w_up,
    b_up,
    w_down,
    b_down,
    ln1_gain,
    ln1_bias,
    ln2_gain,
    ln2_bias,
    w_router,
):
    packs, per_piece, features = tokens.shape
    row_count = packs * per_piece
    first_pos = lax.axis_index("seq") * per_piece
    positions = first_pos + jnp.arange(per_piece, dtype=jnp.int32)
    full_positions = jnp.arange(PAD_LEN, dtype=jnp.int32)
    place_own = places_of(group, positions)
    place_full = places_of(group, full_positions)
    ends = jnp.where(group == 1, LONG_LEN, 3 * SHORT_LEN).astype(jnp.int32)
    active = ((select > 0) & (positions[None, :] < ends[:, None])).astype(jnp.float32)
    active_rows = active.reshape(row_count, 1)
    xfloat = tokens.reshape(row_count, features).astype(jnp.float32)
    router = jax.nn.sigmoid(jnp.dot(xfloat, w_router, precision=lax.Precision.HIGHEST))
    normed, first_back = jax.vjp(norm_rows, xfloat, ln1_gain, ln1_bias)
    normed_low = normed.astype(jnp.bfloat16)
    qkv_bias = jnp.concatenate([b_query, jnp.zeros_like(b_query), b_value])
    triple = (jnp.dot(normed_low, w_qkv, preferred_element_type=jnp.float32) + qkv_bias).astype(
        jnp.bfloat16
    )
    queries = triple[:, :features].reshape(packs, per_piece, HEADS, HEAD_DIM)
    keys_own = triple[:, features : 2 * features].reshape(packs, per_piece, features)
    values_own = triple[:, 2 * features :].reshape(packs, per_piece, features)
    mask_own = active.astype(jnp.bfloat16)
    keys_all, values_all, mask_all = (
        lax.all_gather(keys_own, "seq", axis=1, tiled=True),
        lax.all_gather(values_own, "seq", axis=1, tiled=True),
        lax.all_gather(mask_own, "seq", axis=1, tiled=True),
    )
    mixed_heads, log_total = attend(
        queries, split_heads(keys_all), split_heads(values_all), place_own, place_full, mask_all
    )
    mixed_low = mixed_heads.reshape(row_count, features).astype(jnp.bfloat16)
    attended = jnp.dot(mixed_low, w_out, preferred_element_type=jnp.float32) + b_out
    summed = xfloat + attended
    second, second_back = jax.vjp(norm_rows, summed, ln2_gain, ln2_bias)
    second_low = second.astype(jnp.bfloat16)
    pre_act = jnp.dot(second_low, w_up, preferred_element_type=jnp.float32) + b_up
    gelu_out, gelu_back = jax.vjp(partial(jax.nn.gelu, approximate=False), pre_act)
    hidden_low = gelu_out.astype(jnp.bfloat16)
    branch = attended + (jnp.dot(hidden_low, w_down, preferred_element_type=jnp.float32) + b_down)
    gate_rows = active_rows * router[:, None]
    output = (xfloat + gate_rows * branch).astype(jnp.bfloat16).reshape(packs, per_piece, features)
    place_range = jnp.arange(3, dtype=jnp.int32)
    onehot = (place_full[:, :, None] == place_range[None, None, :]).astype(jnp.float32)
    counts = jnp.sum(mask_all.astype(jnp.float32)[:, :, None] * onehot, axis=1)
    image_lengths = jnp.where(group == 1, LONG_LEN, SHORT_LEN).astype(jnp.float32)
    fractions = lax.all_gather(counts / image_lengths[:, None], "dp", axis=0, tiled=True)
    grad_rows = cotangent.reshape(row_count, features).astype(jnp.float32)
    grad_logit = jnp.sum(grad_rows * branch, axis=1) * active_rows[:, 0] * router * (1.0 - router)
    grad_branch = gate_rows * grad_rows
    grad_mlp = grad_branch.astype(jnp.bfloat16)
    grad_down = jnp.einsum("rk,rd->kd", hidden_low, grad_mlp, preferred_element_type=jnp.float32)
    grad_down_bias = jnp.sum(grad_mlp.astype(jnp.float32), axis=0)
    grad_hidden = jnp.einsum("rd,kd->rk", grad_mlp, w_down, preferred_element_type=jnp.float32)
    grad_pre = gelu_back(grad_hidden)[0].astype(jnp.bfloat16)
    grad_up = jnp.einsum("rd,rk->dk", second_low, grad_pre, preferred_element_type=jnp.float32)
    grad_up_bias = jnp.sum(grad_pre.astype(jnp.float32), axis=0)
    grad_second = jnp.einsum("rk,dk->rd", grad_pre, w_up, preferred_element_type=jnp.float32)
    grad_summed, grad_ln2_gain, grad_ln2_bias = second_back(grad_second)
    grad_attended = (grad_branch + grad_summed).astype(jnp.bfloat16)
    grad_out = jnp.einsum("rd,re->de", mixed_low, grad_attended, preferred_element_type=jnp.float32)
    grad_out_bias = jnp.sum(grad_attended.astype(jnp.float32), axis=0)
    grad_mixed = jnp.einsum("re,de->rd", grad_attended, w_out, preferred_element_type=jnp.float32)
    grad_heads = grad_mixed.astype(jnp.bfloat16).reshape(packs, per_piece, HEADS, HEAD_DIM)
    back_k, back_v, back_m = (
        lax.all_gather(keys_own, "seq", axis=1, tiled=True),
        lax.all_gather(values_own, "seq", axis=1, tiled=True),
        lax.all_gather(mask_own, "seq", axis=1, tiled=True),
    )
    back_kh = split_heads(back_k)
    back_vh = split_heads(back_v)
    key_probs, grad_scores, delta = back_parts(
        queries, back_kh, back_vh, place_own, place_full, back_m, log_total, grad_heads, None
    )
    grad_queries = jnp.einsum(
        "bqhk,bkhe->bqhe", grad_scores, back_kh, preferred_element_type=jnp.float32
    ) * HEAD_DIM ** (-0.5)
    grad_keys, grad_values = key_side_grads(key_probs, grad_scores, queries, grad_heads)
    keys_grad_own, values_grad_own = (
        lax.psum_scatter(
            grad_keys.reshape(back_k.shape).astype(jnp.bfloat16),
            "seq",
            scatter_dimension=1,
            tiled=True,
        ).astype(jnp.float32),
        lax.psum_scatter(
            grad_values.reshape(back_v.shape).astype(jnp.bfloat16),
            "seq",
            scatter_dimension=1,
            tiled=True,
        ).astype(jnp.float32),
    )
    grad_triple = jnp.concatenate(
        [
            grad_queries.reshape(row_count, features),
            keys_grad_own.reshape(row_count, features),
            values_grad_own.reshape(row_count, features),
        ],
        axis=1,
    ).astype(jnp.bfloat16)
    grad_qkv = jnp.einsum("rd,rk->dk", normed_low, grad_triple, preferred_element_type=jnp.float32)
    column_sums = jnp.sum(grad_triple.astype(jnp.float32), axis=0)
    grad_query_bias = column_sums[:features]
    grad_value_bias = column_sums[2 * features :]
    grad_normed = jnp.einsum("rk,dk->rd", grad_triple, w_qkv, preferred_element_type=jnp.float32)
    grad_first, grad_ln1_gain, grad_ln1_bias = first_back(grad_normed)
    grad_router = jnp.dot(grad_logit, xfloat, precision=lax.Precision.HIGHEST)
    grad_input = grad_rows + grad_summed + grad_first + grad_logit[:, None] * w_router[None, :]
    input_grad = grad_input.astype(jnp.bfloat16).reshape(packs, per_piece, features)
    (
        share_qkv,
        share_query_bias,
        share_value_bias,
        share_out,
        share_out_bias,
        share_up,
        share_up_bias,
        share_down,
        share_down_bias,
        share_ln1_gain,
        share_ln1_bias,
        share_ln2_gain,
        share_ln2_bias,
        share_router,
    ) = (
        lax.psum_scatter(
            grad_qkv.astype(jnp.bfloat16), "dp", scatter_dimension=0, tiled=True
        ).astype(jnp.float32),
        lax.psum_scatter(
            grad_query_bias.astype(jnp.bfloat16), "dp", scatter_dimension=0, tiled=True
        ).astype(jnp.float32),
        lax.psum_scatter(
            grad_value_bias.astype(jnp.bfloat16), "dp", scatter_dimension=0, tiled=True
        ).astype(jnp.float32),
        lax.psum_scatter(
            grad_out.astype(jnp.bfloat16), "dp", scatter_dimension=0, tiled=True
        ).astype(jnp.float32),
        lax.psum_scatter(
            grad_out_bias.astype(jnp.bfloat16), "dp", scatter_dimension=0, tiled=True
        ).astype(jnp.float32),
        lax.psum_scatter(
            grad_up.astype(jnp.bfloat16), "dp", scatter_dimension=0, tiled=True
        ).astype(jnp.float32),
        lax.psum_scatter(
            grad_up_bias.astype(jnp.bfloat16), "dp", scatter_dimension=0, tiled=True
        ).astype(jnp.float32),
        lax.psum_scatter(
            grad_down.astype(jnp.bfloat16), "dp", scatter_dimension=0, tiled=True
        ).astype(jnp.float32),
        lax.psum_scatter(
            grad_down_bias.astype(jnp.bfloat16), "dp", scatter_dimension=0, tiled=True
        ).astype(jnp.float32),
        lax.psum_scatter(
            grad_ln1_gain.astype(jnp.bfloat16), "dp", scatter_dimension=0, tiled=True
        ).astype(jnp.float32),
        lax.psum_scatter(
            grad_ln1_bias.astype(jnp.bfloat16), "dp", scatter_dimension=0, tiled=True
        ).astype(jnp.float32),
        lax.psum_scatter(
            grad_ln2_gain.astype(jnp.bfloat16), "dp", scatter_dimension=0, tiled=True
        ).astype(jnp.float32),
        lax.psum_scatter(
            grad_ln2_bias.astype(jnp.bfloat16), "dp", scatter_dimension=0, tiled=True
        ).astype(jnp.float32),
        lax.psum_scatter(
            grad_router.astype(jnp.bfloat16), "dp", scatter_dimension=0, tiled=True
        ).astype(jnp.float32),
    )
    totals = (
        lax.psum(share_qkv.astype(jnp.bfloat16), "seq").astype(jnp.float32),
        lax.psum(share_query_bias.astype(jnp.bfloat16), "seq").astype(jnp.float32),
        lax.psum(share_value_bias.astype(jnp.bfloat16), "seq").astype(jnp.float32),
        lax.psum(share_out.astype(jnp.bfloat16), "seq").astype(jnp.float32),
        lax.psum(share_out_bias.astype(jnp.bfloat16), "seq").astype(jnp.float32),
        lax.psum(share_up.astype(jnp.bfloat16), "seq").astype(jnp.float32),
        lax.psum(share_up_bias.astype(jnp.bfloat16), "seq").astype(jnp.float32),
        lax.psum(share_down.astype(jnp.bfloat16), "seq").astype(jnp.float32),
        lax.psum(share_down_bias.astype(jnp.bfloat16), "seq").astype(jnp.float32),
        lax.psum(share_ln1_gain.astype(jnp.bfloat16), "seq").astype(jnp.float32),
        lax.psum(share_ln1_bias.astype(jnp.bfloat16), "seq").astype(jnp.float32),
        lax.psum(share_ln2_gain.astype(jnp.bfloat16), "seq").astype(jnp.float32),
        lax.psum(share_ln2_bias.astype(jnp.bfloat16), "seq").astype(jnp.float32),
        lax.psum(share_router.astype(jnp.bfloat16), "seq").astype(jnp.float32),
    )
    return (
        output,
        input_grad,
        totals[0],
        totals[1],
        totals[2],
        totals[3],
        totals[4],
        totals[5],
        totals[6],
        totals[7],
        totals[8],
        totals[9],
        totals[10],
        totals[11],
        totals[12],
        totals[13],
        fractions,
    )


def solution(mesh):
    in_specs = (
        P("dp", "seq", None),
        P("dp", "seq", None),
        P("dp"),
        P("dp", "seq"),
        P(),
        P(),
        P(),
        P(),
        P(),
        P(),
        P(),
        P(),
        P(),
        P(),
        P(),
        P(),
        P(),
        P(),
    )
    out_specs = (
        P("dp", "seq", None),
        P("dp", "seq", None),
        P("dp", None),
        P("dp"),
        P("dp"),
        P("dp", None),
        P("dp"),
        P("dp", None),
        P("dp"),
        P("dp", None),
        P("dp"),
        P("dp"),
        P("dp"),
        P("dp"),
        P("dp"),
        P("dp"),
        P(),
    )
    fast = mesh.shape["dp"] == 16 and mesh.shape["seq"] == 2
    return jax.shard_map(
        fused if fast else on_device, mesh=mesh, in_specs=in_specs, out_specs=out_specs, check_vma=False
    )
```

```python
from functools import partial
from itertools import product

import jax
import jax.numpy as jnp
from jax import lax
from jax.experimental import pallas as pl
from jax.experimental.pallas import tpu as pltpu
from jax.sharding import PartitionSpec as P

HEADS = 12
HEAD_DIM = 64
PAD_LEN = 640
LONG_LEN = 577
SHORT_LEN = 197
WIDTH = 768
HIDDEN = 3072

epsilon = 1e-06
masked_floor = -1000000000.0
MESH_ID = pl.DeviceIdType.MESH
bf16 = jnp.bfloat16
f32 = jnp.float32

HALF = WIDTH // 2
OWN = PAD_LEN // 2
HID = HIDDEN // 2
BLOCKS = HID // HALF
PAIRS = HALF // 128
MT = 640
AT = 640
LT = 320
SMALL = 16
PIECES = {
    "up0_0": ("up0", "lxyh", 0, 128),
    "up0_1": ("up0", "xzy", 128, 128),
    "up0_2": ("up0", "zyx", 256, 128),
    "up1_0": ("up1", "lxyh", 0, 128),
    "up1_1": ("up1", "zxy", 128, 256),
    "up2": ("up2", "yzx", 0, 384),
    "up3": ("up3", "zyx", 0, 384),
    "dA0": ("dA0", "yxlh", 0, 384),
    "dB0": ("dB0", "xylh", 0, 384),
    "dA1": ("dA1", "xylh", 0, 384),
    "dB1": ("dB1", "xylh", 0, 384),
    "out_0": ("out", "xylh", 0, 128),
    "out_1": ("out", "yzx", 128, 256),
    "q_0": ("q", "xylh", 0, 128),
    "q_1": ("q", "xyz", 128, 256),
    "k_0": ("k", "xyz", 0, 128),
    "k_1": ("k", "yxlh", 128, 256),
    "v_0": ("v", "xyz", 0, 128),
    "v_1": ("v", "xylh", 128, 128),
    "v_2": ("v", "yxlh", 256, 128),
}
HALVED = ("dB0", "dA1", "dB1")
SCHEDULE = {
    "u0": (
        (1, "up0_2"), (1, "up0_0"),
    ),
    "j0": (
        (0, "dB0"),
    ),
    "u1": (
        (1, "up1_1"), (1, "up0_1"),
    ),
    "j1": (
        (1, "dA0"), (1, "dB0"),
    ),
    "j2": (
        (0, "dA1"), (0, "dB1"), (2, "up0_1"), (1, "up1_0"), (1, "up2"),
    ),
    "u3": (
        (1, "up3"), (2, "dB0"),
    ),
    "j3": (
        (1, "dA1"),
    ),
    "out": (
        (1, "out_1"), (1, "dB1"),
    ),
    "gmx": (
        (1, "out_0"), (2, "up1_0"), (2, "up0_0"), (2, "up2"),
    ),
    "h0": (
        (2, "dA1"),
    ),
    "h1": (
        (3, "dB0"), (2, "dA0"), (2, "dB1"), (2, "out_1"),
    ),
    "q": (
        (1, "q_0"), (3, "up0_0"), (3, "dA1"), (1, "q_1"), (2, "out_0"),
    ),
    "k": (
        (1, "k_1"), (3, "dA0"),
    ),
    "v": (
        (3, "dB1"), (3, "up0_1"), (1, "v_1"), (1, "k_0"), (4, "dB0"), (4, "up0_0"), (2, "q_0"), (1, "v_2"),
    ),
    "fb": (
        (1, "small"), (3, "out_0"), (4, "dA1"), (2, "q_1"), (2, "k_1"), (4, "dB1"), (3, "q_0"), (2, "v_1"),
        (4, "up0_1"), (4, "dA0"), (2, "small"), (5, "up0_0"), (3, "up1_0"), (2, "v_2"), (2, "k_0"), (1, "v_0"),
        (4, "out_0"), (3, "out_1"), (3, "q_1"), (3, "small"), (2, "up3"),
    ),
    "end": (
        (3, "v_1"), (3, "k_1"), (4, "up1_0"), (3, "up2"), (4, "q_0"), (3, "k_0"), (2, "up0_2"), (3, "v_2"),
        (2, "up1_1"), (4, "small"), (2, "v_0"), (5, "dA0"), (5, "dB1"), (3, "up3"), (4, "v_1"), (4, "out_1"),
        (4, "k_1"), (3, "up0_2"), (3, "up1_1"), (5, "dA1"), (5, "up1_0"), (3, "v_0"), (4, "up2"), (5, "dB0"),
        (4, "v_2"), (5, "q_0"), (4, "q_1"), (4, "k_0"), (5, "out_0"), (4, "up3"), (5, "small"), (4, "up0_2"),
        (5, "v_1"), (4, "up1_1"), (5, "k_1"), (4, "v_0"), (5, "v_2"),
    ),
}


def dot_nn(a, b):
    return lax.dot_general(a, b, (((1,), (0,)), ((), ())), preferred_element_type=f32)


def dot_nt(a, b):
    return lax.dot_general(a, b, (((1,), (1,)), ((), ())), preferred_element_type=f32)


def dot_tn(a, b):
    return lax.dot_general(a, b, (((0,), (0,)), ((), ())), preferred_element_type=f32)


def row_stats(values):
    average = jnp.mean(values, axis=-1, keepdims=True)
    centred = values - average
    variance = jnp.mean(centred * centred, axis=-1, keepdims=True)
    rstd = lax.rsqrt(variance + epsilon)
    return centred * rstd, rstd


def norm_back(unit, rstd, grad, gain):
    q = grad * gain
    return rstd * (
        q - jnp.mean(q, axis=-1, keepdims=True) - unit * jnp.mean(q * unit, axis=-1, keepdims=True)
    )


def piece_shapes(name):
    grad, order, _, width = PIECES[name]
    left = [1 if grad[0] == "d" and axis in "lh" else 4 if axis == "z" else 2 for axis in order]
    tile = [192 if grad[0] == "d" else 48, width]
    shapes = [(left + tile, bf16)]
    for k, axis in enumerate(order):
        shapes.append(([3] * (axis == "z") + left[k + 1 :] + tile, bf16))
    return shapes + [(tile, f32)]


def first_slot(name, k):
    slot = 0
    for other, (_, order, _, _) in PIECES.items():
        for i, axis in enumerate(order):
            if other == name and i == k:
                return slot
            slot += 3 if axis == "z" else 2 if i == 0 and other in HALVED else 1
    return slot


def layer_kernel(*refs):
    (tokens, cotangent, group, select, w_qkv, b_query, b_value, w_out, b_out, w_up, b_up, w_down,
     b_down, ln1_gain, ln1_bias, ln2_gain, ln2_bias, w_router) = refs[:18]
    o_output, o_input, o_qkv, o_out, o_up, o_down, o_small = refs[18:25]
    (X, G, SEL, VEC, BUP, NRM, WQ, WO, WU, WD, TRI, PR, MIX, SUM, SEC, GM, QAUX, KAUX, GATE, ACT,
     HIDJ, GPJ, ACCD, ACCS, GSB, GSR, DSB, DSR, GATT, GMX, DTR, DKT, DVT, INV, SECT, NSR, SB, SBL, SBR) = refs[25:64]
    n_bufs = sum(len(p[1]) + 2 for p in PIECES.values())
    piece_bufs = refs[64 : 64 + n_bufs]
    (lsem, esem_s, esem_r, csem_s, csem_r, ssem_s, ssem_r, fsem_s, fsem_r) = refs[64 + n_bufs :]
    dp = lax.axis_index("dp")
    c = lax.axis_index("seq")
    x = lax.rem(dp, 2)
    y = lax.rem(lax.div(dp, 2), 2)
    z = lax.div(dp, 4)
    peer = (dp, 1 - c)
    xp = ((z * 2 + y) * 2 + (1 - x), c)
    yp = ((z * 2 + (1 - y)) * 2 + x, c)
    zs = [lax.rem(z + k, 4) for k in (1, 2, 3)]
    zp = [((zk * 2 + y) * 2 + x, c) for zk in zs]
    own = pl.multiple_of(c * OWN, OWN)
    oth = pl.multiple_of((1 - c) * OWN, OWN)
    chalf = pl.multiple_of(c * HALF, HALF)
    chid = pl.multiple_of(c * HID, HID)
    lead = (c == 0).astype(f32)

    barrier = pltpu.get_barrier_semaphore()
    for other in [peer, xp, yp] + zp:
        pl.semaphore_signal(barrier, inc=1, device_id=other, device_id_type=MESH_ID)

    loads = {}

    def load(name, src, dst):
        copy = pltpu.make_async_copy(src, dst, lsem.at[len(loads)])
        copy.start()
        loads[name] = copy

    load("tok", tokens.at[0], X.at[pl.ds(own, OWN)])
    load("sel", select, SEL.at[c])
    for i, v in enumerate(
        (b_query, b_value, b_out, b_down, ln1_gain, ln1_bias, ln2_gain, ln2_bias, w_router)
    ):
        load("v%d" % i, v, VEC.at[i, 0])
    for k in range(3):
        load(
            "wq%d" % k,
            w_qkv.at[:, pl.ds(pl.multiple_of(k * WIDTH + c * HALF, 128), HALF)],
            WQ.at[:, pl.ds(k * HALF, HALF)],
        )
    load("cot", cotangent.at[0], G.at[pl.ds(own, OWN)])

    pl.semaphore_wait(barrier, 6)

    sends = []
    counts = {"e": 0, "c": 0}

    def to_core(src, dst):
        i = counts["e"]
        counts["e"] += 1
        copy = pltpu.make_async_remote_copy(
            src_ref=src, dst_ref=dst, send_sem=esem_s.at[i], recv_sem=esem_r.at[i],
            device_id=peer, device_id_type=MESH_ID,
        )
        copy.start()
        sends.append(copy)
        return copy

    ex_sel = to_core(select, SEL.at[c])
    ex_tok = to_core(tokens.at[0], X.at[pl.ds(own, OWN)])
    ex_cot = to_core(cotangent.at[0], G.at[pl.ds(own, OWN)])
    load("bup", b_up, BUP.at[0])
    load("wo", w_out, WO)
    load("wu", w_up.at[:, pl.ds(chid, HID)], WU)
    load("wd", w_down.at[pl.ds(chid, HID)], WD)

    SB[...] = jnp.zeros_like(SB)

    def vec(i):
        return VEC[i]

    def project(start):
        @pl.loop(0, OWN // LT)
        def _(t):
            rows = pl.ds(pl.multiple_of(start + t * LT, 32), LT)
            xf = X[rows, :].astype(f32)
            unit, _ = row_stats(xf)
            NRM[rows, :] = (unit * vec(4) + vec(5)).astype(bf16)
            logit = jnp.sum(xf * vec(8), axis=-1, keepdims=True)
            GATE[rows, :] = 1.0 / (1.0 + jnp.exp(-logit))

        if start is own:
            for k in range(3):
                loads["wq%d" % k].wait()
        rows = pl.ds(start, OWN)
        nr = NRM[rows, :]
        for k in range(3):
            r = dot_nn(nr, WQ[:, k * HALF : (k + 1) * HALF])
            if k == 0:
                r = (r + VEC[0, :, pl.ds(chalf, HALF)]).astype(bf16).astype(f32) * HEAD_DIM ** (-0.5)
            if k == 2:
                r = r + VEC[1, :, pl.ds(chalf, HALF)]
            TRI[rows, k * HALF : (k + 1) * HALF] = r.astype(bf16)

    loads["tok"].wait()
    for i in range(9):
        loads["v%d" % i].wait()
    project(own)

    loads["sel"].wait()
    ex_sel.wait_recv()
    gv = jnp.full((1, 1), group[0], jnp.int32)
    long_col = jnp.broadcast_to(gv, (PAD_LEN, 1)) == 1
    pos_col = lax.broadcasted_iota(jnp.int32, (PAD_LEN, 1), 0)
    short_col = (pos_col >= SHORT_LEN).astype(jnp.int32) + (pos_col >= 2 * SHORT_LEN).astype(jnp.int32)
    place_col = jnp.where(long_col, 0, short_col)
    end_col = jnp.where(long_col, LONG_LEN, 3 * SHORT_LEN)
    sel_col = jnp.zeros((PAD_LEN, 8), f32)
    for part in range(2):
        bits = jnp.broadcast_to((SEL[part] > 0).astype(f32), (8, OWN)).astype(bf16)
        spread = (
            lax.broadcasted_iota(jnp.int32, (PAD_LEN, OWN), 0)
            == lax.broadcasted_iota(jnp.int32, (PAD_LEN, OWN), 1) + part * OWN
        ).astype(f32).astype(bf16)
        sel_col = sel_col + dot_nt(spread, bits)
    act_col = jnp.where(pos_col < end_col, sel_col[:, 0:1], 0.0)
    ACT[...] = act_col
    lane = lax.broadcasted_iota(jnp.int32, (1, 128), 1)
    same = jnp.bitwise_and(lane, HEAD_DIM - 1) == place_col
    QAUX[...] = jnp.where(same, 1.0, 0.0).astype(bf16)
    KAUX[...] = jnp.where(same & (act_col > 0.5), 0.0, -1e30).astype(bf16)
    length = jnp.where(jnp.broadcast_to(gv, (1, 1)) == 1, float(LONG_LEN), float(SHORT_LEN))
    for j in range(3):
        count = jnp.sum(jnp.where(place_col == j, act_col, 0.0), axis=0, keepdims=True)
        SB[13 + j : 14 + j, 0:128] = jnp.where(lane == dp, count / length * lead, 0.0)

    ex_tok.wait_recv()
    project(oth)

    low_lanes = lax.broadcasted_iota(jnp.int32, (1, 128), 1) < HEAD_DIM

    def head_part(v, side):
        keep = low_lanes if side == 0 else jnp.logical_not(low_lanes)
        return jnp.where(keep, v, jnp.zeros_like(v))

    def pair_lanes(hp):
        return [slice(k * HALF + hp * 128, k * HALF + hp * 128 + 128) for k in range(3)]

    def with_ones(v, side):
        return jnp.where(lane == (1 - side) * HEAD_DIM, jnp.ones_like(v), head_part(v, side))

    def scores(head):
        qlanes, klanes, _ = pair_lanes(head // 2)
        keep = low_lanes if head % 2 == 0 else jnp.logical_not(low_lanes)
        return dot_nt(
            jnp.where(keep, TRI[:, qlanes], QAUX[...]), jnp.where(keep, TRI[:, klanes], KAUX[...])
        )

    ex_mix, both = [], []
    ahead = scores(0)
    for head in range(2 * PAIRS):
        s = ahead
        if head + 1 < 2 * PAIRS:
            ahead = scores(head + 1)
        qlanes, _, vlanes = pair_lanes(head // 2)
        e = jnp.exp(s - jnp.max(s, axis=-1, keepdims=True)).astype(bf16)
        PR[head] = e
        both.append(dot_nn(e, with_ones(TRI[:, vlanes], head % 2)))
        if head % 2 == 1:
            scale = 1.0 / jnp.where(low_lanes, both[-2][:, HEAD_DIM : HEAD_DIM + 1], both[-1][:, 0:1])
            INV[:, qlanes] = scale
            MIX[c, :, qlanes] = (jnp.where(low_lanes, both[-2], both[-1]) * scale).astype(bf16)
            ex_mix.append(to_core(MIX.at[c, :, qlanes], MIX.at[c, :, qlanes]))

    loads["wo"].wait()

    @pl.loop(0, PAD_LEN // MT)
    def _(t):
        rows = pl.ds(pl.multiple_of(t * MT, MT), MT)
        SUM[rows, :] = X[rows, :].astype(f32) + (dot_nn(MIX[c, rows, :], WO[pl.ds(chalf, HALF), :]) + vec(2))

    loads["cot"].wait()
    ex_cot.wait_recv()

    @pl.loop(0, PAD_LEN // LT)
    def _(t):
        rows = pl.ds(pl.multiple_of(t * LT, LT), LT)
        GM[rows, :] = (ACT[rows, :] * GATE[rows, :] * G[rows, :].astype(f32)).astype(bf16)

    for e in ex_mix:
        e.wait_recv()

    @pl.loop(0, PAD_LEN // MT)
    def _(t):
        rows = pl.ds(pl.multiple_of(t * MT, MT), MT)
        s = SUM[rows, :] + dot_nn(MIX[1 - c, rows, :], WO[pl.ds(pl.multiple_of(HALF - chalf, HALF), HALF), :])
        SUM[rows, :] = s
        unit, _ = row_stats(s)
        SEC[rows, :] = (unit * vec(6) + vec(7)).astype(bf16)

    SECT[...] = jnp.swapaxes(SEC[...], 0, 1)

    for n in ("bup", "wu", "wd"):
        loads[n].wait()

    def remote(src, dst, dev, i):
        return pltpu.make_async_remote_copy(
            src_ref=src, dst_ref=dst, send_sem=csem_s.at[i], recv_sem=csem_r.at[i],
            device_id=dev, device_id_type=MESH_ID,
        )

    pieces = {}

    zl, zh = lax.rem(z, 2), lax.div(z, 2)
    lp = (((z + 1 - 2 * zl) * 2 + y) * 2 + x, c)
    where = {"x": x, "y": y, "l": zl, "h": zh}
    partner = {"x": xp, "y": yp, "l": lp, "h": zp[1]}

    class Piece:
        def __init__(self, name, buffers, dst_ref, only_z=None):
            self.name, self.order = name, PIECES[name][1]
            self.src, self.recv, self.fin = buffers[0], buffers[1:-1], buffers[-1]
            self.only_z = only_z
            self.cur = self.src
            self.number = len(pieces)
            self.copies = []
            self.keep = pltpu.make_async_copy(self.fin, dst_ref, csem_r.at[first_slot(name, 0)])
            self.give = pltpu.make_async_remote_copy(
                src_ref=self.fin, dst_ref=dst_ref, send_sem=fsem_s.at[self.number],
                recv_sem=fsem_r.at[self.number], device_id=peer, device_id_type=MESH_ID,
            )
            pieces[name] = self

        def send(self, k, part=None):
            axis, recv = self.order[k], self.recv[k]
            slot = first_slot(self.name, k)
            self.copies = self.copies if k == 0 else []
            if axis == "z":
                for kk in range(3):
                    self.begin(self.cur.at[zs[kk]], recv.at[kk], zp[kk], slot + kk)
            elif part is not None:
                self.begin(self.cur.at[1 - where[axis], part], recv.at[part], partner[axis], slot + part)
            else:
                self.begin(self.cur.at[1 - where[axis]], recv, partner[axis], slot)

        def begin(self, src, dst, dev, slot):
            cp = remote(src, dst, dev, slot)
            cp.start()
            sends.append(cp)
            self.copies.append(cp)

        def add(self, k):
            for cp in self.copies:
                cp.wait_recv()
            axis, recv = self.order[k], self.recv[k]
            last = k == len(self.order) - 1
            mine_at = z if axis == "z" else where[axis]
            if axis in "lh" and self.only_z is not None:
                mine_at = 0
            for idx in product(*(range(n) for n in self.src.shape[k + 1 : -2])):
                mine = self.cur[(mine_at,) + idx]
                if axis == "z":
                    total = mine.astype(f32) + recv[(0,) + idx].astype(f32)
                    total = total + (recv[(1,) + idx].astype(f32) + recv[(2,) + idx].astype(f32))
                elif last:
                    total = mine.astype(f32) + recv[idx].astype(f32)
                else:
                    total = mine + recv[idx]
                if last:
                    self.fin[...] = total
                elif axis == "z":
                    recv[(0,) + idx] = total.astype(bf16)
                else:
                    recv[idx] = total
            self.cur = recv.at[0] if axis == "z" else recv

        def step(self, act, part=None):
            k = act - 1
            if act <= 1:
                self.send(0, part)
            elif k < len(self.order):
                if self.only_z is None or k < 2:
                    self.add(k - 1)
                    self.send(k)
                elif k == 2:
                    self.add(1)
                    self.copies = [remote(self.cur.at[0], self.recv[2], lp, first_slot(self.name, 2))]
                    self.copy_l = self.copies[0]
                    pl.when(zl != self.down_l)(self.copy_l.start)
                else:
                    self.copy_h = remote(self.recv[2].at[0], self.recv[3], zp[1], first_slot(self.name, 3))

                    @pl.when(zl == self.down_l)
                    def _():
                        self.add(2)
                        pl.when(zh != c)(self.copy_h.start)

                    self.cur = self.recv[2]
                    self.copies = [self.copy_h]
            else:

                def finish():
                    self.add(len(self.order) - 1)
                    self.keep.start()
                    self.give.start()

                if self.only_z is None:
                    finish()
                else:
                    pl.when(z == self.only_z)(finish)

        def end(self):
            keep, give = self.keep, self.give
            if self.only_z is None:
                keep.wait()
                give.wait()
                return

            @pl.when(z == self.only_z)
            def _():
                keep.wait()
                give.wait_send()

            pl.when(z == self.only_z + 2 - 4 * c)(give.wait_recv)
            pl.when(zl != self.down_l)(self.copy_l.wait_send)

            @pl.when(zl == self.down_l)
            def _():
                pl.when(zh != c)(self.copy_h.wait_send)

    for i, (name, (grad, _, first_col, width)) in enumerate(PIECES.items()):
        lanes_from = {"up": (o_up, chid), "ou": (o_out, chalf), "q": (o_qkv, chalf), "k": (o_qkv, chalf + WIDTH),
                      "v": (o_qkv, chalf + 2 * WIDTH), "dA": (o_down, 0), "dB": (o_down, HALF)}[grad[:2]]
        start_at = lanes_from[1] + first_col + (int(grad[2:]) * HALF if grad[:2] == "up" else 0)
        dst_ref = lanes_from[0].at[:, pl.ds(pl.multiple_of(start_at, 128), width)]
        n_bufs = len(PIECES[name][1]) + 2
        p = Piece(name, piece_bufs[:n_bufs], dst_ref, 2 * c + int(grad[2:]) if grad[0] == "d" else None)
        p.down_l = int(grad[2:]) if grad[0] == "d" else None
        piece_bufs = piece_bufs[n_bufs:]

    def keep_grad(grad, rows, value):
        for name, (g, _, first_col, width) in PIECES.items():
            if g == grad:
                src, order = pieces[name].src, pieces[name].order
                tile = src.shape[-2]
                for i in range(HALF // tile):
                    if grad[0] == "d":
                        place = {"l": 0, "h": 0, "y": rows, "x": i}
                    else:
                        place = {"z": 2 * rows + i // 4, "h": rows, "l": i // 4, "y": i // 2 % 2, "x": i % 2}
                    src[tuple(place[axis] for axis in order)] = value[
                        tile * i : tile * (i + 1), first_col : first_col + width
                    ].astype(bf16)

    class Small:
        def step(self, act, part=None):
            (self.first, self.second, self.third, self.fourth, self.fifth)[act - 1]()

        def first(self):
            self.got = self.send(0, SB.at[pl.ds(pl.multiple_of(8 - 8 * c, 8), 8)], peer)

        def send(self, slot, src, dev):
            copy = pltpu.make_async_remote_copy(
                src_ref=src, dst_ref=SBR.at[slot], send_sem=ssem_s.at[slot], recv_sem=ssem_r.at[slot],
                device_id=dev, device_id_type=MESH_ID,
            )
            copy.start()
            sends.append(copy)
            return [copy]

        def gather(self, mine, slots):
            for cp in self.got:
                cp.wait_recv()
            for slot in slots:
                mine = mine + SBR[slot]
            return mine

        def second(self):
            SBL[0] = self.gather(SB[pl.ds(pl.multiple_of(8 * c, 8), 8), :], (0,))
            self.got = self.send(1, SBL.at[0], xp)

        def third(self):
            SBL[1] = self.gather(SBL[0], (1,))
            self.got = self.send(2, SBL.at[1], yp)

        def fourth(self):
            SBL[2] = self.gather(SBL[1], (2,))
            self.got = []
            for k in range(3):
                self.got += self.send(3 + k, SBL.at[2], zp[k])

        def fifth(self):
            SBL[3] = self.gather(SBL[2], (3, 4, 5))
            rows = o_small.at[pl.ds(pl.multiple_of(8 * c, 8), 8)]
            self.keep = pltpu.make_async_copy(SBL.at[3], rows, lsem.at[N_LOADS + 2])
            self.give = pltpu.make_async_remote_copy(
                src_ref=SBL.at[3], dst_ref=rows, send_sem=ssem_s.at[6], recv_sem=ssem_r.at[6],
                device_id=peer, device_id_type=MESH_ID,
            )
            self.keep.start()
            self.give.start()

        def end(self):
            self.keep.wait()
            self.give.wait()

    pieces["small"] = Small()

    def at(point):
        for act, name in SCHEDULE.get(point, ()):
            p = pieces[name]
            p.step(act, None if act > 1 or name not in HALVED else act)

    for j in range(BLOCKS):
        cols = slice(j * HALF, (j + 1) * HALF)
        bj = BUP[:, pl.ds(pl.multiple_of(chid + j * HALF, 128), HALF)]

        pre = dot_nn(SEC[...], WU[:, cols]) + bj
        gh = dot_nt(GM[...], WD[cols, :])
        cdf = 0.5 * (1.0 + lax.erf(pre * (2.0 ** -0.5)))
        HIDJ[...] = (pre * cdf).astype(bf16)
        slope = cdf + pre * (0.3989422804014327 * jnp.exp(-0.5 * pre * pre))
        GPJ[...] = (gh * slope).astype(bf16)

        def accumulate():
            d = dot_nn(HIDJ[...], WD[cols, :])
            s = dot_nt(GPJ[...], WU[:, cols])
            if j > 0:
                d = ACCD[...] + d
                s = ACCS[...] + s
            ACCD[...] = d
            ACCS[...] = s
            if j == BLOCKS - 1:
                GSB[...] = s.astype(bf16)

        if j == BLOCKS - 1:
            accumulate()

        if j == BLOCKS - 1:
            ex_gs = to_core(GSB, GSR)

            @pl.loop(0, OWN // LT)
            def _(t):
                r = pl.ds(pl.multiple_of(t * LT, LT), LT)
                DSB[r, :] = ACCD[pl.ds(pl.multiple_of(oth + t * LT, 32), LT), :].astype(bf16)

            ex_ds = to_core(DSB, DSR)

        for part in range(2):
            g = dot_nn(SECT[part * HALF : (part + 1) * HALF, :], GPJ[...])
            keep_grad("up%d" % j, part, g)
        at("u%d" % j)
        SB[pl.ds(9 + 2 * c + j // 2, 1), (j % 2) * HALF : (j % 2 + 1) * HALF] = jnp.sum(
            GPJ[...].astype(f32), axis=0, keepdims=True
        )
        for part in range(2):
            g = dot_tn(HIDJ[...], GM[:, part * HALF : (part + 1) * HALF])
            keep_grad("d%s%d" % ("AB"[part], j // 2), j % 2, g)
        at("j%d" % j)
        if j < BLOCKS - 1:
            accumulate()

    ex_gs.wait_recv()

    zero_row = jnp.zeros((1, WIDTH), f32)

    def col_sum(v):
        return jnp.sum(v, axis=0, keepdims=True)

    def second_back(t, carry):
        rows = pl.ds(pl.multiple_of(t * LT, LT), LT)
        gs = ACCS[rows, :] + GSR[rows, :].astype(f32)
        unit, rstd = row_stats(SUM[rows, :])
        back = norm_back(unit, rstd, gs, vec(6))
        ACCS[rows, :] = back
        ga = (ACT[rows, :] * GATE[rows, :] * G[rows, :].astype(f32) + back).astype(bf16)
        GATT[rows, :] = ga
        return (
            carry[0] + col_sum(gs * unit), carry[1] + col_sum(gs), carry[2] + col_sum(ga.astype(f32)),
            carry[3] + col_sum(GM[rows, :].astype(f32)),
        )

    sums = lax.fori_loop(0, PAD_LEN // LT, second_back, (zero_row,) * 4)
    for row, value in zip((6, 7, 2, 3), sums):
        SB[row : row + 1, :] = value * lead
    at("sb")

    for part in range(2):
        g = dot_tn(MIX[part], GATT[:, pl.ds(chalf, HALF)])
        keep_grad("out", part, g)
    at("out")

    @pl.loop(0, PAD_LEN // MT)
    def _(t):
        rows = pl.ds(pl.multiple_of(t * MT, MT), MT)
        GMX[rows, :] = (dot_nt(GATT[rows, :], WO[pl.ds(chalf, HALF), :]) * INV[rows, :]).astype(bf16)

    at("gmx")

    for hp in range(PAIRS):
        qlanes, klanes, vlanes = pair_lanes(hp)
        kp = TRI[:, klanes]
        vp = TRI[:, vlanes]
        gp = GMX[:, qlanes]
        dots = gp.astype(f32) * MIX[c, :, qlanes].astype(f32)
        qt = jnp.swapaxes(TRI[:, qlanes], 0, 1)
        gt = jnp.swapaxes(gp, 0, 1)
        dq = jnp.zeros((PAD_LEN, 128), f32)
        for side in range(2):
            half = slice(side * HEAD_DIM, (side + 1) * HEAD_DIM)
            e = PR[2 * hp + side]
            dpr = dot_nt(head_part(gp, side), vp)
            delta = jnp.sum(head_part(dots, side), axis=-1, keepdims=True)
            ds = (e.astype(f32) * (dpr - delta)).astype(bf16)
            dq = dq + dot_nn(ds, head_part(kp, side))
            DKT[half, :] = dot_nn(qt[half, :], ds)
            DVT[half, :] = dot_nn(gt[half, :], e)
        DTR[:, qlanes] = (dq * HEAD_DIM ** (-0.5)).astype(bf16)
        DTR[:, klanes] = jnp.swapaxes(DKT[...], 0, 1).astype(bf16)
        DTR[:, vlanes] = jnp.swapaxes(DVT[...], 0, 1).astype(bf16)
        at("h%d" % hp)

    for k in range(3):
        blk = DTR[:, k * HALF : (k + 1) * HALF]
        if k != 1:
            SB[k // 2 : k // 2 + 1, pl.ds(chalf, HALF)] = col_sum(blk.astype(f32))
        for part in range(2):
            g = dot_tn(NRM[:, part * HALF : (part + 1) * HALF], blk)
            keep_grad("qkv"[k], part, g)
        at("qkv"[k])

    ex_ds.wait_send()
    DSB[...] = dot_nt(DTR[pl.ds(oth, OWN), :], WQ[...]).astype(bf16)
    ex_ns = to_core(DSB, NSR)
    at("ns")
    ex_ds.wait_recv()
    ex_gs.wait_send()
    ex_ns.wait_recv()
    OUTB, INB = GSB.at[0:OWN], GSB.at[OWN:PAD_LEN]

    def first_back(t, carry):
        r = pl.ds(pl.multiple_of(t * 80, 80), 80)
        rows = pl.ds(pl.multiple_of(own + t * 80, 80), 80)
        xf = X[rows, :].astype(f32)
        unit, rstd = row_stats(xf)
        gn = dot_nt(DTR[rows, :], WQ[...]) + NSR[r, :].astype(f32)
        first = norm_back(unit, rstd, gn, vec(4))
        gf = G[rows, :].astype(f32)
        gate = ACT[rows, :] * GATE[rows, :]
        branch = SUM[rows, :] - xf + ACCD[rows, :] + DSR[r, :].astype(f32) + vec(3)
        OUTB[r, :] = (xf + gate * branch).astype(bf16)
        gl = jnp.sum(gf * branch, axis=-1, keepdims=True) * (gate * (1.0 - GATE[rows, :]))
        INB[r, :] = (gf + ACCS[rows, :] + first + gl * vec(8)).astype(bf16)
        return (carry[0] + col_sum(gn * unit), carry[1] + col_sum(gn), carry[2] + col_sum(gl * xf))

    sums = lax.fori_loop(0, OWN // 80, first_back, (zero_row,) * 3)
    for row, value in zip((4, 5, 8), sums):
        SB[row : row + 1, :] = value
    keep_out = pltpu.make_async_copy(OUTB, o_output.at[0], lsem.at[len(loads)])
    keep_in = pltpu.make_async_copy(INB, o_input.at[0], lsem.at[len(loads) + 1])
    keep_out.start()
    keep_in.start()

    at("fb")
    at("end")
    for p in pieces.values():
        p.end()
    for cp in sends:
        if cp is not ex_ds and cp is not ex_gs:
            cp.wait_send()
    for cp in (keep_out, keep_in):
        cp.wait()


N_LOADS = 2 + 9 + 3 + 5
BIG = (0, 1, 2, 5, 7, 9)
SMALLS = (3, 4, 6, 10, 11, 12, 13, 14, 15)


def place_kernel(*refs):
    src, dst, bufs, (vec, up, share, sem) = refs[:7], refs[7:24], refs[24:31], refs[31:]
    dp = lax.axis_index("dp")
    ins = [pltpu.make_async_copy(src[i], bufs[i], sem.at[i]) for i in range(7)]
    outs = [pltpu.make_async_copy(bufs[i], dst[k], sem.at[7 + i]) for i, k in enumerate(BIG)]
    for i in (6, 0, 1, 2, 3, 4, 5):
        ins[i].start()
    ins[6].wait()
    rows = bufs[6][...]
    mine = pltpu.roll(rows, lax.rem(dp * (WIDTH - 48), WIDTH), 1)
    for i in range(9):
        vec[i] = mine[i : i + 1, :48]
    bufs[6][...] = pltpu.roll(rows, lax.rem(lax.rem(dp, 4) * (WIDTH - 192), WIDTH), 1)
    up[...] = bufs[6][pl.ds(9 + lax.div(dp, 4), 1), :192]
    share[...] = rows[13:16, :16]
    smalls = [pltpu.make_async_copy(vec.at[i], dst[k], sem.at[13 + i]) for i, k in enumerate(SMALLS)]
    smalls += [pltpu.make_async_copy(up, dst[8], sem.at[22]), pltpu.make_async_copy(share, dst[16], sem.at[23])]
    for cp in smalls:
        cp.start()
    for a, b in zip(ins, outs):
        a.wait()
        b.start()
    for cp in outs + smalls:
        cp.wait()


def fused(
    tokens, cotangent, group, select, w_qkv, b_query, b_value, w_out, b_out, w_up, b_up, w_down,
    b_down, ln1_gain, ln1_bias, ln2_gain, ln2_bias, w_router,
):
    args = (
        tokens, cotangent, group, select, w_qkv, b_query, b_value, w_out, b_out, w_up, b_up, w_down,
        b_down, ln1_gain, ln1_bias, ln2_gain, ln2_bias, w_router,
    )
    anywhere = pl.BlockSpec(memory_space=pl.ANY)
    shape = jax.ShapeDtypeStruct
    mids = (
        shape((1, OWN, WIDTH), bf16), shape((1, OWN, WIDTH), bf16), shape((48, 3 * WIDTH), f32),
        shape((48, WIDTH), f32), shape((48, HIDDEN), f32), shape((192, WIDTH), f32),
        shape((SMALL, WIDTH), f32),
    )
    v = pltpu.VMEM
    sq = (PAD_LEN, WIDTH)
    scratch = [
        v(sq, bf16), v(sq, bf16), v((2, 1, OWN), jnp.int32), v((9, 1, WIDTH), f32), v((1, HIDDEN), f32),
        v(sq, bf16), v((WIDTH, 3 * HALF), bf16), v((WIDTH, WIDTH), bf16), v((WIDTH, HID), bf16),
        v((HID, WIDTH), bf16), v((PAD_LEN, 3 * HALF), bf16), v((2 * PAIRS, PAD_LEN, PAD_LEN), bf16),
        v((2, PAD_LEN, HALF), bf16), v(sq, f32), v(sq, bf16), v(sq, bf16), v((PAD_LEN, 128), bf16), v((PAD_LEN, 128), bf16),
        v((PAD_LEN, 1), f32), v((PAD_LEN, 1), f32),
        v((PAD_LEN, HALF), bf16), v((PAD_LEN, HALF), bf16), v(sq, f32), v(sq, f32), v(sq, bf16), v(sq, bf16),
        v((OWN, WIDTH), bf16), v((OWN, WIDTH), bf16), v(sq, bf16), v((PAD_LEN, HALF), bf16),
        v((PAD_LEN, 3 * HALF), bf16), v((128, PAD_LEN), f32), v((128, PAD_LEN), f32),
        v((PAD_LEN, HALF), f32), v((WIDTH, PAD_LEN), bf16), v((OWN, WIDTH), bf16),
        v((SMALL, WIDTH), f32), v((4, 8, WIDTH), f32), v((6, 8, WIDTH), f32),
    ] + [v(*b) for name in PIECES for b in piece_shapes(name)] + [
        pltpu.SemaphoreType.DMA((N_LOADS + 4,)),
        pltpu.SemaphoreType.DMA((9,)), pltpu.SemaphoreType.DMA((9,)),
        pltpu.SemaphoreType.DMA((first_slot(None, 0),)), pltpu.SemaphoreType.DMA((first_slot(None, 0),)),
        pltpu.SemaphoreType.DMA((7,)), pltpu.SemaphoreType.DMA((7,)),
        pltpu.SemaphoreType.DMA((len(PIECES),)), pltpu.SemaphoreType.DMA((len(PIECES),)),
    ]
    mid = pl.pallas_call(
        layer_kernel,
        out_shape=mids,
        in_specs=[anywhere, anywhere, pl.BlockSpec(memory_space=pltpu.SMEM)] + [anywhere] * 15,
        out_specs=[anywhere] * 7,
        scratch_shapes=scratch,
        compiler_params=pltpu.CompilerParams(
            collective_id=0, has_side_effects=True, vmem_limit_bytes=60 << 20
        ),
        name="layer",
    )(*args)
    outs = (
        mids[0], mids[1], mids[2], shape((1, 48), f32), shape((1, 48), f32), mids[3], shape((1, 48), f32),
        mids[4], shape((1, 192), f32), mids[5],
    ) + (shape((1, 48), f32),) * 6 + (shape((3, 16), f32),)
    out = pl.pallas_call(
        place_kernel,
        out_shape=outs,
        in_specs=[anywhere] * 7,
        out_specs=[anywhere] * 17,
        scratch_shapes=[v(m.shape, m.dtype) for m in mids]
        + [v((9, 1, 48), f32), v((1, 192), f32), v((3, 16), f32), pltpu.SemaphoreType.DMA((24,))],
        name="place",
    )(*mid)
    return tuple(o.reshape(-1) if o.shape[0] == 1 and o.ndim == 2 else o for o in out[:16]) + (out[16].T,)


def norm_rows(values, norm_gain, norm_shift):
    average = jnp.mean(values, axis=-1, keepdims=True)
    centred = values - average
    variance = jnp.mean(centred * centred, axis=-1, keepdims=True)
    return centred * lax.rsqrt(variance + epsilon) * norm_gain + norm_shift


def places_of(group, slot_pos):
    short_place = jnp.minimum(slot_pos // SHORT_LEN, 2)
    return jnp.where(group[:, None] == 1, 0, short_place[None, :])


def split_heads(flat_rows):
    return flat_rows.reshape(flat_rows.shape[0], flat_rows.shape[1], HEADS, HEAD_DIM)


def masked_scores(queries, key_heads, query_place, key_place, key_mask):
    score_scale = HEAD_DIM ** (-0.5)
    scores = (
        jnp.einsum("bqhe,bkhe->bqhk", queries, key_heads, preferred_element_type=jnp.float32)
        * score_scale
    )
    key_live = (key_mask.astype(jnp.float32)[:, None, None, :] > 0.5) & (
        query_place[:, :, None, None] == key_place[:, None, None, :]
    )
    return (jnp.where(key_live, scores, masked_floor), key_live.astype(jnp.float32))


def attend(queries, key_heads, value_heads, query_place, key_place, key_mask):
    masked, key_weight = masked_scores(queries, key_heads, query_place, key_place, key_mask)
    row_max = jnp.max(masked, axis=-1, keepdims=True)
    exponent = jnp.exp(masked - row_max) * key_weight
    row_sum = jnp.sum(exponent, axis=-1, keepdims=True)
    weights = (exponent / row_sum).astype(jnp.bfloat16)
    mixed_heads = jnp.einsum(
        "bqhk,bkhe->bqhe", weights, value_heads, preferred_element_type=jnp.float32
    )
    return (mixed_heads, row_max + jnp.log(row_sum))


def back_parts(
    queries, key_heads, value_heads, query_place, key_place, key_mask, log_total, grad_heads, delta
):
    masked, key_weight = masked_scores(queries, key_heads, query_place, key_place, key_mask)
    key_probs = jnp.exp(masked - log_total) * key_weight
    grad_probs = jnp.einsum(
        "bqhe,bkhe->bqhk", grad_heads, value_heads, preferred_element_type=jnp.float32
    )
    delta = jnp.sum(key_probs * grad_probs, axis=-1, keepdims=True)
    grad_scores = (key_probs * (grad_probs - delta)).astype(jnp.bfloat16)
    return (key_probs, grad_scores, delta)


def key_side_grads(key_probs, grad_scores, queries, grad_heads):
    score_scale = HEAD_DIM ** (-0.5)
    grad_values = jnp.einsum(
        "bqhk,bqhe->bkhe",
        key_probs.astype(jnp.bfloat16),
        grad_heads,
        preferred_element_type=jnp.float32,
    )
    grad_keys = (
        jnp.einsum("bqhk,bqhe->bkhe", grad_scores, queries, preferred_element_type=jnp.float32)
        * score_scale
    )
    return (grad_keys, grad_values)


def on_device(
    tokens,
    cotangent,
    group,
    select,
    w_qkv,
    b_query,
    b_value,
    w_out,
    b_out,
    w_up,
    b_up,
    w_down,
    b_down,
    ln1_gain,
    ln1_bias,
    ln2_gain,
    ln2_bias,
    w_router,
):
    packs, per_piece, features = tokens.shape
    row_count = packs * per_piece
    first_pos = lax.axis_index("seq") * per_piece
    positions = first_pos + jnp.arange(per_piece, dtype=jnp.int32)
    full_positions = jnp.arange(PAD_LEN, dtype=jnp.int32)
    place_own = places_of(group, positions)
    place_full = places_of(group, full_positions)
    ends = jnp.where(group == 1, LONG_LEN, 3 * SHORT_LEN).astype(jnp.int32)
    active = ((select > 0) & (positions[None, :] < ends[:, None])).astype(jnp.float32)
    active_rows = active.reshape(row_count, 1)
    xfloat = tokens.reshape(row_count, features).astype(jnp.float32)
    router = jax.nn.sigmoid(jnp.dot(xfloat, w_router, precision=lax.Precision.HIGHEST))
    normed, first_back = jax.vjp(norm_rows, xfloat, ln1_gain, ln1_bias)
    normed_low = normed.astype(jnp.bfloat16)
    qkv_bias = jnp.concatenate([b_query, jnp.zeros_like(b_query), b_value])
    triple = (jnp.dot(normed_low, w_qkv, preferred_element_type=jnp.float32) + qkv_bias).astype(
        jnp.bfloat16
    )
    queries = triple[:, :features].reshape(packs, per_piece, HEADS, HEAD_DIM)
    keys_own = triple[:, features : 2 * features].reshape(packs, per_piece, features)
    values_own = triple[:, 2 * features :].reshape(packs, per_piece, features)
    mask_own = active.astype(jnp.bfloat16)
    keys_all, values_all, mask_all = (
        lax.all_gather(keys_own, "seq", axis=1, tiled=True),
        lax.all_gather(values_own, "seq", axis=1, tiled=True),
        lax.all_gather(mask_own, "seq", axis=1, tiled=True),
    )
    mixed_heads, log_total = attend(
        queries, split_heads(keys_all), split_heads(values_all), place_own, place_full, mask_all
    )
    mixed_low = mixed_heads.reshape(row_count, features).astype(jnp.bfloat16)
    attended = jnp.dot(mixed_low, w_out, preferred_element_type=jnp.float32) + b_out
    summed = xfloat + attended
    second, second_back = jax.vjp(norm_rows, summed, ln2_gain, ln2_bias)
    second_low = second.astype(jnp.bfloat16)
    pre_act = jnp.dot(second_low, w_up, preferred_element_type=jnp.float32) + b_up
    gelu_out, gelu_back = jax.vjp(partial(jax.nn.gelu, approximate=False), pre_act)
    hidden_low = gelu_out.astype(jnp.bfloat16)
    branch = attended + (jnp.dot(hidden_low, w_down, preferred_element_type=jnp.float32) + b_down)
    gate_rows = active_rows * router[:, None]
    output = (xfloat + gate_rows * branch).astype(jnp.bfloat16).reshape(packs, per_piece, features)
    place_range = jnp.arange(3, dtype=jnp.int32)
    onehot = (place_full[:, :, None] == place_range[None, None, :]).astype(jnp.float32)
    counts = jnp.sum(mask_all.astype(jnp.float32)[:, :, None] * onehot, axis=1)
    image_lengths = jnp.where(group == 1, LONG_LEN, SHORT_LEN).astype(jnp.float32)
    fractions = lax.all_gather(counts / image_lengths[:, None], "dp", axis=0, tiled=True)
    grad_rows = cotangent.reshape(row_count, features).astype(jnp.float32)
    grad_logit = jnp.sum(grad_rows * branch, axis=1) * active_rows[:, 0] * router * (1.0 - router)
    grad_branch = gate_rows * grad_rows
    grad_mlp = grad_branch.astype(jnp.bfloat16)
    grad_down = jnp.einsum("rk,rd->kd", hidden_low, grad_mlp, preferred_element_type=jnp.float32)
    grad_down_bias = jnp.sum(grad_mlp.astype(jnp.float32), axis=0)
    grad_hidden = jnp.einsum("rd,kd->rk", grad_mlp, w_down, preferred_element_type=jnp.float32)
    grad_pre = gelu_back(grad_hidden)[0].astype(jnp.bfloat16)
    grad_up = jnp.einsum("rd,rk->dk", second_low, grad_pre, preferred_element_type=jnp.float32)
    grad_up_bias = jnp.sum(grad_pre.astype(jnp.float32), axis=0)
    grad_second = jnp.einsum("rk,dk->rd", grad_pre, w_up, preferred_element_type=jnp.float32)
    grad_summed, grad_ln2_gain, grad_ln2_bias = second_back(grad_second)
    grad_attended = (grad_branch + grad_summed).astype(jnp.bfloat16)
    grad_out = jnp.einsum("rd,re->de", mixed_low, grad_attended, preferred_element_type=jnp.float32)
    grad_out_bias = jnp.sum(grad_attended.astype(jnp.float32), axis=0)
    grad_mixed = jnp.einsum("re,de->rd", grad_attended, w_out, preferred_element_type=jnp.float32)
    grad_heads = grad_mixed.astype(jnp.bfloat16).reshape(packs, per_piece, HEADS, HEAD_DIM)
    back_k, back_v, back_m = (
        lax.all_gather(keys_own, "seq", axis=1, tiled=True),
        lax.all_gather(values_own, "seq", axis=1, tiled=True),
        lax.all_gather(mask_own, "seq", axis=1, tiled=True),
    )
    back_kh = split_heads(back_k)
    back_vh = split_heads(back_v)
    key_probs, grad_scores, delta = back_parts(
        queries, back_kh, back_vh, place_own, place_full, back_m, log_total, grad_heads, None
    )
    grad_queries = jnp.einsum(
        "bqhk,bkhe->bqhe", grad_scores, back_kh, preferred_element_type=jnp.float32
    ) * HEAD_DIM ** (-0.5)
    grad_keys, grad_values = key_side_grads(key_probs, grad_scores, queries, grad_heads)
    keys_grad_own, values_grad_own = (
        lax.psum_scatter(
            grad_keys.reshape(back_k.shape).astype(jnp.bfloat16),
            "seq",
            scatter_dimension=1,
            tiled=True,
        ).astype(jnp.float32),
        lax.psum_scatter(
            grad_values.reshape(back_v.shape).astype(jnp.bfloat16),
            "seq",
            scatter_dimension=1,
            tiled=True,
        ).astype(jnp.float32),
    )
    grad_triple = jnp.concatenate(
        [
            grad_queries.reshape(row_count, features),
            keys_grad_own.reshape(row_count, features),
            values_grad_own.reshape(row_count, features),
        ],
        axis=1,
    ).astype(jnp.bfloat16)
    grad_qkv = jnp.einsum("rd,rk->dk", normed_low, grad_triple, preferred_element_type=jnp.float32)
    column_sums = jnp.sum(grad_triple.astype(jnp.float32), axis=0)
    grad_query_bias = column_sums[:features]
    grad_value_bias = column_sums[2 * features :]
    grad_normed = jnp.einsum("rk,dk->rd", grad_triple, w_qkv, preferred_element_type=jnp.float32)
    grad_first, grad_ln1_gain, grad_ln1_bias = first_back(grad_normed)
    grad_router = jnp.dot(grad_logit, xfloat, precision=lax.Precision.HIGHEST)
    grad_input = grad_rows + grad_summed + grad_first + grad_logit[:, None] * w_router[None, :]
    input_grad = grad_input.astype(jnp.bfloat16).reshape(packs, per_piece, features)
    (
        share_qkv,
        share_query_bias,
        share_value_bias,
        share_out,
        share_out_bias,
        share_up,
        share_up_bias,
        share_down,
        share_down_bias,
        share_ln1_gain,
        share_ln1_bias,
        share_ln2_gain,
        share_ln2_bias,
        share_router,
    ) = (
        lax.psum_scatter(
            grad_qkv.astype(jnp.bfloat16), "dp", scatter_dimension=0, tiled=True
        ).astype(jnp.float32),
        lax.psum_scatter(
            grad_query_bias.astype(jnp.bfloat16), "dp", scatter_dimension=0, tiled=True
        ).astype(jnp.float32),
        lax.psum_scatter(
            grad_value_bias.astype(jnp.bfloat16), "dp", scatter_dimension=0, tiled=True
        ).astype(jnp.float32),
        lax.psum_scatter(
            grad_out.astype(jnp.bfloat16), "dp", scatter_dimension=0, tiled=True
        ).astype(jnp.float32),
        lax.psum_scatter(
            grad_out_bias.astype(jnp.bfloat16), "dp", scatter_dimension=0, tiled=True
        ).astype(jnp.float32),
        lax.psum_scatter(
            grad_up.astype(jnp.bfloat16), "dp", scatter_dimension=0, tiled=True
        ).astype(jnp.float32),
        lax.psum_scatter(
            grad_up_bias.astype(jnp.bfloat16), "dp", scatter_dimension=0, tiled=True
        ).astype(jnp.float32),
        lax.psum_scatter(
            grad_down.astype(jnp.bfloat16), "dp", scatter_dimension=0, tiled=True
        ).astype(jnp.float32),
        lax.psum_scatter(
            grad_down_bias.astype(jnp.bfloat16), "dp", scatter_dimension=0, tiled=True
        ).astype(jnp.float32),
        lax.psum_scatter(
            grad_ln1_gain.astype(jnp.bfloat16), "dp", scatter_dimension=0, tiled=True
        ).astype(jnp.float32),
        lax.psum_scatter(
            grad_ln1_bias.astype(jnp.bfloat16), "dp", scatter_dimension=0, tiled=True
        ).astype(jnp.float32),
        lax.psum_scatter(
            grad_ln2_gain.astype(jnp.bfloat16), "dp", scatter_dimension=0, tiled=True
        ).astype(jnp.float32),
        lax.psum_scatter(
            grad_ln2_bias.astype(jnp.bfloat16), "dp", scatter_dimension=0, tiled=True
        ).astype(jnp.float32),
        lax.psum_scatter(
            grad_router.astype(jnp.bfloat16), "dp", scatter_dimension=0, tiled=True
        ).astype(jnp.float32),
    )
    totals = (
        lax.psum(share_qkv.astype(jnp.bfloat16), "seq").astype(jnp.float32),
        lax.psum(share_query_bias.astype(jnp.bfloat16), "seq").astype(jnp.float32),
        lax.psum(share_value_bias.astype(jnp.bfloat16), "seq").astype(jnp.float32),
        lax.psum(share_out.astype(jnp.bfloat16), "seq").astype(jnp.float32),
        lax.psum(share_out_bias.astype(jnp.bfloat16), "seq").astype(jnp.float32),
        lax.psum(share_up.astype(jnp.bfloat16), "seq").astype(jnp.float32),
        lax.psum(share_up_bias.astype(jnp.bfloat16), "seq").astype(jnp.float32),
        lax.psum(share_down.astype(jnp.bfloat16), "seq").astype(jnp.float32),
        lax.psum(share_down_bias.astype(jnp.bfloat16), "seq").astype(jnp.float32),
        lax.psum(share_ln1_gain.astype(jnp.bfloat16), "seq").astype(jnp.float32),
        lax.psum(share_ln1_bias.astype(jnp.bfloat16), "seq").astype(jnp.float32),
        lax.psum(share_ln2_gain.astype(jnp.bfloat16), "seq").astype(jnp.float32),
        lax.psum(share_ln2_bias.astype(jnp.bfloat16), "seq").astype(jnp.float32),
        lax.psum(share_router.astype(jnp.bfloat16), "seq").astype(jnp.float32),
    )
    return (
        output,
        input_grad,
        totals[0],
        totals[1],
        totals[2],
        totals[3],
        totals[4],
        totals[5],
        totals[6],
        totals[7],
        totals[8],
        totals[9],
        totals[10],
        totals[11],
        totals[12],
        totals[13],
        fractions,
    )


def solution(mesh):
    in_specs = (
        P("dp", "seq", None),
        P("dp", "seq", None),
        P("dp"),
        P("dp", "seq"),
        P(),
        P(),
        P(),
        P(),
        P(),
        P(),
        P(),
        P(),
        P(),
        P(),
        P(),
        P(),
        P(),
        P(),
    )
    out_specs = (
        P("dp", "seq", None),
        P("dp", "seq", None),
        P("dp", None),
        P("dp"),
        P("dp"),
        P("dp", None),
        P("dp"),
        P("dp", None),
        P("dp"),
        P("dp", None),
        P("dp"),
        P("dp"),
        P("dp"),
        P("dp"),
        P("dp"),
        P("dp"),
        P(),
    )
    fast = mesh.shape["dp"] == 16 and mesh.shape["seq"] == 2
    return jax.shard_map(
        fused if fast else on_device, mesh=mesh, in_specs=in_specs, out_specs=out_specs, check_vma=False
    )
```
